32 devices in a mesh: dp: 16 (over z, x, core), tensor: 2 (over y).
Axes of the slice: x: 2, y: 2, z: 4, core: 2. Of those that a mesh axis runs over, the one named last changes fastest.
Arguments:
- tokens: bfloat16 [18688, 1024], P(('dp', 'tensor')), may hold values from -6 to 6
- cotangent: bfloat16 [18688, 1024], P(('dp', 'tensor')), may hold values from -6 to 6
- token_valid: int32 [32, 584], P('dp'), may hold values 0 or 1
- image_valid: int32 [32], P('dp'), may hold values 0 or 1
- first_gain: bfloat16 [1024], P('dp'), may hold values from 0.25 to 1.75
- first_shift: bfloat16 [1024], P('dp'), may hold values from -3 to 3
- input_weight: bfloat16 [1024, 3, 1024], P('dp', None, 'tensor'), may hold values from -0.1875 to 0.1875
- input_bias: bfloat16 [2, 1024], P(None, 'tensor'), may hold values from -3 to 3
- output_weight: bfloat16 [1024, 1024], P('tensor', 'dp'), may hold values from -0.75 to 0.75
- output_bias: bfloat16 [1024], P('dp'), may hold values from -3 to 3
- second_gain: bfloat16 [1024], P('dp'), may hold values from 0.25 to 1.75
- second_shift: bfloat16 [1024], P('dp'), may hold values from -3 to 3
- up_weight: bfloat16 [1024, 4096], P('dp', 'tensor'), may hold values from -0.1875 to 0.1875
- up_bias: bfloat16 [4096], P('tensor'), may hold values from -3 to 3
- down_weight: bfloat16 [4096, 1024], P('tensor', 'dp'), may hold values from -0.09375 to 0.09375
- down_bias: bfloat16 [1024], P('dp'), may hold values from -3 to 3
Outputs:
- block_out: bfloat16 [18688, 1024], P(('dp', 'tensor'))
- grad_tokens: float32 [18688, 1024], P(('dp', 'tensor'))
- grad_first_gain: float32 [1024], P('dp')
- grad_first_shift: float32 [1024], P('dp')
- grad_input_weight: float32 [1024, 3, 1024], P('dp', None, 'tensor')
- grad_input_bias: float32 [2, 1024], P(None, 'tensor')
- grad_output_weight: float32 [1024, 1024], P('tensor', 'dp')
- grad_output_bias: float32 [1024], P('dp')
- grad_second_gain: float32 [1024], P('dp')
- grad_second_shift: float32 [1024], P('dp')
- grad_up_weight: float32 [1024, 4096], P('dp', 'tensor')
- grad_up_bias: float32 [4096], P('tensor')
- grad_down_weight: float32 [4096, 1024], P('tensor', 'dp')
- grad_down_bias: float32 [1024], P('dp')
The draws below stay inside these ranges and needn't reach their ends.
All inputs are finite; a program needn't handle non-finite values. No bound on the sum of `token_valid` or of `image_valid` on one device may be relied on, other than what follows from the above.
Results may differ from the reference program's by a relative error of at most 0.018.
Values may be sent and summed in bfloat16 or wider, within the bound.
A program may use at most 192 MiB of HBM per device.

```python
import jax
import jax.numpy as jnp
from jax import lax

D = 1024
HEADS = 16
HEAD_DIM = 64
FF = 4096
SEQ = 584
IMG_TEN = 1
IMAGES = 32
TOKENS = 18688
N_TENSOR = 2


def place_ends(array, stream_key, low, largest):
    shape = array.shape
    spot = [jax.random.randint(jax.random.fold_in(stream_key, axis), (), 0, shape[axis]) for axis in range(len(shape))]
    array = array.at[tuple(spot)].set(low)
    longest = shape.index(max(shape))
    spot[longest] = (spot[longest] + 1) % shape[longest]
    return array.at[tuple(spot)].set(largest)


def shard_levels(stream_key, dims, shards, smallest, top_value):
    factor_of, own = 1.0, jax.random.fold_in(stream_key, 6)
    for axis_at, blocks in shards:
        heights = jnp.exp(jax.random.uniform(jax.random.fold_in(own, axis_at), (blocks,), jnp.float32, smallest / len(shards), top_value / len(shards)))
        factor_of = factor_of * jnp.repeat(heights, dims[axis_at] // blocks).reshape([-1 if axis == axis_at else 1 for axis in range(len(dims))])
    return factor_of


def normal_values(stream_key, shape, deviation, bound, cuts=(), kind=jnp.bfloat16):
    values = jax.random.normal(stream_key, shape, jnp.float32) * deviation
    if len(cuts) > 0:
        values = shard_levels(stream_key, shape, cuts, -0.22, 0.18) * values
    return jnp.clip(values, min=-bound, max=bound).astype(kind)


def setup_inputs(seed: int = 0) -> dict:
    splits = jax.random.split(jax.random.key(seed), 17)
    return {
        "tokens": normal_values(splits[0], (TOKENS, D), 1.0, 6.0, ((0, 32),)),
        "cotangent": normal_values(splits[1], (TOKENS, D), 1.0, 6.0, ((0, 32),)),
        "token_valid": place_ends((jax.random.randint(splits[2], (IMAGES, SEQ), 0, 584) < 577).astype(jnp.int32), jax.random.fold_in(splits[2], 1), 0, 1),
        "image_valid": place_ends((jax.random.randint(splits[3], (IMAGES,), 0, 64) < 61).astype(jnp.int32), jax.random.fold_in(splits[3], 1), 0, 1),
        "first_gain": jnp.clip(1.0 + 0.15 * jax.random.normal(splits[4], (D,), jnp.float32), 0.25, 1.75).astype(jnp.bfloat16),
        "first_shift": normal_values(splits[5], (D,), 0.5, 3.0, ((0, 16),)),
        "input_weight": normal_values(splits[6], (D, 3, D), D ** -0.5, 0.1875, ((0, 16), (2, 2))),
        "input_bias": normal_values(splits[7], (2, D), 0.5, 3.0, ((1, 2),)),
        "output_weight": normal_values(splits[8], (D, D), (D // 16) ** -0.5, 0.75, ((0, 2), (1, 16))),
        "output_bias": normal_values(splits[9], (D,), 0.5, 3.0, ((0, 16),)),
        "second_gain": jnp.clip(1.0 + 0.15 * jax.random.normal(splits[10], (D,), jnp.float32), 0.25, 1.75).astype(jnp.bfloat16),
        "second_shift": normal_values(splits[11], (D,), 0.5, 3.0, ((0, 16),)),
        "up_weight": normal_values(splits[12], (D, FF), D ** -0.5, 0.1875, ((0, 16), (1, 2))),
        "up_bias": normal_values(splits[13], (FF,), 0.5, 3.0, ((0, 2),)),
        "down_weight": normal_values(splits[14], (FF, D), FF ** -0.5, 0.09375, ((0, 2), (1, 16))),
        "down_bias": normal_values(splits[15], (D,), 0.5, 3.0, ((0, 16),)),
    }


@jax.custom_vjp
def low(v):
    return lax.optimization_barrier(v.astype(jnp.bfloat16)).astype(jnp.float32)

@jax.custom_vjp
def low_back(v):
    return v

def low_keep(v):
    return (low(v), None)

def low_pass(kept, grad):
    return (grad,)

def back_keep(v):
    return (v, None)

def back_low(kept, grad):
    return (low(grad),)
low.defvjp(low_keep, low_pass)
low_back.defvjp(back_keep, back_low)

def layer_norm(inputs, gain, shift):
    center = inputs - lax.optimization_barrier(jnp.mean(inputs, axis=-1, keepdims=True))
    spread = lax.optimization_barrier(jnp.mean(center * center, axis=-1, keepdims=True))
    return center * lax.rsqrt(spread + 1e-06) * gain + shift

def group_forward(params, inputs, key_ok, row_mask):
    first_gain, first_shift, input_weight, input_bias, output_weight, output_bias, second_gain, second_shift, up_weight, up_bias, down_weight, down_bias = params
    highest = lax.Precision.HIGHEST
    images = inputs.shape[0]
    first = low(layer_norm(inputs, first_gain, first_shift))
    project = jnp.einsum('gsd,dce->gsce', first, input_weight, precision=highest)
    queries = low(low_back(project[:, :, 0] + input_bias[0]))
    keyset = low(low_back(project[:, :, 1]))
    values = low(low_back(project[:, :, 2] + input_bias[1]))
    head_shape = (images, SEQ, HEADS, HEAD_DIM)
    scores = jnp.einsum('gqhe,gkhe->ghqk', queries.reshape(head_shape), keyset.reshape(head_shape), precision=highest) * HEAD_DIM ** (-0.5)
    scores = low_back(scores)
    scores = jnp.where(key_ok[:, None, None, :], scores, -1000000000.0)
    log_total = jax.nn.logsumexp(scores, axis=-1, keepdims=True)
    attn_probs = low(jnp.exp(scores - log_total))
    mixed = jnp.einsum('ghqk,gkhe->gqhe', attn_probs, values.reshape(head_shape), precision=highest)
    mixed = low(low_back(mixed.reshape(images, SEQ, D)))
    parts = jnp.einsum('gsje,jed->gsjd', mixed.reshape(images, SEQ, N_TENSOR, D // N_TENSOR), output_weight.reshape(N_TENSOR, D // N_TENSOR, D), precision=highest)
    attended = low_back(lax.optimization_barrier(jnp.sum(low(parts), axis=2)))
    middle = inputs + attended + output_bias
    second = low(layer_norm(middle, second_gain, second_shift))
    hidden = low_back(jnp.einsum('gsd,df->gsf', second, up_weight, precision=highest) + up_bias)
    active = low(jax.nn.gelu(hidden, approximate=False))
    mlp_parts = jnp.einsum('gsjf,jfd->gsjd', active.reshape(images, SEQ, N_TENSOR, FF // N_TENSOR), down_weight.reshape(N_TENSOR, FF // N_TENSOR, D), precision=highest)
    lifted = low_back(lax.optimization_barrier(jnp.sum(low(mlp_parts), axis=2)))
    return row_mask[:, :, None] * (middle + lifted + down_bias)

def reference(tokens, cotangent, token_valid, image_valid, first_gain, first_shift, input_weight, input_bias, output_weight, output_bias, second_gain, second_shift, up_weight, up_bias, down_weight, down_bias):
    params = tuple((weight_arg.astype(jnp.float32) for weight_arg in (first_gain, first_shift, input_weight, input_bias, output_weight, output_bias, second_gain, second_shift, up_weight, up_bias, down_weight, down_bias)))
    groups = IMAGES // IMG_TEN
    inputs = tokens.astype(jnp.float32).reshape(groups, IMG_TEN, SEQ, D)
    positions = jnp.arange(SEQ, dtype=jnp.int32)
    key_ok = ((token_valid > 0) | (positions[None, :] == 0)).reshape(groups, IMG_TEN, SEQ)
    row_mask = (token_valid * image_valid[:, None]).astype(jnp.float32).reshape(groups, IMG_TEN, SEQ)

    def whole(weights, values_in):

        def one_group(pieces):
            return jax.checkpoint(group_forward)(weights, pieces[0], pieces[1], pieces[2])
        return lax.map(one_group, (values_in, key_ok, row_mask))
    outputs, pullback = jax.vjp(whole, params, inputs)
    grads, grad_inputs = pullback(cotangent.astype(jnp.float32).reshape(groups, IMG_TEN, SEQ, D))
    return (outputs.reshape(TOKENS, D).astype(jnp.bfloat16), grad_inputs.reshape(TOKENS, D), grads[0], grads[1], grads[2], grads[3], grads[4], grads[5], grads[6], grads[7], grads[8], grads[9], grads[10], grads[11])
```

```python
import functools

import jax
import jax.numpy as jnp
from jax import lax
from jax.experimental import pallas as pl
from jax.experimental.pallas import tpu as pltpu
from jax.sharding import PartitionSpec as P

HEAD_DIM = 64
MESH = pl.DeviceIdType.MESH
f32 = jnp.float32
bf16 = jnp.bfloat16

def layer_norm(inputs, gain, shift):
    center = inputs - jnp.mean(inputs, axis=-1, keepdims=True)
    spread = jnp.mean(center * center, axis=-1, keepdims=True)
    return center * lax.rsqrt(spread + 1e-06) * gain + shift


def norm_backward(inputs, gain, upstream):
    center = inputs - jnp.mean(inputs, axis=-1, keepdims=True)
    spread = jnp.mean(center * center, axis=-1, keepdims=True)
    scaled = lax.rsqrt(spread + 1e-06)
    unit = center * scaled
    weighted = upstream * gain
    grad_inputs = scaled * (
        weighted
        - jnp.mean(weighted, axis=-1, keepdims=True)
        - unit * jnp.mean(weighted * unit, axis=-1, keepdims=True)
    )
    return (grad_inputs, jnp.sum(upstream * unit, axis=0), jnp.sum(upstream, axis=0))


def gelu_slope(hidden):
    return (
        0.5 * (1.0 + lax.erf(hidden * 0.7071067811865476))
        + hidden * jnp.exp(-0.5 * hidden * hidden) * 0.3989422804014327
    )


def general_device(
    tokens,
    cotangent,
    token_valid,
    image_valid,
    first_gain,
    first_shift,
    input_weight,
    input_bias,
    output_weight,
    output_bias,
    second_gain,
    second_shift,
    up_weight,
    up_bias,
    down_weight,
    down_bias,
):
    f32 = jnp.float32
    bf16 = jnp.bfloat16
    gathered = (
        lax.all_gather(first_gain, "dp", axis=0, tiled=True),
        lax.all_gather(first_shift, "dp", axis=0, tiled=True),
        lax.all_gather(input_weight, "dp", axis=0, tiled=True),
        lax.all_gather(output_weight, "dp", axis=1, tiled=True),
        lax.all_gather(output_bias, "dp", axis=0, tiled=True),
        lax.all_gather(second_gain, "dp", axis=0, tiled=True),
        lax.all_gather(second_shift, "dp", axis=0, tiled=True),
        lax.all_gather(up_weight, "dp", axis=0, tiled=True),
        lax.all_gather(down_weight, "dp", axis=1, tiled=True),
        lax.all_gather(down_bias, "dp", axis=0, tiled=True),
    )
    (
        gain_one,
        shift_one,
        in_full,
        out_full,
        out_shift,
        gain_two,
        shift_two,
        up_full,
        down_full,
        down_shift,
    ) = gathered
    gain_one = gain_one.astype(f32)
    shift_one = shift_one.astype(f32)
    out_shift = out_shift.astype(f32)
    gain_two = gain_two.astype(f32)
    shift_two = shift_two.astype(f32)
    down_shift = down_shift.astype(f32)
    tensor_at = lax.axis_index("tensor")
    groups = lax.axis_size("tensor")
    own_rows = tokens.shape[0]
    width = tokens.shape[1]
    length = token_valid.shape[1]
    positions = lax.broadcasted_iota(jnp.int32, token_valid.shape, 1)
    key_ok = (token_valid > 0) | (positions == 0)
    mask_all = (token_valid * image_valid[:, None]).astype(f32).reshape(-1)
    row_mask = lax.dynamic_slice_in_dim(mask_all, tensor_at * own_rows, own_rows)[:, None]
    images = token_valid.shape[0]
    local_width = in_full.shape[2]
    local_heads = local_width // HEAD_DIM
    hidden_width = up_full.shape[1]
    scale = HEAD_DIM ** (-0.5)
    head_shape = (images, length, local_heads, HEAD_DIM)
    inputs = tokens.astype(f32)
    first_own = layer_norm(inputs, gain_one, shift_one).astype(bf16)
    first_all = lax.all_gather(first_own, "tensor", axis=0, tiled=True)
    project = jnp.einsum("rd,dce->rce", first_all, in_full, preferred_element_type=f32)
    bias_in = input_bias.astype(f32)
    queries = (project[:, 0] + bias_in[0]).astype(bf16).reshape(head_shape)
    keyset = project[:, 1].astype(bf16).reshape(head_shape)
    values = (project[:, 2] + bias_in[1]).astype(bf16).reshape(head_shape)

    def scores_of(query_img, key_img, ok_img):
        scores = jnp.einsum("qhe,khe->hqk", query_img, key_img, preferred_element_type=f32) * scale
        return jnp.where(ok_img[None, None, :], scores, -1000000000.0)

    def attend(pieces):
        query_img, key_img, value_img, ok_img = pieces
        scores = scores_of(query_img, key_img, ok_img)
        highest = jnp.max(scores, axis=-1, keepdims=True)
        log_total = highest + jnp.log(jnp.sum(jnp.exp(scores - highest), axis=-1, keepdims=True))
        attn_probs = jnp.exp(scores - log_total).astype(bf16)
        mixed_img = jnp.einsum("hqk,khe->qhe", attn_probs, value_img, preferred_element_type=f32)
        return (mixed_img.astype(bf16), log_total)

    mixed, log_totals = lax.map(attend, (queries, keyset, values, key_ok))
    mixed_rows = mixed.reshape(images * length, local_width)
    attended = lax.psum_scatter(
        jnp.dot(mixed_rows, out_full, preferred_element_type=f32).astype(jnp.bfloat16),
        "tensor",
        scatter_dimension=0,
        tiled=True,
    ).astype(jnp.float32)
    middle = inputs + attended + out_shift
    second_own = layer_norm(middle, gain_two, shift_two).astype(bf16)
    second_all = lax.all_gather(second_own, "tensor", axis=0, tiled=True)
    hidden = jnp.dot(second_all, up_full, preferred_element_type=f32) + up_bias.astype(f32)
    active = jax.nn.gelu(hidden, approximate=False).astype(bf16)
    lifted = lax.psum_scatter(
        jnp.dot(active, down_full, preferred_element_type=f32).astype(jnp.bfloat16),
        "tensor",
        scatter_dimension=0,
        tiled=True,
    ).astype(jnp.float32)
    block_out = (row_mask * (middle + lifted + down_shift)).astype(bf16)
    grad_last = row_mask * cotangent.astype(f32)
    first_all, second_all = (
        lax.all_gather(first_own, "tensor", axis=0, tiled=True),
        lax.all_gather(second_own, "tensor", axis=0, tiled=True),
    )
    grad_lift = lax.all_gather(grad_last.astype(bf16), "tensor", axis=0, tiled=True)
    grad_active = jnp.einsum("rd,fd->rf", grad_lift, down_full, preferred_element_type=f32)
    grad_hidden = (grad_active * gelu_slope(hidden)).astype(bf16)
    grad_down = jnp.einsum("rf,rd->fd", active, grad_lift, preferred_element_type=f32)
    grad_up = jnp.einsum("rd,rf->df", second_all, grad_hidden, preferred_element_type=f32)
    grad_up_bias = jnp.sum(grad_hidden.astype(f32), axis=0)
    grad_second = lax.psum_scatter(
        jnp.einsum("rf,df->rd", grad_hidden, up_full, preferred_element_type=f32).astype(
            jnp.bfloat16
        ),
        "tensor",
        scatter_dimension=0,
        tiled=True,
    ).astype(jnp.float32)
    grad_middle, grad_gain_two, grad_shift_two = norm_backward(middle, gain_two, grad_second)
    grad_middle = grad_middle + grad_last
    grad_mid_all = lax.all_gather(grad_middle.astype(bf16), "tensor", axis=0, tiled=True)
    grad_mixed = jnp.einsum("rd,ed->re", grad_mid_all, out_full, preferred_element_type=f32).astype(
        bf16
    )
    grad_out_weight = jnp.einsum("re,rd->ed", mixed_rows, grad_mid_all, preferred_element_type=f32)

    def attend_back(pieces):
        query_img, key_img, value_img, ok_img, total_img, grad_img = pieces
        scores = scores_of(query_img, key_img, ok_img)
        attn_probs = jnp.exp(scores - total_img)
        grad_values = jnp.einsum(
            "hqk,qhe->khe", attn_probs.astype(bf16), grad_img, preferred_element_type=f32
        )
        grad_probs = jnp.einsum("qhe,khe->hqk", grad_img, value_img, preferred_element_type=f32)
        grad_scores = (
            attn_probs * (grad_probs - jnp.sum(attn_probs * grad_probs, axis=-1, keepdims=True))
        ).astype(bf16)
        grad_queries = (
            jnp.einsum("hqk,khe->qhe", grad_scores, key_img, preferred_element_type=f32) * scale
        )
        grad_keys = (
            jnp.einsum("hqk,qhe->khe", grad_scores, query_img, preferred_element_type=f32) * scale
        )
        return jnp.stack([grad_queries, grad_keys, grad_values], axis=1).astype(bf16)

    grad_project = lax.map(
        attend_back, (queries, keyset, values, key_ok, log_totals, grad_mixed.reshape(head_shape))
    )
    grad_project = grad_project.reshape(images * length, 3, local_width)
    grad_in_weight = jnp.einsum("rd,rce->dce", first_all, grad_project, preferred_element_type=f32)
    grad_in_bias = jnp.sum(grad_project[:, 0::2].astype(f32), axis=0)
    grad_first = lax.psum_scatter(
        jnp.einsum("rce,dce->rd", grad_project, in_full, preferred_element_type=f32).astype(
            jnp.bfloat16
        ),
        "tensor",
        scatter_dimension=0,
        tiled=True,
    ).astype(jnp.float32)
    grad_inputs, grad_gain_one, grad_shift_one = norm_backward(inputs, gain_one, grad_first)
    grad_inputs = grad_inputs + grad_middle
    grad_in_own, grad_out_own, grad_up_own, grad_down_own = (
        lax.psum_scatter(
            grad_in_weight.astype(jnp.bfloat16), "dp", scatter_dimension=0, tiled=True
        ).astype(jnp.float32),
        lax.psum_scatter(
            grad_out_weight.astype(jnp.bfloat16), "dp", scatter_dimension=1, tiled=True
        ).astype(jnp.float32),
        lax.psum_scatter(
            grad_up.astype(jnp.bfloat16), "dp", scatter_dimension=0, tiled=True
        ).astype(jnp.float32),
        lax.psum_scatter(
            grad_down.astype(jnp.bfloat16), "dp", scatter_dimension=1, tiled=True
        ).astype(jnp.float32),
    )
    vectors = jnp.stack(
        [
            grad_gain_one,
            grad_shift_one,
            jnp.sum(grad_middle, axis=0),
            grad_gain_two,
            grad_shift_two,
            jnp.sum(grad_last, axis=0),
        ]
    )
    bias_share = input_bias.shape[1]
    up_share = up_bias.shape[0]
    placed_bias = lax.dynamic_update_slice(
        jnp.zeros((2, width), f32), grad_in_bias, (0, tensor_at * local_width)
    )
    placed_up = lax.dynamic_update_slice(
        jnp.zeros((hidden_width * groups,), f32), grad_up_bias, (tensor_at * hidden_width,)
    )
    vectors, placed_bias, placed_up = lax.psum((vectors, placed_bias, placed_up), ("dp", "tensor"))
    share = first_gain.shape[0]
    dp_at = lax.axis_index("dp")
    vectors = lax.dynamic_slice_in_dim(vectors, dp_at * share, share, 1)
    bias_own = lax.dynamic_slice_in_dim(placed_bias, tensor_at * bias_share, bias_share, 1)
    up_bias_own = lax.dynamic_slice_in_dim(placed_up, tensor_at * up_share, up_share, 0)
    return (
        block_out,
        grad_inputs,
        vectors[0],
        vectors[1],
        grad_in_own,
        bias_own,
        grad_out_own,
        vectors[2],
        vectors[3],
        vectors[4],
        grad_up_own,
        up_bias_own,
        grad_down_own,
        vectors[5],
    )


def split_of(n):
    a = (n * 4 // 7) // 128 * 128
    return a, n - a

class Place:
    def __init__(self, ring, n):
        d = lax.axis_index("dp")
        t = lax.axis_index("tensor")
        self.d, self.t, self.ring = d, t, ring
        self.chip, self.core = d // 2, d % 2
        half = ring // 2
        self.pos = jnp.where(self.chip % 2 == 0, self.chip // 2, ring - 1 - self.chip // 2)
        self.right = (self.chip_at(1) * 2 + self.core, t)
        self.left = (self.chip_at(-1) * 2 + self.core, t)
        self.across = (d, 1 - t)
        self.sibling = (d + 1 - 2 * self.core, t)
        a, b = split_of(n)
        self.n, self.a, self.b = n, a, b
        self.own_cols = (pl.multiple_of(t * n, 128), n)
        self.other_cols = (pl.multiple_of((1 - t) * n, 128), n)
        self.ring_cols = (pl.multiple_of(t * a, 128), 2 * n - a)
        self.mine_a = (pl.multiple_of(t * (2 * n - a), 128), a)
        self.their_a = (pl.multiple_of((1 - t) * (2 * n - a), 128), a)
        self.their_b = (pl.multiple_of(n - t * b, 128), b)
        self.mine_b = (pl.multiple_of(n - (1 - t) * b, 128), b)

    def chip_at(self, offset):
        ring = self.ring
        spot = (self.pos + offset + ring) % ring
        return jnp.where(spot < ring // 2, 2 * spot, 2 * (ring - 1 - spot) + 1)

def greet(targets):
    bar = pltpu.get_barrier_semaphore()
    for a in targets:
        pl.semaphore_signal(bar, inc=1, device_id=a, device_id_type=MESH)
    pl.semaphore_wait(bar, len(targets))

def rcopy(src, dst, sems, k, dev):
    return pltpu.make_async_remote_copy(src_ref=src, dst_ref=dst, send_sem=sems[0].at[k], recv_sem=sems[1].at[k],
        device_id=dev, device_id_type=MESH)

def ag_kernel(ring, sh, full, ring_s, ring_r, y_s, y_r, c_s, c_r, l_sem):
    rows, n = sh.shape
    w = Place(ring, n)
    half = rows // 2
    far = ring // 2
    greet((w.right, w.left, w.across, w.sibling))
    rs, ys, cs = (ring_s, ring_r), (y_s, y_r), (c_s, c_r)
    def block(offset, cols, lo=0, size=rows):
        base = w.chip_at(offset) * (2 * rows) + w.core * rows + lo
        return full.at[pl.ds(pl.multiple_of(base, 8), size), pl.ds(cols[0], cols[1])]
    pend = []
    def go(src, dst, sems, k, dev):
        cp = rcopy(src, dst, sems, k, dev); cp.start(); pend.append(cp); return cp
    own = block(0, w.own_cols)
    keep = pltpu.make_async_copy(sh, own, l_sem.at[0]); keep.start()
    y0 = go(sh, own, ys, 0, w.across)
    r1 = go(sh, own, rs, 0, w.right)
    l1 = go(sh, own, rs, 8, w.left)
    c0 = go(sh, own, cs, 0, w.sibling)
    y0.wait_recv()
    tb = block(0, w.their_b)
    r1b = go(tb, tb, rs, 1, w.right)
    l1b = go(tb, tb, rs, 9, w.left)
    ot = block(0, w.other_cols)
    c1 = go(ot, ot, cs, 1, w.sibling)
    crecv = [c0, c1]; yrecv = []
    arr_r, arr_l = [r1, r1b], [l1, l1b]
    ci = 2; yi = 1
    for s in range(1, far + 1):
        new_y = []
        lasts = s == far
        spans = []
        for dirn in (0, 1):
            arrived = arr_r if dirn == 0 else arr_l
            off = -s if dirn == 0 else s
            for cp in arrived: cp.wait_recv()
            lo, size = (0, rows) if not lasts else ((0, half) if dirn == 0 else (half, half))
            if s < far:
                nlo, nsize = (0, rows) if s + 1 < far else ((0, half) if dirn == 0 else (half, half))
                ref = block(off, w.ring_cols, nlo, nsize)
                cp = go(ref, ref, rs, dirn * 8 + 1 + s, w.right if dirn == 0 else w.left)
                if dirn == 0: arr_r = [cp]
                else: arr_l = [cp]
            ref = block(off, w.mine_a, lo, size)
            new_y.append((go(ref, ref, ys, yi, w.across), off, lo, size)); yi += 1
            ref = block(off, w.ring_cols, lo, size)
            crecv.append(go(ref, ref, cs, ci, w.sibling)); ci += 1
        for cp, off, lo, size in yrecv:
            cp.wait_recv()
            ref = block(off, w.their_a, lo, size)
            crecv.append(go(ref, ref, cs, ci, w.sibling)); ci += 1
        yrecv = new_y
    for cp, off, lo, size in yrecv:
        cp.wait_recv()
        ref = block(off, w.their_a, lo, size)
        crecv.append(go(ref, ref, cs, ci, w.sibling)); ci += 1
    for cp in crecv: cp.wait_recv()
    for cp in pend: cp.wait_send()
    keep.wait()

def gather_group(shard, dp, cid):
    rows, n = shard.shape
    ring = dp // 2
    dma = pltpu.SemaphoreType.DMA
    return pl.pallas_call(functools.partial(ag_kernel, ring),
        out_shape=jax.ShapeDtypeStruct((rows * dp, 2 * n), bf16),
        in_specs=[pl.BlockSpec(memory_space=pl.ANY)], out_specs=pl.BlockSpec(memory_space=pl.ANY),
        scratch_shapes=[dma((16,)), dma((16,)), dma((16,)), dma((16,)), dma((24,)), dma((24,)), dma((1,))],
        compiler_params=pltpu.CompilerParams(collective_id=cid, has_side_effects=True), name="gather_group")(shard)

def rs_kernel(ring, g, out, pv, rc, ry, rr, rl, rb, l_sem, c_s, c_r, y_s, y_r, ring_s, ring_r):
    _, _, rows, wide = g.shape
    n = wide // 2
    w = Place(ring, n)
    half = rows // 2
    far = ring // 2
    greet((w.right, w.left, w.across, w.sibling))
    cs, ys, rs = (c_s, c_r), (y_s, y_r), (ring_s, ring_r)
    pend = []
    def go(src, dst, sems, k, dev):
        cp = rcopy(src, dst, sems, k, dev); cp.start(); pend.append(cp); return cp
    order = [far]
    for k in range(far - 1, 0, -1): order += [k, -k]
    order.append(0)
    ccp, lcp, ycp = {}, {}, {}
    for i, k in enumerate(order):
        chip = w.chip_at(k)
        ccp[k] = go(g.at[chip, 1 - w.core], rc.at[i], cs, i, w.sibling)
        lcp[k] = pltpu.make_async_copy(g.at[chip, w.core], pv.at[i], l_sem.at[i]); lcp[k].start()
    def addto(ref, lo, size, cols, other):
        start, width = cols
        ch = 8 if size % 16 else 16
        @pl.loop(0, size // ch)
        def _(r):
            rw = pl.ds(pl.multiple_of(lo + r * ch, ch), ch)
            v = ref[rw, pl.ds(start, width)].astype(f32) + other[pl.ds(pl.multiple_of(lo + r * ch, ch), ch), :].astype(f32)
            ref[rw, pl.ds(start, width)] = v.astype(bf16)
    idx = {k: i for i, k in enumerate(order)}
    def core_add(k):
        i = idx[k]
        ccp[k].wait_recv(); lcp[k].wait()
        addto(pv.at[i], 0, rows, (0, wide), rc.at[i])
        ref = pv.at[i, :, pl.ds(w.their_a[0], w.a)]
        ycp[k] = go(ref, ry.at[i], ys, i, w.across)
    def y_add(k):
        i = idx[k]
        ycp[k].wait_recv()
        addto(pv.at[i], 0, rows, w.mine_a, ry.at[i])
    rcp = {}
    core_add(order[0])
    ringw = pl.ds(w.ring_cols[0], w.ring_cols[1])
    for j, k in enumerate(order):
        if j + 1 < len(order): core_add(order[j + 1])
        y_add(k)
        i = idx[k]
        if k == far:
            rcp["r", 0] = go(pv.at[i, pl.ds(0, half), ringw], rr.at[0, pl.ds(0, half)], rs, 0, w.right)
            rcp["l", 0] = go(pv.at[i, pl.ds(half, half), ringw], rl.at[0, pl.ds(half, half)], rs, 8, w.left)
            continue
        st = far - abs(k)
        if k > 0:
            rcp["r", st - 1].wait_recv()
            addto(pv.at[i], 0, half if st == 1 else rows, w.ring_cols, rr.at[st - 1])
            rcp["r", st] = go(pv.at[i, :, ringw], rr.at[st], rs, st, w.right)
        elif k < 0:
            rcp["l", st - 1].wait_recv()
            if st == 1: addto(pv.at[i], half, half, w.ring_cols, rl.at[0])
            else: addto(pv.at[i], 0, rows, w.ring_cols, rl.at[st - 1])
            rcp["l", st] = go(pv.at[i, :, ringw], rl.at[st], rs, 8 + st, w.left)
        else:
            rcp["r", far - 1].wait_recv(); rcp["l", far - 1].wait_recv()
            addto(pv.at[i], 0, rows, w.ring_cols, rr.at[far - 1])
            addto(pv.at[i], 0, rows, w.ring_cols, rl.at[far - 1])
            fin = go(pv.at[i, :, pl.ds(w.their_b[0], w.b)], rb, ys, len(order), w.across)
            fin.wait_recv()
            addto(pv.at[i], 0, rows, w.mine_b, rb)
            ch = 16
            @pl.loop(0, rows // ch)
            def _(r):
                rw = pl.ds(pl.multiple_of(r * ch, ch), ch)
                out[rw, :] = pv[i, rw, pl.ds(w.own_cols[0], n)].astype(f32)
    for cp in pend: cp.wait_send()

def scatter_group(g, dp, cid):
    depth, wide = g.shape
    rows = depth // dp
    n = wide // 2
    a, b = split_of(n)
    ring = dp // 2
    dma = pltpu.SemaphoreType.DMA
    V = pltpu.VMEM
    return pl.pallas_call(functools.partial(rs_kernel, ring),
        out_shape=jax.ShapeDtypeStruct((rows, n), f32),
        in_specs=[pl.BlockSpec(memory_space=pl.ANY)], out_specs=pl.BlockSpec(memory_space=pltpu.VMEM),
        scratch_shapes=[V((ring, rows, wide), bf16), V((ring, rows, wide), bf16), V((ring, rows, a), bf16),
            V((ring // 2, rows, 2 * n - a), bf16), V((ring // 2, rows, 2 * n - a), bf16), V((rows, b), bf16),
            dma((ring,)), dma((ring,)), dma((ring,)), dma((ring + 1,)), dma((ring + 1,)), dma((16,)), dma((16,))],
        compiler_params=pltpu.CompilerParams(collective_id=cid, has_side_effects=True, vmem_limit_bytes=56 << 20), name="scatter_group")(
        g.reshape(ring, 2, rows, wide))


def vec_kernel(dp, v, out, s_sem, r_sem, l_sem):
    d = lax.axis_index("dp")
    t = lax.axis_index("tensor")
    peers = [(lax.rem(d + i, dp), t) for i in range(1, dp)] + [(d, 1 - t)]
    greet(peers)
    keep = pltpu.make_async_copy(v, out.at[d], l_sem.at[0])
    keep.start()
    copies = []
    for i, a in enumerate(peers):
        slot = d if i < dp - 1 else dp
        cp = rcopy(v, out.at[slot], (s_sem, r_sem), i, a)
        cp.start()
        copies.append(cp)
    for cp in copies:
        cp.wait()
    keep.wait()


def gather_vectors(v, dp, cid):
    dma = pltpu.SemaphoreType.DMA
    return pl.pallas_call(
        functools.partial(vec_kernel, dp),
        out_shape=jax.ShapeDtypeStruct((dp + 1,) + v.shape, v.dtype),
        in_specs=[pl.BlockSpec(memory_space=pl.ANY)],
        out_specs=pl.BlockSpec(memory_space=pl.ANY),
        scratch_shapes=[dma((dp,)), dma((dp,)), dma((1,))],
        compiler_params=pltpu.CompilerParams(collective_id=cid, has_side_effects=True),
        name="gather_vectors",
    )(v)


def sum_kernel(dp, v, out, buf, s_sem, r_sem):
    d = lax.axis_index("dp")
    t = lax.axis_index("tensor")
    peers = [(d, 1 - t)]
    k = 1
    while k < dp:
        peers.append((d + k - 2 * k * ((d // k) % 2), t))
        k *= 2
    greet(peers)
    out[...] = v[...]
    for i, a in enumerate(peers):
        buf[i, 0] = out[...]
        cp = rcopy(buf.at[i, 0], buf.at[i, 1], (s_sem, r_sem), i, a)
        cp.start()
        cp.wait()
        out[...] = out[...] + buf[i, 1]


def sum_vectors(v, dp, cid):
    dma = pltpu.SemaphoreType.DMA
    steps = dp.bit_length()
    return pl.pallas_call(
        functools.partial(sum_kernel, dp),
        out_shape=jax.ShapeDtypeStruct(v.shape, v.dtype),
        in_specs=[pl.BlockSpec(memory_space=pltpu.VMEM)],
        out_specs=pl.BlockSpec(memory_space=pltpu.VMEM),
        scratch_shapes=[pltpu.VMEM((steps, 2) + v.shape, v.dtype), dma((steps,)), dma((steps,))],
        compiler_params=pltpu.CompilerParams(collective_id=cid, has_side_effects=True),
        name="sum_vectors",
    )(v)


def paired_device(
    tokens,
    cotangent,
    token_valid,
    image_valid,
    first_gain,
    first_shift,
    input_weight,
    input_bias,
    output_weight,
    output_bias,
    second_gain,
    second_shift,
    up_weight,
    up_bias,
    down_weight,
    down_bias,
):
    dp = lax.axis_size("dp")
    d = lax.axis_index("dp")
    t = lax.axis_index("tensor")
    length, width = tokens.shape
    share = first_gain.shape[0]
    cols = output_weight.shape[0]
    ff = up_weight.shape[1]
    heads = width // HEAD_DIM
    dot = functools.partial(jnp.einsum, preferred_element_type=f32)
    shard1 = jnp.concatenate([input_weight.reshape(share, 3 * cols), output_weight.T], axis=1)
    vec = jnp.concatenate(
        [first_gain, first_shift, output_bias, second_gain, second_shift, down_bias, up_bias, input_bias.reshape(-1)]
    )
    tail = -vec.shape[0] % 1024
    vec = jnp.concatenate([vec, jnp.zeros((tail,), bf16)]).reshape(8, -1)
    small = gather_vectors(vec, dp, 3).reshape(dp + 1, -1)
    per = small[:dp, : 6 * share].reshape(dp, 6, share).transpose(1, 0, 2).reshape(6, width).astype(f32)
    gain_one, shift_one, out_shift, gain_two, shift_two, down_shift = per
    own_b, other_b = vec.reshape(-1)[6 * share :], small[dp, 6 * share :]
    low_b = jnp.where(t == 0, own_b, other_b)
    high_b = jnp.where(t == 0, other_b, own_b)
    up_b = jnp.concatenate([low_b[:ff], high_b[:ff]]).astype(f32)
    in_b = jnp.concatenate(
        [low_b[ff : ff + 2 * cols].reshape(2, cols), high_b[ff : ff + 2 * cols].reshape(2, cols)], axis=1
    ).astype(f32)
    w1 = gather_group(shard1, dp, 1)
    w2 = gather_group(up_weight, dp, 1)
    w3 = gather_group(down_weight.T, dp, 1)
    tv = lax.dynamic_index_in_dim(token_valid, t, 0, keepdims=False)
    iv = lax.dynamic_index_in_dim(image_valid, t, 0, keepdims=False)
    key_ok = (tv > 0) | (jnp.arange(length) == 0)
    row_mask = (tv * iv).astype(f32)[:, None]
    scale = HEAD_DIM ** (-0.5)
    inputs = tokens.astype(f32)
    first = layer_norm(inputs, gain_one, shift_one).astype(bf16)
    proj = dot("rd,dc->rc", first, w1)

    def part(k):
        lo = k * cols
        return jnp.concatenate([proj[:, lo : lo + cols], proj[:, 4 * cols + lo : 5 * cols + lo]], axis=1)

    q = (part(0) + in_b[0]).astype(bf16).reshape(length, heads, HEAD_DIM)
    k = part(1).astype(bf16).reshape(length, heads, HEAD_DIM)
    v = (part(2) + in_b[1]).astype(bf16).reshape(length, heads, HEAD_DIM)
    wo = jnp.concatenate([w1[:, 3 * cols : 4 * cols], w1[:, 7 * cols :]], axis=1)
    scores = jnp.where(key_ok[None, None, :], dot("qhe,khe->hqk", q, k) * scale, -1000000000.0)
    highest = jnp.max(scores, axis=-1, keepdims=True)
    log_total = highest + jnp.log(jnp.sum(jnp.exp(scores - highest), axis=-1, keepdims=True))
    probs = jnp.exp(scores - log_total)
    mixed = dot("hqk,khe->qhe", probs.astype(bf16), v).astype(bf16).reshape(length, width)
    middle = inputs + dot("re,de->rd", mixed, wo) + out_shift
    second = layer_norm(middle, gain_two, shift_two).astype(bf16)
    hidden = dot("rd,df->rf", second, w2) + up_b
    active = jax.nn.gelu(hidden, approximate=False).astype(bf16)
    block_out = (row_mask * (middle + dot("rf,df->rd", active, w3) + down_shift)).astype(bf16)
    grad_last = row_mask * cotangent.astype(f32)
    gr = grad_last.astype(bf16)
    g3 = dot("rd,rf->df", gr, active).astype(bf16)
    dhid = (dot("rd,df->rf", gr, w3) * gelu_slope(hidden)).astype(bf16)
    g2 = dot("rd,rf->df", second, dhid).astype(bf16)
    dsecond = dot("rf,df->rd", dhid, w2)
    dmiddle, g_gain2, g_shift2 = norm_backward(middle, gain_two, dsecond)
    dmiddle = dmiddle + grad_last
    mr = dmiddle.astype(bf16)
    dmixed = dot("rd,de->re", mr, wo).astype(bf16)
    gwo = dot("rd,re->de", mr, mixed).astype(bf16)
    dm = dmixed.reshape(length, heads, HEAD_DIM)
    dv = dot("hqk,qhe->khe", probs.astype(bf16), dm).astype(bf16).reshape(length, width)
    dprobs = dot("qhe,khe->hqk", dm, v)
    ds = (probs * (dprobs - jnp.sum(probs * dprobs, axis=-1, keepdims=True))).astype(bf16)
    dq = (dot("hqk,khe->qhe", ds, k) * scale).astype(bf16).reshape(length, width)
    dk = (dot("hqk,qhe->khe", ds, q) * scale).astype(bf16).reshape(length, width)
    c = cols
    zero = jnp.zeros((length, c), bf16)
    dcat = jnp.concatenate([dq[:, :c], dk[:, :c], dv[:, :c], zero, dq[:, c:], dk[:, c:], dv[:, c:], zero], axis=1)
    gin = dot("rd,rc->dc", first, dcat).astype(bf16)
    g1 = jnp.concatenate([gin[:, : 3 * c], gwo[:, :c], gin[:, 4 * c : 7 * c], gwo[:, c:]], axis=1)
    dfirst = dot("rc,dc->rd", dcat, w1)
    grad_inputs, g_gain1, g_shift1 = norm_backward(inputs, gain_one, dfirst)
    grad_inputs = grad_inputs + dmiddle
    o3 = scatter_group(g3, dp, 2)
    o2 = scatter_group(g2, dp, 2)
    o1 = scatter_group(g1, dp, 2)
    rows = jnp.stack(
        [
            g_gain1,
            g_shift1,
            jnp.sum(dmiddle, axis=0),
            g_gain2,
            g_shift2,
            jnp.sum(grad_last, axis=0),
            jnp.sum(dq.astype(f32), axis=0),
            jnp.sum(dv.astype(f32), axis=0),
        ]
    )
    rows = jnp.concatenate([rows, jnp.sum(dhid.astype(f32), axis=0).reshape(-1, width)])
    rows = sum_vectors(rows, dp, 4)
    vectors = lax.dynamic_slice_in_dim(rows[:6], d * share, share, 1)
    bias_own = lax.dynamic_slice_in_dim(rows[6:8], t * cols, cols, 1)
    up_own = lax.dynamic_slice_in_dim(rows[8:].reshape(-1), t * ff, ff, 0)
    return (
        block_out,
        grad_inputs,
        vectors[0],
        vectors[1],
        o1[:, : 3 * cols].reshape(share, 3, cols),
        bias_own,
        o1[:, 3 * cols :].T,
        vectors[2],
        vectors[3],
        vectors[4],
        o2,
        up_own,
        o3.T,
        vectors[5],
    )


def solution(mesh):
    in_specs = (
        P(("dp", "tensor"), None),
        P(("dp", "tensor"), None),
        P("dp", None),
        P("dp"),
        P("dp"),
        P("dp"),
        P("dp", None, "tensor"),
        P(None, "tensor"),
        P("tensor", "dp"),
        P("dp"),
        P("dp"),
        P("dp"),
        P("dp", "tensor"),
        P("tensor"),
        P("tensor", "dp"),
        P("dp"),
    )
    out_specs = (
        P(("dp", "tensor"), None),
        P(("dp", "tensor"), None),
        P("dp"),
        P("dp"),
        P("dp", None, "tensor"),
        P(None, "tensor"),
        P("tensor", "dp"),
        P("dp"),
        P("dp"),
        P("dp"),
        P("dp", "tensor"),
        P("tensor"),
        P("tensor", "dp"),
        P("dp"),
    )
    ready = mesh.shape["tensor"] == 2 and mesh.shape["dp"] == 16
    body = paired_device if ready else general_device
    return jax.shard_map(
        body, mesh=mesh, in_specs=in_specs, out_specs=out_specs, check_vma=False
    )
```

```python
import functools
import types

import jax
import jax.numpy as jnp
from jax import lax
from jax.experimental import pallas as pl
from jax.experimental.pallas import tpu as pltpu
from jax.sharding import PartitionSpec as P

HEAD_DIM = 64
MESH = pl.DeviceIdType.MESH
f32 = jnp.float32
bf16 = jnp.bfloat16
NN, NT, TN = ((1,), (0,)), ((1,), (1,)), ((0,), (0,))


def layer_norm(inputs, gain, shift):
    center = inputs - jnp.mean(inputs, axis=-1, keepdims=True)
    spread = jnp.mean(center * center, axis=-1, keepdims=True)
    return center * lax.rsqrt(spread + 1e-06) * gain + shift


def norm_backward(inputs, gain, upstream):
    center = inputs - jnp.mean(inputs, axis=-1, keepdims=True)
    spread = jnp.mean(center * center, axis=-1, keepdims=True)
    scaled = lax.rsqrt(spread + 1e-06)
    unit = center * scaled
    weighted = upstream * gain
    grad_inputs = scaled * (
        weighted
        - jnp.mean(weighted, axis=-1, keepdims=True)
        - unit * jnp.mean(weighted * unit, axis=-1, keepdims=True)
    )
    return (grad_inputs, jnp.sum(upstream * unit, axis=0), jnp.sum(upstream, axis=0))


def gelu_slope(hidden):
    return (
        0.5 * (1.0 + lax.erf(hidden * 0.7071067811865476))
        + hidden * jnp.exp(-0.5 * hidden * hidden) * 0.3989422804014327
    )


def general_device(
    tokens,
    cotangent,
    token_valid,
    image_valid,
    first_gain,
    first_shift,
    input_weight,
    input_bias,
    output_weight,
    output_bias,
    second_gain,
    second_shift,
    up_weight,
    up_bias,
    down_weight,
    down_bias,
):
    f32 = jnp.float32
    bf16 = jnp.bfloat16
    gathered = (
        lax.all_gather(first_gain, "dp", axis=0, tiled=True),
        lax.all_gather(first_shift, "dp", axis=0, tiled=True),
        lax.all_gather(input_weight, "dp", axis=0, tiled=True),
        lax.all_gather(output_weight, "dp", axis=1, tiled=True),
        lax.all_gather(output_bias, "dp", axis=0, tiled=True),
        lax.all_gather(second_gain, "dp", axis=0, tiled=True),
        lax.all_gather(second_shift, "dp", axis=0, tiled=True),
        lax.all_gather(up_weight, "dp", axis=0, tiled=True),
        lax.all_gather(down_weight, "dp", axis=1, tiled=True),
        lax.all_gather(down_bias, "dp", axis=0, tiled=True),
    )
    (
        gain_one,
        shift_one,
        in_full,
        out_full,
        out_shift,
        gain_two,
        shift_two,
        up_full,
        down_full,
        down_shift,
    ) = gathered
    gain_one = gain_one.astype(f32)
    shift_one = shift_one.astype(f32)
    out_shift = out_shift.astype(f32)
    gain_two = gain_two.astype(f32)
    shift_two = shift_two.astype(f32)
    down_shift = down_shift.astype(f32)
    tensor_at = lax.axis_index("tensor")
    groups = lax.axis_size("tensor")
    own_rows = tokens.shape[0]
    width = tokens.shape[1]
    length = token_valid.shape[1]
    positions = lax.broadcasted_iota(jnp.int32, token_valid.shape, 1)
    key_ok = (token_valid > 0) | (positions == 0)
    mask_all = (token_valid * image_valid[:, None]).astype(f32).reshape(-1)
    row_mask = lax.dynamic_slice_in_dim(mask_all, tensor_at * own_rows, own_rows)[:, None]
    images = token_valid.shape[0]
    local_width = in_full.shape[2]
    local_heads = local_width // HEAD_DIM
    hidden_width = up_full.shape[1]
    scale = HEAD_DIM ** (-0.5)
    head_shape = (images, length, local_heads, HEAD_DIM)
    inputs = tokens.astype(f32)
    first_own = layer_norm(inputs, gain_one, shift_one).astype(bf16)
    first_all = lax.all_gather(first_own, "tensor", axis=0, tiled=True)
    project = jnp.einsum("rd,dce->rce", first_all, in_full, preferred_element_type=f32)
    bias_in = input_bias.astype(f32)
    queries = (project[:, 0] + bias_in[0]).astype(bf16).reshape(head_shape)
    keyset = project[:, 1].astype(bf16).reshape(head_shape)
    values = (project[:, 2] + bias_in[1]).astype(bf16).reshape(head_shape)

    def scores_of(query_img, key_img, ok_img):
        scores = jnp.einsum("qhe,khe->hqk", query_img, key_img, preferred_element_type=f32) * scale
        return jnp.where(ok_img[None, None, :], scores, -1000000000.0)

    def attend(pieces):
        query_img, key_img, value_img, ok_img = pieces
        scores = scores_of(query_img, key_img, ok_img)
        highest = jnp.max(scores, axis=-1, keepdims=True)
        log_total = highest + jnp.log(jnp.sum(jnp.exp(scores - highest), axis=-1, keepdims=True))
        attn_probs = jnp.exp(scores - log_total).astype(bf16)
        mixed_img = jnp.einsum("hqk,khe->qhe", attn_probs, value_img, preferred_element_type=f32)
        return (mixed_img.astype(bf16), log_total)

    mixed, log_totals = lax.map(attend, (queries, keyset, values, key_ok))
    mixed_rows = mixed.reshape(images * length, local_width)
    attended = lax.psum_scatter(
        jnp.dot(mixed_rows, out_full, preferred_element_type=f32).astype(jnp.bfloat16),
        "tensor",
        scatter_dimension=0,
        tiled=True,
    ).astype(jnp.float32)
    middle = inputs + attended + out_shift
    second_own = layer_norm(middle, gain_two, shift_two).astype(bf16)
    second_all = lax.all_gather(second_own, "tensor", axis=0, tiled=True)
    hidden = jnp.dot(second_all, up_full, preferred_element_type=f32) + up_bias.astype(f32)
    active = jax.nn.gelu(hidden, approximate=False).astype(bf16)
    lifted = lax.psum_scatter(
        jnp.dot(active, down_full, preferred_element_type=f32).astype(jnp.bfloat16),
        "tensor",
        scatter_dimension=0,
        tiled=True,
    ).astype(jnp.float32)
    block_out = (row_mask * (middle + lifted + down_shift)).astype(bf16)
    grad_last = row_mask * cotangent.astype(f32)
    first_all, second_all = (
        lax.all_gather(first_own, "tensor", axis=0, tiled=True),
        lax.all_gather(second_own, "tensor", axis=0, tiled=True),
    )
    grad_lift = lax.all_gather(grad_last.astype(bf16), "tensor", axis=0, tiled=True)
    grad_active = jnp.einsum("rd,fd->rf", grad_lift, down_full, preferred_element_type=f32)
    grad_hidden = (grad_active * gelu_slope(hidden)).astype(bf16)
    grad_down = jnp.einsum("rf,rd->fd", active, grad_lift, preferred_element_type=f32)
    grad_up = jnp.einsum("rd,rf->df", second_all, grad_hidden, preferred_element_type=f32)
    grad_up_bias = jnp.sum(grad_hidden.astype(f32), axis=0)
    grad_second = lax.psum_scatter(
        jnp.einsum("rf,df->rd", grad_hidden, up_full, preferred_element_type=f32).astype(
            jnp.bfloat16
        ),
        "tensor",
        scatter_dimension=0,
        tiled=True,
    ).astype(jnp.float32)
    grad_middle, grad_gain_two, grad_shift_two = norm_backward(middle, gain_two, grad_second)
    grad_middle = grad_middle + grad_last
    grad_mid_all = lax.all_gather(grad_middle.astype(bf16), "tensor", axis=0, tiled=True)
    grad_mixed = jnp.einsum("rd,ed->re", grad_mid_all, out_full, preferred_element_type=f32).astype(
        bf16
    )
    grad_out_weight = jnp.einsum("re,rd->ed", mixed_rows, grad_mid_all, preferred_element_type=f32)

    def attend_back(pieces):
        query_img, key_img, value_img, ok_img, total_img, grad_img = pieces
        scores = scores_of(query_img, key_img, ok_img)
        attn_probs = jnp.exp(scores - total_img)
        grad_values = jnp.einsum(
            "hqk,qhe->khe", attn_probs.astype(bf16), grad_img, preferred_element_type=f32
        )
        grad_probs = jnp.einsum("qhe,khe->hqk", grad_img, value_img, preferred_element_type=f32)
        grad_scores = (
            attn_probs * (grad_probs - jnp.sum(attn_probs * grad_probs, axis=-1, keepdims=True))
        ).astype(bf16)
        grad_queries = (
            jnp.einsum("hqk,khe->qhe", grad_scores, key_img, preferred_element_type=f32) * scale
        )
        grad_keys = (
            jnp.einsum("hqk,qhe->khe", grad_scores, query_img, preferred_element_type=f32) * scale
        )
        return jnp.stack([grad_queries, grad_keys, grad_values], axis=1).astype(bf16)

    grad_project = lax.map(
        attend_back, (queries, keyset, values, key_ok, log_totals, grad_mixed.reshape(head_shape))
    )
    grad_project = grad_project.reshape(images * length, 3, local_width)
    grad_in_weight = jnp.einsum("rd,rce->dce", first_all, grad_project, preferred_element_type=f32)
    grad_in_bias = jnp.sum(grad_project[:, 0::2].astype(f32), axis=0)
    grad_first = lax.psum_scatter(
        jnp.einsum("rce,dce->rd", grad_project, in_full, preferred_element_type=f32).astype(
            jnp.bfloat16
        ),
        "tensor",
        scatter_dimension=0,
        tiled=True,
    ).astype(jnp.float32)
    grad_inputs, grad_gain_one, grad_shift_one = norm_backward(inputs, gain_one, grad_first)
    grad_inputs = grad_inputs + grad_middle
    grad_in_own, grad_out_own, grad_up_own, grad_down_own = (
        lax.psum_scatter(
            grad_in_weight.astype(jnp.bfloat16), "dp", scatter_dimension=0, tiled=True
        ).astype(jnp.float32),
        lax.psum_scatter(
            grad_out_weight.astype(jnp.bfloat16), "dp", scatter_dimension=1, tiled=True
        ).astype(jnp.float32),
        lax.psum_scatter(
            grad_up.astype(jnp.bfloat16), "dp", scatter_dimension=0, tiled=True
        ).astype(jnp.float32),
        lax.psum_scatter(
            grad_down.astype(jnp.bfloat16), "dp", scatter_dimension=1, tiled=True
        ).astype(jnp.float32),
    )
    vectors = jnp.stack(
        [
            grad_gain_one,
            grad_shift_one,
            jnp.sum(grad_middle, axis=0),
            grad_gain_two,
            grad_shift_two,
            jnp.sum(grad_last, axis=0),
        ]
    )
    bias_share = input_bias.shape[1]
    up_share = up_bias.shape[0]
    placed_bias = lax.dynamic_update_slice(
        jnp.zeros((2, width), f32), grad_in_bias, (0, tensor_at * local_width)
    )
    placed_up = lax.dynamic_update_slice(
        jnp.zeros((hidden_width * groups,), f32), grad_up_bias, (tensor_at * hidden_width,)
    )
    vectors, placed_bias, placed_up = lax.psum((vectors, placed_bias, placed_up), ("dp", "tensor"))
    share = first_gain.shape[0]
    dp_at = lax.axis_index("dp")
    vectors = lax.dynamic_slice_in_dim(vectors, dp_at * share, share, 1)
    bias_own = lax.dynamic_slice_in_dim(placed_bias, tensor_at * bias_share, bias_share, 1)
    up_bias_own = lax.dynamic_slice_in_dim(placed_up, tensor_at * up_share, up_share, 0)
    return (
        block_out,
        grad_inputs,
        vectors[0],
        vectors[1],
        grad_in_own,
        bias_own,
        grad_out_own,
        vectors[2],
        vectors[3],
        vectors[4],
        grad_up_own,
        up_bias_own,
        grad_down_own,
        vectors[5],
    )


def mul(a, b, dims):
    return lax.dot_general(a, b, (dims, ((), ())), preferred_element_type=f32)


def iota(shape, axis):
    return lax.broadcasted_iota(jnp.int32, shape, axis)


def tile(j, size):
    return pl.ds(pl.multiple_of(j * size, size), size)


def split_of(n):
    a = (n * 4 // 7) // 128 * 128
    return a, n - a


class Place:
    def __init__(self, dp, n):
        d = lax.axis_index("dp")
        t = lax.axis_index("tensor")
        ring = dp // 2
        self.dp, self.d, self.t, self.ring, self.far = dp, d, t, ring, ring // 2
        self.chip, self.core = d // 2, d % 2
        self.pos = jnp.where(self.chip % 2 == 0, self.chip // 2, ring - 1 - self.chip // 2)
        self.right = (self.chip_at(1) * 2 + self.core, t)
        self.left = (self.chip_at(-1) * 2 + self.core, t)
        self.across = (d, 1 - t)
        self.sibling = (d + 1 - 2 * self.core, t)
        a, b = split_of(n)
        self.n, self.a, self.b = n, a, b
        self.own_cols = (pl.multiple_of(t * n, 128), n)
        self.other_cols = (pl.multiple_of((1 - t) * n, 128), n)
        self.ring_cols = (pl.multiple_of(t * a, 128), 2 * n - a)
        self.mine_a = (pl.multiple_of(t * (2 * n - a), 128), a)
        self.their_a = (pl.multiple_of((1 - t) * (2 * n - a), 128), a)
        self.their_b = (pl.multiple_of(n - t * b, 128), b)
        self.mine_b = (pl.multiple_of(n - (1 - t) * b, 128), b)

    def chip_at(self, offset):
        ring = self.ring
        spot = (self.pos + offset + ring) % ring
        return jnp.where(spot < ring // 2, 2 * spot, 2 * (ring - 1 - spot) + 1)


def greet(targets):
    bar = pltpu.get_barrier_semaphore()
    for a in targets:
        pl.semaphore_signal(bar, inc=1, device_id=a, device_id_type=MESH)
    pl.semaphore_wait(bar, len(targets))


def rcopy(src, dst, send, recv, dev):
    return pltpu.make_async_remote_copy(
        src_ref=src, dst_ref=dst, send_sem=send, recv_sem=recv, device_id=dev, device_id_type=MESH
    )


class Gather:
    def __init__(self, w, g, shard, full, sems):
        self.w, self.g, self.shard, self.full, self.sems = w, g, shard, full, sems
        self.rows = shard.shape[0]

    def block(self, offset, cols, span=None):
        w = self.w
        lo, size = span or (0, self.rows)
        base = w.chip_at(offset) * (2 * self.rows) + w.core * self.rows + lo
        return self.full.at[pl.ds(pl.multiple_of(base, 16), size), pl.ds(cols[0], cols[1])]

    def span(self, s, dirn):
        half = self.rows // 2
        return (0, self.rows) if s < self.w.far else (dirn * half, half)

    def off(self, s, dirn):
        return s if dirn else -s

    def make(self, kind, src, dst, k, dev):
        send, recv = self.sems[kind]
        return rcopy(src, dst, send.at[self.g, k], recv.at[self.g, k], dev)

    def y(self, s, dirn):
        if s == 0:
            return self.make("y", self.shard, self.block(0, self.w.own_cols), 0, self.w.across)
        ref = self.block(self.off(s, dirn), self.w.mine_a, self.span(s, dirn))
        return self.make("y", ref, ref, 2 * s - 1 + dirn, self.w.across)

    def ring(self, s, dirn, part=0):
        dev = self.w.left if dirn else self.w.right
        k = dirn * (self.w.far + 1)
        if s == 1 and part == 0:
            return self.make("r", self.shard, self.block(0, self.w.own_cols), k, dev)
        if s == 1:
            ref = self.block(0, self.w.their_b)
            return self.make("r", ref, ref, k + 1, dev)
        ref = self.block(self.off(s - 1, dirn), self.w.ring_cols, self.span(s, dirn))
        return self.make("r", ref, ref, k + s, dev)

    def sib(self, k):
        w = self.w
        if k == 0:
            src, dst = self.shard, self.block(0, w.own_cols)
        elif k == 1:
            src = dst = self.block(0, w.other_cols)
        else:
            which, rest = divmod(k - 2, 2 * w.far)
            s, dirn = rest // 2 + 1, rest % 2
            cols = w.their_a if which else w.ring_cols
            src = dst = self.block(self.off(s, dirn), cols, self.span(s, dirn))
        return self.make("c", src, dst, k, w.sibling)

    def keep(self):
        return pltpu.make_async_copy(self.shard, self.block(0, self.w.own_cols), self.sems["k"].at[self.g])

    def start(self):
        self.y(0, 0).start()
        self.ring(1, 0).start()
        self.ring(1, 1).start()
        self.sib(0).start()
        self.keep().start()

    def first_y(self):
        self.y(0, 0).wait_recv()
        self.ring(1, 0, 1).start()
        self.ring(1, 1, 1).start()
        self.sib(1).start()

    def hop(self, s):
        for dirn in (0, 1):
            self.ring(s, dirn).wait_recv()
            if s == 1:
                self.ring(s, dirn, 1).wait_recv()
            if s < self.w.far:
                self.ring(s + 1, dirn).start()
            self.y(s, dirn).start()
            self.sib(2 * s + dirn).start()

    def cross(self, s):
        for dirn in (0, 1):
            self.y(s, dirn).wait_recv()
            self.sib(2 + 2 * self.w.far + 2 * (s - 1) + dirn).start()

    def end(self):
        far = self.w.far
        for k in range(2 + 4 * far):
            self.sib(k).wait()
        self.keep().wait()

    def drain(self):
        far = self.w.far
        self.y(0, 0).wait_send()
        for dirn in (0, 1):
            self.ring(1, dirn).wait_send()
            self.ring(1, dirn, 1).wait_send()
            for s in range(1, far + 1):
                self.y(s, dirn).wait_send()
                if s > 1:
                    self.ring(s, dirn).wait_send()


def gather_sems(dp, groups):
    far = dp // 4
    dma = pltpu.SemaphoreType.DMA
    sizes = (2 * (far + 1), 2 * far + 1, 4 * far + 2)
    return [dma((groups, k)) for k in sizes for _ in (0, 1)] + [dma((groups,))]


def stream(count, parts, sem, body):
    def copies(j):
        slot = lax.rem(j, 2)
        return [
            pltpu.make_async_copy(src(j), buf.at[slot], sem.at[i, slot]) for i, (src, buf) in enumerate(parts)
        ]

    for cp in copies(jnp.int32(0)):
        cp.start()

    @pl.loop(0, count)
    def _(j):
        @pl.when(j + 1 < count)
        def _():
            for cp in copies(j + 1):
                cp.start()

        for cp in copies(j):
            cp.wait()
        body(j, lax.rem(j, 2))


def ticks(j, table):
    for at, events in table.items():

        @pl.when(j == at)
        def _(events=events):
            for e in events:
                e()


def normalize(x):
    center = x - jnp.mean(x, axis=-1, keepdims=True)
    scaled = lax.rsqrt(jnp.mean(center * center, axis=-1, keepdims=True) + 1e-06)
    return center * scaled, scaled


def attend_pair(m, i, rows, full):
    width = m.mixed.shape[1]
    ps = tile(i, 128)
    q2 = m.qkv[0:rows, ps]
    k2 = m.qkv[:, pl.ds(pl.multiple_of(width + i * 128, 128), 128)]
    v2 = m.qkv[:, pl.ds(pl.multiple_of(2 * width + i * 128, 128), 128)]
    lq, lk = iota((rows, 128), 1), iota((full, 128), 1)
    outs = []
    logs = m.logs[0:rows, :]
    for h in (0, 1):
        spare = 64 * (1 - h)
        own_q = (lq < 64) if h == 0 else (lq >= 64)
        own_k = (lk < 64) if h == 0 else (lk >= 64)
        qh = jnp.where(own_q, q2, jnp.where(lq == spare, 1.0, 0.0).astype(bf16))
        kh = jnp.where(lk == spare, m.key_bias[...], k2)
        scores = mul(qh, kh, NT)
        top = jnp.max(scores, axis=1, keepdims=True)
        probs = jnp.exp(scores - top).astype(bf16)
        out = mul(probs, jnp.where(own_k, v2, jnp.ones_like(v2)), NN)
        turned = pltpu.roll(out, 64, 1)
        outs.append(out / turned)
        total = jnp.where(own_q, turned, out)
        logs = jnp.where(lq == 2 * i + h, top + jnp.log(total), logs)
    m.logs[0:rows, :] = logs
    m.mixed[0:rows, ps] = jnp.where(lq < 64, outs[0], outs[1]).astype(bf16)


FWD_IN = ("vec", "bias", "iw", "ow", "uw", "dw", "tok", "cot", "kb", "rm")
FWD_OUT = ("w1", "w2", "w3", "qkv_o", "mixed_o", "logs_o", "mid_o", "act_o", "slope_o", "p3_o", "lhs1_o", "lhs2_o", "gr_o", "vecs_o")


def fwd_kernel(dp, rows, names, *refs):
    m = types.SimpleNamespace(**dict(zip(names, refs)))
    m.key_bias = m.kb
    n = m.uw.shape[1]
    w = Place(dp, n)
    length, width = m.tok.shape
    full = m.qkv.shape[0]
    share = m.sh1.shape[0]
    cols = n // 4
    sems = {"r": (m.ring_s, m.ring_r), "y": (m.y_s, m.y_r), "c": (m.c_s, m.c_r), "k": m.k_sem}
    g1 = Gather(w, 0, m.sh1, m.w1, sems)
    g2 = Gather(w, 1, m.uw, m.w2, sems)
    g3 = Gather(w, 2, m.sh3, m.w3, sems)
    tok_in = pltpu.make_async_copy(m.tok, m.xs.at[pl.ds(0, length)], m.l_sem.at[0])
    cot_in = pltpu.make_async_copy(m.cot, m.gr.at[pl.ds(0, length)], m.l_sem.at[1])
    tok_in.start()
    cot_in.start()
    peers = [(lax.rem(w.d + i, dp), w.t) for i in range(1, dp)] + [w.across]
    bar = pltpu.get_barrier_semaphore()
    for a in peers:
        pl.semaphore_signal(bar, inc=1, device_id=a, device_id_type=MESH)
    for s in range(3):
        m.sh1[:, tile(s, cols)] = m.iw[:, s, :]
    m.sh1[:, tile(3, cols)] = m.ow[...].T
    pl.semaphore_wait(bar, len(peers))
    g1.start()
    spot = pl.ds(pl.multiple_of(w.chip * 128, 128), 128)

    def vec_copy(i):
        return rcopy(m.vec, m.vbuf.at[w.core, :, spot], m.v_s.at[i], m.v_r.at[i], peers[i])

    bias_copy = rcopy(m.bias, m.bbuf.at[w.t], m.v_s.at[dp - 1], m.v_r.at[dp - 1], w.across)
    for i in range(dp - 1):
        vec_copy(i).start()
    bias_copy.start()
    m.vbuf[w.core, :, spot] = m.vec[...]
    m.bbuf[w.t] = m.bias[...]
    m.sh3[...] = m.dw[...].T
    zero_rows = pl.ds(rows, full - rows)
    for ref in (m.qkv, m.act, m.mixed):
        ref[zero_rows, :] = jnp.zeros((full - rows, ref.shape[1]), bf16)
    m.logs[...] = jnp.zeros(m.logs.shape, f32)
    m.mid[zero_rows, :] = jnp.zeros((full - rows, width), f32)
    tail = pl.ds(length, full - length)
    tok_in.wait()
    cot_in.wait()
    m.xs[tail, :] = jnp.zeros((full - length, width), bf16)
    m.gr[tail, :] = jnp.zeros((full - length, width), bf16)
    for i in range(dp - 1):
        vec_copy(i).wait()
    bias_copy.wait()
    vecs = m.vbuf[0].astype(f32) + m.vbuf[1].astype(f32)
    m.vecs[...] = vecs
    m.qb[...] = jnp.zeros(m.qb.shape, f32)
    for side in (0, 1):
        b = m.bbuf[side].astype(f32)
        m.ub[4 * side : 4 * side + 4, :] = b[0:4]
        m.qb[side : side + 1, :] = b[4:5]
        m.qb[4 + side : 5 + side, :] = b[5:6]
    ch = 64

    @pl.loop(0, full // ch)
    def _(r):
        rs = tile(r, ch)
        unit, _ = normalize(m.xs[rs, :].astype(f32))
        m.ln[rs, :] = (unit * m.vecs[0:1, :] + m.vecs[1:2, :]).astype(bf16)
        m.gr[rs, :] = (m.gr[rs, :].astype(f32) * m.rm[rs, 0:1]).astype(bf16)

    def turned(src, k):
        tt, lhs = m.turn.at[k], (m.lhs1, m.lhs2, m.lhs3)[k]

        @pl.loop(0, width // 256)
        def _(j):
            tt[tile(j, 2)] = src[:, tile(j, 256)].T.reshape(2, 2, share, full)

        return turn_copies(k)

    def turn_copies(k):
        tt, lhs = m.turn.at[k], (m.lhs1, m.lhs2, m.lhs3)[k]
        keep = pltpu.make_async_copy(tt.at[:, w.core], lhs.at[:, :, pl.ds(0, full)], m.t_sem.at[k])
        give = rcopy(
            tt.at[:, 1 - w.core], lhs.at[:, :, pl.ds(full, full)], m.t_s.at[k], m.t_r.at[k], w.sibling
        )
        return keep, give

    outs = []

    def save(src, dst, k):
        cp = pltpu.make_async_copy(src, dst, m.o_sem.at[k])
        outs.append(lambda: pltpu.make_async_copy(src, dst, m.o_sem.at[k]))
        cp.start()

    for k, src in ((0, m.ln), (2, m.gr)):
        for cp in turned(src, k):
            cp.start()
    save(m.gr, m.gr_o, 0)
    save(m.vecs, m.vecs_o, 1)
    g1.first_y()
    g1.hop(1)
    g1.hop(2)
    g1.cross(1)
    g1.hop(3)
    g2.start()
    g1.cross(2)
    g1.hop(4)
    g2.first_y()
    g1.cross(3)
    g1.cross(4)
    g1.end()

    def qkv_tile(j, slot):
        ticks(j, {1: [lambda: g2.hop(1)]})
        p = mul(m.ln[0:rows, :], m.wt[slot], NN) + m.qb[pl.ds(j, 1), :]
        scale = jnp.where(j < 2, HEAD_DIM**-0.5, 1.0)
        m.qkv[0:rows, tile(j, cols)] = (p.astype(bf16).astype(f32) * scale).astype(bf16)

    def in_cols(ref, j, extra=0):
        return ref.at[:, pl.ds(pl.multiple_of((j % 2) * n + (j // 2) * cols + extra, 128), cols)]

    stream(6, [(lambda j: in_cols(m.w1, j), m.wt)], m.s_sem, qkv_tile)
    save(m.qkv, m.qkv_o, 2)

    @pl.loop(0, width // 128)
    def _(i):
        ticks(
            i,
            {
                2: [lambda: g2.hop(2)],
                4: [lambda: g2.cross(1)],
                6: [lambda: g2.hop(3), g3.start],
                7: [lambda: g2.cross(2)],
            },
        )
        attend_pair(m, i, rows, full)

    save(m.mixed, m.mixed_o, 3)
    m.lt[...] = m.logs[...].T[0 : m.lt.shape[0], :]
    save(m.lt, m.logs_o, 4)
    m.mid[0:rows, :] = m.xs[0:rows, :].astype(f32) + m.vecs[2:3, :]

    def out_tile(j, slot):
        m.mid[0:rows, :] += mul(m.mixed[0:rows, tile(j, cols)], m.wt[slot], NT)

    stream(2, [(lambda j: in_cols(m.w1, 6 + j), m.wt)], m.s_sem, out_tile)
    g2.hop(4)
    g3.first_y()
    save(m.mid, m.mid_o, 5)
    for cp in turn_copies(0):
        cp.wait()
    save(m.lhs1, m.lhs1_o, 6)

    @pl.loop(0, full // ch)
    def _(r):
        rs = tile(r, ch)
        unit, _ = normalize(m.mid[rs, :])
        m.ln[rs, :] = (unit * m.vecs[3:4, :] + m.vecs[4:5, :]).astype(bf16)

    g2.cross(3)
    for cp in turned(m.ln, 1):
        cp.start()
    g2.cross(4)
    g2.end()

    def act_copies(j):
        cs = tile(j, cols)
        yield rcopy(m.act.at[:, cs], m.act_sib.at[:, cs], m.a_s.at[j], m.a_r.at[j], w.sibling)
        yield pltpu.make_async_copy(m.act.at[:, cs], m.act_o.at[:, cs], m.a_sem.at[0, j])
        yield pltpu.make_async_copy(m.slope.at[:, cs], m.slope_o.at[:, cs], m.a_sem.at[1, j])

    def up_tile(j, slot):
        ticks(j, {0: [lambda: g3.hop(1)], 6: [lambda: g3.hop(2)]})
        cs = tile(j, cols)
        hidden = mul(m.ln[0:rows, :], m.wt[slot], NN) + m.ub[pl.ds(j, 1), :]
        phi = 0.5 * (1.0 + lax.erf(hidden * 0.7071067811865476))
        m.act[0:rows, cs] = (hidden * phi).astype(bf16)
        m.slope[0:rows, cs] = (
            phi + hidden * jnp.exp(-0.5 * hidden * hidden) * 0.3989422804014327
        ).astype(bf16)
        for cp in act_copies(j):
            cp.start()

    def flat(ref):
        return lambda j: ref.at[:, tile(j, cols)]

    m.slope[zero_rows, :] = jnp.zeros((full - rows, m.slope.shape[1]), bf16)
    stream(8, [(flat(m.w2), m.wt)], m.s_sem, up_tile)
    for cp in turn_copies(2):
        cp.wait()

    def p3_copy(j):
        cs = tile(j, cols)
        return pltpu.make_async_copy(m.p3.at[:, :, cs], m.p3_o.at[:, :, cs], m.a_sem.at[2, j])

    @pl.loop(0, 8)
    def _(j):
        ticks(j, {1: [lambda: g3.cross(1)], 6: [lambda: g3.hop(3)], 7: [lambda: g3.cross(2)]})
        next(act_copies(j)).wait_recv()
        cs = tile(j, cols)
        lhs = m.lhs3[...].reshape(w.ring * share, 2 * full)
        part = mul(lhs[:, 0:full], m.act[:, cs], NN) + mul(lhs[:, full:], m.act_sib[:, cs], NN)
        m.p3[:, :, cs] = part.astype(bf16).reshape(w.ring, share, cols)
        p3_copy(j).start()

    for cp in turn_copies(1):
        cp.wait()
    save(m.lhs2, m.lhs2_o, 7)
    g3.hop(4)
    g3.cross(3)
    g3.cross(4)

    @pl.loop(0, 8)
    def _(j):
        give, a, b = act_copies(j)
        give.wait_send()
        a.wait()
        b.wait()
        p3_copy(j).wait()

    for again in outs:
        again().wait()
    for g in (g1, g2):
        g.drain()
    g3.end()
    g3.drain()


def forward(args, dp, length, width, n, share):
    rows = -(-length // 16) * 16
    full = -(-length // 128) * 128
    cols = n // 4
    ring = dp // 2
    depth = share * dp
    heads = width // HEAD_DIM
    V, dma = pltpu.VMEM, pltpu.SemaphoreType.DMA
    S = jax.ShapeDtypeStruct
    out = dict(
        w1=S((depth, 2 * n), bf16),
        w2=S((depth, 2 * n), bf16),
        w3=S((depth, 2 * n), bf16),
        qkv_o=S((full, 3 * width), bf16),
        mixed_o=S((full, width), bf16),
        logs_o=S((heads, full), f32),
        mid_o=S((full, width), f32),
        act_o=S((full, 2 * n), bf16),
        slope_o=S((full, 2 * n), bf16),
        p3_o=S((ring, share, 2 * n), bf16),
        lhs1_o=S((ring, share, 2 * full), bf16),
        lhs2_o=S((ring, share, 2 * full), bf16),
        gr_o=S((full, width), bf16),
        vecs_o=S((8, width), f32),
    )
    scratch = dict(
        sh1=V((share, n), bf16),
        sh3=V((share, n), bf16),
        xs=V((full, width), bf16),
        gr=V((full, width), bf16),
        ln=V((full, width), bf16),
        qkv=V((full, 3 * width), bf16),
        mixed=V((full, width), bf16),
        logs=V((full, 128), f32),
        lt=V((heads, full), f32),
        mid=V((full, width), f32),
        act=V((full, 2 * n), bf16),
        act_sib=V((full, 2 * n), bf16),
        slope=V((full, 2 * n), bf16),
        p3=V((ring, share, 2 * n), bf16),
        turn=V((3, ring, 2, share, full), bf16),
        lhs1=V((ring, share, 2 * full), bf16),
        lhs2=V((ring, share, 2 * full), bf16),
        lhs3=V((ring, share, 2 * full), bf16),
        wt=V((2, depth, cols), bf16),
        vbuf=V((2, 8, width), bf16),
        bbuf=V((2, 8, cols), bf16),
        vecs=V((8, width), f32),
        ub=V((8, cols), f32),
        qb=V((8, cols), f32),
    )
    gs = gather_sems(dp, 3)
    scratch.update(zip(("ring_s", "ring_r", "y_s", "y_r", "c_s", "c_r", "k_sem"), gs))
    scratch.update(
        v_s=dma((dp,)),
        v_r=dma((dp,)),
        l_sem=dma((2,)),
        s_sem=dma((1, 2)),
        t_sem=dma((3,)),
        t_s=dma((3,)),
        t_r=dma((3,)),
        a_s=dma((8,)),
        a_r=dma((8,)),
        a_sem=dma((3, 8)),
        o_sem=dma((8,)),
    )
    names = FWD_IN + tuple(out) + tuple(scratch)
    hbm = pl.BlockSpec(memory_space=pl.ANY)
    vm = pl.BlockSpec(memory_space=pltpu.VMEM)
    specs = [hbm if k in ("uw", "tok", "cot") else vm for k in FWD_IN]
    got = pl.pallas_call(
        functools.partial(fwd_kernel, dp, rows, names),
        out_shape=list(out.values()),
        in_specs=specs,
        out_specs=[hbm] * len(out),
        scratch_shapes=list(scratch.values()),
        compiler_params=pltpu.CompilerParams(
            collective_id=1, has_side_effects=True, vmem_limit_bytes=62 << 20
        ),
        name="forward",
    )(*args)
    return types.SimpleNamespace(**dict(zip(out, got)))


def prepare(
    tokens, cotangent, token_valid, image_valid, first_gain, first_shift, input_weight, input_bias, output_weight,
    output_bias, second_gain, second_shift, up_weight, up_bias, down_weight, down_bias,
):
    d = lax.axis_index("dp")
    t = lax.axis_index("tensor")
    length = tokens.shape[0]
    full = -(-length // 128) * 128
    share = first_gain.shape[0]
    n = up_weight.shape[1]
    cols = n // 4
    vec = jnp.stack([first_gain, first_shift, output_bias, second_gain, second_shift, down_bias])
    vec = jnp.concatenate([vec, vec], axis=1)
    vec = jnp.where(iota(vec.shape, 1) // share == d % 2, vec, jnp.zeros_like(vec))
    vec = jnp.pad(vec, ((0, 2), (0, 0)))
    bias = jnp.pad(jnp.concatenate([up_bias.reshape(4, cols), input_bias]), ((0, 2), (0, 0)))
    valid = lax.dynamic_index_in_dim(token_valid, t, 0, keepdims=False)
    image = lax.dynamic_index_in_dim(image_valid, t, 0, keepdims=False)
    pad = (0, full - length)
    key_ok = jnp.pad((valid > 0) | (jnp.arange(length) == 0), pad)
    kb = jnp.broadcast_to(jnp.where(key_ok, 0.0, -1e9).astype(bf16)[:, None], (full, 128))
    rm = jnp.broadcast_to(jnp.pad((valid * image).astype(f32), pad)[:, None], (full, 128))
    return (vec, bias, input_weight, output_weight, up_weight, down_weight, tokens, cotangent, kb, rm)


def rs_kernel(ring, g, out, pv, rc, ry, rr, rl, rb, l_sem, c_s, c_r, y_s, y_r, ring_s, ring_r):
    _, _, rows, wide = g.shape
    n = wide // 2
    w = Place(2 * ring, n)
    half = rows // 2
    far = ring // 2
    greet((w.right, w.left, w.across, w.sibling))
    cs, ys, rs = (c_s, c_r), (y_s, y_r), (ring_s, ring_r)
    pend = []
    def go(src, dst, sems, k, dev):
        cp = rcopy(src, dst, sems[0].at[k], sems[1].at[k], dev); cp.start(); pend.append(cp); return cp
    order = [far]
    for k in range(far - 1, 0, -1): order += [k, -k]
    order.append(0)
    ccp, lcp, ycp = {}, {}, {}
    for i, k in enumerate(order):
        chip = w.chip_at(k)
        ccp[k] = go(g.at[chip, 1 - w.core], rc.at[i], cs, i, w.sibling)
        lcp[k] = pltpu.make_async_copy(g.at[chip, w.core], pv.at[i], l_sem.at[i]); lcp[k].start()
    def addto(ref, lo, size, cols, other):
        start, width = cols
        ch = 8 if size % 16 else 16
        @pl.loop(0, size // ch)
        def _(r):
            rw = pl.ds(pl.multiple_of(lo + r * ch, ch), ch)
            v = ref[rw, pl.ds(start, width)].astype(f32) + other[pl.ds(pl.multiple_of(lo + r * ch, ch), ch), :].astype(f32)
            ref[rw, pl.ds(start, width)] = v.astype(bf16)
    idx = {k: i for i, k in enumerate(order)}
    def core_add(k):
        i = idx[k]
        ccp[k].wait_recv(); lcp[k].wait()
        addto(pv.at[i], 0, rows, (0, wide), rc.at[i])
        ref = pv.at[i, :, pl.ds(w.their_a[0], w.a)]
        ycp[k] = go(ref, ry.at[i], ys, i, w.across)
    def y_add(k):
        i = idx[k]
        ycp[k].wait_recv()
        addto(pv.at[i], 0, rows, w.mine_a, ry.at[i])
    rcp = {}
    core_add(order[0])
    ringw = pl.ds(w.ring_cols[0], w.ring_cols[1])
    for j, k in enumerate(order):
        if j + 1 < len(order): core_add(order[j + 1])
        y_add(k)
        i = idx[k]
        if k == far:
            rcp["r", 0] = go(pv.at[i, pl.ds(0, half), ringw], rr.at[0, pl.ds(0, half)], rs, 0, w.right)
            rcp["l", 0] = go(pv.at[i, pl.ds(half, half), ringw], rl.at[0, pl.ds(half, half)], rs, 8, w.left)
            continue
        st = far - abs(k)
        if k > 0:
            rcp["r", st - 1].wait_recv()
            addto(pv.at[i], 0, half if st == 1 else rows, w.ring_cols, rr.at[st - 1])
            rcp["r", st] = go(pv.at[i, :, ringw], rr.at[st], rs, st, w.right)
        elif k < 0:
            rcp["l", st - 1].wait_recv()
            if st == 1: addto(pv.at[i], half, half, w.ring_cols, rl.at[0])
            else: addto(pv.at[i], 0, rows, w.ring_cols, rl.at[st - 1])
            rcp["l", st] = go(pv.at[i, :, ringw], rl.at[st], rs, 8 + st, w.left)
        else:
            rcp["r", far - 1].wait_recv(); rcp["l", far - 1].wait_recv()
            addto(pv.at[i], 0, rows, w.ring_cols, rr.at[far - 1])
            addto(pv.at[i], 0, rows, w.ring_cols, rl.at[far - 1])
            fin = go(pv.at[i, :, pl.ds(w.their_b[0], w.b)], rb, ys, len(order), w.across)
            fin.wait_recv()
            addto(pv.at[i], 0, rows, w.mine_b, rb)
            ch = 16
            @pl.loop(0, rows // ch)
            def _(r):
                rw = pl.ds(pl.multiple_of(r * ch, ch), ch)
                out[rw, :] = pv[i, rw, pl.ds(w.own_cols[0], n)].astype(f32)
    for cp in pend: cp.wait_send()

def scatter_group(g, dp, cid):
    depth, wide = g.shape
    rows = depth // dp
    n = wide // 2
    a, b = split_of(n)
    ring = dp // 2
    dma = pltpu.SemaphoreType.DMA
    V = pltpu.VMEM
    return pl.pallas_call(functools.partial(rs_kernel, ring),
        out_shape=jax.ShapeDtypeStruct((rows, n), f32),
        in_specs=[pl.BlockSpec(memory_space=pl.ANY)], out_specs=pl.BlockSpec(memory_space=pltpu.VMEM),
        scratch_shapes=[V((ring, rows, wide), bf16), V((ring, rows, wide), bf16), V((ring, rows, a), bf16),
            V((ring // 2, rows, 2 * n - a), bf16), V((ring // 2, rows, 2 * n - a), bf16), V((rows, b), bf16),
            dma((ring,)), dma((ring,)), dma((ring,)), dma((ring + 1,)), dma((ring + 1,)), dma((16,)), dma((16,))],
        compiler_params=pltpu.CompilerParams(collective_id=cid, has_side_effects=True, vmem_limit_bytes=56 << 20), name="scatter_group")(
        g.reshape(ring, 2, rows, wide))


def sum_kernel(dp, v, out, buf, s_sem, r_sem):
    d = lax.axis_index("dp")
    t = lax.axis_index("tensor")
    peers = [(d, 1 - t)]
    k = 1
    while k < dp:
        peers.append((d + k - 2 * k * ((d // k) % 2), t))
        k *= 2
    greet(peers)
    out[...] = v[...]
    for i, a in enumerate(peers):
        buf[i, 0] = out[...]
        cp = rcopy(buf.at[i, 0], buf.at[i, 1], s_sem.at[i], r_sem.at[i], a)
        cp.start()
        cp.wait()
        out[...] = out[...] + buf[i, 1]


def sum_vectors(v, dp, cid):
    dma = pltpu.SemaphoreType.DMA
    steps = dp.bit_length()
    return pl.pallas_call(
        functools.partial(sum_kernel, dp),
        out_shape=jax.ShapeDtypeStruct(v.shape, v.dtype),
        in_specs=[pl.BlockSpec(memory_space=pltpu.VMEM)],
        out_specs=pl.BlockSpec(memory_space=pltpu.VMEM),
        scratch_shapes=[pltpu.VMEM((steps, 2) + v.shape, v.dtype), dma((steps,)), dma((steps,))],
        compiler_params=pltpu.CompilerParams(collective_id=cid, has_side_effects=True),
        name="sum_vectors",
    )(v)


def paired_device(*args):
    dp = lax.axis_size("dp")
    d = lax.axis_index("dp")
    t = lax.axis_index("tensor")
    tokens, cotangent = args[0], args[1]
    length, width = tokens.shape
    share, n = args[12].shape
    cols = n // 4
    ready = prepare(*args)
    o = forward(ready, dp, length, width, n, share)
    dot = functools.partial(jnp.einsum, preferred_element_type=f32)
    heads = width // HEAD_DIM
    gain_one, shift_one, out_shift, gain_two, shift_two, down_shift = o.vecs_o[:6]
    row_mask = ready[9][:length, 0:1]
    key_ok = ready[8][:length, 0] == 0
    scale = HEAD_DIM ** (-0.5)
    inputs = tokens.astype(f32)
    first = layer_norm(inputs, gain_one, shift_one).astype(bf16)
    q = (o.qkv_o[:length, :width] * jnp.bfloat16(8.0)).reshape(length, heads, HEAD_DIM)
    k = o.qkv_o[:length, width : 2 * width].reshape(length, heads, HEAD_DIM)
    v = o.qkv_o[:length, 2 * width :].reshape(length, heads, HEAD_DIM)
    w1, w2, w3 = o.w1, o.w2, o.w3
    wo = jnp.concatenate([w1[:, 3 * cols : 4 * cols], w1[:, 7 * cols :]], axis=1)
    middle = o.mid_o[:length]
    second = layer_norm(middle, gain_two, shift_two).astype(bf16)
    active = o.act_o[:length]
    mixed = o.mixed_o[:length]
    block_out = (row_mask * (middle + dot("rf,df->rd", active, w3) + down_shift)).astype(bf16)
    grad_last = row_mask * cotangent.astype(f32)
    gr = grad_last.astype(bf16)
    g3 = dot("rd,rf->df", gr, active).astype(bf16)
    dhid = (dot("rd,df->rf", gr, w3) * o.slope_o[:length].astype(f32)).astype(bf16)
    g2 = dot("rd,rf->df", second, dhid).astype(bf16)
    dsecond = dot("rf,df->rd", dhid, w2)
    dmiddle, g_gain2, g_shift2 = norm_backward(middle, gain_two, dsecond)
    dmiddle = dmiddle + grad_last
    mr = dmiddle.astype(bf16)
    dmixed = dot("rd,de->re", mr, wo).astype(bf16)
    gwo = dot("rd,re->de", mr, mixed).astype(bf16)
    scores = jnp.where(key_ok[None, None, :], dot("qhe,khe->hqk", q, k) * scale, -1000000000.0)
    probs = jnp.exp(scores - o.logs_o[:, :length, None])
    dm = dmixed.reshape(length, heads, HEAD_DIM)
    dv = dot("hqk,qhe->khe", probs.astype(bf16), dm).astype(bf16).reshape(length, width)
    dprobs = dot("qhe,khe->hqk", dm, v)
    ds = (probs * (dprobs - jnp.sum(probs * dprobs, axis=-1, keepdims=True))).astype(bf16)
    dq = (dot("hqk,khe->qhe", ds, k) * scale).astype(bf16).reshape(length, width)
    dk = (dot("hqk,qhe->khe", ds, q) * scale).astype(bf16).reshape(length, width)
    c = cols
    zero = jnp.zeros((length, c), bf16)
    dcat = jnp.concatenate([dq[:, :c], dk[:, :c], dv[:, :c], zero, dq[:, c:], dk[:, c:], dv[:, c:], zero], axis=1)
    gin = dot("rd,rc->dc", first, dcat).astype(bf16)
    g1 = jnp.concatenate([gin[:, : 3 * c], gwo[:, :c], gin[:, 4 * c : 7 * c], gwo[:, c:]], axis=1)
    dfirst = dot("rc,dc->rd", dcat, w1)
    grad_inputs, g_gain1, g_shift1 = norm_backward(inputs, gain_one, dfirst)
    grad_inputs = grad_inputs + dmiddle
    o3 = scatter_group(g3, dp, 2)
    o2 = scatter_group(g2, dp, 2)
    o1 = scatter_group(g1, dp, 2)
    rows = jnp.stack(
        [
            g_gain1,
            g_shift1,
            jnp.sum(dmiddle, axis=0),
            g_gain2,
            g_shift2,
            jnp.sum(grad_last, axis=0),
            jnp.sum(dq.astype(f32), axis=0),
            jnp.sum(dv.astype(f32), axis=0),
        ]
    )
    rows = jnp.concatenate([rows, jnp.sum(dhid.astype(f32), axis=0).reshape(-1, width)])
    rows = sum_vectors(rows, dp, 4)
    vectors = lax.dynamic_slice_in_dim(rows[:6], d * share, share, 1)
    bias_own = lax.dynamic_slice_in_dim(rows[6:8], t * cols, cols, 1)
    up_own = lax.dynamic_slice_in_dim(rows[8:].reshape(-1), t * n, n, 0)
    return (
        block_out,
        grad_inputs,
        vectors[0],
        vectors[1],
        o1[:, : 3 * cols].reshape(share, 3, cols),
        bias_own,
        o1[:, 3 * cols :].T,
        vectors[2],
        vectors[3],
        vectors[4],
        o2,
        up_own,
        o3.T,
        vectors[5],
    )


def solution(mesh):
    in_specs = (
        P(("dp", "tensor"), None),
        P(("dp", "tensor"), None),
        P("dp", None),
        P("dp"),
        P("dp"),
        P("dp"),
        P("dp", None, "tensor"),
        P(None, "tensor"),
        P("tensor", "dp"),
        P("dp"),
        P("dp"),
        P("dp"),
        P("dp", "tensor"),
        P("tensor"),
        P("tensor", "dp"),
        P("dp"),
    )
    out_specs = (
        P(("dp", "tensor"), None),
        P(("dp", "tensor"), None),
        P("dp"),
        P("dp"),
        P("dp", None, "tensor"),
        P(None, "tensor"),
        P("tensor", "dp"),
        P("dp"),
        P("dp"),
        P("dp"),
        P("dp", "tensor"),
        P("tensor"),
        P("tensor", "dp"),
        P("dp"),
    )
    ready = mesh.shape["tensor"] == 2 and mesh.shape["dp"] == 16
    body = paired_device if ready else general_device
    return jax.shard_map(
        body, mesh=mesh, in_specs=in_specs, out_specs=out_specs, check_vma=False
    )
```

```python
import functools
import types

import jax
import jax.numpy as jnp
from jax import lax
from jax.experimental import pallas as pl
from jax.experimental.pallas import tpu as pltpu
from jax.sharding import PartitionSpec as P

HEAD_DIM = 64
MESH = pl.DeviceIdType.MESH
f32 = jnp.float32
bf16 = jnp.bfloat16
NN, NT, TN = ((1,), (0,)), ((1,), (1,)), ((0,), (0,))


def layer_norm(inputs, gain, shift):
    center = inputs - jnp.mean(inputs, axis=-1, keepdims=True)
    spread = jnp.mean(center * center, axis=-1, keepdims=True)
    return center * lax.rsqrt(spread + 1e-06) * gain + shift


def norm_backward(inputs, gain, upstream):
    center = inputs - jnp.mean(inputs, axis=-1, keepdims=True)
    spread = jnp.mean(center * center, axis=-1, keepdims=True)
    scaled = lax.rsqrt(spread + 1e-06)
    unit = center * scaled
    weighted = upstream * gain
    grad_inputs = scaled * (
        weighted
        - jnp.mean(weighted, axis=-1, keepdims=True)
        - unit * jnp.mean(weighted * unit, axis=-1, keepdims=True)
    )
    return (grad_inputs, jnp.sum(upstream * unit, axis=0), jnp.sum(upstream, axis=0))


def gelu_slope(hidden):
    return (
        0.5 * (1.0 + lax.erf(hidden * 0.7071067811865476))
        + hidden * jnp.exp(-0.5 * hidden * hidden) * 0.3989422804014327
    )


def general_device(
    tokens,
    cotangent,
    token_valid,
    image_valid,
    first_gain,
    first_shift,
    input_weight,
    input_bias,
    output_weight,
    output_bias,
    second_gain,
    second_shift,
    up_weight,
    up_bias,
    down_weight,
    down_bias,
):
    f32 = jnp.float32
    bf16 = jnp.bfloat16
    gathered = (
        lax.all_gather(first_gain, "dp", axis=0, tiled=True),
        lax.all_gather(first_shift, "dp", axis=0, tiled=True),
        lax.all_gather(input_weight, "dp", axis=0, tiled=True),
        lax.all_gather(output_weight, "dp", axis=1, tiled=True),
        lax.all_gather(output_bias, "dp", axis=0, tiled=True),
        lax.all_gather(second_gain, "dp", axis=0, tiled=True),
        lax.all_gather(second_shift, "dp", axis=0, tiled=True),
        lax.all_gather(up_weight, "dp", axis=0, tiled=True),
        lax.all_gather(down_weight, "dp", axis=1, tiled=True),
        lax.all_gather(down_bias, "dp", axis=0, tiled=True),
    )
    (
        gain_one,
        shift_one,
        in_full,
        out_full,
        out_shift,
        gain_two,
        shift_two,
        up_full,
        down_full,
        down_shift,
    ) = gathered
    gain_one = gain_one.astype(f32)
    shift_one = shift_one.astype(f32)
    out_shift = out_shift.astype(f32)
    gain_two = gain_two.astype(f32)
    shift_two = shift_two.astype(f32)
    down_shift = down_shift.astype(f32)
    tensor_at = lax.axis_index("tensor")
    groups = lax.axis_size("tensor")
    own_rows = tokens.shape[0]
    width = tokens.shape[1]
    length = token_valid.shape[1]
    positions = lax.broadcasted_iota(jnp.int32, token_valid.shape, 1)
    key_ok = (token_valid > 0) | (positions == 0)
    mask_all = (token_valid * image_valid[:, None]).astype(f32).reshape(-1)
    row_mask = lax.dynamic_slice_in_dim(mask_all, tensor_at * own_rows, own_rows)[:, None]
    images = token_valid.shape[0]
    local_width = in_full.shape[2]
    local_heads = local_width // HEAD_DIM
    hidden_width = up_full.shape[1]
    scale = HEAD_DIM ** (-0.5)
    head_shape = (images, length, local_heads, HEAD_DIM)
    inputs = tokens.astype(f32)
    first_own = layer_norm(inputs, gain_one, shift_one).astype(bf16)
    first_all = lax.all_gather(first_own, "tensor", axis=0, tiled=True)
    project = jnp.einsum("rd,dce->rce", first_all, in_full, preferred_element_type=f32)
    bias_in = input_bias.astype(f32)
    queries = (project[:, 0] + bias_in[0]).astype(bf16).reshape(head_shape)
    keyset = project[:, 1].astype(bf16).reshape(head_shape)
    values = (project[:, 2] + bias_in[1]).astype(bf16).reshape(head_shape)

    def scores_of(query_img, key_img, ok_img):
        scores = jnp.einsum("qhe,khe->hqk", query_img, key_img, preferred_element_type=f32) * scale
        return jnp.where(ok_img[None, None, :], scores, -1000000000.0)

    def attend(pieces):
        query_img, key_img, value_img, ok_img = pieces
        scores = scores_of(query_img, key_img, ok_img)
        highest = jnp.max(scores, axis=-1, keepdims=True)
        log_total = highest + jnp.log(jnp.sum(jnp.exp(scores - highest), axis=-1, keepdims=True))
        attn_probs = jnp.exp(scores - log_total).astype(bf16)
        mixed_img = jnp.einsum("hqk,khe->qhe", attn_probs, value_img, preferred_element_type=f32)
        return (mixed_img.astype(bf16), log_total)

    mixed, log_totals = lax.map(attend, (queries, keyset, values, key_ok))
    mixed_rows = mixed.reshape(images * length, local_width)
    attended = lax.psum_scatter(
        jnp.dot(mixed_rows, out_full, preferred_element_type=f32).astype(jnp.bfloat16),
        "tensor",
        scatter_dimension=0,
        tiled=True,
    ).astype(jnp.float32)
    middle = inputs + attended + out_shift
    second_own = layer_norm(middle, gain_two, shift_two).astype(bf16)
    second_all = lax.all_gather(second_own, "tensor", axis=0, tiled=True)
    hidden = jnp.dot(second_all, up_full, preferred_element_type=f32) + up_bias.astype(f32)
    active = jax.nn.gelu(hidden, approximate=False).astype(bf16)
    lifted = lax.psum_scatter(
        jnp.dot(active, down_full, preferred_element_type=f32).astype(jnp.bfloat16),
        "tensor",
        scatter_dimension=0,
        tiled=True,
    ).astype(jnp.float32)
    block_out = (row_mask * (middle + lifted + down_shift)).astype(bf16)
    grad_last = row_mask * cotangent.astype(f32)
    first_all, second_all = (
        lax.all_gather(first_own, "tensor", axis=0, tiled=True),
        lax.all_gather(second_own, "tensor", axis=0, tiled=True),
    )
    grad_lift = lax.all_gather(grad_last.astype(bf16), "tensor", axis=0, tiled=True)
    grad_active = jnp.einsum("rd,fd->rf", grad_lift, down_full, preferred_element_type=f32)
    grad_hidden = (grad_active * gelu_slope(hidden)).astype(bf16)
    grad_down = jnp.einsum("rf,rd->fd", active, grad_lift, preferred_element_type=f32)
    grad_up = jnp.einsum("rd,rf->df", second_all, grad_hidden, preferred_element_type=f32)
    grad_up_bias = jnp.sum(grad_hidden.astype(f32), axis=0)
    grad_second = lax.psum_scatter(
        jnp.einsum("rf,df->rd", grad_hidden, up_full, preferred_element_type=f32).astype(
            jnp.bfloat16
        ),
        "tensor",
        scatter_dimension=0,
        tiled=True,
    ).astype(jnp.float32)
    grad_middle, grad_gain_two, grad_shift_two = norm_backward(middle, gain_two, grad_second)
    grad_middle = grad_middle + grad_last
    grad_mid_all = lax.all_gather(grad_middle.astype(bf16), "tensor", axis=0, tiled=True)
    grad_mixed = jnp.einsum("rd,ed->re", grad_mid_all, out_full, preferred_element_type=f32).astype(
        bf16
    )
    grad_out_weight = jnp.einsum("re,rd->ed", mixed_rows, grad_mid_all, preferred_element_type=f32)

    def attend_back(pieces):
        query_img, key_img, value_img, ok_img, total_img, grad_img = pieces
        scores = scores_of(query_img, key_img, ok_img)
        attn_probs = jnp.exp(scores - total_img)
        grad_values = jnp.einsum(
            "hqk,qhe->khe", attn_probs.astype(bf16), grad_img, preferred_element_type=f32
        )
        grad_probs = jnp.einsum("qhe,khe->hqk", grad_img, value_img, preferred_element_type=f32)
        grad_scores = (
            attn_probs * (grad_probs - jnp.sum(attn_probs * grad_probs, axis=-1, keepdims=True))
        ).astype(bf16)
        grad_queries = (
            jnp.einsum("hqk,khe->qhe", grad_scores, key_img, preferred_element_type=f32) * scale
        )
        grad_keys = (
            jnp.einsum("hqk,qhe->khe", grad_scores, query_img, preferred_element_type=f32) * scale
        )
        return jnp.stack([grad_queries, grad_keys, grad_values], axis=1).astype(bf16)

    grad_project = lax.map(
        attend_back, (queries, keyset, values, key_ok, log_totals, grad_mixed.reshape(head_shape))
    )
    grad_project = grad_project.reshape(images * length, 3, local_width)
    grad_in_weight = jnp.einsum("rd,rce->dce", first_all, grad_project, preferred_element_type=f32)
    grad_in_bias = jnp.sum(grad_project[:, 0::2].astype(f32), axis=0)
    grad_first = lax.psum_scatter(
        jnp.einsum("rce,dce->rd", grad_project, in_full, preferred_element_type=f32).astype(
            jnp.bfloat16
        ),
        "tensor",
        scatter_dimension=0,
        tiled=True,
    ).astype(jnp.float32)
    grad_inputs, grad_gain_one, grad_shift_one = norm_backward(inputs, gain_one, grad_first)
    grad_inputs = grad_inputs + grad_middle
    grad_in_own, grad_out_own, grad_up_own, grad_down_own = (
        lax.psum_scatter(
            grad_in_weight.astype(jnp.bfloat16), "dp", scatter_dimension=0, tiled=True
        ).astype(jnp.float32),
        lax.psum_scatter(
            grad_out_weight.astype(jnp.bfloat16), "dp", scatter_dimension=1, tiled=True
        ).astype(jnp.float32),
        lax.psum_scatter(
            grad_up.astype(jnp.bfloat16), "dp", scatter_dimension=0, tiled=True
        ).astype(jnp.float32),
        lax.psum_scatter(
            grad_down.astype(jnp.bfloat16), "dp", scatter_dimension=1, tiled=True
        ).astype(jnp.float32),
    )
    vectors = jnp.stack(
        [
            grad_gain_one,
            grad_shift_one,
            jnp.sum(grad_middle, axis=0),
            grad_gain_two,
            grad_shift_two,
            jnp.sum(grad_last, axis=0),
        ]
    )
    bias_share = input_bias.shape[1]
    up_share = up_bias.shape[0]
    placed_bias = lax.dynamic_update_slice(
        jnp.zeros((2, width), f32), grad_in_bias, (0, tensor_at * local_width)
    )
    placed_up = lax.dynamic_update_slice(
        jnp.zeros((hidden_width * groups,), f32), grad_up_bias, (tensor_at * hidden_width,)
    )
    vectors, placed_bias, placed_up = lax.psum((vectors, placed_bias, placed_up), ("dp", "tensor"))
    share = first_gain.shape[0]
    dp_at = lax.axis_index("dp")
    vectors = lax.dynamic_slice_in_dim(vectors, dp_at * share, share, 1)
    bias_own = lax.dynamic_slice_in_dim(placed_bias, tensor_at * bias_share, bias_share, 1)
    up_bias_own = lax.dynamic_slice_in_dim(placed_up, tensor_at * up_share, up_share, 0)
    return (
        block_out,
        grad_inputs,
        vectors[0],
        vectors[1],
        grad_in_own,
        bias_own,
        grad_out_own,
        vectors[2],
        vectors[3],
        vectors[4],
        grad_up_own,
        up_bias_own,
        grad_down_own,
        vectors[5],
    )


def mul(a, b, dims):
    return lax.dot_general(a, b, (dims, ((), ())), preferred_element_type=f32)


def iota(shape, axis):
    return lax.broadcasted_iota(jnp.int32, shape, axis)


def tile(j, size):
    return pl.ds(pl.multiple_of(j * size, size), size)


def split_of(n):
    a = (n * 4 // 7) // 128 * 128
    return a, n - a


class Place:
    def __init__(self, dp, n):
        d = lax.axis_index("dp")
        t = lax.axis_index("tensor")
        ring = dp // 2
        self.dp, self.d, self.t, self.ring, self.far = dp, d, t, ring, ring // 2
        self.chip, self.core = d // 2, d % 2
        self.pos = jnp.where(self.chip % 2 == 0, self.chip // 2, ring - 1 - self.chip // 2)
        self.right = (self.chip_at(1) * 2 + self.core, t)
        self.left = (self.chip_at(-1) * 2 + self.core, t)
        self.across = (d, 1 - t)
        self.sibling = (d + 1 - 2 * self.core, t)
        a, b = split_of(n)
        self.n, self.a, self.b = n, a, b
        self.own_cols = (pl.multiple_of(t * n, 128), n)
        self.other_cols = (pl.multiple_of((1 - t) * n, 128), n)
        self.ring_cols = (pl.multiple_of(t * a, 128), 2 * n - a)
        self.mine_a = (pl.multiple_of(t * (2 * n - a), 128), a)
        self.their_a = (pl.multiple_of((1 - t) * (2 * n - a), 128), a)
        self.their_b = (pl.multiple_of(n - t * b, 128), b)
        self.mine_b = (pl.multiple_of(n - (1 - t) * b, 128), b)

    def chip_at(self, offset):
        ring = self.ring
        spot = (self.pos + offset + ring) % ring
        return jnp.where(spot < ring // 2, 2 * spot, 2 * (ring - 1 - spot) + 1)


def greet(targets):
    bar = pltpu.get_barrier_semaphore()
    for a in targets:
        pl.semaphore_signal(bar, inc=1, device_id=a, device_id_type=MESH)
    pl.semaphore_wait(bar, len(targets))


def rcopy(src, dst, send, recv, dev):
    return pltpu.make_async_remote_copy(
        src_ref=src, dst_ref=dst, send_sem=send, recv_sem=recv, device_id=dev, device_id_type=MESH
    )


class Gather:
    def __init__(self, w, g, shard, full, sems):
        self.w, self.g, self.shard, self.full, self.sems = w, g, shard, full, sems
        self.rows = shard.shape[0]

    def block(self, offset, cols, span=None):
        w = self.w
        lo, size = span or (0, self.rows)
        base = w.chip_at(offset) * (2 * self.rows) + w.core * self.rows + lo
        return self.full.at[pl.ds(pl.multiple_of(base, 16), size), pl.ds(cols[0], cols[1])]

    def span(self, s, dirn):
        half = self.rows // 2
        return (0, self.rows) if s < self.w.far else (dirn * half, half)

    def off(self, s, dirn):
        return s if dirn else -s

    def make(self, kind, src, dst, k, dev):
        send, recv = self.sems[kind]
        return rcopy(src, dst, send.at[self.g, k], recv.at[self.g, k], dev)

    def y(self, s, dirn):
        if s == 0:
            return self.make("y", self.shard, self.block(0, self.w.own_cols), 0, self.w.across)
        ref = self.block(self.off(s, dirn), self.w.mine_a, self.span(s, dirn))
        return self.make("y", ref, ref, 2 * s - 1 + dirn, self.w.across)

    def ring(self, s, dirn, part=0):
        dev = self.w.left if dirn else self.w.right
        k = dirn * (self.w.far + 1)
        if s == 1 and part == 0:
            return self.make("r", self.shard, self.block(0, self.w.own_cols), k, dev)
        if s == 1:
            ref = self.block(0, self.w.their_b)
            return self.make("r", ref, ref, k + 1, dev)
        ref = self.block(self.off(s - 1, dirn), self.w.ring_cols, self.span(s, dirn))
        return self.make("r", ref, ref, k + s, dev)

    def sib(self, k):
        w = self.w
        if k == 0:
            src, dst = self.shard, self.block(0, w.own_cols)
        elif k == 1:
            src = dst = self.block(0, w.other_cols)
        else:
            which, rest = divmod(k - 2, 2 * w.far)
            s, dirn = rest // 2 + 1, rest % 2
            cols = w.their_a if which else w.ring_cols
            src = dst = self.block(self.off(s, dirn), cols, self.span(s, dirn))
        return self.make("c", src, dst, k, w.sibling)

    def keep(self):
        return pltpu.make_async_copy(self.shard, self.block(0, self.w.own_cols), self.sems["k"].at[self.g])

    def start(self):
        self.y(0, 0).start()
        self.ring(1, 0).start()
        self.ring(1, 1).start()
        self.sib(0).start()
        self.keep().start()

    def first_y(self):
        self.y(0, 0).wait_recv()
        self.ring(1, 0, 1).start()
        self.ring(1, 1, 1).start()
        self.sib(1).start()

    def hop(self, s):
        for dirn in (0, 1):
            self.ring(s, dirn).wait_recv()
            if s == 1:
                self.ring(s, dirn, 1).wait_recv()
            if s < self.w.far:
                self.ring(s + 1, dirn).start()
            self.y(s, dirn).start()
            self.sib(2 * s + dirn).start()

    def cross(self, s):
        for dirn in (0, 1):
            self.y(s, dirn).wait_recv()
            self.sib(2 + 2 * self.w.far + 2 * (s - 1) + dirn).start()

    def end(self):
        far = self.w.far
        for k in range(2 + 4 * far):
            self.sib(k).wait()
        self.keep().wait()

    def drain(self):
        far = self.w.far
        self.y(0, 0).wait_send()
        for dirn in (0, 1):
            self.ring(1, dirn).wait_send()
            self.ring(1, dirn, 1).wait_send()
            for s in range(1, far + 1):
                self.y(s, dirn).wait_send()
                if s > 1:
                    self.ring(s, dirn).wait_send()


def gather_sems(dp, groups):
    far = dp // 4
    dma = pltpu.SemaphoreType.DMA
    sizes = (2 * (far + 1), 2 * far + 1, 4 * far + 2)
    return [dma((groups, k)) for k in sizes for _ in (0, 1)] + [dma((groups,))]


def stream(count, parts, sem, body):
    def copies(j):
        slot = lax.rem(j, 2)
        return [
            pltpu.make_async_copy(src(j), buf.at[slot], sem.at[i, slot]) for i, (src, buf) in enumerate(parts)
        ]

    for cp in copies(jnp.int32(0)):
        cp.start()

    @pl.loop(0, count)
    def _(j):
        @pl.when(j + 1 < count)
        def _():
            for cp in copies(j + 1):
                cp.start()

        for cp in copies(j):
            cp.wait()
        body(j, lax.rem(j, 2))


def ticks(j, table):
    for at, events in table.items():

        @pl.when(j == at)
        def _(events=events):
            for e in events:
                e()


def normalize(x):
    center = x - jnp.mean(x, axis=-1, keepdims=True)
    scaled = lax.rsqrt(jnp.mean(center * center, axis=-1, keepdims=True) + 1e-06)
    return center * scaled, scaled


def attend_pair(m, i, rows, full):
    width = m.mixed.shape[1]
    ps = tile(i, 128)
    q2 = m.qkv[0:rows, ps]
    k2 = m.qkv[:, pl.ds(pl.multiple_of(width + i * 128, 128), 128)]
    v2 = m.qkv[:, pl.ds(pl.multiple_of(2 * width + i * 128, 128), 128)]
    lq, lk = iota((rows, 128), 1), iota((full, 128), 1)
    outs = []
    logs = m.logs[0:rows, :]
    for h in (0, 1):
        spare = 64 * (1 - h)
        own_q = (lq < 64) if h == 0 else (lq >= 64)
        own_k = (lk < 64) if h == 0 else (lk >= 64)
        qh = jnp.where(own_q, q2, jnp.where(lq == spare, 1.0, 0.0).astype(bf16))
        kh = jnp.where(lk == spare, m.key_bias[...], k2)
        scores = mul(qh, kh, NT)
        top = jnp.max(scores, axis=1, keepdims=True)
        probs = jnp.exp(scores - top).astype(bf16)
        out = mul(probs, jnp.where(own_k, v2, jnp.ones_like(v2)), NN)
        turned = pltpu.roll(out, 64, 1)
        outs.append(out / turned)
        total = jnp.where(own_q, turned, out)
        logs = jnp.where(lq == 2 * i + h, top + jnp.log(total), logs)
    m.logs[0:rows, :] = logs
    m.mixed[0:rows, ps] = jnp.where(lq < 64, outs[0], outs[1]).astype(bf16)


FWD_IN = ("vec", "bias", "iw", "ow", "uw", "dw", "tok", "cot", "kb", "rm")
FWD_OUT = ("w1", "w2", "w3", "qkv_o", "mixed_o", "logs_o", "mid_o", "act_o", "slope_o", "p3_o", "lhs1_o", "lhs2_o", "gr_o", "vecs_o")


def fwd_kernel(dp, rows, names, *refs):
    m = types.SimpleNamespace(**dict(zip(names, refs)))
    m.key_bias = m.kb
    n = m.uw.shape[1]
    w = Place(dp, n)
    length, width = m.tok.shape
    full = m.qkv.shape[0]
    share = m.sh1.shape[0]
    cols = n // 4
    sems = {"r": (m.ring_s, m.ring_r), "y": (m.y_s, m.y_r), "c": (m.c_s, m.c_r), "k": m.k_sem}
    g1 = Gather(w, 0, m.sh1, m.w1, sems)
    g2 = Gather(w, 1, m.uw, m.w2, sems)
    g3 = Gather(w, 2, m.sh3, m.w3, sems)
    tok_in = pltpu.make_async_copy(m.tok, m.xs.at[pl.ds(0, length)], m.l_sem.at[0])
    cot_in = pltpu.make_async_copy(m.cot, m.gr.at[pl.ds(0, length)], m.l_sem.at[1])
    tok_in.start()
    cot_in.start()
    peers = [(lax.rem(w.d + i, dp), w.t) for i in range(1, dp)] + [w.across]
    bar = pltpu.get_barrier_semaphore()
    for a in peers:
        pl.semaphore_signal(bar, inc=1, device_id=a, device_id_type=MESH)
    for s in range(3):
        m.sh1[:, tile(s, cols)] = m.iw[:, s, :]
    m.sh1[:, tile(3, cols)] = m.ow[...].T
    pl.semaphore_wait(bar, len(peers))
    g1.start()
    spot = pl.ds(pl.multiple_of(w.chip * 128, 128), 128)

    def vec_copy(i):
        return rcopy(m.vec, m.vbuf.at[w.core, :, spot], m.v_s.at[i], m.v_r.at[i], peers[i])

    bias_copy = rcopy(m.bias, m.bbuf.at[w.t], m.v_s.at[dp - 1], m.v_r.at[dp - 1], w.across)
    for i in range(dp - 1):
        vec_copy(i).start()
    bias_copy.start()
    m.vbuf[w.core, :, spot] = m.vec[...]
    m.bbuf[w.t] = m.bias[...]
    m.sh3[...] = m.dw[...].T
    zero_rows = pl.ds(rows, full - rows)
    for ref in (m.qkv, m.act, m.mixed):
        ref[zero_rows, :] = jnp.zeros((full - rows, ref.shape[1]), bf16)
    m.logs[...] = jnp.zeros(m.logs.shape, f32)
    m.mid[zero_rows, :] = jnp.zeros((full - rows, width), f32)
    tail = pl.ds(length, full - length)
    tok_in.wait()
    cot_in.wait()
    m.xs[tail, :] = jnp.zeros((full - length, width), bf16)
    m.gr[tail, :] = jnp.zeros((full - length, width), bf16)
    for i in range(dp - 1):
        vec_copy(i).wait()
    bias_copy.wait()
    vecs = m.vbuf[0].astype(f32) + m.vbuf[1].astype(f32)
    m.vecs[...] = vecs
    m.qb[...] = jnp.zeros(m.qb.shape, f32)
    for side in (0, 1):
        b = m.bbuf[side].astype(f32)
        m.ub[4 * side : 4 * side + 4, :] = b[0:4]
        m.qb[side : side + 1, :] = b[4:5]
        m.qb[4 + side : 5 + side, :] = b[5:6]
    ch = 64

    @pl.loop(0, full // ch)
    def _(r):
        rs = tile(r, ch)
        unit, _ = normalize(m.xs[rs, :].astype(f32))
        m.ln[rs, :] = (unit * m.vecs[0:1, :] + m.vecs[1:2, :]).astype(bf16)
        m.gr[rs, :] = (m.gr[rs, :].astype(f32) * m.rm[rs, 0:1]).astype(bf16)

    def turned(src, k):
        tt, lhs = m.turn.at[k], (m.lhs1, m.lhs2, m.lhs3)[k]

        @pl.loop(0, width // 256)
        def _(j):
            tt[tile(j, 2)] = src[:, tile(j, 256)].T.reshape(2, 2, share, full)

        return turn_copies(k)

    def turn_copies(k):
        tt, lhs = m.turn.at[k], (m.lhs1, m.lhs2, m.lhs3)[k]
        keep = pltpu.make_async_copy(tt.at[:, w.core], lhs.at[:, :, pl.ds(0, full)], m.t_sem.at[k])
        give = rcopy(
            tt.at[:, 1 - w.core], lhs.at[:, :, pl.ds(full, full)], m.t_s.at[k], m.t_r.at[k], w.sibling
        )
        return keep, give

    outs = []

    def save(src, dst, k):
        cp = pltpu.make_async_copy(src, dst, m.o_sem.at[k])
        outs.append(lambda: pltpu.make_async_copy(src, dst, m.o_sem.at[k]))
        cp.start()

    for k, src in ((0, m.ln), (2, m.gr)):
        for cp in turned(src, k):
            cp.start()
    save(m.gr, m.gr_o, 0)
    save(m.vecs, m.vecs_o, 1)
    g1.first_y()
    g1.hop(1)
    g1.hop(2)
    g1.cross(1)
    g1.hop(3)
    g2.start()
    g1.cross(2)
    g1.hop(4)
    g2.first_y()
    g1.cross(3)
    g1.cross(4)
    g1.end()

    def qkv_tile(j, slot):
        ticks(j, {1: [lambda: g2.hop(1)]})
        p = mul(m.ln[0:rows, :], m.wt[slot], NN) + m.qb[pl.ds(j, 1), :]
        scale = jnp.where(j < 2, HEAD_DIM**-0.5, 1.0)
        m.qkv[0:rows, tile(j, cols)] = (p.astype(bf16).astype(f32) * scale).astype(bf16)

    def in_cols(ref, j, extra=0):
        return ref.at[:, pl.ds(pl.multiple_of((j % 2) * n + (j // 2) * cols + extra, 128), cols)]

    stream(6, [(lambda j: in_cols(m.w1, j), m.wt)], m.s_sem, qkv_tile)
    save(m.qkv, m.qkv_o, 2)

    @pl.loop(0, width // 128)
    def _(i):
        ticks(
            i,
            {
                2: [lambda: g2.hop(2)],
                4: [lambda: g2.cross(1)],
                6: [lambda: g2.hop(3), g3.start],
                7: [lambda: g2.cross(2)],
            },
        )
        attend_pair(m, i, rows, full)

    save(m.mixed, m.mixed_o, 3)
    m.lt[...] = m.logs[...].T[0 : m.lt.shape[0], :]
    save(m.lt, m.logs_o, 4)
    m.mid[0:rows, :] = m.xs[0:rows, :].astype(f32) + m.vecs[2:3, :]

    def out_tile(j, slot):
        m.mid[0:rows, :] += mul(m.mixed[0:rows, tile(j, cols)], m.wt[slot], NT)

    stream(2, [(lambda j: in_cols(m.w1, 6 + j), m.wt)], m.s_sem, out_tile)
    g2.hop(4)
    g3.first_y()
    save(m.mid, m.mid_o, 5)
    for cp in turn_copies(0):
        cp.wait()
    save(m.lhs1, m.lhs1_o, 6)

    @pl.loop(0, full // ch)
    def _(r):
        rs = tile(r, ch)
        unit, _ = normalize(m.mid[rs, :])
        m.ln[rs, :] = (unit * m.vecs[3:4, :] + m.vecs[4:5, :]).astype(bf16)

    g2.cross(3)
    for cp in turned(m.ln, 1):
        cp.start()
    g2.cross(4)
    g2.end()

    def act_copies(j):
        cs = tile(j, cols)
        yield rcopy(m.act.at[:, cs], m.act_sib.at[:, cs], m.a_s.at[j], m.a_r.at[j], w.sibling)
        yield pltpu.make_async_copy(m.act.at[:, cs], m.act_o.at[:, cs], m.a_sem.at[0, j])
        yield pltpu.make_async_copy(m.slope.at[:, cs], m.slope_o.at[:, cs], m.a_sem.at[1, j])

    def up_tile(j, slot):
        ticks(j, {0: [lambda: g3.hop(1)], 6: [lambda: g3.hop(2)]})
        cs = tile(j, cols)
        hidden = mul(m.ln[0:rows, :], m.wt[slot], NN) + m.ub[pl.ds(j, 1), :]
        phi = 0.5 * (1.0 + lax.erf(hidden * 0.7071067811865476))
        m.act[0:rows, cs] = (hidden * phi).astype(bf16)
        m.slope[0:rows, cs] = (
            phi + hidden * jnp.exp(-0.5 * hidden * hidden) * 0.3989422804014327
        ).astype(bf16)
        for cp in act_copies(j):
            cp.start()

    def flat(ref):
        return lambda j: ref.at[:, tile(j, cols)]

    m.slope[zero_rows, :] = jnp.zeros((full - rows, m.slope.shape[1]), bf16)
    stream(8, [(flat(m.w2), m.wt)], m.s_sem, up_tile)
    for cp in turn_copies(2):
        cp.wait()

    def p3_copy(j):
        cs = tile(j, cols)
        return pltpu.make_async_copy(m.p3.at[:, :, cs], m.p3_o.at[:, :, cs], m.a_sem.at[2, j])

    @pl.loop(0, 8)
    def _(j):
        ticks(j, {1: [lambda: g3.cross(1)], 6: [lambda: g3.hop(3)], 7: [lambda: g3.cross(2)]})
        next(act_copies(j)).wait_recv()
        cs = tile(j, cols)
        lhs = m.lhs3[...].reshape(w.ring * share, 2 * full)
        part = mul(lhs[:, 0:full], m.act[:, cs], NN) + mul(lhs[:, full:], m.act_sib[:, cs], NN)
        m.p3[:, :, cs] = part.astype(bf16).reshape(w.ring, share, cols)
        p3_copy(j).start()

    for cp in turn_copies(1):
        cp.wait()
    save(m.lhs2, m.lhs2_o, 7)
    g3.hop(4)
    g3.cross(3)
    g3.cross(4)

    @pl.loop(0, 8)
    def _(j):
        give, a, b = act_copies(j)
        give.wait_send()
        a.wait()
        b.wait()
        p3_copy(j).wait()

    for again in outs:
        again().wait()
    for g in (g1, g2):
        g.drain()
    g3.end()
    g3.drain()


def forward(args, dp, length, width, n, share):
    rows = -(-length // 16) * 16
    full = -(-length // 128) * 128
    cols = n // 4
    ring = dp // 2
    depth = share * dp
    heads = width // HEAD_DIM
    V, dma = pltpu.VMEM, pltpu.SemaphoreType.DMA
    S = jax.ShapeDtypeStruct
    out = dict(
        w1=S((depth, 2 * n), bf16),
        w2=S((depth, 2 * n), bf16),
        w3=S((depth, 2 * n), bf16),
        qkv_o=S((full, 3 * width), bf16),
        mixed_o=S((full, width), bf16),
        logs_o=S((heads, full), f32),
        mid_o=S((full, width), f32),
        act_o=S((full, 2 * n), bf16),
        slope_o=S((full, 2 * n), bf16),
        p3_o=S((ring, share, 2 * n), bf16),
        lhs1_o=S((ring, share, 2 * full), bf16),
        lhs2_o=S((ring, share, 2 * full), bf16),
        gr_o=S((full, width), bf16),
        vecs_o=S((8, width), f32),
    )
    scratch = dict(
        sh1=V((share, n), bf16),
        sh3=V((share, n), bf16),
        xs=V((full, width), bf16),
        gr=V((full, width), bf16),
        ln=V((full, width), bf16),
        qkv=V((full, 3 * width), bf16),
        mixed=V((full, width), bf16),
        logs=V((full, 128), f32),
        lt=V((heads, full), f32),
        mid=V((full, width), f32),
        act=V((full, 2 * n), bf16),
        act_sib=V((full, 2 * n), bf16),
        slope=V((full, 2 * n), bf16),
        p3=V((ring, share, 2 * n), bf16),
        turn=V((3, ring, 2, share, full), bf16),
        lhs1=V((ring, share, 2 * full), bf16),
        lhs2=V((ring, share, 2 * full), bf16),
        lhs3=V((ring, share, 2 * full), bf16),
        wt=V((2, depth, cols), bf16),
        vbuf=V((2, 8, width), bf16),
        bbuf=V((2, 8, cols), bf16),
        vecs=V((8, width), f32),
        ub=V((8, cols), f32),
        qb=V((8, cols), f32),
    )
    gs = gather_sems(dp, 3)
    scratch.update(zip(("ring_s", "ring_r", "y_s", "y_r", "c_s", "c_r", "k_sem"), gs))
    scratch.update(
        v_s=dma((dp,)),
        v_r=dma((dp,)),
        l_sem=dma((2,)),
        s_sem=dma((1, 2)),
        t_sem=dma((3,)),
        t_s=dma((3,)),
        t_r=dma((3,)),
        a_s=dma((8,)),
        a_r=dma((8,)),
        a_sem=dma((3, 8)),
        o_sem=dma((8,)),
    )
    names = FWD_IN + tuple(out) + tuple(scratch)
    hbm = pl.BlockSpec(memory_space=pl.ANY)
    vm = pl.BlockSpec(memory_space=pltpu.VMEM)
    specs = [hbm if k in ("uw", "tok", "cot") else vm for k in FWD_IN]
    got = pl.pallas_call(
        functools.partial(fwd_kernel, dp, rows, names),
        out_shape=list(out.values()),
        in_specs=specs,
        out_specs=[hbm] * len(out),
        scratch_shapes=list(scratch.values()),
        compiler_params=pltpu.CompilerParams(
            collective_id=1, has_side_effects=True, vmem_limit_bytes=62 << 20
        ),
        name="forward",
    )(*args)
    return types.SimpleNamespace(**dict(zip(out, got)))


def prepare(
    tokens, cotangent, token_valid, image_valid, first_gain, first_shift, input_weight, input_bias, output_weight,
    output_bias, second_gain, second_shift, up_weight, up_bias, down_weight, down_bias,
):
    d = lax.axis_index("dp")
    t = lax.axis_index("tensor")
    length = tokens.shape[0]
    full = -(-length // 128) * 128
    share = first_gain.shape[0]
    n = up_weight.shape[1]
    cols = n // 4
    vec = jnp.stack([first_gain, first_shift, output_bias, second_gain, second_shift, down_bias])
    vec = jnp.concatenate([vec, vec], axis=1)
    vec = jnp.where(iota(vec.shape, 1) // share == d % 2, vec, jnp.zeros_like(vec))
    vec = jnp.pad(vec, ((0, 2), (0, 0)))
    bias = jnp.pad(jnp.concatenate([up_bias.reshape(4, cols), input_bias]), ((0, 2), (0, 0)))
    valid = lax.dynamic_index_in_dim(token_valid, t, 0, keepdims=False)
    image = lax.dynamic_index_in_dim(image_valid, t, 0, keepdims=False)
    pad = (0, full - length)
    key_ok = jnp.pad((valid > 0) | (jnp.arange(length) == 0), pad)
    kb = jnp.broadcast_to(jnp.where(key_ok, 0.0, -1e9).astype(bf16)[:, None], (full, 128))
    rm = jnp.broadcast_to(jnp.pad((valid * image).astype(f32), pad)[:, None], (full, 128))
    return (vec, bias, input_weight, output_weight, up_weight, down_weight, tokens, cotangent, kb, rm)


class Scatter:
    def __init__(self, w, g, part, ry, rr, rl, rb, out, sems):
        self.w, self.g, self.part, self.sems = w, g, part, sems
        self.ry, self.rr, self.rl, self.rb, self.out = ry, rr, rl, rb, out
        self.rows = part.shape[1]
        far = w.far
        self.order = [far] + [k * sign for k in range(far - 1, 0, -1) for sign in (1, -1)] + [0]

    def make(self, kind, src, dst, k, dev):
        send, recv = self.sems[kind]
        return rcopy(src, dst, send.at[self.g, k], recv.at[self.g, k], dev)

    def cross(self, k):
        w = self.w
        chip = w.chip_at(k)
        src = self.part.at[chip, :, pl.ds(w.their_a[0], w.a)]
        return self.make("y", src, self.ry.at[chip], self.order.index(k), w.across)

    def ring(self, s, dirn):
        w = self.w
        chip = w.chip_at(s - w.far if dirn else w.far - s)
        half = self.rows // 2
        span = pl.ds(dirn * half, half) if s == 0 else pl.ds(0, self.rows)
        src = self.part.at[chip, span, pl.ds(w.ring_cols[0], w.ring_cols[1])]
        dst = (self.rl if dirn else self.rr).at[s, span]
        return self.make("r", src, dst, dirn * w.far + s, w.left if dirn else w.right)

    def swap(self):
        w = self.w
        src = self.part.at[w.chip_at(0), :, pl.ds(w.their_b[0], w.b)]
        return self.make("y", src, self.rb, len(self.order), w.across)

    def add(self, k, lo, size, cols, other):
        chip = self.w.chip_at(k)
        part = self.part
        ch = 16

        @pl.loop(0, size // ch)
        def _(r):
            rs = pl.ds(pl.multiple_of(lo + r * ch, ch), ch)
            cs = pl.ds(cols[0], cols[1])
            part[chip, rs, cs] = (part[chip, rs, cs].astype(f32) + other[rs, :].astype(f32)).astype(bf16)

    def cross_all(self):
        for k in self.order:
            self.cross(k).start()

    def take(self, *ks):
        for k in ks:
            self.cross(k).wait_recv()
            self.add(k, 0, self.rows, self.w.mine_a, self.ry.at[self.w.chip_at(k)])

    def launch(self):
        self.take(self.w.far)
        self.ring(0, 0).start()
        self.ring(0, 1).start()

    def step(self, s):
        far, half = self.w.far, self.rows // 2
        for dirn in (0, 1):
            self.ring(s - 1, dirn).wait_recv()
            k = s - far if dirn else far - s
            got = (self.rl if dirn else self.rr).at[s - 1]
            lo, size = (dirn * half, half) if s == 1 else (0, self.rows)
            self.add(k, lo, size, self.w.ring_cols, got)
            self.ring(s, dirn).start()

    def final(self):
        far = self.w.far
        for dirn in (0, 1):
            self.ring(far - 1, dirn).wait_recv()
            self.add(0, 0, self.rows, self.w.ring_cols, (self.rl if dirn else self.rr).at[far - 1])
        self.swap().start()

    def last(self):
        w = self.w
        self.swap().wait_recv()
        self.add(0, 0, self.rows, w.mine_b, self.rb)
        chip = w.chip_at(0)
        self.out[...] = self.part[chip, :, pl.ds(w.own_cols[0], w.n)].astype(f32)

    def drain(self):
        for k in self.order:
            self.cross(k).wait_send()
        for s in range(self.w.far):
            self.ring(s, 0).wait_send()
            self.ring(s, 1).wait_send()
        self.swap().wait_send()


def attend_back(m, i, rows, full):
    width = m.mx.shape[1]
    heads = m.logs.shape[0]
    ps = tile(i, 128)
    ks = pl.ds(pl.multiple_of(width + i * 128, 128), 128)
    vs = pl.ds(pl.multiple_of(2 * width + i * 128, 128), 128)
    q2, do2 = m.qkv[:, ps], m.dmix[:, ps]
    k2, v2 = m.qkv[0:rows, ks], m.qkv[0:rows, vs]
    lq, lk = iota((full, 128), 1), iota((rows, 128), 1)
    both = (do2.astype(f32) * m.mx[:, ps].astype(f32)).T
    dqs, dks, dvs = [], [], []
    for h in (0, 1):
        spare = 64 * (1 - h)
        own_q = (lq < 64) if h == 0 else (lq >= 64)
        own_k = (lk < 64) if h == 0 else (lk >= 64)
        qh = jnp.where(own_q, q2, jnp.where(lq == spare, 1.0, 0.0).astype(bf16))
        kh = jnp.where(lk == spare, m.kb[0:rows, :], k2)
        probs = jnp.exp(mul(kh, qh, NT) - m.logs[pl.ds(2 * i + h, 1), :])
        dvs.append(mul(probs.astype(bf16), do2, NN))
        dprobs = mul(jnp.where(own_k, v2, jnp.zeros_like(v2)), do2, NT)
        inner = jnp.sum(both[64 * h : 64 * h + 64, :], axis=0, keepdims=True)
        ds = (probs * (dprobs - inner)).astype(bf16)
        dks.append(mul(ds, q2, NN))
        dqs.append(mul(ds, k2, TN))
    dv = jnp.where(lk < 64, dvs[0], dvs[1]).astype(bf16)
    dk = jnp.where(lk < 64, dks[0], dks[1]).astype(bf16)
    dq = (jnp.where(lq < 64, dqs[0], dqs[1]) * HEAD_DIM**-0.5).astype(bf16)
    m.dh[:, ps] = dq
    m.dh[0:rows, ks] = dk
    m.dh[0:rows, vs] = dv
    m.vsum[6:7, ps] = jnp.sum(dq.astype(f32), axis=0, keepdims=True)
    m.vsum[7:8, ps] = jnp.sum(dv.astype(f32), axis=0, keepdims=True)


BWD_IN = ("w1", "w2", "w3", "qkv_i", "mixed", "logs", "mid", "act", "slope", "p3", "lhs1_i", "lhs2_i", "gr_i", "vecs", "kb", "rm", "tok")
BWD_OUT = ("bo", "gt", "g1", "g2", "g3", "gv")


def bwd_kernel(dp, rows, names, *refs):
    m = types.SimpleNamespace(**dict(zip(names, refs)))
    n = m.w2.shape[1] // 2
    w = Place(dp, n)
    length, width = m.tok.shape
    full = m.qkv_i.shape[0]
    share = m.p3.shape[1]
    cols = n // 4
    far = w.far
    sems = {"y": (m.y_s, m.y_r), "r": (m.ring_s, m.ring_r)}

    def group(g, slot):
        return Scatter(
            w, g, m.part.at[slot], m.ry.at[slot], m.rr.at[slot], m.rl.at[slot], m.rb.at[slot], m.og.at[g], sems
        )

    s3, s2, s1 = group(0, 0), group(1, 1), group(2, 0)

    def flip(k):
        return (w.d + k - 2 * k * ((w.d // k) % 2), w.t)

    flips = [w.across]
    k = 1
    while k < dp:
        flips.append(flip(k))
        k *= 2
    p3_in = pltpu.make_async_copy(m.p3, m.part.at[0], m.l_sem.at[0])
    loads = [
        pltpu.make_async_copy(src, dst, m.l_sem.at[1 + i])
        for i, (src, dst) in enumerate(
            (
                (m.gr_i, m.gr),
                (m.lhs2_i, m.lhs),
                (m.mid, m.dm),
                (m.mixed, m.mx),
                (m.qkv_i, m.qkv),
            )
        )
    ]
    p3_in.start()
    for cp in loads:
        cp.start()
    greet([w.right, w.left] + flips)
    give_mixed = rcopy(m.mixed, m.mx_sib, m.x_s.at[0], m.x_r.at[0], w.sibling)
    give_mixed.start()
    zero_rows = pl.ds(rows, full - rows)
    m.dh[zero_rows, :] = jnp.zeros((full - rows, 2 * n), bf16)
    m.dmix[zero_rows, :] = jnp.zeros((full - rows, width), bf16)
    m.acc[...] = jnp.zeros(m.acc.shape, f32)
    m.vsum[...] = jnp.zeros(m.vsum.shape, f32)
    m.vacc[...] = jnp.zeros(m.vacc.shape, f32)
    p3_in.wait()
    s3.cross_all()
    loads[0].wait()

    def flat(ref):
        return lambda j: ref.at[:, tile(j, cols)]

    def dh_copy(j):
        cs = tile(j, cols)
        return rcopy(m.dh.at[:, cs], m.dh_sib.at[:, cs], m.h_s.at[j], m.h_r.at[j], w.sibling)

    def dh_tile(j, slot):
        ticks(j, {3: [s3.launch], 7: [lambda: s3.take(far - 1, 1 - far)]})
        d = mul(m.gr[0:rows, :], m.wt[slot], NN) * m.st[slot, 0:rows, :].astype(f32)
        d = d.astype(bf16)
        m.dh[0:rows, tile(j, cols)] = d
        m.vsum[pl.ds(8 + j // 2, 1), tile(j % 2, cols)] = jnp.sum(d.astype(f32), axis=0, keepdims=True)
        dh_copy(j).start()

    stream(8, [(flat(m.w3), m.wt), (flat(m.slope), m.st)], m.s_sem, dh_tile)
    loads[1].wait()

    @pl.loop(0, 8)
    def _(j):
        ticks(j, {1: [lambda: s3.step(1)], 6: [lambda: s3.take(far - 2, 2 - far)]})
        dh_copy(j).wait()
        cs = tile(j, cols)
        lhs = m.lhs[...].reshape(w.ring * share, 2 * full)
        part = mul(lhs[:, 0:full], m.dh[:, cs], NN) + mul(lhs[:, full:], m.dh_sib[:, cs], NN)
        m.part[1, :, :, cs] = part.astype(bf16).reshape(w.ring, share, cols)

    s2.cross_all()
    lhs1_in = pltpu.make_async_copy(m.lhs1_i, m.lhs, m.l_sem.at[1])
    lhs1_in.start()

    def second_tile(j, slot):
        ticks(j, {1: [lambda: s3.step(2)], 7: [lambda: s3.take(far - 3, 3 - far)]})
        m.acc[0:rows, :] += mul(m.dh[0:rows, tile(j, cols)], m.wt[slot], NT)

    stream(8, [(flat(m.w2), m.wt)], m.s_sem, second_tile)
    loads[2].wait()
    ch = 64

    def fold(k, x):
        m.vacc[k] += jnp.sum(x.reshape(ch // 8, 8, width), axis=0)

    def norm_back(unit, scaled, gain, up):
        weighted = up * gain
        return scaled * (
            weighted
            - jnp.mean(weighted, axis=-1, keepdims=True)
            - unit * jnp.mean(weighted * unit, axis=-1, keepdims=True)
        )

    @pl.loop(0, full // ch)
    def _(r):
        rs = tile(r, ch)
        unit, scaled = normalize(m.dm[rs, :])
        up = m.acc[rs, :]
        grad = m.gr[rs, :].astype(f32)
        down = norm_back(unit, scaled, m.vecs[3:4, :], up) + grad
        m.dm[rs, :] = down
        m.gr[rs, :] = down.astype(bf16)
        fold(2, down)
        fold(3, up * unit)
        fold(4, up)
        fold(5, grad)

    @pl.loop(0, width // 256)
    def _(j):
        m.turn[tile(j, 2)] = m.gr[:, tile(j, 256)].T.reshape(2, 2, share, full)

    keep_turn = pltpu.make_async_copy(m.turn.at[:, w.core], m.lhs4.at[:, :, pl.ds(0, full)], m.t_sem.at[0])
    give_turn = rcopy(
        m.turn.at[:, 1 - w.core], m.lhs4.at[:, :, pl.ds(full, full)], m.x_s.at[1], m.x_r.at[1], w.sibling
    )
    keep_turn.start()
    give_turn.start()
    s3.step(3)

    def in_cols(ref, j):
        return ref.at[:, pl.ds(pl.multiple_of((j % 2) * n + (j // 2) * cols, 128), cols)]

    def mixed_tile(j, slot):
        m.dmix[0:rows, tile(j, cols)] = mul(m.gr[0:rows, :], m.wt[slot], NN).astype(bf16)

    stream(2, [(lambda j: in_cols(m.w1, 6 + j), m.wt)], m.s_sem, mixed_tile)
    m.acc[...] = jnp.zeros(m.acc.shape, f32)
    loads[3].wait()
    loads[4].wait()
    keep_turn.wait()
    give_turn.wait()

    def q_copies(half):
        for slot in range(3):
            cs = pl.ds(slot * width + half * cols, cols)
            k = 3 * half + slot
            yield rcopy(m.dh.at[:, cs], m.dh_sib.at[:, cs], m.q_s.at[k], m.q_r.at[k], w.sibling)

    def send_q(half):
        for cp in q_copies(half):
            cp.start()

    @pl.loop(0, width // 128)
    def _(i):
        ticks(
            i,
            {
                0: [lambda: s2.launch()],
                1: [lambda: s3.take(0), s3.final],
                2: [lambda: s2.take(far - 1, 1 - far), lambda: s2.step(1)],
                3: [s3.last, lambda: s2.take(far - 2, 2 - far)],
                4: [lambda: send_q(0)],
                5: [lambda: s2.step(2), lambda: s2.take(far - 3, 3 - far)],
            },
        )
        attend_back(m, i, rows, full)

    send_q(1)
    s2.step(3)
    s3.drain()
    give_mixed.wait()
    lhs1_in.wait()

    def weight_tile(lhs, own, sib, src, dst):
        lhs = lhs.reshape(w.ring * share, 2 * full)
        part = mul(lhs[:, 0:full], own[:, src], NN) + mul(lhs[:, full:], sib[:, src], NN)
        m.part[0, :, :, dst] = part.astype(bf16).reshape(w.ring, share, cols)

    @pl.loop(0, 2)
    def _(j):
        dst = pl.ds(pl.multiple_of(j * n + 3 * cols, 128), cols)
        weight_tile(m.lhs4[...], m.mx, m.mx_sib, tile(j, cols), dst)

    for half in (0, 1):
        for cp in q_copies(half):
            cp.wait()

        @pl.loop(0, 3)
        def _(slot, half=half):
            src = pl.ds(pl.multiple_of(slot * width + half * cols, 128), cols)
            dst = pl.ds(pl.multiple_of(half * n + slot * cols, 128), cols)
            weight_tile(m.lhs[...], m.dh, m.dh_sib, src, dst)

    s2.take(0)
    s1.cross_all()
    tok_in = pltpu.make_async_copy(m.tok, m.xs.at[pl.ds(0, length)], m.l_sem.at[2])
    tok_in.start()

    def first_tile(j, slot):
        ticks(j, {3: [s2.final, s1.launch]})
        m.acc[0:rows, :] += mul(m.dh[0:rows, tile(j, cols)], m.wt[slot], NT)

    stream(6, [(lambda j: in_cols(m.w1, j), m.wt)], m.s_sem, first_tile)
    s2.last()
    s1.take(far - 1, 1 - far)
    s1.step(1)
    tok_in.wait()
    tail = pl.ds(length, full - length)
    m.xs[tail, :] = jnp.zeros((full - length, width), bf16)

    @pl.loop(0, full // ch)
    def _(r):
        rs = tile(r, ch)
        unit, scaled = normalize(m.xs[rs, :].astype(f32))
        up = m.acc[rs, :]
        m.dm[rs, :] += norm_back(unit, scaled, m.vecs[0:1, :], up)
        fold(0, up * unit)
        fold(1, up)

    m.vsum[0:6, :] = jnp.sum(m.vacc[...], axis=1)
    m.acc[...] = jnp.zeros(m.acc.shape, f32)
    gt_out = pltpu.make_async_copy(m.dm.at[pl.ds(0, length)], m.gt, m.l_sem.at[3])
    gt_out.start()
    mid_in = pltpu.make_async_copy(m.mid, m.dm, m.l_sem.at[4])

    def swap_mid():
        gt_out.wait()
        mid_in.start()

    def vec_copy(s):
        return rcopy(m.vswap.at[s, 0], m.vswap.at[s, 1], m.v_s.at[s], m.v_r.at[s], flips[s])

    def vec_start(s):
        m.vswap[s, 0] = m.vsum[...]
        vec_copy(s).start()

    def vec_end(s):
        vec_copy(s).wait()
        m.vsum[...] += m.vswap[s, 1]

    def vec_step(s):
        if s:
            vec_end(s - 1)
        if s < len(flips):
            vec_start(s)

    table = {1 + s: [functools.partial(vec_step, s)] for s in range(6)}
    table[3] = table[3] + [swap_mid]
    table[4] = table[4] + [lambda: s1.take(far - 2, 2 - far)]
    table[7] = [lambda: s1.step(2)]

    def block_tile(j, slot):
        ticks(j, table)
        m.acc[0:rows, :] += mul(m.st[slot, 0:rows, :], m.wt[slot], NT)

    stream(8, [(flat(m.w3), m.wt), (flat(m.act), m.st)], m.s_sem, block_tile)
    mid_in.wait()

    @pl.loop(0, full // ch)
    def _(r):
        rs = tile(r, ch)
        m.xs[rs, :] = (m.rm[rs, 0:1] * (m.dm[rs, :] + m.acc[rs, :] + m.vecs[5:6, :])).astype(bf16)

    outs = [
        pltpu.make_async_copy(m.xs.at[pl.ds(0, length)], m.bo, m.l_sem.at[0]),
        pltpu.make_async_copy(m.og.at[0], m.g3, m.l_sem.at[1]),
        pltpu.make_async_copy(m.og.at[1], m.g2, m.l_sem.at[2]),
        pltpu.make_async_copy(m.vsum, m.gv, m.l_sem.at[3]),
    ]
    for cp in outs:
        cp.start()
    s1.take(far - 3, 3 - far)
    s1.step(3)
    s1.take(0)
    s1.final()
    s1.last()
    g1_out = pltpu.make_async_copy(m.og.at[2], m.g1, m.l_sem.at[5])
    g1_out.start()
    s2.drain()
    s1.drain()
    for cp in outs:
        cp.wait()
    g1_out.wait()


def backward(o, kb, rm, tokens, dp, n, share):
    length, width = tokens.shape
    rows = -(-length // 16) * 16
    full = -(-length // 128) * 128
    cols = n // 4
    ring = dp // 2
    far = ring // 2
    depth = share * dp
    a, b = split_of(n)
    V, dma = pltpu.VMEM, pltpu.SemaphoreType.DMA
    S = jax.ShapeDtypeStruct
    steps = dp.bit_length()
    out = dict(
        bo=S((length, width), bf16),
        gt=S((length, width), f32),
        g1=S((share, n), f32),
        g2=S((share, n), f32),
        g3=S((share, n), f32),
        gv=S((16, width), f32),
    )
    scratch = dict(
        part=V((2, ring, share, 2 * n), bf16),
        ry=V((2, ring, share, a), bf16),
        rr=V((2, far, share, 2 * n - a), bf16),
        rl=V((2, far, share, 2 * n - a), bf16),
        rb=V((2, share, b), bf16),
        og=V((3, share, n), f32),
        dh=V((full, 2 * n), bf16),
        dh_sib=V((full, 2 * n), bf16),
        mx=V((full, width), bf16),
        mx_sib=V((full, width), bf16),
        lhs=V((ring, share, 2 * full), bf16),
        lhs4=V((ring, share, 2 * full), bf16),
        turn=V((ring, 2, share, full), bf16),
        qkv=V((full, 3 * width), bf16),
        dmix=V((full, width), bf16),
        gr=V((full, width), bf16),
        acc=V((full, width), f32),
        dm=V((full, width), f32),
        xs=V((full, width), bf16),
        wt=V((2, depth, cols), bf16),
        st=V((2, full, cols), bf16),
        vsum=V((16, width), f32),
        vacc=V((6, 8, width), f32),
        vswap=V((steps, 2, 16, width), f32),
        y_s=dma((3, ring + 1)),
        y_r=dma((3, ring + 1)),
        ring_s=dma((3, 2 * far)),
        ring_r=dma((3, 2 * far)),
        l_sem=dma((6,)),
        s_sem=dma((2, 2)),
        t_sem=dma((1,)),
        x_s=dma((2,)),
        x_r=dma((2,)),
        h_s=dma((8,)),
        h_r=dma((8,)),
        q_s=dma((6,)),
        q_r=dma((6,)),
        v_s=dma((steps,)),
        v_r=dma((steps,)),
    )
    args = (
        o.w1, o.w2, o.w3, o.qkv_o, o.mixed_o, o.logs_o, o.mid_o, o.act_o, o.slope_o, o.p3_o, o.lhs1_o, o.lhs2_o, o.gr_o,
        o.vecs_o, kb, rm, tokens,
    )
    names = BWD_IN + tuple(out) + tuple(scratch)
    hbm = pl.BlockSpec(memory_space=pl.ANY)
    vm = pl.BlockSpec(memory_space=pltpu.VMEM)
    specs = [vm if k in ("logs", "vecs", "kb", "rm") else hbm for k in BWD_IN]
    got = pl.pallas_call(
        functools.partial(bwd_kernel, dp, rows, names),
        out_shape=list(out.values()),
        in_specs=specs,
        out_specs=[hbm] * len(out),
        scratch_shapes=list(scratch.values()),
        compiler_params=pltpu.CompilerParams(
            collective_id=2, has_side_effects=True, vmem_limit_bytes=62 << 20
        ),
        name="backward",
    )(*args)
    return types.SimpleNamespace(**dict(zip(out, got)))


def paired_device(*args):
    dp = lax.axis_size("dp")
    d = lax.axis_index("dp")
    t = lax.axis_index("tensor")
    tokens = args[0]
    length, width = tokens.shape
    share, n = args[12].shape
    cols = n // 4
    ready = prepare(*args)
    o = forward(ready, dp, length, width, n, share)
    r = backward(o, ready[8], ready[9], tokens, dp, n, share)
    vectors = lax.dynamic_slice_in_dim(r.gv[:6], d * share, share, 1)
    bias_own = lax.dynamic_slice_in_dim(r.gv[6:8], t * cols, cols, 1)
    up_own = lax.dynamic_slice_in_dim(r.gv[8:12].reshape(-1), t * n, n, 0)
    return (
        r.bo,
        r.gt,
        vectors[0],
        vectors[1],
        r.g1[:, : 3 * cols].reshape(share, 3, cols),
        bias_own,
        r.g1[:, 3 * cols :].T,
        vectors[2],
        vectors[3],
        vectors[4],
        r.g2,
        up_own,
        r.g3.T,
        vectors[5],
    )


def solution(mesh):
    in_specs = (
        P(("dp", "tensor"), None),
        P(("dp", "tensor"), None),
        P("dp", None),
        P("dp"),
        P("dp"),
        P("dp"),
        P("dp", None, "tensor"),
        P(None, "tensor"),
        P("tensor", "dp"),
        P("dp"),
        P("dp"),
        P("dp"),
        P("dp", "tensor"),
        P("tensor"),
        P("tensor", "dp"),
        P("dp"),
    )
    out_specs = (
        P(("dp", "tensor"), None),
        P(("dp", "tensor"), None),
        P("dp"),
        P("dp"),
        P("dp", None, "tensor"),
        P(None, "tensor"),
        P("tensor", "dp"),
        P("dp"),
        P("dp"),
        P("dp"),
        P("dp", "tensor"),
        P("tensor"),
        P("tensor", "dp"),
        P("dp"),
    )
    ready = mesh.shape["tensor"] == 2 and mesh.shape["dp"] == 16
    body = paired_device if ready else general_device
    return jax.shard_map(
        body, mesh=mesh, in_specs=in_specs, out_specs=out_specs, check_vma=False
    )
```

```python
import functools
import types

import jax
import jax.numpy as jnp
from jax import lax
from jax.experimental import pallas as pl
from jax.experimental.pallas import tpu as pltpu
from jax.sharding import PartitionSpec as P

HEAD_DIM = 64
MESH = pl.DeviceIdType.MESH
f32 = jnp.float32
bf16 = jnp.bfloat16
NN, NT, TN = ((1,), (0,)), ((1,), (1,)), ((0,), (0,))
VM_LIMIT = 63 << 20


def layer_norm(inputs, gain, shift):
    center = inputs - jnp.mean(inputs, axis=-1, keepdims=True)
    spread = jnp.mean(center * center, axis=-1, keepdims=True)
    return center * lax.rsqrt(spread + 1e-06) * gain + shift


def norm_backward(inputs, gain, upstream):
    center = inputs - jnp.mean(inputs, axis=-1, keepdims=True)
    spread = jnp.mean(center * center, axis=-1, keepdims=True)
    scaled = lax.rsqrt(spread + 1e-06)
    unit = center * scaled
    weighted = upstream * gain
    grad_inputs = scaled * (
        weighted
        - jnp.mean(weighted, axis=-1, keepdims=True)
        - unit * jnp.mean(weighted * unit, axis=-1, keepdims=True)
    )
    return (grad_inputs, jnp.sum(upstream * unit, axis=0), jnp.sum(upstream, axis=0))


def gelu_slope(hidden):
    return (
        0.5 * (1.0 + lax.erf(hidden * 0.7071067811865476))
        + hidden * jnp.exp(-0.5 * hidden * hidden) * 0.3989422804014327
    )


def general_device(
    tokens,
    cotangent,
    token_valid,
    image_valid,
    first_gain,
    first_shift,
    input_weight,
    input_bias,
    output_weight,
    output_bias,
    second_gain,
    second_shift,
    up_weight,
    up_bias,
    down_weight,
    down_bias,
):
    f32 = jnp.float32
    bf16 = jnp.bfloat16
    gathered = (
        lax.all_gather(first_gain, "dp", axis=0, tiled=True),
        lax.all_gather(first_shift, "dp", axis=0, tiled=True),
        lax.all_gather(input_weight, "dp", axis=0, tiled=True),
        lax.all_gather(output_weight, "dp", axis=1, tiled=True),
        lax.all_gather(output_bias, "dp", axis=0, tiled=True),
        lax.all_gather(second_gain, "dp", axis=0, tiled=True),
        lax.all_gather(second_shift, "dp", axis=0, tiled=True),
        lax.all_gather(up_weight, "dp", axis=0, tiled=True),
        lax.all_gather(down_weight, "dp", axis=1, tiled=True),
        lax.all_gather(down_bias, "dp", axis=0, tiled=True),
    )
    (
        gain_one,
        shift_one,
        in_full,
        out_full,
        out_shift,
        gain_two,
        shift_two,
        up_full,
        down_full,
        down_shift,
    ) = gathered
    gain_one = gain_one.astype(f32)
    shift_one = shift_one.astype(f32)
    out_shift = out_shift.astype(f32)
    gain_two = gain_two.astype(f32)
    shift_two = shift_two.astype(f32)
    down_shift = down_shift.astype(f32)
    tensor_at = lax.axis_index("tensor")
    groups = lax.axis_size("tensor")
    own_rows = tokens.shape[0]
    width = tokens.shape[1]
    length = token_valid.shape[1]
    positions = lax.broadcasted_iota(jnp.int32, token_valid.shape, 1)
    key_ok = (token_valid > 0) | (positions == 0)
    mask_all = (token_valid * image_valid[:, None]).astype(f32).reshape(-1)
    row_mask = lax.dynamic_slice_in_dim(mask_all, tensor_at * own_rows, own_rows)[:, None]
    images = token_valid.shape[0]
    local_width = in_full.shape[2]
    local_heads = local_width // HEAD_DIM
    hidden_width = up_full.shape[1]
    scale = HEAD_DIM ** (-0.5)
    head_shape = (images, length, local_heads, HEAD_DIM)
    inputs = tokens.astype(f32)
    first_own = layer_norm(inputs, gain_one, shift_one).astype(bf16)
    first_all = lax.all_gather(first_own, "tensor", axis=0, tiled=True)
    project = jnp.einsum("rd,dce->rce", first_all, in_full, preferred_element_type=f32)
    bias_in = input_bias.astype(f32)
    queries = (project[:, 0] + bias_in[0]).astype(bf16).reshape(head_shape)
    keyset = project[:, 1].astype(bf16).reshape(head_shape)
    values = (project[:, 2] + bias_in[1]).astype(bf16).reshape(head_shape)

    def scores_of(query_img, key_img, ok_img):
        scores = jnp.einsum("qhe,khe->hqk", query_img, key_img, preferred_element_type=f32) * scale
        return jnp.where(ok_img[None, None, :], scores, -1000000000.0)

    def attend(pieces):
        query_img, key_img, value_img, ok_img = pieces
        scores = scores_of(query_img, key_img, ok_img)
        highest = jnp.max(scores, axis=-1, keepdims=True)
        log_total = highest + jnp.log(jnp.sum(jnp.exp(scores - highest), axis=-1, keepdims=True))
        attn_probs = jnp.exp(scores - log_total).astype(bf16)
        mixed_img = jnp.einsum("hqk,khe->qhe", attn_probs, value_img, preferred_element_type=f32)
        return (mixed_img.astype(bf16), log_total)

    mixed, log_totals = lax.map(attend, (queries, keyset, values, key_ok))
    mixed_rows = mixed.reshape(images * length, local_width)
    attended = lax.psum_scatter(
        jnp.dot(mixed_rows, out_full, preferred_element_type=f32).astype(jnp.bfloat16),
        "tensor",
        scatter_dimension=0,
        tiled=True,
    ).astype(jnp.float32)
    middle = inputs + attended + out_shift
    second_own = layer_norm(middle, gain_two, shift_two).astype(bf16)
    second_all = lax.all_gather(second_own, "tensor", axis=0, tiled=True)
    hidden = jnp.dot(second_all, up_full, preferred_element_type=f32) + up_bias.astype(f32)
    active = jax.nn.gelu(hidden, approximate=False).astype(bf16)
    lifted = lax.psum_scatter(
        jnp.dot(active, down_full, preferred_element_type=f32).astype(jnp.bfloat16),
        "tensor",
        scatter_dimension=0,
        tiled=True,
    ).astype(jnp.float32)
    block_out = (row_mask * (middle + lifted + down_shift)).astype(bf16)
    grad_last = row_mask * cotangent.astype(f32)
    first_all, second_all = (
        lax.all_gather(first_own, "tensor", axis=0, tiled=True),
        lax.all_gather(second_own, "tensor", axis=0, tiled=True),
    )
    grad_lift = lax.all_gather(grad_last.astype(bf16), "tensor", axis=0, tiled=True)
    grad_active = jnp.einsum("rd,fd->rf", grad_lift, down_full, preferred_element_type=f32)
    grad_hidden = (grad_active * gelu_slope(hidden)).astype(bf16)
    grad_down = jnp.einsum("rf,rd->fd", active, grad_lift, preferred_element_type=f32)
    grad_up = jnp.einsum("rd,rf->df", second_all, grad_hidden, preferred_element_type=f32)
    grad_up_bias = jnp.sum(grad_hidden.astype(f32), axis=0)
    grad_second = lax.psum_scatter(
        jnp.einsum("rf,df->rd", grad_hidden, up_full, preferred_element_type=f32).astype(
            jnp.bfloat16
        ),
        "tensor",
        scatter_dimension=0,
        tiled=True,
    ).astype(jnp.float32)
    grad_middle, grad_gain_two, grad_shift_two = norm_backward(middle, gain_two, grad_second)
    grad_middle = grad_middle + grad_last
    grad_mid_all = lax.all_gather(grad_middle.astype(bf16), "tensor", axis=0, tiled=True)
    grad_mixed = jnp.einsum("rd,ed->re", grad_mid_all, out_full, preferred_element_type=f32).astype(
        bf16
    )
    grad_out_weight = jnp.einsum("re,rd->ed", mixed_rows, grad_mid_all, preferred_element_type=f32)

    def attend_back(pieces):
        query_img, key_img, value_img, ok_img, total_img, grad_img = pieces
        scores = scores_of(query_img, key_img, ok_img)
        attn_probs = jnp.exp(scores - total_img)
        grad_values = jnp.einsum(
            "hqk,qhe->khe", attn_probs.astype(bf16), grad_img, preferred_element_type=f32
        )
        grad_probs = jnp.einsum("qhe,khe->hqk", grad_img, value_img, preferred_element_type=f32)
        grad_scores = (
            attn_probs * (grad_probs - jnp.sum(attn_probs * grad_probs, axis=-1, keepdims=True))
        ).astype(bf16)
        grad_queries = (
            jnp.einsum("hqk,khe->qhe", grad_scores, key_img, preferred_element_type=f32) * scale
        )
        grad_keys = (
            jnp.einsum("hqk,qhe->khe", grad_scores, query_img, preferred_element_type=f32) * scale
        )
        return jnp.stack([grad_queries, grad_keys, grad_values], axis=1).astype(bf16)

    grad_project = lax.map(
        attend_back, (queries, keyset, values, key_ok, log_totals, grad_mixed.reshape(head_shape))
    )
    grad_project = grad_project.reshape(images * length, 3, local_width)
    grad_in_weight = jnp.einsum("rd,rce->dce", first_all, grad_project, preferred_element_type=f32)
    grad_in_bias = jnp.sum(grad_project[:, 0::2].astype(f32), axis=0)
    grad_first = lax.psum_scatter(
        jnp.einsum("rce,dce->rd", grad_project, in_full, preferred_element_type=f32).astype(
            jnp.bfloat16
        ),
        "tensor",
        scatter_dimension=0,
        tiled=True,
    ).astype(jnp.float32)
    grad_inputs, grad_gain_one, grad_shift_one = norm_backward(inputs, gain_one, grad_first)
    grad_inputs = grad_inputs + grad_middle
    grad_in_own, grad_out_own, grad_up_own, grad_down_own = (
        lax.psum_scatter(
            grad_in_weight.astype(jnp.bfloat16), "dp", scatter_dimension=0, tiled=True
        ).astype(jnp.float32),
        lax.psum_scatter(
            grad_out_weight.astype(jnp.bfloat16), "dp", scatter_dimension=1, tiled=True
        ).astype(jnp.float32),
        lax.psum_scatter(
            grad_up.astype(jnp.bfloat16), "dp", scatter_dimension=0, tiled=True
        ).astype(jnp.float32),
        lax.psum_scatter(
            grad_down.astype(jnp.bfloat16), "dp", scatter_dimension=1, tiled=True
        ).astype(jnp.float32),
    )
    vectors = jnp.stack(
        [
            grad_gain_one,
            grad_shift_one,
            jnp.sum(grad_middle, axis=0),
            grad_gain_two,
            grad_shift_two,
            jnp.sum(grad_last, axis=0),
        ]
    )
    bias_share = input_bias.shape[1]
    up_share = up_bias.shape[0]
    placed_bias = lax.dynamic_update_slice(
        jnp.zeros((2, width), f32), grad_in_bias, (0, tensor_at * local_width)
    )
    placed_up = lax.dynamic_update_slice(
        jnp.zeros((hidden_width * groups,), f32), grad_up_bias, (tensor_at * hidden_width,)
    )
    vectors, placed_bias, placed_up = lax.psum((vectors, placed_bias, placed_up), ("dp", "tensor"))
    share = first_gain.shape[0]
    dp_at = lax.axis_index("dp")
    vectors = lax.dynamic_slice_in_dim(vectors, dp_at * share, share, 1)
    bias_own = lax.dynamic_slice_in_dim(placed_bias, tensor_at * bias_share, bias_share, 1)
    up_bias_own = lax.dynamic_slice_in_dim(placed_up, tensor_at * up_share, up_share, 0)
    return (
        block_out,
        grad_inputs,
        vectors[0],
        vectors[1],
        grad_in_own,
        bias_own,
        grad_out_own,
        vectors[2],
        vectors[3],
        vectors[4],
        grad_up_own,
        up_bias_own,
        grad_down_own,
        vectors[5],
    )


def mul(a, b, dims):
    return lax.dot_general(a, b, (dims, ((), ())), preferred_element_type=f32)


def iota(shape, axis):
    return lax.broadcasted_iota(jnp.int32, shape, axis)


def tile(j, size):
    return pl.ds(pl.multiple_of(j * size, size), size)


class Place:
    def __init__(self, dp):
        d = lax.axis_index("dp")
        t = lax.axis_index("tensor")
        ring = dp // 2
        self.dp, self.d, self.t, self.ring, self.far = dp, d, t, ring, ring // 2
        self.chip, self.core = d // 2, d % 2
        self.pos = jnp.where(self.chip % 2 == 0, self.chip // 2, ring - 1 - self.chip // 2)
        self.right = (self.chip_at(1) * 2 + self.core, t)
        self.left = (self.chip_at(-1) * 2 + self.core, t)
        self.across = (d, 1 - t)
        self.sibling = (d + 1 - 2 * self.core, t)

    def chip_at(self, offset):
        ring = self.ring
        spot = (self.pos + offset + ring) % ring
        return jnp.where(spot < ring // 2, 2 * spot, 2 * (ring - 1 - spot) + 1)


class Columns:
    def __init__(self, w, n, a):
        t, b = w.t, n - a
        self.n, self.a, self.b = n, a, b
        self.own = (pl.multiple_of(t * n, 128), n)
        self.other = (pl.multiple_of((1 - t) * n, 128), n)
        self.ring = (pl.multiple_of(t * a, 128), 2 * n - a)
        self.mine_a = (pl.multiple_of(t * (2 * n - a), 128), a)
        self.their_a = (pl.multiple_of((1 - t) * (2 * n - a), 128), a)
        self.their_b = (pl.multiple_of(n - t * b, 128), b)
        self.mine_b = (pl.multiple_of(n - (1 - t) * b, 128), b)


def outer(n, i):
    return n // 2 + 128 * (1 - i) * (n // 1024)


def greet(targets):
    bar = pltpu.get_barrier_semaphore()
    for a in targets:
        pl.semaphore_signal(bar, inc=1, device_id=a, device_id_type=MESH)
    pl.semaphore_wait(bar, len(targets))


def rcopy(src, dst, send, recv, dev):
    return pltpu.make_async_remote_copy(
        src_ref=src, dst_ref=dst, send_sem=send, recv_sem=recv, device_id=dev, device_id_type=MESH
    )


class Gather:
    def __init__(self, w, g, shard, full, sems):
        self.w, self.g, self.shard, self.full, self.sems = w, g, shard, full, sems
        self.rows, n = shard.shape
        self.cols = Columns(w, n, outer(n, g % 2))

    def block(self, offset, cols, span=None):
        w = self.w
        lo, size = span or (0, self.rows)
        base = w.chip_at(offset) * (2 * self.rows) + w.core * self.rows + lo
        return self.full.at[pl.ds(pl.multiple_of(base, 16), size), pl.ds(cols[0], cols[1])]

    def span(self, s, dirn):
        half = self.rows // 2
        return (0, self.rows) if s < self.w.far else (dirn * half, half)

    def off(self, s, dirn):
        return s if dirn else -s

    def make(self, kind, src, dst, k, dev):
        send, recv = self.sems[kind]
        return rcopy(src, dst, send.at[self.g, k], recv.at[self.g, k], dev)

    def y(self, s, dirn):
        if s == 0:
            return self.make("y", self.shard, self.block(0, self.cols.own), 0, self.w.across)
        ref = self.block(self.off(s, dirn), self.cols.mine_a, self.span(s, dirn))
        return self.make("y", ref, ref, 2 * s - 1 + dirn, self.w.across)

    def ring(self, s, dirn, part=0):
        dev = self.w.left if dirn else self.w.right
        k = dirn * (self.w.far + 1)
        if s == 1 and part == 0:
            return self.make("r", self.shard, self.block(0, self.cols.own), k, dev)
        if s == 1:
            ref = self.block(0, self.cols.their_b)
            return self.make("r", ref, ref, k + 1, dev)
        ref = self.block(self.off(s - 1, dirn), self.cols.ring, self.span(s, dirn))
        return self.make("r", ref, ref, k + s, dev)

    def sib(self, k):
        w = self.w
        if k == 0:
            src, dst = self.shard, self.block(0, self.cols.own)
        elif k == 1:
            src = dst = self.block(0, self.cols.other)
        else:
            which, rest = divmod(k - 2, 2 * w.far)
            s, dirn = rest // 2 + 1, rest % 2
            cols = self.cols.their_a if which else self.cols.ring
            src = dst = self.block(self.off(s, dirn), cols, self.span(s, dirn))
        return self.make("c", src, dst, k, w.sibling)

    def keep(self):
        return pltpu.make_async_copy(self.shard, self.block(0, self.cols.own), self.sems["k"].at[self.g])

    def S(self):
        self.y(0, 0).start()
        self.ring(1, 0).start()
        self.ring(1, 1).start()
        self.sib(0).start()
        self.keep().start()

    def Y(self):
        self.y(0, 0).wait_recv()
        self.ring(1, 0, 1).start()
        self.ring(1, 1, 1).start()
        self.sib(1).start()

    def h(self, s):
        for dirn in (0, 1):
            self.ring(s, dirn).wait_recv()
            if s == 1:
                self.ring(s, dirn, 1).wait_recv()
            if s < self.w.far:
                self.ring(s + 1, dirn).start()
            self.y(s, dirn).start()
            self.sib(2 * s + dirn).start()

    def c(self, s):
        for dirn in (0, 1):
            self.y(s, dirn).wait_recv()
            self.sib(2 + 2 * self.w.far + 2 * (s - 1) + dirn).start()

    def events(self):
        h, c = (lambda s: functools.partial(self.h, s)), (lambda s: functools.partial(self.c, s))
        return [self.S, self.Y, h(1), h(2), c(1), h(3), c(2), h(4), c(3), c(4), self.E]

    def E(self):
        for k in range(2 + 4 * self.w.far):
            self.sib(k).wait()
        self.keep().wait()

    def drain(self):
        far = self.w.far
        self.y(0, 0).wait_send()
        for dirn in (0, 1):
            self.ring(1, dirn).wait_send()
            self.ring(1, dirn, 1).wait_send()
            for s in range(1, far + 1):
                self.y(s, dirn).wait_send()
                if s > 1:
                    self.ring(s, dirn).wait_send()


class Scatter:
    def __init__(self, w, g, part, ry, rr, rl, rb, out, sems):
        self.w, self.g, self.part, self.sems, self.out = w, g, part, sems, out
        self.rows, n = part.shape[1], part.shape[2] // 2
        self.cols = c = Columns(w, n, outer(n, g % 2))
        self.ry = ry.at[:, :, pl.ds(0, c.a)]
        self.rr = rr.at[:, :, pl.ds(0, 2 * n - c.a)]
        self.rl = rl.at[:, :, pl.ds(0, 2 * n - c.a)]
        self.rb = rb.at[:, pl.ds(0, c.b)]
        far = w.far
        self.order = [far] + [k * sign for k in range(far - 1, 0, -1) for sign in (1, -1)] + [0]

    def make(self, kind, src, dst, k, dev):
        send, recv = self.sems[kind]
        return rcopy(src, dst, send.at[self.g, k], recv.at[self.g, k], dev)

    def cross(self, k):
        w = self.w
        chip = w.chip_at(k)
        src = self.part.at[chip, :, pl.ds(*self.cols.their_a)]
        return self.make("y", src, self.ry.at[chip], self.order.index(k), w.across)

    def ring(self, s, dirn):
        w = self.w
        chip = w.chip_at(s - w.far if dirn else w.far - s)
        half = self.rows // 2
        span = pl.ds(dirn * half, half) if s == 0 else pl.ds(0, self.rows)
        src = self.part.at[chip, span, pl.ds(*self.cols.ring)]
        dst = (self.rl if dirn else self.rr).at[s, span]
        return self.make("r", src, dst, dirn * w.far + s, w.left if dirn else w.right)

    def swap(self):
        w = self.w
        src = self.part.at[w.chip_at(0), :, pl.ds(*self.cols.their_b)]
        return self.make("y", src, self.rb, len(self.order), w.across)

    def add(self, k, lo, size, cols, other):
        chip = self.w.chip_at(k)
        part = self.part
        ch = 16

        @pl.loop(0, size // ch)
        def _(r):
            rs = pl.ds(pl.multiple_of(lo + r * ch, ch), ch)
            cs = pl.ds(cols[0], cols[1])
            part[chip, rs, cs] = (part[chip, rs, cs].astype(f32) + other[rs, :].astype(f32)).astype(bf16)

    def events(self):
        s, t = (lambda k: functools.partial(self.s, k)), (lambda k: functools.partial(self.t, k))
        return [self.A, self.L, t(3), s(1), t(2), s(2), t(1), s(3), t(0), self.F, self.Z]

    def both(self, k):
        return (k, -k) if k else (0,)

    def A(self):
        for k in (self.w.far, self.w.far - 1, 1 - self.w.far):
            self.cross(k).start()

    def take(self, k):
        self.cross(k).wait_recv()
        self.add(k, 0, self.rows, self.cols.mine_a, self.ry.at[self.w.chip_at(k)])

    def L(self):
        self.cross(self.w.far).wait_recv()
        for k in self.both(self.w.far - 2):
            self.cross(k).start()
        self.add(self.w.far, 0, self.rows, self.cols.mine_a, self.ry.at[self.w.chip_at(self.w.far)])
        self.ring(0, 0).start()
        self.ring(0, 1).start()

    def t(self, k):
        for i in self.both(k):
            self.take(i)
        if k > 1:
            for i in self.both(k - 2):
                self.cross(i).start()

    def s(self, s):
        far, half = self.w.far, self.rows // 2
        for dirn in (0, 1):
            self.ring(s - 1, dirn).wait_recv()
            k = s - far if dirn else far - s
            got = (self.rl if dirn else self.rr).at[s - 1]
            lo, size = (dirn * half, half) if s == 1 else (0, self.rows)
            self.add(k, lo, size, self.cols.ring, got)
            self.ring(s, dirn).start()

    def F(self):
        far = self.w.far
        for dirn in (0, 1):
            self.ring(far - 1, dirn).wait_recv()
            self.add(0, 0, self.rows, self.cols.ring, (self.rl if dirn else self.rr).at[far - 1])
        self.swap().start()

    def Z(self):
        self.swap().wait_recv()
        self.add(0, 0, self.rows, self.cols.mine_b, self.rb)
        chip = self.w.chip_at(0)
        self.out[...] = self.part[chip, :, pl.ds(*self.cols.own)].astype(f32)

    def drain(self):
        for k in self.order:
            self.cross(k).wait_send()
        for s in range(self.w.far):
            self.ring(s, 0).wait_send()
            self.ring(s, 1).wait_send()
        self.swap().wait_send()


class Plan:
    def __init__(self, groups, table):
        self.events, self.table = [g.events() for g in groups], table

    def after(self, name):
        for code in self.table.get(name, ()):
            self.events[code // 100][code % 100]()

    def tick(self, j, name, first, count):
        for k in range(count):
            at = name + str(first + k)
            if at in self.table:

                @pl.when(j == k)
                def _(at=at):
                    self.after(at)


def stream(count, parts, sem, body, begun=False):
    def copies(j):
        slot = lax.rem(j, 2)
        return [pltpu.make_async_copy(src(j), dst(slot), sem.at[i, slot]) for i, (src, dst) in enumerate(parts)]

    def begin():
        for cp in copies(jnp.int32(0)):
            cp.start()

    def run():
        @pl.loop(0, count)
        def _(j):
            @pl.when(j + 1 < count)
            def _():
                for cp in copies(j + 1):
                    cp.start()

            for cp in copies(j):
                cp.wait()
            body(j, lax.rem(j, 2))

    return begin, run


def normalize(x):
    center = x - jnp.mean(x, axis=-1, keepdims=True)
    scaled = lax.rsqrt(jnp.mean(center * center, axis=-1, keepdims=True) + 1e-06)
    return center * scaled, scaled


def lanes_of(pair, blk):
    base = (pair // 2) * (4 * blk) + (pair % 2) * 128
    return [pl.ds(pl.multiple_of(base + s * blk, 128), 128) for s in range(4)]


def attend_pair(m, i, rows, full, blk):
    qs, ks, vs, ms = lanes_of(i, blk)
    q2, k2, v2 = m.qkvm[0:rows, qs], m.qkvm[:, ks], m.qkvm[:, vs]
    lq, lk = iota((rows, 128), 1), iota((full, 128), 1)
    outs = []
    logs = m.logs[0:rows, :]
    for h in (0, 1):
        spare = 64 * (1 - h)
        own_q = (lq < 64) if h == 0 else (lq >= 64)
        own_k = (lk < 64) if h == 0 else (lk >= 64)
        qh = jnp.where(own_q, q2, jnp.where(lq == spare, 1.0, 0.0).astype(bf16))
        kh = jnp.where(lk == spare, m.kb[...], k2)
        scores = mul(qh, kh, NT)
        top = jnp.max(scores, axis=1, keepdims=True)
        probs = jnp.exp(scores - top).astype(bf16)
        out = mul(probs, jnp.where(own_k, v2, jnp.ones_like(v2)), NN)
        turned = pltpu.roll(out, 64, 1)
        outs.append(out / turned)
        total = jnp.where(own_q, turned, out)
        logs = jnp.where(lq == 2 * i + h, top + jnp.log(total), logs)
    m.logs[0:rows, :] = logs
    m.qkvm[0:rows, ms] = jnp.where(lq < 64, outs[0], outs[1]).astype(bf16)


def attend_back(m, i, rows, full, blk):
    qs, ks, vs, ms = lanes_of(i, blk)
    q2, do2 = m.qkvm[:, qs], m.dmix[:, tile(i, 128)]
    k2, v2 = m.qkvm[0:rows, ks], m.qkvm[0:rows, vs]
    lq, lk = iota((full, 128), 1), iota((rows, 128), 1)
    both = (do2.astype(f32) * m.qkvm[:, ms].astype(f32)).T
    dqs, dks, dvs = [], [], []
    for h in (0, 1):
        spare = 64 * (1 - h)
        own_q = (lq < 64) if h == 0 else (lq >= 64)
        own_k = (lk < 64) if h == 0 else (lk >= 64)
        qh = jnp.where(own_q, q2, jnp.where(lq == spare, 1.0, 0.0).astype(bf16))
        kh = jnp.where(lk == spare, m.kb[0:rows, :], k2)
        probs = jnp.exp(mul(kh, qh, NT) - m.logs[pl.ds(2 * i + h, 1), :])
        dvs.append(mul(probs.astype(bf16), do2, NN))
        dprobs = mul(jnp.where(own_k, v2, jnp.zeros_like(v2)), do2, NT)
        inner = jnp.sum(both[64 * h : 64 * h + 64, :], axis=0, keepdims=True)
        ds = (probs * (dprobs - inner)).astype(bf16)
        dks.append(mul(ds, q2, NN))
        dqs.append(mul(ds, k2, TN))
    dv = jnp.where(lk < 64, dvs[0], dvs[1]).astype(bf16)
    dk = jnp.where(lk < 64, dks[0], dks[1]).astype(bf16)
    dq = (jnp.where(lq < 64, dqs[0], dqs[1]) * HEAD_DIM**-0.5).astype(bf16)
    m.dh[0:full, qs] = dq
    m.dh[0:rows, ks] = dk
    m.dh[0:rows, vs] = dv
    at = ((i // 2) % 2) * (2 * blk) + (i // 4) * blk + (i % 2) * 128
    ns = pl.ds(pl.multiple_of(at, 128), 128)
    m.vsum[6:7, ns] = jnp.sum(dq.astype(f32), axis=0, keepdims=True)
    m.vsum[7:8, ns] = jnp.sum(dv.astype(f32), axis=0, keepdims=True)


FWD_IN = ("six", "ubias", "ibias", "iw", "ow", "uw", "dw", "tok", "cot", "valid", "image")


def fwd_kernel(dp, rows, names, table, *refs):
    m = types.SimpleNamespace(**dict(zip(names, refs)))
    n = m.uw.shape[1] // 2
    w = Place(dp)
    length, width = m.tok.shape
    full = m.qkvm.shape[0]
    share = m.sh1.shape[1]
    cols = m.ibias.shape[1]
    blk = n // 4
    sems = {"r": (m.ring_s, m.ring_r), "y": (m.y_s, m.y_r), "c": (m.c_s, m.c_r), "k": m.k_sem}
    groups = [Gather(w, i, m.sh1.at[i], m.w1.at[i], sems) for i in (0, 1)]
    groups += [Gather(w, 2 + i, m.uw.at[:, pl.ds(i * n, n)], m.w2.at[i], sems) for i in (0, 1)]
    groups += [Gather(w, 4 + i, m.dw.at[:, pl.ds(i * n, n)], m.w3.at[i], sems) for i in (0, 1)]
    plan = Plan(groups, table)
    loads = [
        pltpu.make_async_copy(src, dst, m.l_sem.at[i])
        for i, (src, dst) in enumerate(
            (
                (m.iw, m.iwv),
                (m.ow, m.owv),
                (m.six, m.sixv),
                (m.ubias, m.ubv),
                (m.ibias, m.ibv),
                (m.tok, m.xs.at[pl.ds(0, length)]),
                (m.cot, m.gr.at[pl.ds(0, length)]),
                (m.valid, m.tv),
            )
        )
    ]
    for cp in loads:
        cp.start()
    peers = [(lax.rem(w.d + i, dp), w.t) for i in range(1, dp)] + [w.across]
    bar = pltpu.get_barrier_semaphore()
    for a in peers:
        pl.semaphore_signal(bar, inc=1, device_id=a, device_id_type=MESH)
    loads[0].wait()
    loads[1].wait()
    for i in (0, 1):
        part = slice(i * blk, (i + 1) * blk)
        for s in range(3):
            m.sh1[i, :, s * blk : (s + 1) * blk] = m.iwv[s, :, part]
        m.sh1[i, :, 3 * blk :] = m.owv[:, part]
    pl.semaphore_wait(bar, len(peers))
    plan.after("go")
    for cp in loads[2:5]:
        cp.wait()
    spot = pl.ds(pl.multiple_of(w.chip * 128, 128), 128)
    m.vecf[...] = jnp.zeros((8, 128), f32)
    m.vecf[0:6, 0:share] = m.sixv[...].astype(f32)
    vec = m.vecf[...]
    vec = jnp.where(w.core == 0, vec, pltpu.roll(vec, share, 1))
    bias = jnp.zeros((8, cols), f32)
    for r in range(6):
        row = m.ubv[:, r * cols : (r + 1) * cols] if r < 4 else m.ibv[r - 4 : r - 3, :]
        bias = jnp.where(iota((8, cols), 0) == r, jnp.broadcast_to(row.astype(f32), (8, cols)), bias)
    m.packv[...] = bias.astype(bf16)
    m.vec[...] = vec.astype(bf16)

    def vec_copy(i):
        return rcopy(m.vec, m.vbuf.at[w.core, :, spot], m.v_s.at[i], m.v_r.at[i], peers[i])

    bias_copy = rcopy(m.packv, m.bbuf.at[w.t], m.v_s.at[dp - 1], m.v_r.at[dp - 1], w.across)
    for i in range(dp - 1):
        vec_copy(i).start()
    bias_copy.start()
    m.vbuf[w.core, :, spot] = m.vec[...]
    m.bbuf[w.t] = m.packv[...]
    plan.after("pre0")
    zero_rows = pl.ds(rows, full - rows)
    m.qkvm[zero_rows, :] = jnp.zeros((full - rows, m.qkvm.shape[1]), bf16)
    m.act[zero_rows, :] = jnp.zeros((full - rows, m.act.shape[1]), bf16)
    m.slope[zero_rows, :] = jnp.zeros((full - rows, m.slope.shape[1]), bf16)
    m.logs[...] = jnp.zeros(m.logs.shape, f32)
    m.mid[zero_rows, :] = jnp.zeros((full - rows, width), f32)
    for cp in loads[5:]:
        cp.wait()
    tail = pl.ds(length, full - length)
    m.xs[tail, :] = jnp.zeros((full - length, width), bf16)
    m.gr[tail, :] = jnp.zeros((full - length, width), bf16)
    m.row[...] = jnp.zeros(m.row.shape, f32)
    m.row[0:1, 0:length] = m.tv[pl.ds(w.t, 1), :].astype(f32)
    ok = jnp.broadcast_to(m.row[0:1, :], (128, full)).T
    m.rm[...] = ok * m.image[w.t].astype(f32)
    m.kb[...] = jnp.where((ok > 0) | (iota((full, 128), 0) == 0), 0.0, -1e9).astype(bf16)
    for i in range(dp - 1):
        vec_copy(i).wait()
    bias_copy.wait()
    m.vecs[...] = m.vbuf[0].astype(f32) + m.vbuf[1].astype(f32)
    m.qb[...] = jnp.zeros(m.qb.shape, f32)
    for side in (0, 1):
        b = m.bbuf[side].astype(f32)
        for r in range(4):
            at = (r // 2) * 4 + side * 2 + r % 2
            m.ub[at : at + 1, :] = b[r : r + 1]
        for i in (0, 1):
            at = 2 * i + side
            m.qb[at : at + 1, 0:blk] = b[4:5, i * blk : (i + 1) * blk]
            m.qb[at : at + 1, 2 * blk : 3 * blk] = b[5:6, i * blk : (i + 1) * blk]
    ch = 128

    @pl.loop(0, full // ch)
    def _(r):
        rs = tile(r, ch)
        unit, _ = normalize(m.xs[rs, :].astype(f32))
        m.ln[rs, :] = (unit * m.vecs[0:1, :] + m.vecs[1:2, :]).astype(bf16)
        m.gr[rs, :] = (m.gr[rs, :].astype(f32) * m.rm[rs, 0:1]).astype(bf16)

    plan.after("pre1")

    def turn_copies(k):
        tt, lhs = m.turn.at[k], (m.lhs1, m.lhs2, m.lhs3)[k]
        keep = pltpu.make_async_copy(tt.at[:, w.core], lhs.at[:, :, pl.ds(0, full)], m.t_sem.at[k])
        give = rcopy(
            tt.at[:, 1 - w.core], lhs.at[:, :, pl.ds(full, full)], m.t_s.at[k], m.t_r.at[k], w.sibling
        )
        return keep, give

    def turn(src, k):
        tt = m.turn.at[k]

        @pl.loop(0, width // 256)
        def _(j):
            tt[tile(j, 2)] = src[:, tile(j, 256)].T.reshape(2, 2, share, full)

        for cp in turn_copies(k):
            cp.start()

    outs = []

    def save(src, dst):
        k = len(outs)
        cp = pltpu.make_async_copy(src, dst, m.o_sem.at[k])
        outs.append(lambda: pltpu.make_async_copy(src, dst, m.o_sem.at[k]))
        cp.start()

    save(m.gr, m.gr_o)
    save(m.vecs, m.vecs_o)
    save(m.kb, m.kb_o)
    save(m.rm, m.rm_o)
    turn(m.ln, 0)
    plan.after("pre2")
    turn(m.gr, 2)
    plan.after("pre3")

    def qkv_stream(i):
        def body(j, slot):
            p = mul(m.ln[0:rows, :], m.wt[slot], NN) + m.qb[pl.ds(2 * i + j, 1), :]
            p = p.astype(bf16).astype(f32)
            p = jnp.where(iota(p.shape, 1) < blk, p * HEAD_DIM**-0.5, p)
            at = pl.ds(pl.multiple_of(i * 2 * n + j * n, 128), 3 * blk)
            m.qkvm[0:rows, at] = p.astype(bf16)
            plan.tick(j, "qk", 2 * i, 2)

        src = lambda j: m.w1.at[i, :, pl.ds(pl.multiple_of(j * n, 128), 3 * blk)]
        return stream(2, [(src, lambda slot: m.wt.at[slot])], m.s_sem, body)

    def attention(i):
        @pl.loop(0, 4)
        def _(j):
            attend_pair(m, 4 * i + j, rows, full, blk)
            plan.tick(j, "at", 4 * i, 4)

    for i in (0, 1):
        begin, run = qkv_stream(i)
        begin()
        run()
        attention(i)

    def out_tile(j, slot):
        ds = tile(j, 256)
        total = m.xs[0:rows, ds].astype(f32) + m.vecs[2:3, ds]
        for k in range(4):
            at = k * n + 3 * blk
            total += mul(m.qkvm[0:rows, at : at + blk], m.wo[slot, k], NT)
        m.mid[0:rows, ds] = total
        plan.tick(j, "out", 0, 4)

    def out_src(k):
        at = (k % 2) * n + 3 * blk
        return lambda j: m.w1.at[k // 2, tile(j, 256), pl.ds(at, blk)]

    begin, run = stream(
        width // 256, [(out_src(k), lambda slot, k=k: m.wo.at[slot, k]) for k in range(4)], m.s_sem, out_tile
    )
    begin()
    save(m.qkvm, m.qkvm_o)
    m.lt[...] = m.logs[...].T[0 : m.lt.shape[0], :]
    save(m.lt, m.logs_o)
    run()
    save(m.mid, m.mid_o)
    for cp in turn_copies(0):
        cp.wait()
    save(m.lhs1, m.lhs1_o)

    @pl.loop(0, full // ch)
    def _(r):
        rs = tile(r, ch)
        unit, _ = normalize(m.mid[rs, :])
        m.ln[rs, :] = (unit * m.vecs[3:4, :] + m.vecs[4:5, :]).astype(bf16)

    plan.after("ln2")
    turn(m.ln, 1)
    plan.after("turn")

    def act_copies(j):
        cs = tile(j, cols)
        here, there = m.act.at[pl.ds(0, full), cs], m.act.at[pl.ds(full, full), cs]
        yield rcopy(here, there, m.a_s.at[j], m.a_r.at[j], w.sibling)
        yield pltpu.make_async_copy(here, m.act_o.at[:, cs], m.a_sem.at[0, j])
        yield pltpu.make_async_copy(m.slope.at[:, cs], m.slope_o.at[:, cs], m.a_sem.at[1, j])

    def up_stream(i):
        def body(j, slot):
            k = 4 * i + j
            cs = tile(k, cols)
            hidden = mul(m.ln[0:rows, :], m.wt[slot, :, 0:cols], NN) + m.ub[pl.ds(k, 1), :]
            phi = 0.5 * (1.0 + lax.erf(hidden * 0.7071067811865476))
            m.act[0:rows, cs] = (hidden * phi).astype(bf16)
            m.slope[0:rows, cs] = (
                phi + hidden * jnp.exp(-0.5 * hidden * hidden) * 0.3989422804014327
            ).astype(bf16)
            for cp in act_copies(k):
                cp.start()
            plan.tick(j, "up", 4 * i, 4)

        src = lambda j: m.w2.at[i, :, tile(j, cols)]
        return stream(4, [(src, lambda slot: m.wt.at[slot, :, pl.ds(0, cols)])], m.s_sem, body)

    for i in (0, 1):
        begin, run = up_stream(i)
        begin()
        run()
    for cp in turn_copies(2):
        cp.wait()

    def p3_copy(j):
        cs = tile(j % 2, n)
        return pltpu.make_async_copy(m.p3.at[j // 2, :, :, cs], m.p3_o.at[j // 2, :, :, cs], m.p_sem.at[j])

    @pl.loop(0, 4)
    def _(j):
        for k in (0, 1):
            next(act_copies(2 * j + k)).wait_recv()
        lhs = m.lhs3[...].reshape(w.ring * share, 2 * full)
        part = mul(lhs, m.act[:, tile(j, n)], NN).astype(bf16)
        m.p3[j // 2, :, :, tile(j % 2, n)] = part.reshape(w.ring, share, n)
        p3_copy(j).start()
        plan.tick(j, "gw", 0, 4)

    for cp in turn_copies(1):
        cp.wait()
    save(m.lhs2, m.lhs2_o)

    @pl.loop(0, 8)
    def _(j):
        give, a, b = act_copies(j)
        give.wait_send()
        a.wait()
        b.wait()

    @pl.loop(0, 4)
    def _(j):
        p3_copy(j).wait()

    plan.after("fin")
    for again in outs:
        again().wait()
    for g in groups:
        g.drain()


FWD_PLAN = {
    "go": (0, 300, 1, 100),
    "pre0": (2, 101, 3, 102),
    "pre2": (5, 4, 104, 200, 7, 103),
    "pre3": (6, 201, 500, 301, 8, 9, 105, 10),
    "qk0": (202,),
    "at1": (106, 107, 400),
    "at2": (108, 109, 203, 204),
    "at3": (110,),
    "qk2": (302,),
    "at4": (205, 303, 206, 401),
    "at6": (304, 207, 501, 208, 305),
    "at7": (402, 502, 209),
    "out1": (306, 308, 307),
    "ln2": (403,),
    "turn": (210,),
    "up1": (503, 309),
    "up3": (405, 310),
    "up6": (404, 406, 505),
    "gw0": (407, 504, 408, 507, 506),
    "gw1": (508,),
    "gw2": (409, 509),
    "gw3": (510, 410),
}


def gather_sems(dp, groups):
    far = dp // 4
    dma = pltpu.SemaphoreType.DMA
    sizes = (2 * (far + 1), 2 * far + 1, 4 * far + 2)
    return [dma((groups, k)) for k in sizes for _ in (0, 1)] + [dma((groups,))]


def sizes_of(length):
    return -(-length // 16) * 16, -(-length // 128) * 128


def forward(args, dp, length, width, n, share):
    rows, full = sizes_of(length)
    cols, blk = n // 2, n // 4
    ring = dp // 2
    depth = share * dp
    heads = width // HEAD_DIM
    V, dma = pltpu.VMEM, pltpu.SemaphoreType.DMA
    S = jax.ShapeDtypeStruct
    out = dict(
        w1=S((2, depth, 2 * n), bf16),
        w2=S((2, depth, 2 * n), bf16),
        w3=S((2, depth, 2 * n), bf16),
        qkvm_o=S((full, 4 * n), bf16),
        logs_o=S((heads, full), f32),
        mid_o=S((full, width), f32),
        act_o=S((full, 4 * n), bf16),
        slope_o=S((full, 4 * n), bf16),
        p3_o=S((2, ring, share, 2 * n), bf16),
        lhs1_o=S((ring, share, 2 * full), bf16),
        lhs2_o=S((ring, share, 2 * full), bf16),
        gr_o=S((full, width), bf16),
        vecs_o=S((8, width), f32),
        kb_o=S((full, 128), bf16),
        rm_o=S((full, 128), f32),
    )
    scratch = dict(
        sh1=V((2, share, n), bf16),
        iwv=V((3, share, cols), bf16),
        owv=V((share, cols), bf16),
        sixv=V((6, share), bf16),
        ubv=V((1, 2 * n), bf16),
        ibv=V((2, cols), bf16),
        vecf=V((8, 128), f32),
        packv=V((8, cols), bf16),
        tv=V((2, length), jnp.int32),
        row=V((8, full), f32),
        vec=V((8, 128), bf16),
        kb=V((full, 128), bf16),
        rm=V((full, 128), f32),
        xs=V((full, width), bf16),
        gr=V((full, width), bf16),
        ln=V((full, width), bf16),
        qkvm=V((full, 4 * n), bf16),
        logs=V((full, 128), f32),
        lt=V((heads, full), f32),
        mid=V((full, width), f32),
        act=V((2 * full, 4 * n), bf16),
        slope=V((full, 4 * n), bf16),
        p3=V((2, ring, share, 2 * n), bf16),
        turn=V((3, ring, 2, share, full), bf16),
        lhs1=V((ring, share, 2 * full), bf16),
        lhs2=V((ring, share, 2 * full), bf16),
        lhs3=V((ring, share, 2 * full), bf16),
        wt=V((2, depth, 3 * blk), bf16),
        wo=V((2, 4, 256, blk), bf16),
        vbuf=V((2, 8, width), bf16),
        bbuf=V((2, 8, cols), bf16),
        vecs=V((8, width), f32),
        ub=V((8, cols), f32),
        qb=V((8, 3 * blk), f32),
    )
    gs = gather_sems(dp, 6)
    scratch.update(zip(("ring_s", "ring_r", "y_s", "y_r", "c_s", "c_r", "k_sem"), gs))
    scratch.update(
        v_s=dma((dp,)),
        v_r=dma((dp,)),
        l_sem=dma((8,)),
        s_sem=dma((4, 2)),
        t_sem=dma((3,)),
        t_s=dma((3,)),
        t_r=dma((3,)),
        a_s=dma((8,)),
        a_r=dma((8,)),
        a_sem=dma((2, 8)),
        p_sem=dma((4,)),
        o_sem=dma((9,)),
    )
    names = FWD_IN + tuple(out) + tuple(scratch)
    hbm = pl.BlockSpec(memory_space=pl.ANY)
    specs = [pl.BlockSpec(memory_space=pltpu.SMEM) if k == "image" else hbm for k in FWD_IN]
    got = pl.pallas_call(
        functools.partial(fwd_kernel, dp, rows, names, FWD_PLAN),
        out_shape=list(out.values()),
        in_specs=specs,
        out_specs=[hbm] * len(out),
        scratch_shapes=list(scratch.values()),
        compiler_params=pltpu.CompilerParams(collective_id=1, has_side_effects=True, vmem_limit_bytes=VM_LIMIT),
        name="forward",
    )(*args)
    return types.SimpleNamespace(**dict(zip(out, got)))


BWD_IN = (
    "w1", "w2", "w3", "qkvm_i", "logs_i", "mid", "act_i", "slope", "p3", "lhs1_i", "lhs2_i", "gr_i", "vecs_i", "kb_i", "rm_i", "tok"
)


def bwd_kernel(dp, rows, names, table, *refs):
    m = types.SimpleNamespace(**dict(zip(names, refs)))
    n = m.w2.shape[2] // 2
    w = Place(dp)
    length, width = m.tok.shape
    full = m.qkvm.shape[0]
    share = m.p3.shape[2]
    cols, blk = n // 2, n // 4
    sems = {"y": (m.y_s, m.y_r), "r": (m.ring_s, m.ring_r)}

    def group(g, slot):
        i = g % 2
        where = m.og.at[g // 2, :, pl.ds(i * n, n)]
        at = 2 * slot + i
        return Scatter(w, g, m.part.at[at], m.ry.at[at], m.rr.at[at], m.rl.at[at], m.rb.at[at], where, sems)

    groups = [group(0, 0), group(1, 0), group(2, 1), group(3, 1), group(4, 0), group(5, 0)]
    plan = Plan(groups, table)

    def flip(k):
        return (w.d + k - 2 * k * ((w.d // k) % 2), w.t)

    flips = [w.across]
    k = 1
    while k < dp:
        flips.append(flip(k))
        k *= 2
    early = [
        pltpu.make_async_copy(src, dst, m.l_sem.at[i])
        for i, (src, dst) in enumerate(
            (
                (m.gr_i, m.gr),
                (m.p3.at[0], m.part.at[0]),
                (m.p3.at[1], m.part.at[1]),
                (m.lhs2_i, m.lhs),
                (m.mid, m.dm),
                (m.vecs_i, m.vecs),
                (m.qkvm_i, m.qkvm),
                (m.kb_i, m.kb),
                (m.logs_i, m.logs),
                (m.rm_i, m.rm),
            )
        )
    ]

    def dh_copy(j):
        cs = tile(j, cols)
        here, there = m.dh.at[pl.ds(0, full), cs], m.dh.at[pl.ds(full, full), cs]
        return rcopy(here, there, m.h_s.at[j], m.h_r.at[j], w.sibling)

    def dh_tile(j, slot):
        d = mul(m.gr[0:rows, :], m.wt[slot], NN) * m.st[slot, 0:rows, :].astype(f32)
        d = d.astype(bf16)
        m.dh[0:rows, tile(j, cols)] = d
        nat = ((j // 2) % 2) * 4 + (j // 4) * 2 + j % 2
        m.vsum[pl.ds(8 + nat // 2, 1), tile(nat % 2, cols)] = jnp.sum(d.astype(f32), axis=0, keepdims=True)
        dh_copy(j).start()
        plan.tick(j, "dh", 0, 8)

    begin, run = stream(
        8,
        [
            (lambda j: m.w3.at[j // 4, :, tile(j % 4, cols)], lambda slot: m.wt.at[slot]),
            (lambda j: m.slope.at[:, tile(j, cols)], lambda slot: m.st.at[slot]),
        ],
        m.s_sem,
        dh_tile,
    )
    early[0].start()
    early[1].start()
    begin()
    for cp in early[2:]:
        cp.start()
    greet([w.right, w.left] + flips)
    zero_rows = pl.ds(rows, full - rows)
    m.dh[zero_rows, :] = jnp.zeros((full - rows, 4 * n), bf16)
    m.dmix[zero_rows, :] = jnp.zeros((full - rows, width), bf16)
    m.acc[zero_rows, :] = jnp.zeros((full - rows, width), f32)
    m.vsum[...] = jnp.zeros(m.vsum.shape, f32)
    m.vacc[...] = jnp.zeros(m.vacc.shape, f32)
    early[0].wait()
    early[1].wait()
    early[2].wait()
    plan.after("load")
    run()

    def w_stream(ref, body):
        src = lambda j: ref.at[:, tile(j, 256), :]
        return stream(width // 256, [(src, lambda slot: m.wn.at[slot])], m.s_sem, body)

    def second_tile(j, slot):
        ds = tile(j, 256)
        m.acc[0:rows, ds] = mul(m.dh[0:rows, 0 : 2 * n], m.wn[slot, 0], NT) + mul(
            m.dh[0:rows, 2 * n :], m.wn[slot, 1], NT
        )
        plan.tick(j, "ds", 0, 4)

    begin, run = w_stream(m.w2, second_tile)
    begin()
    early[3].wait()

    @pl.loop(0, 4)
    def _(j):
        for k in (0, 1):
            dh_copy(2 * j + k).wait()
        lhs = m.lhs[...].reshape(w.ring * share, 2 * full)
        part = mul(lhs, m.dh[:, tile(j, n)], NN).astype(bf16)
        m.part[2 + j // 2, :, :, tile(j % 2, n)] = part.reshape(w.ring, share, n)
        plan.tick(j, "gu", 0, 4)

    lhs1_in = pltpu.make_async_copy(m.lhs1_i, m.lhs, m.l_sem.at[0])
    lhs1_in.start()
    run()
    early[4].wait()
    early[5].wait()

    def mixed_tile(j, slot):
        m.dmix[0:rows, tile(j, blk)] = mul(m.gr[0:rows, :], m.wt[slot, :, 0:blk], NN).astype(bf16)
        plan.tick(j, "mx", 0, 4)

    begin, run = stream(
        4,
        [
            (
                lambda j: m.w1.at[j // 2, :, pl.ds(pl.multiple_of((j % 2) * n + 3 * blk, 128), blk)],
                lambda slot: m.wt.at[slot, :, pl.ds(0, blk)],
            )
        ],
        m.s_sem,
        mixed_tile,
    )
    begin()
    ch = 128

    def fold(k, x):
        m.vacc[k] += jnp.sum(x.reshape(ch // 8, 8, width), axis=0)

    def norm_back(unit, scaled, gain, up):
        weighted = up * gain
        return scaled * (
            weighted
            - jnp.mean(weighted, axis=-1, keepdims=True)
            - unit * jnp.mean(weighted * unit, axis=-1, keepdims=True)
        )

    @pl.loop(0, full // ch)
    def _(r):
        rs = tile(r, ch)
        unit, scaled = normalize(m.dm[rs, :])
        up = m.acc[rs, :]
        grad = m.gr[rs, :].astype(f32)
        down = norm_back(unit, scaled, m.vecs[3:4, :], up) + grad
        m.dm[rs, :] = down
        m.gr[rs, :] = down.astype(bf16)
        fold(2, down)
        fold(3, up * unit)
        fold(4, up)
        fold(5, grad)

    plan.after("ln2")

    @pl.loop(0, width // 256)
    def _(j):
        m.turn[tile(j, 2)] = m.gr[:, tile(j, 256)].T.reshape(2, 2, share, full)

    keep_turn = pltpu.make_async_copy(m.turn.at[:, w.core], m.lhs4.at[:, :, pl.ds(0, full)], m.t_sem.at[0])
    give_turn = rcopy(
        m.turn.at[:, 1 - w.core], m.lhs4.at[:, :, pl.ds(full, full)], m.x_s.at[0], m.x_r.at[0], w.sibling
    )
    keep_turn.start()
    give_turn.start()
    plan.after("turn")
    run()
    for cp in early[6:]:
        cp.wait()
    for k in range(4):
        at = pl.ds(k * n + 3 * blk, blk)
        m.dh[0:full, at] = m.qkvm[:, at]
    keep_turn.wait()
    give_turn.wait()

    def q_copy(k):
        cs = tile(k, n)
        here, there = m.dh.at[pl.ds(0, full), cs], m.dh.at[pl.ds(full, full), cs]
        return rcopy(here, there, m.q_s.at[k], m.q_r.at[k], w.sibling)

    def attention(first, count):
        @pl.loop(0, count)
        def _(j):
            attend_back(m, first + j, rows, full, blk)

            @pl.when((first + j) % 2 == 1)
            def _():
                q_copy((first + j) // 2).start()

            plan.tick(j, "at", first, count)

    def weights(i):
        @pl.loop(0, 2)
        def _(j):
            base = 2 * i * n + j * n
            q_copy(2 * i + j).wait()
            for ref, lo, size in ((m.lhs, 0, 3 * blk), (m.lhs4, 3 * blk, blk)):
                lhs = ref[...].reshape(w.ring * share, 2 * full)
                src = pl.ds(pl.multiple_of(base + lo, 128), size)
                dst = pl.ds(pl.multiple_of(j * n + lo, 128), size)
                part = mul(lhs, m.dh[:, src], NN).astype(bf16)
                m.part[i, :, :, dst] = part.reshape(w.ring, share, size)
            plan.tick(j, "gw", 2 * i, 2)

    attention(0, 5)
    groups[0].drain()
    lhs1_in.wait()
    weights(0)
    attention(5, 3)

    def first_tile(j, slot):
        total = jnp.zeros((rows, 256), f32)
        for k in range(4):
            lo = (k % 2) * n
            total += mul(m.dh[0:rows, k * n : k * n + 3 * blk], m.wn[slot, k // 2, :, lo : lo + 3 * blk], NT)
        m.acc[0:rows, tile(j, 256)] = total
        plan.tick(j, "df", 0, 4)

    begin, run = w_stream(m.w1, first_tile)
    begin()
    groups[1].drain()
    weights(1)
    tok_in = pltpu.make_async_copy(m.tok, m.xs.at[pl.ds(0, length)], m.l_sem.at[2])
    act_in = pltpu.make_async_copy(m.act_i, m.dh.at[pl.ds(full, full)], m.l_sem.at[1])
    tok_in.start()
    act_in.start()
    run()
    tok_in.wait()
    tail = pl.ds(length, full - length)
    m.xs[tail, :] = jnp.zeros((full - length, width), bf16)

    def block_tile(j, slot):
        ds = tile(j, 256)
        act = m.dh.at[pl.ds(full, rows)]
        m.acc[0:rows, ds] = mul(act[:, 0 : 2 * n], m.wn[slot, 0], NT) + mul(act[:, 2 * n :], m.wn[slot, 1], NT)
        plan.tick(j, "bo", 0, 4)

    begin, run = w_stream(m.w3, block_tile)
    begin()

    @pl.loop(0, full // ch)
    def _(r):
        rs = tile(r, ch)
        unit, scaled = normalize(m.xs[rs, :].astype(f32))
        up = m.acc[rs, :]
        m.dm[rs, :] += norm_back(unit, scaled, m.vecs[0:1, :], up)
        fold(0, up * unit)
        fold(1, up)

    m.vsum[0:6, :] = jnp.sum(m.vacc[...], axis=1)
    gt_out = pltpu.make_async_copy(m.dm.at[pl.ds(0, length)], m.gt, m.l_sem.at[3])
    gt_out.start()

    def vec_copy(s):
        return rcopy(m.vswap.at[s, 0], m.vswap.at[s, 1], m.v_s.at[s], m.v_r.at[s], flips[s])

    def vec_step(s):
        if s:
            vec_copy(s - 1).wait()
            m.vsum[...] += m.vswap[s - 1, 1]
        if s < len(flips):
            m.vswap[s, 0] = m.vsum[...]
            vec_copy(s).start()

    vec_step(0)
    plan.after("ln1")
    act_in.wait()
    run()
    vec_step(1)
    plan.after("v1")
    gt_out.wait()
    mid_in = pltpu.make_async_copy(m.mid, m.dm, m.l_sem.at[4])
    mid_in.start()
    vec_step(2)
    plan.after("v2")
    mid_in.wait()

    @pl.loop(0, full // ch)
    def _(r):
        rs = tile(r, ch)
        m.xs[rs, :] = (m.rm[rs, 0:1] * (m.dm[rs, :] + m.acc[rs, :] + m.vecs[5:6, :])).astype(bf16)

    bo_out = pltpu.make_async_copy(m.xs.at[pl.ds(0, length)], m.bo, m.l_sem.at[0])
    bo_out.start()
    vec_step(3)
    plan.after("v3")
    vec_step(4)
    plan.after("v4")
    vec_step(5)
    outs = [
        pltpu.make_async_copy(m.vsum, m.gv, m.l_sem.at[1]),
        pltpu.make_async_copy(m.og, m.go, m.l_sem.at[2]),
    ]
    outs[0].start()
    plan.after("fin")
    outs[1].start()
    for g in groups[2:]:
        g.drain()
    bo_out.wait()
    for cp in outs:
        cp.wait()


BWD_PLAN = {
    "load": (0, 100),
    "dh2": (1,),
    "gu0": (101, 2, 3),
    "gu3": (102, 103),
    "ds2": (4, 5, 200, 104, 300, 105),
    "mx0": (6, 201, 8, 7),
    "at0": (301, 202, 203, 106),
    "at1": (107, 9),
    "at3": (204, 205, 302, 303),
    "at4": (206, 10, 304),
    "gw1": (400, 207, 108, 109, 208),
    "at5": (401, 305),
    "at7": (402, 209, 403, 110),
    "gw2": (306, 307),
    "gw3": (500, 404),
    "df1": (501, 405),
    "df2": (308,),
    "df3": (502, 406, 503, 210),
    "ln1": (504,),
    "bo0": (505, 309, 407),
    "bo2": (408, 506, 507, 310),
    "bo3": (508,),
    "v3": (409, 509, 410),
    "v4": (510,),
}


def backward(o, tokens, dp, n, share):
    length, width = tokens.shape
    rows, full = sizes_of(length)
    cols = n // 2
    ring = dp // 2
    far = ring // 2
    depth = share * dp
    a = outer(n, 0)
    V, dma = pltpu.VMEM, pltpu.SemaphoreType.DMA
    S = jax.ShapeDtypeStruct
    steps = dp.bit_length()
    out = dict(
        bo=S((length, width), bf16),
        gt=S((length, width), f32),
        go=S((3, share, 2 * n), f32),
        gv=S((16, width), f32),
    )
    wide = 2 * n - outer(n, 1)
    scratch = dict(
        part=V((4, ring, share, 2 * n), bf16),
        ry=V((4, ring, share, a), bf16),
        rr=V((4, far, share, wide), bf16),
        rl=V((4, far, share, wide), bf16),
        rb=V((4, share, n - outer(n, 1)), bf16),
        og=V((3, share, 2 * n), f32),
        dh=V((2 * full, 4 * n), bf16),
        qkvm=V((full, 4 * n), bf16),
        lhs=V((ring, share, 2 * full), bf16),
        lhs4=V((ring, share, 2 * full), bf16),
        turn=V((ring, 2, share, full), bf16),
        dmix=V((full, width), bf16),
        gr=V((full, width), bf16),
        acc=V((full, width), f32),
        dm=V((full, width), f32),
        xs=V((full, width), bf16),
        wt=V((2, depth, cols), bf16),
        st=V((2, full, cols), bf16),
        wn=V((2, 2, 256, 2 * n), bf16),
        logs=V((width // HEAD_DIM, full), f32),
        vecs=V((8, width), f32),
        kb=V((full, 128), bf16),
        rm=V((full, 128), f32),
        vsum=V((16, width), f32),
        vacc=V((6, 8, width), f32),
        vswap=V((steps, 2, 16, width), f32),
        y_s=dma((6, ring + 1)),
        y_r=dma((6, ring + 1)),
        ring_s=dma((6, 2 * far)),
        ring_r=dma((6, 2 * far)),
        l_sem=dma((10,)),
        s_sem=dma((2, 2)),
        t_sem=dma((1,)),
        x_s=dma((1,)),
        x_r=dma((1,)),
        h_s=dma((8,)),
        h_r=dma((8,)),
        q_s=dma((4,)),
        q_r=dma((4,)),
        v_s=dma((steps,)),
        v_r=dma((steps,)),
    )
    args = (
        o.w1, o.w2, o.w3, o.qkvm_o, o.logs_o, o.mid_o, o.act_o, o.slope_o, o.p3_o, o.lhs1_o, o.lhs2_o, o.gr_o, o.vecs_o,
        o.kb_o, o.rm_o, tokens,
    )
    names = BWD_IN + tuple(out) + tuple(scratch)
    hbm = pl.BlockSpec(memory_space=pl.ANY)
    got = pl.pallas_call(
        functools.partial(bwd_kernel, dp, rows, names, BWD_PLAN),
        out_shape=list(out.values()),
        in_specs=[hbm] * len(BWD_IN),
        out_specs=[hbm] * len(out),
        scratch_shapes=list(scratch.values()),
        compiler_params=pltpu.CompilerParams(collective_id=2, has_side_effects=True, vmem_limit_bytes=VM_LIMIT),
        name="backward",
    )(*args)
    return types.SimpleNamespace(**dict(zip(out, got)))


def place_kernel(bo, gt, go, bo_o, gt_o, iw_o, ow_o, uw_o, dw_o, bov, gtv, g, iwv, owv, sem):
    share, wide = g.shape[1:]
    n, blk = wide // 2, wide // 8
    ins = [
        pltpu.make_async_copy(go, g, sem.at[0]),
        pltpu.make_async_copy(gt, gtv, sem.at[1]),
        pltpu.make_async_copy(bo, bov, sem.at[2]),
    ]
    for cp in ins:
        cp.start()
    ins[0].wait()
    outs = [pltpu.make_async_copy(g.at[1], uw_o, sem.at[3]), pltpu.make_async_copy(g.at[0], dw_o, sem.at[4])]
    outs[0].start()
    outs[1].start()
    for i in (0, 1):
        part = slice(i * blk, (i + 1) * blk)
        for s in range(3):
            at = i * n + s * blk
            iwv[s, :, part] = g[2, :, at : at + blk]
        owv[:, part] = g[2, :, i * n + 3 * blk : (i + 1) * n]
    outs += [pltpu.make_async_copy(iwv, iw_o, sem.at[5]), pltpu.make_async_copy(owv, ow_o, sem.at[6])]
    outs[2].start()
    outs[3].start()
    ins[1].wait()
    outs.append(pltpu.make_async_copy(gtv, gt_o, sem.at[7]))
    outs[4].start()
    ins[2].wait()
    outs.append(pltpu.make_async_copy(bov, bo_o, sem.at[8]))
    outs[5].start()
    for cp in outs:
        cp.wait()


def place(r, share, n):
    S = jax.ShapeDtypeStruct
    length, width = r.gt.shape
    cols = n // 2
    hbm = pl.BlockSpec(memory_space=pl.ANY)
    out = [
        S((length, width), bf16),
        S((length, width), f32),
        S((3, share, cols), f32),
        S((share, cols), f32),
        S((share, 2 * n), f32),
        S((share, 2 * n), f32),
    ]
    V = pltpu.VMEM
    return pl.pallas_call(
        place_kernel,
        out_shape=out,
        in_specs=[hbm] * 3,
        out_specs=[hbm] * 6,
        scratch_shapes=[
            V((length, width), bf16),
            V((length, width), f32),
            V((3, share, 2 * n), f32),
            V((3, share, cols), f32),
            V((share, cols), f32),
            pltpu.SemaphoreType.DMA((9,)),
        ],
        compiler_params=pltpu.CompilerParams(vmem_limit_bytes=VM_LIMIT),
        name="place",
    )(r.bo, r.gt, r.go)


def paired_device(
    tokens, cotangent, token_valid, image_valid, first_gain, first_shift, input_weight, input_bias, output_weight,
    output_bias, second_gain, second_shift, up_weight, up_bias, down_weight, down_bias,
):
    dp = lax.axis_size("dp")
    d = lax.axis_index("dp")
    t = lax.axis_index("tensor")
    length, width = tokens.shape
    share, wide = up_weight.shape
    n, cols = wide // 2, wide // 4
    six = jnp.stack([first_gain, first_shift, output_bias, second_gain, second_shift, down_bias])
    args = (
        six,
        up_bias.reshape(1, wide),
        input_bias,
        input_weight.transpose(1, 0, 2),
        output_weight.T,
        up_weight,
        down_weight.T,
        tokens,
        cotangent,
        token_valid,
        image_valid,
    )
    o = forward(args, dp, length, width, n, share)
    r = backward(o, tokens, dp, n, share)
    block_out, grad_tokens, g_in, g_out, g_up, g_down = place(r, share, n)
    vectors = lax.dynamic_slice_in_dim(r.gv[:6], d * share, share, 1)
    bias_own = lax.dynamic_slice_in_dim(r.gv[6:8], t * cols, cols, 1)
    up_own = lax.dynamic_slice_in_dim(r.gv[8:12].reshape(-1), t * wide, wide, 0)
    return (
        block_out,
        grad_tokens,
        vectors[0],
        vectors[1],
        g_in.transpose(1, 0, 2),
        bias_own,
        g_out.T,
        vectors[2],
        vectors[3],
        vectors[4],
        g_up,
        up_own,
        g_down.T,
        vectors[5],
    )


def solution(mesh):
    in_specs = (
        P(("dp", "tensor"), None),
        P(("dp", "tensor"), None),
        P("dp", None),
        P("dp"),
        P("dp"),
        P("dp"),
        P("dp", None, "tensor"),
        P(None, "tensor"),
        P("tensor", "dp"),
        P("dp"),
        P("dp"),
        P("dp"),
        P("dp", "tensor"),
        P("tensor"),
        P("tensor", "dp"),
        P("dp"),
    )
    out_specs = (
        P(("dp", "tensor"), None),
        P(("dp", "tensor"), None),
        P("dp"),
        P("dp"),
        P("dp", None, "tensor"),
        P(None, "tensor"),
        P("tensor", "dp"),
        P("dp"),
        P("dp"),
        P("dp"),
        P("dp", "tensor"),
        P("tensor"),
        P("tensor", "dp"),
        P("dp"),
    )
    ready = mesh.shape["tensor"] == 2 and mesh.shape["dp"] == 16
    body = paired_device if ready else general_device
    return jax.shard_map(
        body, mesh=mesh, in_specs=in_specs, out_specs=out_specs, check_vma=False
    )
```

```python
import functools
import types

import jax
import jax.numpy as jnp
from jax import lax
from jax.experimental import pallas as pl
from jax.experimental.pallas import tpu as pltpu
from jax.sharding import PartitionSpec as P

HEAD_DIM = 64
MESH = pl.DeviceIdType.MESH
f32 = jnp.float32
bf16 = jnp.bfloat16
NN, NT, TN = ((1,), (0,)), ((1,), (1,)), ((0,), (0,))
VM_LIMIT = 63 << 20


def layer_norm(inputs, gain, shift):
    center = inputs - jnp.mean(inputs, axis=-1, keepdims=True)
    spread = jnp.mean(center * center, axis=-1, keepdims=True)
    return center * lax.rsqrt(spread + 1e-06) * gain + shift


def norm_backward(inputs, gain, upstream):
    center = inputs - jnp.mean(inputs, axis=-1, keepdims=True)
    spread = jnp.mean(center * center, axis=-1, keepdims=True)
    scaled = lax.rsqrt(spread + 1e-06)
    unit = center * scaled
    weighted = upstream * gain
    grad_inputs = scaled * (
        weighted
        - jnp.mean(weighted, axis=-1, keepdims=True)
        - unit * jnp.mean(weighted * unit, axis=-1, keepdims=True)
    )
    return (grad_inputs, jnp.sum(upstream * unit, axis=0), jnp.sum(upstream, axis=0))


def gelu_slope(hidden):
    return (
        0.5 * (1.0 + lax.erf(hidden * 0.7071067811865476))
        + hidden * jnp.exp(-0.5 * hidden * hidden) * 0.3989422804014327
    )


def general_device(
    tokens,
    cotangent,
    token_valid,
    image_valid,
    first_gain,
    first_shift,
    input_weight,
    input_bias,
    output_weight,
    output_bias,
    second_gain,
    second_shift,
    up_weight,
    up_bias,
    down_weight,
    down_bias,
):
    f32 = jnp.float32
    bf16 = jnp.bfloat16
    gathered = (
        lax.all_gather(first_gain, "dp", axis=0, tiled=True),
        lax.all_gather(first_shift, "dp", axis=0, tiled=True),
        lax.all_gather(input_weight, "dp", axis=0, tiled=True),
        lax.all_gather(output_weight, "dp", axis=1, tiled=True),
        lax.all_gather(output_bias, "dp", axis=0, tiled=True),
        lax.all_gather(second_gain, "dp", axis=0, tiled=True),
        lax.all_gather(second_shift, "dp", axis=0, tiled=True),
        lax.all_gather(up_weight, "dp", axis=0, tiled=True),
        lax.all_gather(down_weight, "dp", axis=1, tiled=True),
        lax.all_gather(down_bias, "dp", axis=0, tiled=True),
    )
    (
        gain_one,
        shift_one,
        in_full,
        out_full,
        out_shift,
        gain_two,
        shift_two,
        up_full,
        down_full,
        down_shift,
    ) = gathered
    gain_one = gain_one.astype(f32)
    shift_one = shift_one.astype(f32)
    out_shift = out_shift.astype(f32)
    gain_two = gain_two.astype(f32)
    shift_two = shift_two.astype(f32)
    down_shift = down_shift.astype(f32)
    tensor_at = lax.axis_index("tensor")
    groups = lax.axis_size("tensor")
    own_rows = tokens.shape[0]
    width = tokens.shape[1]
    length = token_valid.shape[1]
    positions = lax.broadcasted_iota(jnp.int32, token_valid.shape, 1)
    key_ok = (token_valid > 0) | (positions == 0)
    mask_all = (token_valid * image_valid[:, None]).astype(f32).reshape(-1)
    row_mask = lax.dynamic_slice_in_dim(mask_all, tensor_at * own_rows, own_rows)[:, None]
    images = token_valid.shape[0]
    local_width = in_full.shape[2]
    local_heads = local_width // HEAD_DIM
    hidden_width = up_full.shape[1]
    scale = HEAD_DIM ** (-0.5)
    head_shape = (images, length, local_heads, HEAD_DIM)
    inputs = tokens.astype(f32)
    first_own = layer_norm(inputs, gain_one, shift_one).astype(bf16)
    first_all = lax.all_gather(first_own, "tensor", axis=0, tiled=True)
    project = jnp.einsum("rd,dce->rce", first_all, in_full, preferred_element_type=f32)
    bias_in = input_bias.astype(f32)
    queries = (project[:, 0] + bias_in[0]).astype(bf16).reshape(head_shape)
    keyset = project[:, 1].astype(bf16).reshape(head_shape)
    values = (project[:, 2] + bias_in[1]).astype(bf16).reshape(head_shape)

    def scores_of(query_img, key_img, ok_img):
        scores = jnp.einsum("qhe,khe->hqk", query_img, key_img, preferred_element_type=f32) * scale
        return jnp.where(ok_img[None, None, :], scores, -1000000000.0)

    def attend(pieces):
        query_img, key_img, value_img, ok_img = pieces
        scores = scores_of(query_img, key_img, ok_img)
        highest = jnp.max(scores, axis=-1, keepdims=True)
        log_total = highest + jnp.log(jnp.sum(jnp.exp(scores - highest), axis=-1, keepdims=True))
        attn_probs = jnp.exp(scores - log_total).astype(bf16)
        mixed_img = jnp.einsum("hqk,khe->qhe", attn_probs, value_img, preferred_element_type=f32)
        return (mixed_img.astype(bf16), log_total)

    mixed, log_totals = lax.map(attend, (queries, keyset, values, key_ok))
    mixed_rows = mixed.reshape(images * length, local_width)
    attended = lax.psum_scatter(
        jnp.dot(mixed_rows, out_full, preferred_element_type=f32).astype(jnp.bfloat16),
        "tensor",
        scatter_dimension=0,
        tiled=True,
    ).astype(jnp.float32)
    middle = inputs + attended + out_shift
    second_own = layer_norm(middle, gain_two, shift_two).astype(bf16)
    second_all = lax.all_gather(second_own, "tensor", axis=0, tiled=True)
    hidden = jnp.dot(second_all, up_full, preferred_element_type=f32) + up_bias.astype(f32)
    active = jax.nn.gelu(hidden, approximate=False).astype(bf16)
    lifted = lax.psum_scatter(
        jnp.dot(active, down_full, preferred_element_type=f32).astype(jnp.bfloat16),
        "tensor",
        scatter_dimension=0,
        tiled=True,
    ).astype(jnp.float32)
    block_out = (row_mask * (middle + lifted + down_shift)).astype(bf16)
    grad_last = row_mask * cotangent.astype(f32)
    first_all, second_all = (
        lax.all_gather(first_own, "tensor", axis=0, tiled=True),
        lax.all_gather(second_own, "tensor", axis=0, tiled=True),
    )
    grad_lift = lax.all_gather(grad_last.astype(bf16), "tensor", axis=0, tiled=True)
    grad_active = jnp.einsum("rd,fd->rf", grad_lift, down_full, preferred_element_type=f32)
    grad_hidden = (grad_active * gelu_slope(hidden)).astype(bf16)
    grad_down = jnp.einsum("rf,rd->fd", active, grad_lift, preferred_element_type=f32)
    grad_up = jnp.einsum("rd,rf->df", second_all, grad_hidden, preferred_element_type=f32)
    grad_up_bias = jnp.sum(grad_hidden.astype(f32), axis=0)
    grad_second = lax.psum_scatter(
        jnp.einsum("rf,df->rd", grad_hidden, up_full, preferred_element_type=f32).astype(
            jnp.bfloat16
        ),
        "tensor",
        scatter_dimension=0,
        tiled=True,
    ).astype(jnp.float32)
    grad_middle, grad_gain_two, grad_shift_two = norm_backward(middle, gain_two, grad_second)
    grad_middle = grad_middle + grad_last
    grad_mid_all = lax.all_gather(grad_middle.astype(bf16), "tensor", axis=0, tiled=True)
    grad_mixed = jnp.einsum("rd,ed->re", grad_mid_all, out_full, preferred_element_type=f32).astype(
        bf16
    )
    grad_out_weight = jnp.einsum("re,rd->ed", mixed_rows, grad_mid_all, preferred_element_type=f32)

    def attend_back(pieces):
        query_img, key_img, value_img, ok_img, total_img, grad_img = pieces
        scores = scores_of(query_img, key_img, ok_img)
        attn_probs = jnp.exp(scores - total_img)
        grad_values = jnp.einsum(
            "hqk,qhe->khe", attn_probs.astype(bf16), grad_img, preferred_element_type=f32
        )
        grad_probs = jnp.einsum("qhe,khe->hqk", grad_img, value_img, preferred_element_type=f32)
        grad_scores = (
            attn_probs * (grad_probs - jnp.sum(attn_probs * grad_probs, axis=-1, keepdims=True))
        ).astype(bf16)
        grad_queries = (
            jnp.einsum("hqk,khe->qhe", grad_scores, key_img, preferred_element_type=f32) * scale
        )
        grad_keys = (
            jnp.einsum("hqk,qhe->khe", grad_scores, query_img, preferred_element_type=f32) * scale
        )
        return jnp.stack([grad_queries, grad_keys, grad_values], axis=1).astype(bf16)

    grad_project = lax.map(
        attend_back, (queries, keyset, values, key_ok, log_totals, grad_mixed.reshape(head_shape))
    )
    grad_project = grad_project.reshape(images * length, 3, local_width)
    grad_in_weight = jnp.einsum("rd,rce->dce", first_all, grad_project, preferred_element_type=f32)
    grad_in_bias = jnp.sum(grad_project[:, 0::2].astype(f32), axis=0)
    grad_first = lax.psum_scatter(
        jnp.einsum("rce,dce->rd", grad_project, in_full, preferred_element_type=f32).astype(
            jnp.bfloat16
        ),
        "tensor",
        scatter_dimension=0,
        tiled=True,
    ).astype(jnp.float32)
    grad_inputs, grad_gain_one, grad_shift_one = norm_backward(inputs, gain_one, grad_first)
    grad_inputs = grad_inputs + grad_middle
    grad_in_own, grad_out_own, grad_up_own, grad_down_own = (
        lax.psum_scatter(
            grad_in_weight.astype(jnp.bfloat16), "dp", scatter_dimension=0, tiled=True
        ).astype(jnp.float32),
        lax.psum_scatter(
            grad_out_weight.astype(jnp.bfloat16), "dp", scatter_dimension=1, tiled=True
        ).astype(jnp.float32),
        lax.psum_scatter(
            grad_up.astype(jnp.bfloat16), "dp", scatter_dimension=0, tiled=True
        ).astype(jnp.float32),
        lax.psum_scatter(
            grad_down.astype(jnp.bfloat16), "dp", scatter_dimension=1, tiled=True
        ).astype(jnp.float32),
    )
    vectors = jnp.stack(
        [
            grad_gain_one,
            grad_shift_one,
            jnp.sum(grad_middle, axis=0),
            grad_gain_two,
            grad_shift_two,
            jnp.sum(grad_last, axis=0),
        ]
    )
    bias_share = input_bias.shape[1]
    up_share = up_bias.shape[0]
    placed_bias = lax.dynamic_update_slice(
        jnp.zeros((2, width), f32), grad_in_bias, (0, tensor_at * local_width)
    )
    placed_up = lax.dynamic_update_slice(
        jnp.zeros((hidden_width * groups,), f32), grad_up_bias, (tensor_at * hidden_width,)
    )
    vectors, placed_bias, placed_up = lax.psum((vectors, placed_bias, placed_up), ("dp", "tensor"))
    share = first_gain.shape[0]
    dp_at = lax.axis_index("dp")
    vectors = lax.dynamic_slice_in_dim(vectors, dp_at * share, share, 1)
    bias_own = lax.dynamic_slice_in_dim(placed_bias, tensor_at * bias_share, bias_share, 1)
    up_bias_own = lax.dynamic_slice_in_dim(placed_up, tensor_at * up_share, up_share, 0)
    return (
        block_out,
        grad_inputs,
        vectors[0],
        vectors[1],
        grad_in_own,
        bias_own,
        grad_out_own,
        vectors[2],
        vectors[3],
        vectors[4],
        grad_up_own,
        up_bias_own,
        grad_down_own,
        vectors[5],
    )


def mul(a, b, dims):
    return lax.dot_general(a, b, (dims, ((), ())), preferred_element_type=f32)


def iota(shape, axis):
    return lax.broadcasted_iota(jnp.int32, shape, axis)


def tile(j, size):
    return pl.ds(pl.multiple_of(j * size, size), size)


class Place:
    def __init__(self, dp):
        d = lax.axis_index("dp")
        t = lax.axis_index("tensor")
        ring = dp // 2
        self.dp, self.d, self.t, self.ring, self.far = dp, d, t, ring, ring // 2
        self.chip, self.core = d // 2, d % 2
        self.pos = jnp.where(self.chip % 2 == 0, self.chip // 2, ring - 1 - self.chip // 2)
        self.right = (self.chip_at(1) * 2 + self.core, t)
        self.left = (self.chip_at(-1) * 2 + self.core, t)
        self.across = (d, 1 - t)
        self.sibling = (d + 1 - 2 * self.core, t)

    def chip_at(self, offset):
        ring = self.ring
        spot = (self.pos + offset + ring) % ring
        return jnp.where(spot < ring // 2, 2 * spot, 2 * (ring - 1 - spot) + 1)


class Columns:
    def __init__(self, w, n, a):
        t, b = w.t, n - a
        self.n, self.a, self.b = n, a, b
        self.own = (pl.multiple_of(t * n, 128), n)
        self.other = (pl.multiple_of((1 - t) * n, 128), n)
        self.ring = (pl.multiple_of(t * a, 128), 2 * n - a)
        self.mine_a = (pl.multiple_of(t * (2 * n - a), 128), a)
        self.their_a = (pl.multiple_of((1 - t) * (2 * n - a), 128), a)
        self.their_b = (pl.multiple_of(n - t * b, 128), b)
        self.mine_b = (pl.multiple_of(n - (1 - t) * b, 128), b)


def outer(n, i):
    return n // 2 + 128 * (1 - i) * (n // 1024)


def greet(targets):
    bar = pltpu.get_barrier_semaphore()
    for a in targets:
        pl.semaphore_signal(bar, inc=1, device_id=a, device_id_type=MESH)
    pl.semaphore_wait(bar, len(targets))


def rcopy(src, dst, send, recv, dev):
    return pltpu.make_async_remote_copy(
        src_ref=src, dst_ref=dst, send_sem=send, recv_sem=recv, device_id=dev, device_id_type=MESH
    )


class Gather:
    def __init__(self, w, g, shard, full, sems):
        self.w, self.g, self.shard, self.full, self.sems = w, g, shard, full, sems
        self.rows, n = shard.shape
        self.cols = Columns(w, n, outer(n, g % 2))

    def block(self, offset, cols, span=None):
        w = self.w
        lo, size = span or (0, self.rows)
        base = w.chip_at(offset) * (2 * self.rows) + w.core * self.rows + lo
        return self.full.at[pl.ds(pl.multiple_of(base, 16), size), pl.ds(cols[0], cols[1])]

    def span(self, s, dirn):
        half = self.rows // 2
        return (0, self.rows) if s < self.w.far else (dirn * half, half)

    def off(self, s, dirn):
        return s if dirn else -s

    def make(self, kind, src, dst, k, dev):
        send, recv = self.sems[kind]
        return rcopy(src, dst, send.at[self.g, k], recv.at[self.g, k], dev)

    def y(self, s, dirn):
        if s == 0:
            return self.make("y", self.shard, self.block(0, self.cols.own), 0, self.w.across)
        ref = self.block(self.off(s, dirn), self.cols.mine_a, self.span(s, dirn))
        return self.make("y", ref, ref, 2 * s - 1 + dirn, self.w.across)

    def ring(self, s, dirn, part=0):
        dev = self.w.left if dirn else self.w.right
        k = dirn * (self.w.far + 1)
        if s == 1 and part == 0:
            return self.make("r", self.shard, self.block(0, self.cols.own), k, dev)
        if s == 1:
            ref = self.block(0, self.cols.their_b)
            return self.make("r", ref, ref, k + 1, dev)
        ref = self.block(self.off(s - 1, dirn), self.cols.ring, self.span(s, dirn))
        return self.make("r", ref, ref, k + s, dev)

    def sib(self, k):
        w = self.w
        if k == 0:
            src, dst = self.shard, self.block(0, self.cols.own)
        elif k == 1:
            src = dst = self.block(0, self.cols.other)
        else:
            which, rest = divmod(k - 2, 2 * w.far)
            s, dirn = rest // 2 + 1, rest % 2
            cols = self.cols.their_a if which else self.cols.ring
            src = dst = self.block(self.off(s, dirn), cols, self.span(s, dirn))
        return self.make("c", src, dst, k, w.sibling)

    def keep(self):
        return pltpu.make_async_copy(self.shard, self.block(0, self.cols.own), self.sems["k"].at[self.g])

    def S(self):
        self.y(0, 0).start()
        self.ring(1, 0).start()
        self.ring(1, 1).start()
        self.sib(0).start()
        self.keep().start()

    def Y(self):
        self.y(0, 0).wait_recv()
        self.ring(1, 0, 1).start()
        self.ring(1, 1, 1).start()
        self.sib(1).start()

    def h(self, s):
        for dirn in (0, 1):
            self.ring(s, dirn).wait_recv()
            if s == 1:
                self.ring(s, dirn, 1).wait_recv()
            if s < self.w.far:
                self.ring(s + 1, dirn).start()
            self.y(s, dirn).start()
            self.sib(2 * s + dirn).start()

    def c(self, s):
        for dirn in (0, 1):
            self.y(s, dirn).wait_recv()
            self.sib(2 + 2 * self.w.far + 2 * (s - 1) + dirn).start()

    def events(self):
        h, c = (lambda s: functools.partial(self.h, s)), (lambda s: functools.partial(self.c, s))
        return [self.S, self.Y, h(1), h(2), c(1), h(3), c(2), h(4), c(3), c(4), self.E]

    def E(self):
        for k in range(2 + 4 * self.w.far):
            self.sib(k).wait()
        self.keep().wait()

    def drain(self):
        far = self.w.far
        self.y(0, 0).wait_send()
        for dirn in (0, 1):
            self.ring(1, dirn).wait_send()
            self.ring(1, dirn, 1).wait_send()
            for s in range(1, far + 1):
                self.y(s, dirn).wait_send()
                if s > 1:
                    self.ring(s, dirn).wait_send()


class Scatter:
    def __init__(self, w, g, part, ry, rr, rl, rb, out, sems):
        self.w, self.g, self.part, self.sems, self.out = w, g, part, sems, out
        self.rows, n = part.shape[1], part.shape[2] // 2
        self.cols = c = Columns(w, n, outer(n, g % 2))
        self.ry = ry.at[:, :, pl.ds(0, c.a)]
        self.rr = rr.at[:, :, pl.ds(0, 2 * n - c.a)]
        self.rl = rl.at[:, :, pl.ds(0, 2 * n - c.a)]
        self.rb = rb.at[:, pl.ds(0, c.b)]
        far = w.far
        self.order = [far] + [k * sign for k in range(far - 1, 0, -1) for sign in (1, -1)] + [0]

    def make(self, kind, src, dst, k, dev):
        send, recv = self.sems[kind]
        return rcopy(src, dst, send.at[self.g, k], recv.at[self.g, k], dev)

    def cross(self, k):
        w = self.w
        chip = w.chip_at(k)
        src = self.part.at[chip, :, pl.ds(*self.cols.their_a)]
        return self.make("y", src, self.ry.at[chip], self.order.index(k), w.across)

    def ring(self, s, dirn):
        w = self.w
        chip = w.chip_at(s - w.far if dirn else w.far - s)
        half = self.rows // 2
        span = pl.ds(dirn * half, half) if s == 0 else pl.ds(0, self.rows)
        src = self.part.at[chip, span, pl.ds(*self.cols.ring)]
        dst = (self.rl if dirn else self.rr).at[s, span]
        return self.make("r", src, dst, dirn * w.far + s, w.left if dirn else w.right)

    def swap(self):
        w = self.w
        src = self.part.at[w.chip_at(0), :, pl.ds(*self.cols.their_b)]
        return self.make("y", src, self.rb, len(self.order), w.across)

    def add(self, k, lo, size, cols, other):
        chip = self.w.chip_at(k)
        part = self.part
        ch = 16

        @pl.loop(0, size // ch)
        def _(r):
            rs = pl.ds(pl.multiple_of(lo + r * ch, ch), ch)
            cs = pl.ds(cols[0], cols[1])
            part[chip, rs, cs] = (part[chip, rs, cs].astype(f32) + other[rs, :].astype(f32)).astype(bf16)

    def events(self):
        s, t = (lambda k: functools.partial(self.s, k)), (lambda k: functools.partial(self.t, k))
        return [self.A, self.L, t(3), s(1), t(2), s(2), t(1), s(3), t(0), self.F, self.Z]

    def both(self, k):
        return (k, -k) if k else (0,)

    def A(self):
        for k in (self.w.far, self.w.far - 1, 1 - self.w.far):
            self.cross(k).start()

    def take(self, k):
        self.cross(k).wait_recv()
        self.add(k, 0, self.rows, self.cols.mine_a, self.ry.at[self.w.chip_at(k)])

    def L(self):
        self.cross(self.w.far).wait_recv()
        for k in self.both(self.w.far - 2):
            self.cross(k).start()
        self.add(self.w.far, 0, self.rows, self.cols.mine_a, self.ry.at[self.w.chip_at(self.w.far)])
        self.ring(0, 0).start()
        self.ring(0, 1).start()

    def t(self, k):
        for i in self.both(k):
            self.take(i)
        if k > 1:
            for i in self.both(k - 2):
                self.cross(i).start()

    def s(self, s):
        far, half = self.w.far, self.rows // 2
        for dirn in (0, 1):
            self.ring(s - 1, dirn).wait_recv()
            k = s - far if dirn else far - s
            got = (self.rl if dirn else self.rr).at[s - 1]
            lo, size = (dirn * half, half) if s == 1 else (0, self.rows)
            self.add(k, lo, size, self.cols.ring, got)
            self.ring(s, dirn).start()

    def F(self):
        far = self.w.far
        for dirn in (0, 1):
            self.ring(far - 1, dirn).wait_recv()
            self.add(0, 0, self.rows, self.cols.ring, (self.rl if dirn else self.rr).at[far - 1])
        self.swap().start()

    def Z(self):
        self.swap().wait_recv()
        self.add(0, 0, self.rows, self.cols.mine_b, self.rb)
        chip = self.w.chip_at(0)
        self.out[...] = self.part[chip, :, pl.ds(*self.cols.own)].astype(f32)

    def drain(self):
        for k in self.order:
            self.cross(k).wait_send()
        for s in range(self.w.far):
            self.ring(s, 0).wait_send()
            self.ring(s, 1).wait_send()
        self.swap().wait_send()


class Plan:
    def __init__(self, groups, table):
        self.events, self.table = [g.events() for g in groups], table

    def after(self, name):
        for code in self.table.get(name, ()):
            self.events[code // 100][code % 100]()

    def tick(self, j, name, first, count):
        for k in range(count):
            at = name + str(first + k)
            if at in self.table:

                @pl.when(j == k)
                def _(at=at):
                    self.after(at)


def stream(count, parts, sem, body, begun=False):
    def copies(j):
        slot = lax.rem(j, 2)
        return [pltpu.make_async_copy(src(j), dst(slot), sem.at[i, slot]) for i, (src, dst) in enumerate(parts)]

    def begin():
        for cp in copies(jnp.int32(0)):
            cp.start()

    def run():
        @pl.loop(0, count)
        def _(j):
            @pl.when(j + 1 < count)
            def _():
                for cp in copies(j + 1):
                    cp.start()

            for cp in copies(j):
                cp.wait()
            body(j, lax.rem(j, 2))

    return begin, run


def normalize(x):
    center = x - jnp.mean(x, axis=-1, keepdims=True)
    scaled = lax.rsqrt(jnp.mean(center * center, axis=-1, keepdims=True) + 1e-06)
    return center * scaled, scaled


def lanes_of(pair, blk):
    base = (pair // 2) * (4 * blk) + (pair % 2) * 128
    return [pl.ds(pl.multiple_of(base + s * blk, 128), 128) for s in range(4)]


def attend_pair(m, i, rows, full, blk):
    qs, ks, vs, ms = lanes_of(i, blk)
    q2, k2, v2 = m.qkvm[0:rows, qs], m.qkvm[:, ks], m.qkvm[:, vs]
    lq, lk = iota((rows, 128), 1), iota((full, 128), 1)
    outs = []
    logs = m.logs[0:rows, :]
    for h in (0, 1):
        spare = 64 * (1 - h)
        own_q = (lq < 64) if h == 0 else (lq >= 64)
        own_k = (lk < 64) if h == 0 else (lk >= 64)
        qh = jnp.where(own_q, q2, jnp.where(lq == spare, 1.0, 0.0).astype(bf16))
        kh = jnp.where(lk == spare, m.kb[...], k2)
        scores = mul(qh, kh, NT)
        top = jnp.max(scores, axis=1, keepdims=True)
        probs = jnp.exp(scores - top).astype(bf16)
        out = mul(probs, jnp.where(own_k, v2, jnp.ones_like(v2)), NN)
        turned = pltpu.roll(out, 64, 1)
        outs.append(out / turned)
        total = jnp.where(own_q, turned, out)
        logs = jnp.where(lq == 2 * i + h, top + jnp.log(total), logs)
    m.logs[0:rows, :] = logs
    m.qkvm[0:rows, ms] = jnp.where(lq < 64, outs[0], outs[1]).astype(bf16)


def attend_back(m, i, rows, full, blk):
    qs, ks, vs, ms = lanes_of(i, blk)
    q2, do2 = m.qkvm[:, qs], m.ln[:, tile(i, 128)]
    k2, v2 = m.qkvm[0:rows, ks], m.qkvm[0:rows, vs]
    lq, lk = iota((full, 128), 1), iota((rows, 128), 1)
    both = (do2.astype(f32) * m.qkvm[:, ms].astype(f32)).T
    dqs, dks, dvs = [], [], []
    for h in (0, 1):
        spare = 64 * (1 - h)
        own_q = (lq < 64) if h == 0 else (lq >= 64)
        own_k = (lk < 64) if h == 0 else (lk >= 64)
        qh = jnp.where(own_q, q2, jnp.where(lq == spare, 1.0, 0.0).astype(bf16))
        kh = jnp.where(lk == spare, m.kb[0:rows, :], k2)
        probs = jnp.exp(mul(kh, qh, NT) - m.lt[pl.ds(2 * i + h, 1), :])
        dvs.append(mul(probs.astype(bf16), do2, NN))
        dprobs = mul(jnp.where(own_k, v2, jnp.zeros_like(v2)), do2, NT)
        inner = jnp.sum(both[64 * h : 64 * h + 64, :], axis=0, keepdims=True)
        ds = (probs * (dprobs - inner)).astype(bf16)
        dks.append(mul(ds, q2, NN))
        dqs.append(mul(ds, k2, TN))
    dv = jnp.where(lk < 64, dvs[0], dvs[1]).astype(bf16)
    dk = jnp.where(lk < 64, dks[0], dks[1]).astype(bf16)
    dq = (jnp.where(lq < 64, dqs[0], dqs[1]) * HEAD_DIM**-0.5).astype(bf16)
    m.big[0:full, qs] = dq
    m.big[0:rows, ks] = dk
    m.big[0:rows, vs] = dv
    at = ((i // 2) % 2) * (2 * blk) + (i // 4) * blk + (i % 2) * 128
    ns = pl.ds(pl.multiple_of(at, 128), 128)
    m.vsum[6:7, ns] = jnp.sum(dq.astype(f32), axis=0, keepdims=True)
    m.vsum[7:8, ns] = jnp.sum(dv.astype(f32), axis=0, keepdims=True)


LAYER_IN = ("v0", "v1", "v2", "v3", "v4", "v5", "ubias", "ibias", "iw", "ow", "uw", "dw", "tok", "cot", "valid", "image")


def layer_kernel(dp, rows, names, table, *refs):
    m = types.SimpleNamespace(**dict(zip(names, refs)))
    n = m.uw.shape[1] // 2
    w = Place(dp)
    length, width = m.tok.shape
    full = m.qkvm.shape[0]
    share = m.sh1.shape[1]
    cols, blk = n // 2, n // 4
    ch = 128
    sems = {"r": (m.ring_s, m.ring_r), "y": (m.y_s, m.y_r), "c": (m.c_s, m.c_r), "k": m.k_sem}
    groups = [Gather(w, i, m.sh1.at[i], m.w1.at[i], sems) for i in (0, 1)]
    groups += [Gather(w, 2 + i, m.uw.at[:, pl.ds(i * n, n)], m.w2.at[i], sems) for i in (0, 1)]
    groups += [Gather(w, 4 + i, m.dw.at[:, pl.ds(i * n, n)], m.w3.at[i], sems) for i in (0, 1)]
    sums = {"y": (m.sy_s, m.sy_r), "r": (m.sr_s, m.sr_r)}
    for g in range(6):
        at = (0, 1, 2, 3, 0, 1)[g]
        where = m.og.at[g // 2, :, pl.ds((g % 2) * n, n)]
        groups.append(Scatter(w, g, m.part.at[at], m.ry.at[at], m.rr.at[at], m.rl.at[at], m.rb.at[at], where, sums))
    plan = Plan(groups, table)
    gathers, sums6 = groups[:6], groups[6:]

    def flip(k):
        return (w.d + k - 2 * k * ((w.d // k) % 2), w.t)

    flips = [w.across]
    k = 1
    while k < dp:
        flips.append(flip(k))
        k *= 2

    loads = [
        pltpu.make_async_copy(src, dst, m.l_sem.at[i])
        for i, (src, dst) in enumerate(
            (
                (m.iw, m.iwv),
                (m.ow, m.owv),
                (m.ubias, m.ubv),
                (m.ibias, m.ibv),
                (m.tok, m.xs.at[pl.ds(0, length)]),
                (m.cot, m.gr.at[pl.ds(0, length)]),
                (m.valid, m.tv),
            )
        )
    ]
    loads += [
        pltpu.make_async_copy(src, m.sixv.at[i], m.x_sem.at[i])
        for i, src in enumerate((m.v0, m.v1, m.v2, m.v3, m.v4, m.v5))
    ]
    for cp in loads:
        cp.start()
    peers = [(lax.rem(w.d + i, dp), w.t) for i in range(1, dp)] + [w.across]
    bar = pltpu.get_barrier_semaphore()
    for a in peers:
        pl.semaphore_signal(bar, inc=1, device_id=a, device_id_type=MESH)
    loads[0].wait()
    loads[1].wait()
    for i in (0, 1):
        part = slice(i * blk, (i + 1) * blk)
        for s in range(3):
            m.sh1[i, :, s * blk : (s + 1) * blk] = m.iwv[s, :, part]
        m.sh1[i, :, 3 * blk :] = m.owv[:, part]
    pl.semaphore_wait(bar, len(peers))
    plan.after("go")
    for cp in loads[2:4] + loads[7:]:
        cp.wait()
    spot = pl.ds(pl.multiple_of(w.chip * 128, 128), 128)
    m.vecf[...] = jnp.zeros((8, 128), f32)
    for i in range(6):
        m.vecf[i : i + 1, 0:share] = m.sixv[i].astype(f32)
    vec = m.vecf[...]
    vec = jnp.where(w.core == 0, vec, pltpu.roll(vec, share, 1))
    m.biasf[...] = jnp.zeros(m.biasf.shape, f32)
    ub = m.ubv[...].astype(f32)
    for r in range(4 * cols // 128):
        q = r * 128 // cols
        lo = r * 128 - q * cols
        m.biasf[q : q + 1, lo : lo + 128] = ub[r : r + 1, :]
    m.biasf[4:6, :] = m.ibv[...].astype(f32)
    m.packv[...] = m.biasf[...].astype(bf16)
    m.vec[...] = vec.astype(bf16)

    def vec_copy(i):
        return rcopy(m.vec, m.vbuf.at[w.core, :, spot], m.v_s.at[i], m.v_r.at[i], peers[i])

    bias_copy = rcopy(m.packv, m.bbuf.at[w.t], m.v_s.at[dp - 1], m.v_r.at[dp - 1], w.across)
    for i in range(dp - 1):
        vec_copy(i).start()
    bias_copy.start()
    m.vbuf[w.core, :, spot] = m.vec[...]
    m.bbuf[w.t] = m.packv[...]
    plan.after("pre0")
    zero_rows = pl.ds(rows, full - rows)
    m.qkvm[zero_rows, :] = jnp.zeros((full - rows, 4 * n), bf16)
    m.big[zero_rows, :] = jnp.zeros((full - rows, 4 * n), bf16)
    m.acc[zero_rows, :] = jnp.zeros((full - rows, width), f32)
    m.mid[zero_rows, :] = jnp.zeros((full - rows, width), f32)
    m.logs[...] = jnp.zeros(m.logs.shape, f32)
    m.vsum[...] = jnp.zeros(m.vsum.shape, f32)
    m.vacc[...] = jnp.zeros(m.vacc.shape, f32)
    for cp in loads[4:7]:
        cp.wait()
    tail = pl.ds(length, full - length)
    m.xs[tail, :] = jnp.zeros((full - length, width), bf16)
    m.gr[tail, :] = jnp.zeros((full - length, width), bf16)
    m.row[...] = jnp.zeros(m.row.shape, f32)
    m.row[0:1, 0:length] = m.tv[pl.ds(w.t, 1), :].astype(f32)
    ok = jnp.broadcast_to(m.row[0:1, :], (128, full)).T
    m.rm[...] = ok * m.image[w.t].astype(f32)
    m.kb[...] = jnp.where((ok > 0) | (iota((full, 128), 0) == 0), 0.0, -1e9).astype(bf16)
    for i in range(dp - 1):
        vec_copy(i).wait()
    bias_copy.wait()
    m.vecs[...] = m.vbuf[0].astype(f32) + m.vbuf[1].astype(f32)
    m.qb[...] = jnp.zeros(m.qb.shape, f32)
    for side in (0, 1):
        b = m.bbuf[side].astype(f32)
        for r in range(4):
            at = (r // 2) * 4 + side * 2 + r % 2
            m.ub[at : at + 1, :] = b[r : r + 1]
        for i in (0, 1):
            at = 2 * i + side
            m.qb[at : at + 1, 0:blk] = b[4:5, i * blk : (i + 1) * blk]
            m.qb[at : at + 1, 2 * blk : 3 * blk] = b[5:6, i * blk : (i + 1) * blk]

    @pl.loop(0, full // ch)
    def _(r):
        rs = tile(r, ch)
        unit, _ = normalize(m.xs[rs, :].astype(f32))
        m.ln[rs, :] = (unit * m.vecs[0:1, :] + m.vecs[1:2, :]).astype(bf16)
        m.gr[rs, :] = (m.gr[rs, :].astype(f32) * m.rm[rs, 0:1]).astype(bf16)

    plan.after("pre1")

    def turn_copies(k):
        tt, lhs = m.turn.at[k % 2], (m.lhs1, m.lhs3, m.lhs2, m.lhs3)[k]
        keep = pltpu.make_async_copy(tt.at[:, w.core], lhs.at[:, :, pl.ds(0, full)], m.t_sem.at[k])
        give = rcopy(
            tt.at[:, 1 - w.core], lhs.at[:, :, pl.ds(full, full)], m.t_s.at[k], m.t_r.at[k], w.sibling
        )
        return keep, give

    def turn(src, k):
        if k > 1:
            for cp in turn_copies(k - 2):
                cp.wait()
        tt = m.turn.at[k % 2]

        @pl.loop(0, width // 256)
        def _(j):
            tt[tile(j, 2)] = src[:, tile(j, 256)].T.reshape(2, 2, share, full)

        for cp in turn_copies(k):
            cp.start()

    turn(m.ln, 0)
    plan.after("pre2")
    turn(m.gr, 1)
    plan.after("pre3")

    def at_cols(j, lo, size):
        return pl.ds(pl.multiple_of(j * n + lo, 128), size)

    def qkv_stream(i):
        def body(j, slot):
            p = mul(m.ln[0:rows, :], m.wt[slot], NN) + m.qb[pl.ds(2 * i + j, 1), :]
            p = p.astype(bf16).astype(f32)
            p = jnp.where(iota(p.shape, 1) < blk, p * HEAD_DIM**-0.5, p)
            m.qkvm[0:rows, at_cols(2 * i + j, 0, 3 * blk)] = p.astype(bf16)
            plan.tick(j, "qk", 2 * i, 2)

        src = lambda j: m.w1.at[i, :, at_cols(j, 0, 3 * blk)]
        return stream(2, [(src, lambda slot: m.wt.at[slot])], m.s_sem, body)

    for i in (0, 1):
        begin, run = qkv_stream(i)
        begin()
        run()

        @pl.loop(0, 4)
        def _(j, i=i):
            attend_pair(m, 4 * i + j, rows, full, blk)
            plan.tick(j, "at", 4 * i, 4)

    def w_stream(ref, body):
        src = lambda j: ref.at[:, tile(j, 256), :]
        return stream(width // 256, [(src, lambda slot: m.wn.at[slot])], m.s_sem, body)

    def out_tile(j, slot):
        ds = tile(j, 256)
        total = m.xs[0:rows, ds].astype(f32) + m.vecs[2:3, ds]
        for k in range(4):
            own = m.qkvm[0:rows, k * n + 3 * blk : (k + 1) * n]
            lo = (k % 2) * n + 3 * blk
            total += mul(own, m.wn[slot, k // 2, :, lo : lo + blk], NT)
        m.mid[0:rows, ds] = total
        plan.tick(j, "out", 0, 4)

    def out_part(k):
        lo = (k % 2) * n + 3 * blk
        src = lambda j: m.w1.at[k // 2, tile(j, 256), pl.ds(lo, blk)]
        return src, lambda slot: m.wn.at[slot, k // 2, :, pl.ds(lo, blk)]

    begin, run = stream(width // 256, [out_part(k) for k in range(4)], m.s_sem, out_tile)
    begin()
    m.lt[...] = m.logs[...].T[0 : m.lt.shape[0], :]
    run()
    mid_out = pltpu.make_async_copy(m.mid, m.mid_o, m.l_sem.at[0])
    mid_out.start()

    @pl.loop(0, full // ch)
    def _(r):
        rs = tile(r, ch)
        unit, _ = normalize(m.mid[rs, :])
        m.ln[rs, :] = (unit * m.vecs[3:4, :] + m.vecs[4:5, :]).astype(bf16)

    plan.after("ln2")
    turn(m.ln, 2)
    plan.after("turn")

    def halves(ref, cs):
        return ref.at[pl.ds(0, full), cs], ref.at[pl.ds(full, full), cs]

    def act_copy(j):
        here, there = halves(m.big, tile(j, cols))
        return rcopy(here, there, m.a_s.at[j], m.a_r.at[j], w.sibling)

    def act_save(j):
        cs = tile(j, cols)
        return pltpu.make_async_copy(m.big.at[pl.ds(0, full), cs], m.act_o.at[:, cs], m.a_sem.at[0, j])

    def slope_save(j):
        return pltpu.make_async_copy(m.st.at[j % 2], m.slope_o.at[:, tile(j, cols)], m.a_sem.at[1, j])

    def up_stream(i):
        def body(j, slot):
            k = 4 * i + j
            cs = tile(k, cols)
            hidden = mul(m.ln[0:rows, :], m.wt[slot, :, 0:cols], NN) + m.ub[pl.ds(k, 1), :]
            phi = 0.5 * (1.0 + lax.erf(hidden * 0.7071067811865476))
            m.big[0:rows, cs] = (hidden * phi).astype(bf16)
            slope = phi + hidden * jnp.exp(-0.5 * hidden * hidden) * 0.3989422804014327

            @pl.when(k >= 2)
            def _():
                slope_save(k - 2).wait()

            m.st[k % 2, 0:rows, :] = slope.astype(bf16)
            for cp in (act_copy(k), act_save(k), slope_save(k)):
                cp.start()
            plan.tick(j, "up", 4 * i, 4)

        src = lambda j: m.w2.at[i, :, tile(j, cols)]
        return stream(4, [(src, lambda slot: m.wt.at[slot, :, pl.ds(0, cols)])], m.s_sem, body)

    def product(lhs, src):
        return mul(lhs[...].reshape(w.ring * share, 2 * full), m.big[:, src], NN).astype(bf16)

    m.st[:, zero_rows, :] = jnp.zeros((2, full - rows, cols), bf16)
    for i in (0, 1):
        begin, run = up_stream(i)
        begin()
        run()
        if i == 0:
            for cp in turn_copies(1):
                cp.wait()

        @pl.loop(0, 2)
        def _(j, i=i):
            for k in (0, 1):
                act_copy(4 * i + 2 * j + k).wait()
            m.part[i, :, :, tile(j, n)] = product(m.lhs3, tile(2 * i + j, n)).reshape(w.ring, share, n)
            plan.tick(j, "gw", 2 * i, 2)

    pl.semaphore_signal(m.clear, inc=1, device_id=w.sibling, device_id_type=MESH)

    def dh_copy(j):
        here, there = halves(m.big, tile(j, cols))
        return rcopy(here, there, m.h_s.at[j], m.h_r.at[j], w.sibling)

    def dh_stream(i):
        def body(j, slot):
            k = 4 * i + j
            d = mul(m.gr[0:rows, :], m.wt[slot, :, 0:cols], NN) * m.st[slot, 0:rows, :].astype(f32)
            d = d.astype(bf16)
            m.big[0:rows, tile(k, cols)] = d
            nat = (j // 2) * 4 + i * 2 + j % 2
            m.vsum[pl.ds(8 + nat // 2, 1), tile(nat % 2, cols)] = jnp.sum(d.astype(f32), axis=0, keepdims=True)
            dh_copy(k).start()
            plan.tick(j, "dh", 4 * i, 4)

        return stream(
            4,
            [
                (lambda j: m.w3.at[i, :, tile(j, cols)], lambda slot: m.wt.at[slot, :, pl.ds(0, cols)]),
                (lambda j: m.slope_o.at[:, tile(4 * i + j, cols)], lambda slot: m.st.at[slot]),
            ],
            m.s_sem,
            body,
        )

    for k in (6, 7):
        slope_save(jnp.int32(k)).wait()

    @pl.loop(0, 8)
    def _(j):
        act_save(j).wait()

    m.ln[zero_rows, :] = jnp.zeros((full - rows, width), bf16)
    pl.semaphore_wait(m.clear, 1)
    for cp in turn_copies(2):
        cp.wait()

    def second_tile(j, slot):
        ds = tile(j, 256)
        m.acc[0:rows, ds] = mul(m.big[0:rows, 0 : 2 * n], m.wn[slot, 0], NT) + mul(
            m.big[0:rows, 2 * n :], m.wn[slot, 1], NT
        )
        plan.tick(j, "ds", 0, 4)

    for i in (0, 1):
        begin, run = dh_stream(i)
        begin()
        run()
        if i:
            begin, run = w_stream(m.w2, second_tile)
            begin()

        @pl.loop(0, 2)
        def _(j, i=i):
            for k in (0, 1):
                dh_copy(4 * i + 2 * j + k).wait()
            m.part[2 + i, :, :, tile(j, n)] = product(m.lhs2, tile(2 * i + j, n)).reshape(w.ring, share, n)
            plan.tick(j, "gu", 2 * i, 2)

    run()

    def mixed_tile(j, slot):
        m.ln[0:rows, tile(j, blk)] = mul(m.gr[0:rows, :], m.wt[slot, :, 0:blk], NN).astype(bf16)
        plan.tick(j, "mx", 0, 4)

    begin, run = stream(
        4,
        [(lambda j: m.w1.at[j // 2, :, at_cols(j % 2, 3 * blk, blk)], lambda slot: m.wt.at[slot, :, pl.ds(0, blk)])],
        m.s_sem,
        mixed_tile,
    )
    begin()
    mid_out.wait()

    def fold(k, x):
        m.vacc[k] += jnp.sum(x.reshape(ch // 8, 8, width), axis=0)

    def norm_back(unit, scaled, gain, up):
        weighted = up * gain
        return scaled * (
            weighted
            - jnp.mean(weighted, axis=-1, keepdims=True)
            - unit * jnp.mean(weighted * unit, axis=-1, keepdims=True)
        )

    @pl.loop(0, full // ch)
    def _(r):
        rs = tile(r, ch)
        unit, scaled = normalize(m.mid[rs, :])
        up = m.acc[rs, :]
        grad = m.gr[rs, :].astype(f32)
        down = norm_back(unit, scaled, m.vecs[3:4, :], up) + grad
        m.mid[rs, :] = down
        m.gr[rs, :] = down.astype(bf16)
        fold(2, down)
        fold(3, up * unit)
        fold(4, up)
        fold(5, grad)

    plan.after("nb")
    tt = m.turn.at[1]

    @pl.loop(0, width // 256)
    def _(j):
        tt[tile(j, 2)] = m.gr[:, tile(j, 256)].T.reshape(2, 2, share, full)

    for cp in turn_copies(3):
        cp.start()
    plan.after("tb")
    run()
    for k in range(4):
        at = pl.ds(k * n + 3 * blk, blk)
        m.big[0:full, at] = m.qkvm[:, at]
    for cp in turn_copies(3):
        cp.wait()

    def q_copy(k):
        here, there = halves(m.big, tile(k, n))
        return rcopy(here, there, m.q_s.at[k], m.q_r.at[k], w.sibling)

    def attention(first, count):
        @pl.loop(0, count)
        def _(j):
            attend_back(m, first + j, rows, full, blk)

            @pl.when((first + j) % 2 == 1)
            def _():
                q_copy((first + j) // 2).start()

            plan.tick(j, "ab", first, count)

    def weights(i):
        @pl.loop(0, 2)
        def _(j):
            k = 2 * i + j
            q_copy(k).wait()
            for ref, lo, size in ((m.lhs1, 0, 3 * blk), (m.lhs3, 3 * blk, blk)):
                part = product(ref, at_cols(k, lo, size))
                m.part[i, :, :, at_cols(j, lo, size)] = part.reshape(w.ring, share, size)
            plan.tick(j, "ga", 2 * i, 2)

    attention(0, 5)
    sums6[0].drain()
    weights(0)
    attention(5, 3)

    def first_tile(j, slot):
        total = jnp.zeros((rows, 256), f32)
        for k in range(4):
            lo = (k % 2) * n
            total += mul(m.big[0:rows, k * n : k * n + 3 * blk], m.wn[slot, k // 2, :, lo : lo + 3 * blk], NT)
        m.acc[0:rows, tile(j, 256)] = total
        plan.tick(j, "df", 0, 4)

    begin, run = w_stream(m.w1, first_tile)
    begin()
    sums6[1].drain()
    weights(1)
    act_in = pltpu.make_async_copy(m.act_o, m.big.at[pl.ds(full, full)], m.l_sem.at[1])
    act_in.start()
    run()

    def block_tile(j, slot):
        ds = tile(j, 256)
        act = m.big.at[pl.ds(full, rows)]
        m.acc[0:rows, ds] = mul(act[:, 0 : 2 * n], m.wn[slot, 0], NT) + mul(act[:, 2 * n :], m.wn[slot, 1], NT)
        plan.tick(j, "bo", 0, 4)

    begin, run = w_stream(m.w3, block_tile)
    begin()

    @pl.loop(0, full // ch)
    def _(r):
        rs = tile(r, ch)
        unit, scaled = normalize(m.xs[rs, :].astype(f32))
        up = m.acc[rs, :]
        m.mid[rs, :] += norm_back(unit, scaled, m.vecs[0:1, :], up)
        fold(0, up * unit)
        fold(1, up)

    m.vsum[0:6, :] = jnp.sum(m.vacc[...], axis=1)
    gt_out = pltpu.make_async_copy(m.mid.at[pl.ds(0, length)], m.gt, m.l_sem.at[3])
    gt_out.start()

    def sum_copy(s):
        return rcopy(m.vswap.at[s, 0], m.vswap.at[s, 1], m.b_s.at[s], m.b_r.at[s], flips[s])

    def sum_step(s):
        if s:
            sum_copy(s - 1).wait()
            m.vsum[...] += m.vswap[s - 1, 1]
        if s < len(flips):
            m.vswap[s, 0] = m.vsum[...]
            sum_copy(s).start()

    sum_step(0)
    plan.after("ln1")
    act_in.wait()
    run()
    sum_step(1)
    plan.after("v1")
    gt_out.wait()
    mid_in = pltpu.make_async_copy(m.mid_o, m.mid, m.l_sem.at[4])
    mid_in.start()
    sum_step(2)
    plan.after("v2")
    mid_in.wait()

    @pl.loop(0, full // ch)
    def _(r):
        rs = tile(r, ch)
        m.xs[rs, :] = (m.rm[rs, 0:1] * (m.mid[rs, :] + m.acc[rs, :] + m.vecs[5:6, :])).astype(bf16)

    bo_out = pltpu.make_async_copy(m.xs.at[pl.ds(0, length)], m.bo, m.l_sem.at[0])
    bo_out.start()
    sum_step(3)
    plan.after("v3")
    sum_step(4)
    plan.after("v4")
    sum_step(5)
    outs = [
        pltpu.make_async_copy(m.vsum, m.gv, m.l_sem.at[1]),
        pltpu.make_async_copy(m.og, m.go, m.l_sem.at[2]),
    ]
    outs[0].start()
    plan.after("fin")
    outs[1].start()
    for g in gathers + sums6[2:]:
        g.drain()
    bo_out.wait()
    for cp in outs:
        cp.wait()


LAYER_PLAN = {
    "go": (0, 300, 1, 100, 2, 200),
    "pre0": (3, 101),
    "pre1": (5, 4, 102, 6, 7, 201, 301, 8),
    "pre3": (103, 202, 9, 10),
    "qk1": (105, 302, 104),
    "at1": (106, 107, 204, 203, 108),
    "at2": (109,),
    "at3": (400, 303, 110),
    "qk3": (205,),
    "at4": (500,),
    "at6": (401, 305, 207, 304),
    "at7": (206, 208, 501),
    "out0": (402,),
    "out2": (209, 306, 308, 502),
    "out3": (307,),
    "turn": (210, 403),
    "up2": (503, 309),
    "gw0": (405, 310),
    "gw1": (600, 504, 404),
    "up4": (406,),
    "up5": (407,),
    "up7": (505, 601),
    "gw3": (408, 409, 700, 507, 602, 603, 506, 508, 410),
    "dh3": (701,),
    "gu0": (604, 605, 702, 509),
    "gu1": (703, 510),
    "dh6": (606, 607, 704),
    "gu2": (800, 705),
    "gu3": (900,),
    "ds1": (801,),
    "ds3": (802, 706),
    "mx1": (708, 608, 609, 901),
    "mx3": (804, 803, 707),
    "ab2": (805, 902, 903),
    "ab4": (806, 807, 904, 610),
    "ga0": (709,),
    "ga1": (905, 1000),
    "ab6": (1001, 906),
    "ab7": (907, 710, 1002, 1003),
    "ga3": (1100,),
    "df1": (908, 1101, 1004, 1005),
    "df3": (1102, 808, 1103, 1006, 1007, 909, 809, 1008),
    "ln1": (1104, 1105),
    "bo0": (1009,),
    "bo1": (1106, 1107, 1010),
    "v2": (1108, 910, 810, 1109),
    "v4": (1110,),
}


def layer(args, dp, length, width, n, share):
    rows, full = -(-length // 16) * 16, -(-length // 128) * 128
    cols, blk = n // 2, n // 4
    ring = dp // 2
    far = ring // 2
    depth = share * dp
    heads = width // HEAD_DIM
    a, b = outer(n, 0), outer(n, 1)
    steps = dp.bit_length()
    V, dma = pltpu.VMEM, pltpu.SemaphoreType.DMA
    S = jax.ShapeDtypeStruct
    out = dict(
        w1=S((2, depth, 2 * n), bf16),
        w2=S((2, depth, 2 * n), bf16),
        w3=S((2, depth, 2 * n), bf16),
        mid_o=S((full, width), f32),
        act_o=S((full, 4 * n), bf16),
        slope_o=S((full, 4 * n), bf16),
        bo=S((length, width), bf16),
        gt=S((length, width), f32),
        go=S((3, share, 2 * n), f32),
        gv=S((16, width), f32),
    )
    scratch = dict(
        sh1=V((2, share, n), bf16),
        iwv=V((3, share, cols), bf16),
        owv=V((share, cols), bf16),
        sixv=V((6, 1, share), bf16),
        ubv=V((2 * n // 128, 128), bf16),
        biasf=V((8, cols), f32),
        ibv=V((2, cols), bf16),
        vecf=V((8, 128), f32),
        packv=V((8, cols), bf16),
        tv=V((2, length), jnp.int32),
        row=V((8, full), f32),
        vec=V((8, 128), bf16),
        kb=V((full, 128), bf16),
        rm=V((full, 128), f32),
        vbuf=V((2, 8, width), bf16),
        bbuf=V((2, 8, cols), bf16),
        vecs=V((8, width), f32),
        ub=V((8, cols), f32),
        qb=V((8, 3 * blk), f32),
        xs=V((full, width), bf16),
        gr=V((full, width), bf16),
        ln=V((full, width), bf16),
        qkvm=V((full, 4 * n), bf16),
        logs=V((full, 128), f32),
        lt=V((heads, full), f32),
        mid=V((full, width), f32),
        acc=V((full, width), f32),
        big=V((2 * full, 4 * n), bf16),
        st=V((2, full, cols), bf16),
        turn=V((2, ring, 2, share, full), bf16),
        lhs1=V((ring, share, 2 * full), bf16),
        lhs2=V((ring, share, 2 * full), bf16),
        lhs3=V((ring, share, 2 * full), bf16),
        wt=V((2, depth, 3 * blk), bf16),
        wn=V((2, 2, 256, 2 * n), bf16),
        part=V((4, ring, share, 2 * n), bf16),
        ry=V((4, ring, share, a), bf16),
        rr=V((4, far, share, 2 * n - b), bf16),
        rl=V((4, far, share, 2 * n - b), bf16),
        rb=V((4, share, n - b), bf16),
        og=V((3, share, 2 * n), f32),
        vsum=V((16, width), f32),
        vacc=V((6, 8, width), f32),
        vswap=V((steps, 2, 16, width), f32),
        ring_s=dma((6, 2 * (far + 1))),
        ring_r=dma((6, 2 * (far + 1))),
        y_s=dma((6, 2 * far + 1)),
        y_r=dma((6, 2 * far + 1)),
        c_s=dma((6, 4 * far + 2)),
        c_r=dma((6, 4 * far + 2)),
        k_sem=dma((6,)),
        sy_s=dma((6, ring + 1)),
        sy_r=dma((6, ring + 1)),
        sr_s=dma((6, 2 * far)),
        sr_r=dma((6, 2 * far)),
        v_s=dma((dp,)),
        v_r=dma((dp,)),
        b_s=dma((steps,)),
        b_r=dma((steps,)),
        l_sem=dma((7,)),
        x_sem=dma((6,)),
        s_sem=dma((4, 2)),
        t_sem=dma((4,)),
        t_s=dma((4,)),
        t_r=dma((4,)),
        a_s=dma((8,)),
        a_r=dma((8,)),
        a_sem=dma((2, 8)),
        h_s=dma((8,)),
        h_r=dma((8,)),
        q_s=dma((4,)),
        q_r=dma((4,)),
        clear=pltpu.SemaphoreType.REGULAR,
    )
    names = LAYER_IN + tuple(out) + tuple(scratch)
    hbm = pl.BlockSpec(memory_space=pl.ANY)
    specs = [pl.BlockSpec(memory_space=pltpu.SMEM) if k == "image" else hbm for k in LAYER_IN]
    got = pl.pallas_call(
        functools.partial(layer_kernel, dp, rows, names, LAYER_PLAN),
        out_shape=list(out.values()),
        in_specs=specs,
        out_specs=[hbm] * len(out),
        scratch_shapes=list(scratch.values()),
        compiler_params=pltpu.CompilerParams(collective_id=1, has_side_effects=True, vmem_limit_bytes=VM_LIMIT),
        name="layer",
    )(*args)
    return types.SimpleNamespace(**dict(zip(out, got)))


def place_kernel(bo, gt, go, gv, *refs):
    bo_o, gt_o, iw_o, ow_o, uw_o, dw_o, ib_o, ub_o = refs[:8]
    vec_o, (bov, gtv, g, vs, iwv, owv, ibv, ubv, vecv, sem) = refs[8:14], refs[14:]
    d, t = lax.axis_index("dp"), lax.axis_index("tensor")
    share, wide = g.shape[1:]
    n, blk = wide // 2, wide // 8
    cols = 2 * blk
    ins = [
        pltpu.make_async_copy(go, g, sem.at[0]),
        pltpu.make_async_copy(gt, gtv, sem.at[1]),
        pltpu.make_async_copy(bo, bov, sem.at[2]),
        pltpu.make_async_copy(gv, vs, sem.at[3]),
    ]
    for cp in ins:
        cp.start()
    outs = []

    def send(src, dst):
        cp = pltpu.make_async_copy(src, dst, sem.at[4 + len(outs)])
        cp.start()
        outs.append(cp)

    ins[0].wait()
    send(g.at[1], uw_o)
    send(g.at[0], dw_o)
    for i in (0, 1):
        part = slice(i * blk, (i + 1) * blk)
        for s in range(3):
            at = i * n + s * blk
            iwv[s, :, part] = g[2, :, at : at + blk]
        owv[:, part] = g[2, :, i * n + 3 * blk : (i + 1) * n]
    send(iwv, iw_o)
    send(owv, ow_o)
    ins[1].wait()
    send(gtv, gt_o)
    ins[2].wait()
    send(bov, bo_o)
    ins[3].wait()
    ibv[...] = vs[6:8, pl.ds(pl.multiple_of(t * cols, 128), cols)]
    send(ibv, ib_o)
    width = vs.shape[1]
    per = width // 128
    half = wide // width
    up = jnp.where(t == 0, vs[8 : 8 + half, :], vs[8 + half : 8 + 2 * half, :])
    for r in range(wide // 128):
        lo = (r % per) * 128
        ubv[r : r + 1, :] = up[r // per : r // per + 1, lo : lo + 128]
    send(ubv, ub_o)
    own = vs[0:8, pl.ds(pl.multiple_of((d // 2) * 128, 128), 128)]
    own = jnp.where(d % 2 == 0, own, pltpu.roll(own, share, 1))
    for i in range(6):
        vecv[i] = own[i : i + 1, 0:share]
        send(vecv.at[i], vec_o[i])
    for cp in outs:
        cp.wait()


def place(r, share, n):
    S = jax.ShapeDtypeStruct
    length, width = r.gt.shape
    cols = n // 2
    hbm = pl.BlockSpec(memory_space=pl.ANY)
    out = [
        S((length, width), bf16),
        S((length, width), f32),
        S((3, share, cols), f32),
        S((share, cols), f32),
        S((share, 2 * n), f32),
        S((share, 2 * n), f32),
        S((2, cols), f32),
        S((2 * n // 128, 128), f32),
    ] + [S((1, share), f32)] * 6
    V = pltpu.VMEM
    return pl.pallas_call(
        place_kernel,
        out_shape=out,
        in_specs=[hbm] * 4,
        out_specs=[hbm] * 14,
        scratch_shapes=[
            V((length, width), bf16),
            V((length, width), f32),
            V((3, share, 2 * n), f32),
            V((16, width), f32),
            V((3, share, cols), f32),
            V((share, cols), f32),
            V((2, cols), f32),
            V((2 * n // 128, 128), f32),
            V((6, 1, share), f32),
            pltpu.SemaphoreType.DMA((18,)),
        ],
        compiler_params=pltpu.CompilerParams(vmem_limit_bytes=VM_LIMIT),
        name="place",
    )(r.bo, r.gt, r.go, r.gv)


def paired_device(
    tokens, cotangent, token_valid, image_valid, first_gain, first_shift, input_weight, input_bias, output_weight,
    output_bias, second_gain, second_shift, up_weight, up_bias, down_weight, down_bias,
):
    dp = lax.axis_size("dp")
    length, width = tokens.shape
    share, wide = up_weight.shape
    n = wide // 2
    vectors = (first_gain, first_shift, output_bias, second_gain, second_shift, down_bias)
    args = tuple(v.reshape(1, share) for v in vectors) + (
        up_bias.reshape(-1, 128),
        input_bias,
        input_weight.transpose(1, 0, 2),
        output_weight.T,
        up_weight,
        down_weight.T,
        tokens,
        cotangent,
        token_valid,
        image_valid,
    )
    r = layer(args, dp, length, width, n, share)
    block_out, grad_tokens, g_in, g_out, g_up, g_down, g_in_bias, g_up_bias, *g_vec = place(r, share, n)
    g_vec = [v.reshape(share) for v in g_vec]
    return (
        block_out,
        grad_tokens,
        g_vec[0],
        g_vec[1],
        g_in.transpose(1, 0, 2),
        g_in_bias,
        g_out.T,
        g_vec[2],
        g_vec[3],
        g_vec[4],
        g_up,
        g_up_bias.reshape(wide),
        g_down.T,
        g_vec[5],
    )


def solution(mesh):
    in_specs = (
        P(("dp", "tensor"), None),
        P(("dp", "tensor"), None),
        P("dp", None),
        P("dp"),
        P("dp"),
        P("dp"),
        P("dp", None, "tensor"),
        P(None, "tensor"),
        P("tensor", "dp"),
        P("dp"),
        P("dp"),
        P("dp"),
        P("dp", "tensor"),
        P("tensor"),
        P("tensor", "dp"),
        P("dp"),
    )
    out_specs = (
        P(("dp", "tensor"), None),
        P(("dp", "tensor"), None),
        P("dp"),
        P("dp"),
        P("dp", None, "tensor"),
        P(None, "tensor"),
        P("tensor", "dp"),
        P("dp"),
        P("dp"),
        P("dp"),
        P("dp", "tensor"),
        P("tensor"),
        P("tensor", "dp"),
        P("dp"),
    )
    ready = mesh.shape["tensor"] == 2 and mesh.shape["dp"] == 16
    body = paired_device if ready else general_device
    return jax.shard_map(
        body, mesh=mesh, in_specs=in_specs, out_specs=out_specs, check_vma=False
    )
```

```python
import functools
import types

import jax
import jax.numpy as jnp
from jax import lax
from jax.experimental import pallas as pl
from jax.experimental.pallas import tpu as pltpu
from jax.sharding import PartitionSpec as P

HEAD_DIM = 64
MESH = pl.DeviceIdType.MESH
f32 = jnp.float32
bf16 = jnp.bfloat16
NN, NT, TN = ((1,), (0,)), ((1,), (1,)), ((0,), (0,))
VM_LIMIT = 127 << 19


def layer_norm(inputs, gain, shift):
    center = inputs - jnp.mean(inputs, axis=-1, keepdims=True)
    spread = jnp.mean(center * center, axis=-1, keepdims=True)
    return center * lax.rsqrt(spread + 1e-06) * gain + shift


def norm_backward(inputs, gain, upstream):
    center = inputs - jnp.mean(inputs, axis=-1, keepdims=True)
    spread = jnp.mean(center * center, axis=-1, keepdims=True)
    scaled = lax.rsqrt(spread + 1e-06)
    unit = center * scaled
    weighted = upstream * gain
    grad_inputs = scaled * (
        weighted
        - jnp.mean(weighted, axis=-1, keepdims=True)
        - unit * jnp.mean(weighted * unit, axis=-1, keepdims=True)
    )
    return (grad_inputs, jnp.sum(upstream * unit, axis=0), jnp.sum(upstream, axis=0))


def gelu_slope(hidden):
    return (
        0.5 * (1.0 + lax.erf(hidden * 0.7071067811865476))
        + hidden * jnp.exp(-0.5 * hidden * hidden) * 0.3989422804014327
    )


def general_device(
    tokens,
    cotangent,
    token_valid,
    image_valid,
    first_gain,
    first_shift,
    input_weight,
    input_bias,
    output_weight,
    output_bias,
    second_gain,
    second_shift,
    up_weight,
    up_bias,
    down_weight,
    down_bias,
):
    f32 = jnp.float32
    bf16 = jnp.bfloat16
    gathered = (
        lax.all_gather(first_gain, "dp", axis=0, tiled=True),
        lax.all_gather(first_shift, "dp", axis=0, tiled=True),
        lax.all_gather(input_weight, "dp", axis=0, tiled=True),
        lax.all_gather(output_weight, "dp", axis=1, tiled=True),
        lax.all_gather(output_bias, "dp", axis=0, tiled=True),
        lax.all_gather(second_gain, "dp", axis=0, tiled=True),
        lax.all_gather(second_shift, "dp", axis=0, tiled=True),
        lax.all_gather(up_weight, "dp", axis=0, tiled=True),
        lax.all_gather(down_weight, "dp", axis=1, tiled=True),
        lax.all_gather(down_bias, "dp", axis=0, tiled=True),
    )
    (
        gain_one,
        shift_one,
        in_full,
        out_full,
        out_shift,
        gain_two,
        shift_two,
        up_full,
        down_full,
        down_shift,
    ) = gathered
    gain_one = gain_one.astype(f32)
    shift_one = shift_one.astype(f32)
    out_shift = out_shift.astype(f32)
    gain_two = gain_two.astype(f32)
    shift_two = shift_two.astype(f32)
    down_shift = down_shift.astype(f32)
    tensor_at = lax.axis_index("tensor")
    groups = lax.axis_size("tensor")
    own_rows = tokens.shape[0]
    width = tokens.shape[1]
    length = token_valid.shape[1]
    positions = lax.broadcasted_iota(jnp.int32, token_valid.shape, 1)
    key_ok = (token_valid > 0) | (positions == 0)
    mask_all = (token_valid * image_valid[:, None]).astype(f32).reshape(-1)
    row_mask = lax.dynamic_slice_in_dim(mask_all, tensor_at * own_rows, own_rows)[:, None]
    images = token_valid.shape[0]
    local_width = in_full.shape[2]
    local_heads = local_width // HEAD_DIM
    hidden_width = up_full.shape[1]
    scale = HEAD_DIM ** (-0.5)
    head_shape = (images, length, local_heads, HEAD_DIM)
    inputs = tokens.astype(f32)
    first_own = layer_norm(inputs, gain_one, shift_one).astype(bf16)
    first_all = lax.all_gather(first_own, "tensor", axis=0, tiled=True)
    project = jnp.einsum("rd,dce->rce", first_all, in_full, preferred_element_type=f32)
    bias_in = input_bias.astype(f32)
    queries = (project[:, 0] + bias_in[0]).astype(bf16).reshape(head_shape)
    keyset = project[:, 1].astype(bf16).reshape(head_shape)
    values = (project[:, 2] + bias_in[1]).astype(bf16).reshape(head_shape)

    def scores_of(query_img, key_img, ok_img):
        scores = jnp.einsum("qhe,khe->hqk", query_img, key_img, preferred_element_type=f32) * scale
        return jnp.where(ok_img[None, None, :], scores, -1000000000.0)

    def attend(pieces):
        query_img, key_img, value_img, ok_img = pieces
        scores = scores_of(query_img, key_img, ok_img)
        highest = jnp.max(scores, axis=-1, keepdims=True)
        log_total = highest + jnp.log(jnp.sum(jnp.exp(scores - highest), axis=-1, keepdims=True))
        attn_probs = jnp.exp(scores - log_total).astype(bf16)
        mixed_img = jnp.einsum("hqk,khe->qhe", attn_probs, value_img, preferred_element_type=f32)
        return (mixed_img.astype(bf16), log_total)

    mixed, log_totals = lax.map(attend, (queries, keyset, values, key_ok))
    mixed_rows = mixed.reshape(images * length, local_width)
    attended = lax.psum_scatter(
        jnp.dot(mixed_rows, out_full, preferred_element_type=f32).astype(jnp.bfloat16),
        "tensor",
        scatter_dimension=0,
        tiled=True,
    ).astype(jnp.float32)
    middle = inputs + attended + out_shift
    second_own = layer_norm(middle, gain_two, shift_two).astype(bf16)
    second_all = lax.all_gather(second_own, "tensor", axis=0, tiled=True)
    hidden = jnp.dot(second_all, up_full, preferred_element_type=f32) + up_bias.astype(f32)
    active = jax.nn.gelu(hidden, approximate=False).astype(bf16)
    lifted = lax.psum_scatter(
        jnp.dot(active, down_full, preferred_element_type=f32).astype(jnp.bfloat16),
        "tensor",
        scatter_dimension=0,
        tiled=True,
    ).astype(jnp.float32)
    block_out = (row_mask * (middle + lifted + down_shift)).astype(bf16)
    grad_last = row_mask * cotangent.astype(f32)
    first_all, second_all = (
        lax.all_gather(first_own, "tensor", axis=0, tiled=True),
        lax.all_gather(second_own, "tensor", axis=0, tiled=True),
    )
    grad_lift = lax.all_gather(grad_last.astype(bf16), "tensor", axis=0, tiled=True)
    grad_active = jnp.einsum("rd,fd->rf", grad_lift, down_full, preferred_element_type=f32)
    grad_hidden = (grad_active * gelu_slope(hidden)).astype(bf16)
    grad_down = jnp.einsum("rf,rd->fd", active, grad_lift, preferred_element_type=f32)
    grad_up = jnp.einsum("rd,rf->df", second_all, grad_hidden, preferred_element_type=f32)
    grad_up_bias = jnp.sum(grad_hidden.astype(f32), axis=0)
    grad_second = lax.psum_scatter(
        jnp.einsum("rf,df->rd", grad_hidden, up_full, preferred_element_type=f32).astype(
            jnp.bfloat16
        ),
        "tensor",
        scatter_dimension=0,
        tiled=True,
    ).astype(jnp.float32)
    grad_middle, grad_gain_two, grad_shift_two = norm_backward(middle, gain_two, grad_second)
    grad_middle = grad_middle + grad_last
    grad_mid_all = lax.all_gather(grad_middle.astype(bf16), "tensor", axis=0, tiled=True)
    grad_mixed = jnp.einsum("rd,ed->re", grad_mid_all, out_full, preferred_element_type=f32).astype(
        bf16
    )
    grad_out_weight = jnp.einsum("re,rd->ed", mixed_rows, grad_mid_all, preferred_element_type=f32)

    def attend_back(pieces):
        query_img, key_img, value_img, ok_img, total_img, grad_img = pieces
        scores = scores_of(query_img, key_img, ok_img)
        attn_probs = jnp.exp(scores - total_img)
        grad_values = jnp.einsum(
            "hqk,qhe->khe", attn_probs.astype(bf16), grad_img, preferred_element_type=f32
        )
        grad_probs = jnp.einsum("qhe,khe->hqk", grad_img, value_img, preferred_element_type=f32)
        grad_scores = (
            attn_probs * (grad_probs - jnp.sum(attn_probs * grad_probs, axis=-1, keepdims=True))
        ).astype(bf16)
        grad_queries = (
            jnp.einsum("hqk,khe->qhe", grad_scores, key_img, preferred_element_type=f32) * scale
        )
        grad_keys = (
            jnp.einsum("hqk,qhe->khe", grad_scores, query_img, preferred_element_type=f32) * scale
        )
        return jnp.stack([grad_queries, grad_keys, grad_values], axis=1).astype(bf16)

    grad_project = lax.map(
        attend_back, (queries, keyset, values, key_ok, log_totals, grad_mixed.reshape(head_shape))
    )
    grad_project = grad_project.reshape(images * length, 3, local_width)
    grad_in_weight = jnp.einsum("rd,rce->dce", first_all, grad_project, preferred_element_type=f32)
    grad_in_bias = jnp.sum(grad_project[:, 0::2].astype(f32), axis=0)
    grad_first = lax.psum_scatter(
        jnp.einsum("rce,dce->rd", grad_project, in_full, preferred_element_type=f32).astype(
            jnp.bfloat16
        ),
        "tensor",
        scatter_dimension=0,
        tiled=True,
    ).astype(jnp.float32)
    grad_inputs, grad_gain_one, grad_shift_one = norm_backward(inputs, gain_one, grad_first)
    grad_inputs = grad_inputs + grad_middle
    grad_in_own, grad_out_own, grad_up_own, grad_down_own = (
        lax.psum_scatter(
            grad_in_weight.astype(jnp.bfloat16), "dp", scatter_dimension=0, tiled=True
        ).astype(jnp.float32),
        lax.psum_scatter(
            grad_out_weight.astype(jnp.bfloat16), "dp", scatter_dimension=1, tiled=True
        ).astype(jnp.float32),
        lax.psum_scatter(
            grad_up.astype(jnp.bfloat16), "dp", scatter_dimension=0, tiled=True
        ).astype(jnp.float32),
        lax.psum_scatter(
            grad_down.astype(jnp.bfloat16), "dp", scatter_dimension=1, tiled=True
        ).astype(jnp.float32),
    )
    vectors = jnp.stack(
        [
            grad_gain_one,
            grad_shift_one,
            jnp.sum(grad_middle, axis=0),
            grad_gain_two,
            grad_shift_two,
            jnp.sum(grad_last, axis=0),
        ]
    )
    bias_share = input_bias.shape[1]
    up_share = up_bias.shape[0]
    placed_bias = lax.dynamic_update_slice(
        jnp.zeros((2, width), f32), grad_in_bias, (0, tensor_at * local_width)
    )
    placed_up = lax.dynamic_update_slice(
        jnp.zeros((hidden_width * groups,), f32), grad_up_bias, (tensor_at * hidden_width,)
    )
    vectors, placed_bias, placed_up = lax.psum((vectors, placed_bias, placed_up), ("dp", "tensor"))
    share = first_gain.shape[0]
    dp_at = lax.axis_index("dp")
    vectors = lax.dynamic_slice_in_dim(vectors, dp_at * share, share, 1)
    bias_own = lax.dynamic_slice_in_dim(placed_bias, tensor_at * bias_share, bias_share, 1)
    up_bias_own = lax.dynamic_slice_in_dim(placed_up, tensor_at * up_share, up_share, 0)
    return (
        block_out,
        grad_inputs,
        vectors[0],
        vectors[1],
        grad_in_own,
        bias_own,
        grad_out_own,
        vectors[2],
        vectors[3],
        vectors[4],
        grad_up_own,
        up_bias_own,
        grad_down_own,
        vectors[5],
    )


def mul(a, b, dims):
    return lax.dot_general(a, b, (dims, ((), ())), preferred_element_type=f32)


def iota(shape, axis):
    return lax.broadcasted_iota(jnp.int32, shape, axis)


def tile(j, size):
    return pl.ds(pl.multiple_of(j * size, size), size)


class Place:
    def __init__(self, dp):
        d = lax.axis_index("dp")
        t = lax.axis_index("tensor")
        ring = dp // 2
        self.dp, self.d, self.t, self.ring, self.far = dp, d, t, ring, ring // 2
        self.chip, self.core = d // 2, d % 2
        self.pos = jnp.where(self.chip % 2 == 0, self.chip // 2, ring - 1 - self.chip // 2)
        self.right = (self.chip_at(1) * 2 + self.core, t)
        self.left = (self.chip_at(-1) * 2 + self.core, t)
        self.across = (d, 1 - t)
        self.sibling = (d + 1 - 2 * self.core, t)

    def chip_at(self, offset):
        ring = self.ring
        spot = (self.pos + offset + ring) % ring
        return jnp.where(spot < ring // 2, 2 * spot, 2 * (ring - 1 - spot) + 1)


class Columns:
    def __init__(self, w, n, a):
        t, b = w.t, n - a
        self.n, self.a, self.b = n, a, b
        self.own = (pl.multiple_of(t * n, 128), n)
        self.other = (pl.multiple_of((1 - t) * n, 128), n)
        self.ring = (pl.multiple_of(t * a, 128), 2 * n - a)
        self.mine_a = (pl.multiple_of(t * (2 * n - a), 128), a)
        self.their_a = (pl.multiple_of((1 - t) * (2 * n - a), 128), a)
        self.their_b = (pl.multiple_of(n - t * b, 128), b)
        self.mine_b = (pl.multiple_of(n - (1 - t) * b, 128), b)


OUTER = (4, 3, 2, 5, 4, 5, 4, 4, 4, 4, 5, 3, 4, 4)


def greet(targets):
    bar = pltpu.get_barrier_semaphore()
    for a in targets:
        pl.semaphore_signal(bar, inc=1, device_id=a, device_id_type=MESH)
    pl.semaphore_wait(bar, len(targets))


def rcopy(src, dst, send, recv, dev):
    return pltpu.make_async_remote_copy(
        src_ref=src, dst_ref=dst, send_sem=send, recv_sem=recv, device_id=dev, device_id_type=MESH
    )


class Gather:
    def __init__(self, w, g, shard, full, sems):
        self.w, self.g, self.shard, self.full, self.sems = w, g, shard, full, sems
        self.rows, n = shard.shape
        self.cols = Columns(w, n, 128 * OUTER[g])

    def block(self, offset, cols, span=None):
        w = self.w
        lo, size = span or (0, self.rows)
        base = w.chip_at(offset) * (2 * self.rows) + w.core * self.rows + lo
        return self.full.at[pl.ds(pl.multiple_of(base, 16), size), pl.ds(cols[0], cols[1])]

    def span(self, s, dirn):
        half = self.rows // 2
        return (0, self.rows) if s < self.w.far else (dirn * half, half)

    def off(self, s, dirn):
        return s if dirn else -s

    def make(self, kind, src, dst, k, dev):
        send, recv = self.sems[kind]
        return rcopy(src, dst, send.at[self.g, k], recv.at[self.g, k], dev)

    def y(self, s, dirn):
        if s == 0:
            return self.make("y", self.shard, self.block(0, self.cols.own), 0, self.w.across)
        ref = self.block(self.off(s, dirn), self.cols.mine_a, self.span(s, dirn))
        return self.make("y", ref, ref, 2 * s - 1 + dirn, self.w.across)

    def ring(self, s, dirn, part=0):
        dev = self.w.left if dirn else self.w.right
        k = dirn * (self.w.far + 1)
        if s == 1 and part == 0:
            return self.make("r", self.shard, self.block(0, self.cols.own), k, dev)
        if s == 1:
            ref = self.block(0, self.cols.their_b)
            return self.make("r", ref, ref, k + 1, dev)
        ref = self.block(self.off(s - 1, dirn), self.cols.ring, self.span(s, dirn))
        return self.make("r", ref, ref, k + s, dev)

    def sib(self, k):
        w = self.w
        if k == 0:
            src, dst = self.shard, self.block(0, self.cols.own)
        elif k == 1:
            src = dst = self.block(0, self.cols.other)
        else:
            which, rest = divmod(k - 2, 2 * w.far)
            s, dirn = rest // 2 + 1, rest % 2
            cols = self.cols.their_a if which else self.cols.ring
            src = dst = self.block(self.off(s, dirn), cols, self.span(s, dirn))
        return self.make("c", src, dst, k, w.sibling)

    def keep(self):
        return pltpu.make_async_copy(self.shard, self.block(0, self.cols.own), self.sems["k"].at[self.g])

    def S(self):
        self.y(0, 0).start()
        self.ring(1, 0).start()
        self.ring(1, 1).start()
        self.sib(0).start()
        self.keep().start()

    def Y(self):
        self.y(0, 0).wait_recv()
        self.ring(1, 0, 1).start()
        self.ring(1, 1, 1).start()
        self.sib(1).start()

    def h(self, s):
        for dirn in (0, 1):
            self.ring(s, dirn).wait_recv()
            if s == 1:
                self.ring(s, dirn, 1).wait_recv()
            if s < self.w.far:
                self.ring(s + 1, dirn).start()
            self.y(s, dirn).start()
            self.sib(2 * s + dirn).start()

    def c(self, s):
        for dirn in (0, 1):
            self.y(s, dirn).wait_recv()
            self.sib(2 + 2 * self.w.far + 2 * (s - 1) + dirn).start()

    def events(self):
        h, c = (lambda s: functools.partial(self.h, s)), (lambda s: functools.partial(self.c, s))
        return [self.S, self.Y, h(1), h(2), c(1), h(3), c(2), h(4), c(3), c(4), self.E]

    def E(self):
        for k in range(2 + 4 * self.w.far):
            self.sib(k).wait()
        self.keep().wait()

    def drain(self):
        far = self.w.far
        self.y(0, 0).wait_send()
        for dirn in (0, 1):
            self.ring(1, dirn).wait_send()
            self.ring(1, dirn, 1).wait_send()
            for s in range(1, far + 1):
                self.y(s, dirn).wait_send()
                if s > 1:
                    self.ring(s, dirn).wait_send()


class Scatter:
    def __init__(self, w, g, part, ry, rr, rl, rb, out, sems):
        self.w, self.g, self.part, self.sems, self.out = w, g, part, sems, out
        self.rows, n = part.shape[1], part.shape[2] // 2
        self.cols = c = Columns(w, n, 128 * OUTER[7 + g])
        self.ry = ry.at[:, :, pl.ds(0, c.a)]
        self.rr = rr.at[:, :, pl.ds(0, 2 * n - c.a)]
        self.rl = rl.at[:, :, pl.ds(0, 2 * n - c.a)]
        self.rb = rb.at[:, pl.ds(0, c.b)]
        far = w.far
        self.order = [far] + [k * sign for k in range(far - 1, 0, -1) for sign in (1, -1)] + [0]

    def make(self, kind, src, dst, k, dev):
        send, recv = self.sems[kind]
        return rcopy(src, dst, send.at[self.g, k], recv.at[self.g, k], dev)

    def cross(self, k):
        w = self.w
        chip = w.chip_at(k)
        src = self.part.at[chip, :, pl.ds(*self.cols.their_a)]
        return self.make("y", src, self.ry.at[chip], self.order.index(k), w.across)

    def ring(self, s, dirn):
        w = self.w
        chip = w.chip_at(s - w.far if dirn else w.far - s)
        half = self.rows // 2
        span = pl.ds(dirn * half, half) if s == 0 else pl.ds(0, self.rows)
        src = self.part.at[chip, span, pl.ds(*self.cols.ring)]
        dst = (self.rl if dirn else self.rr).at[s, span]
        return self.make("r", src, dst, dirn * w.far + s, w.left if dirn else w.right)

    def swap(self):
        w = self.w
        src = self.part.at[w.chip_at(0), :, pl.ds(*self.cols.their_b)]
        return self.make("y", src, self.rb, len(self.order), w.across)

    def add(self, k, lo, size, cols, other):
        chip = self.w.chip_at(k)
        part = self.part
        ch = 16

        @pl.loop(0, size // ch)
        def _(r):
            rs = pl.ds(pl.multiple_of(lo + r * ch, ch), ch)
            cs = pl.ds(cols[0], cols[1])
            part[chip, rs, cs] = (part[chip, rs, cs].astype(f32) + other[rs, :].astype(f32)).astype(bf16)

    def events(self):
        s, t = (lambda k: functools.partial(self.s, k)), (lambda k: functools.partial(self.t, k))
        return [self.A, self.L, t(3), s(1), t(2), s(2), t(1), s(3), t(0), self.F, self.Z]

    def both(self, k):
        return (k, -k) if k else (0,)

    def A(self):
        for k in (self.w.far, self.w.far - 1, 1 - self.w.far):
            self.cross(k).start()

    def take(self, k):
        self.cross(k).wait_recv()
        self.add(k, 0, self.rows, self.cols.mine_a, self.ry.at[self.w.chip_at(k)])

    def L(self):
        self.cross(self.w.far).wait_recv()
        for k in self.both(self.w.far - 2):
            self.cross(k).start()
        self.add(self.w.far, 0, self.rows, self.cols.mine_a, self.ry.at[self.w.chip_at(self.w.far)])
        self.ring(0, 0).start()
        self.ring(0, 1).start()

    def t(self, k):
        for i in self.both(k):
            self.take(i)
        if k > 1:
            for i in self.both(k - 2):
                self.cross(i).start()

    def s(self, s):
        far, half = self.w.far, self.rows // 2
        for dirn in (0, 1):
            self.ring(s - 1, dirn).wait_recv()
            k = s - far if dirn else far - s
            got = (self.rl if dirn else self.rr).at[s - 1]
            lo, size = (dirn * half, half) if s == 1 else (0, self.rows)
            self.add(k, lo, size, self.cols.ring, got)
            self.ring(s, dirn).start()

    def F(self):
        far = self.w.far
        for dirn in (0, 1):
            self.ring(far - 1, dirn).wait_recv()
            self.add(0, 0, self.rows, self.cols.ring, (self.rl if dirn else self.rr).at[far - 1])
        self.swap().start()

    def Z(self):
        self.swap().wait_recv()
        self.add(0, 0, self.rows, self.cols.mine_b, self.rb)
        chip = self.w.chip_at(0)
        self.out[...] = self.part[chip, :, pl.ds(*self.cols.own)].astype(f32)

    def drain(self):
        for k in self.order:
            self.cross(k).wait_send()
        for s in range(self.w.far):
            self.ring(s, 0).wait_send()
            self.ring(s, 1).wait_send()
        self.swap().wait_send()


class Plan:
    def __init__(self, groups, table):
        self.events, self.table = [g.events() for g in groups], table

    def after(self, name):
        for code in self.table.get(name, ()):
            self.events[code // 100][code % 100]()

    def tick(self, j, name, first, count):
        for k in range(count):
            at = name + str(first + k)
            if at in self.table:

                @pl.when(j == k)
                def _(at=at):
                    self.after(at)


def stream(count, parts, sem, body, begun=False):
    def copies(j):
        slot = lax.rem(j, 2)
        return [pltpu.make_async_copy(src(j), dst(slot), sem.at[i, slot]) for i, (src, dst) in enumerate(parts)]

    def begin():
        for cp in copies(jnp.int32(0)):
            cp.start()

    def run():
        @pl.loop(0, count)
        def _(j):
            @pl.when(j + 1 < count)
            def _():
                for cp in copies(j + 1):
                    cp.start()

            for cp in copies(j):
                cp.wait()
            body(j, lax.rem(j, 2))

    return begin, run


def normalize(x):
    center = x - jnp.mean(x, axis=-1, keepdims=True)
    scaled = lax.rsqrt(jnp.mean(center * center, axis=-1, keepdims=True) + 1e-06)
    return center * scaled, scaled


def lanes_of(pair, blk):
    base = (pair // 2) * (4 * blk) + (pair % 2) * 128
    return [pl.ds(pl.multiple_of(base + s * blk, 128), 128) for s in range(4)]


def attend_pair(m, i, rows, full, blk):
    qs, ks, vs, ms = lanes_of(i, blk)
    q2, k2, v2 = m.qkvm[0:rows, qs], m.qkvm[:, ks], m.qkvm[:, vs]
    lq, lk = iota((rows, 128), 1), iota((full, 128), 1)
    outs = []
    logs = m.logs[0:rows, :]
    for h in (0, 1):
        spare = 64 * (1 - h)
        own_q = (lq < 64) if h == 0 else (lq >= 64)
        own_k = (lk < 64) if h == 0 else (lk >= 64)
        qh = jnp.where(own_q, q2, jnp.where(lq == spare, 1.0, 0.0).astype(bf16))
        kh = jnp.where(lk == spare, m.kb[...], k2)
        scores = mul(qh, kh, NT)
        top = jnp.max(scores, axis=1, keepdims=True)
        probs = jnp.exp(scores - top).astype(bf16)
        out = mul(probs, jnp.where(own_k, v2, jnp.ones_like(v2)), NN)
        turned = pltpu.roll(out, 64, 1)
        outs.append(out / turned)
        total = jnp.where(own_q, turned, out)
        logs = jnp.where(lq == 2 * i + h, top + jnp.log(total), logs)
    m.logs[0:rows, :] = logs
    m.qkvm[0:rows, ms] = jnp.where(lq < 64, outs[0], outs[1]).astype(bf16)


def attend_back(m, i, rows, full, blk):
    qs, ks, vs, ms = lanes_of(i, blk)
    q2, do2 = m.qkvm[:, qs], m.ln[:, tile(i, 128)]
    k2, v2 = m.qkvm[0:rows, ks], m.qkvm[0:rows, vs]
    lq, lk = iota((full, 128), 1), iota((rows, 128), 1)
    both = (do2.astype(f32) * m.qkvm[:, ms].astype(f32)).T
    dqs, dks, dvs = [], [], []
    for h in (0, 1):
        spare = 64 * (1 - h)
        own_q = (lq < 64) if h == 0 else (lq >= 64)
        own_k = (lk < 64) if h == 0 else (lk >= 64)
        qh = jnp.where(own_q, q2, jnp.where(lq == spare, 1.0, 0.0).astype(bf16))
        kh = jnp.where(lk == spare, m.kb[0:rows, :], k2)
        probs = jnp.exp(mul(kh, qh, NT) - m.lt[pl.ds(2 * i + h, 1), :])
        dvs.append(mul(probs.astype(bf16), do2, NN))
        dprobs = mul(jnp.where(own_k, v2, jnp.zeros_like(v2)), do2, NT)
        inner = jnp.sum(both[64 * h : 64 * h + 64, :], axis=0, keepdims=True)
        ds = (probs * (dprobs - inner)).astype(bf16)
        dks.append(mul(ds, q2, NN))
        dqs.append(mul(ds, k2, TN))
    dv = jnp.where(lk < 64, dvs[0], dvs[1]).astype(bf16)
    dk = jnp.where(lk < 64, dks[0], dks[1]).astype(bf16)
    dq = (jnp.where(lq < 64, dqs[0], dqs[1]) * HEAD_DIM**-0.5).astype(bf16)
    m.big[0:full, qs] = dq
    m.big[0:rows, ks] = dk
    m.big[0:rows, vs] = dv
    at = ((i // 2) % 2) * (2 * blk) + (i // 4) * blk + (i % 2) * 128
    ns = pl.ds(pl.multiple_of(at, 128), 128)
    m.vsum[6:7, ns] = jnp.sum(dq.astype(f32), axis=0, keepdims=True)
    m.vsum[7:8, ns] = jnp.sum(dv.astype(f32), axis=0, keepdims=True)


LAYER_IN = ("v0", "v1", "v2", "v3", "v4", "v5", "ubias", "ibias", "iw", "ow", "uw", "dw", "tok", "cot", "valid", "image")


def layer_kernel(dp, rows, names, table, *refs):
    m = types.SimpleNamespace(**dict(zip(names, refs)))
    n = m.uw.shape[1] // 2
    w = Place(dp)
    length, width = m.tok.shape
    full = m.qkvm.shape[0]
    share = m.sh1.shape[1]
    cols, blk = n // 2, n // 4
    ch = 128
    sems = {"r": (m.ring_s, m.ring_r), "y": (m.y_s, m.y_r), "c": (m.c_s, m.c_r), "k": m.k_sem}
    groups = [Gather(w, i, m.sh1.at[i], m.w1.at[i], sems) for i in (0, 1)]
    groups.append(Gather(w, 2, m.ow, m.wo, sems))
    groups += [Gather(w, 3 + i, m.uw.at[:, pl.ds(i * n, n)], m.w2.at[i], sems) for i in (0, 1)]
    groups += [Gather(w, 5 + i, m.dw.at[:, pl.ds(i * n, n)], m.w3.at[i], sems) for i in (0, 1)]
    sums = {"y": (m.sy_s, m.sy_r), "r": (m.sr_s, m.sr_r)}
    slots = [tuple(ref.at[i] for ref in (m.part, m.ry, m.rr, m.rl, m.rb)) for i in range(4)]
    slots.append((m.part5, m.ry5, m.rr5, m.rl5, m.rb5))
    wide = (n, n, n, n, 2 * blk, 3 * blk, 3 * blk)
    lefts = (0, n, 0, n, 6 * blk, 0, 3 * blk)
    for g in range(7):
        part, *rest = slots[(0, 1, 2, 3, 0, 1, 4)[g]]
        part = part.at[:, :, pl.ds(0, 2 * wide[g])]
        where = m.og.at[(0, 0, 1, 1, 2, 2, 2)[g], :, pl.ds(lefts[g], wide[g])]
        groups.append(Scatter(w, g, part, *rest, where, sums))
    plan = Plan(groups, table)
    gathers, sums7 = groups[:7], groups[7:]

    def flip(k):
        return (w.d + k - 2 * k * ((w.d // k) % 2), w.t)

    flips = [w.across]
    k = 1
    while k < dp:
        flips.append(flip(k))
        k *= 2

    loads = [
        pltpu.make_async_copy(src, dst, m.l_sem.at[i])
        for i, (src, dst) in enumerate(
            (
                (m.iw, m.iwv),
                (m.ubias, m.ubv),
                (m.ibias, m.ibv),
                (m.tok, m.xs.at[pl.ds(0, length)]),
                (m.cot, m.gr.at[pl.ds(0, length)]),
                (m.valid, m.tv),
            )
        )
    ]
    loads += [
        pltpu.make_async_copy(src, m.sixv.at[i], m.x_sem.at[i])
        for i, src in enumerate((m.v0, m.v1, m.v2, m.v3, m.v4, m.v5))
    ]
    for cp in loads:
        cp.start()
    peers = [(lax.rem(w.d + i, dp), w.t) for i in range(1, dp)] + [w.across]
    bar = pltpu.get_barrier_semaphore()
    for a in peers:
        pl.semaphore_signal(bar, inc=1, device_id=a, device_id_type=MESH)
    loads[0].wait()
    for i in (0, 1):
        part = slice(i * blk, (i + 1) * blk)
        for s in range(3):
            m.sh1[i, :, s * blk : (s + 1) * blk] = m.iwv[s, :, part]
    pl.semaphore_wait(bar, len(peers))
    plan.after("go")
    for cp in loads[1:3] + loads[6:]:
        cp.wait()
    spot = pl.ds(pl.multiple_of(w.chip * 128, 128), 128)
    m.vecf[...] = jnp.zeros((8, 128), f32)
    for i in range(6):
        m.vecf[i : i + 1, 0:share] = m.sixv[i].astype(f32)
    vec = m.vecf[...]
    vec = jnp.where(w.core == 0, vec, pltpu.roll(vec, share, 1))
    m.biasf[...] = jnp.zeros(m.biasf.shape, f32)
    ub = m.ubv[...].astype(f32)
    for r in range(4 * cols // 128):
        q = r * 128 // cols
        lo = r * 128 - q * cols
        m.biasf[q : q + 1, lo : lo + 128] = ub[r : r + 1, :]
    m.biasf[4:6, :] = m.ibv[...].astype(f32)
    m.packv[...] = m.biasf[...].astype(bf16)
    m.vec[...] = vec.astype(bf16)

    def vec_copy(i):
        return rcopy(m.vec, m.vbuf.at[w.core, :, spot], m.v_s.at[i], m.v_r.at[i], peers[i])

    bias_copy = rcopy(m.packv, m.bbuf.at[w.t], m.v_s.at[dp - 1], m.v_r.at[dp - 1], w.across)
    for i in range(dp - 1):
        vec_copy(i).start()
    bias_copy.start()
    m.vbuf[w.core, :, spot] = m.vec[...]
    m.bbuf[w.t] = m.packv[...]
    plan.after("pre0")
    zero_rows = pl.ds(rows, full - rows)
    m.qkvm[zero_rows, :] = jnp.zeros((full - rows, 4 * n), bf16)
    m.big[zero_rows, :] = jnp.zeros((full - rows, 4 * n), bf16)
    m.acc[zero_rows, :] = jnp.zeros((full - rows, width), f32)
    m.mid[zero_rows, :] = jnp.zeros((full - rows, width), f32)
    m.logs = m.acc.at[:, pl.ds(0, 128)]
    m.logs[0:rows, :] = jnp.zeros((rows, 128), f32)
    m.vsum[...] = jnp.zeros(m.vsum.shape, f32)
    m.vacc[...] = jnp.zeros(m.vacc.shape, f32)
    for cp in loads[3:6]:
        cp.wait()
    tail = pl.ds(length, full - length)
    m.xs[tail, :] = jnp.zeros((full - length, width), bf16)
    m.gr[tail, :] = jnp.zeros((full - length, width), bf16)
    m.row[...] = jnp.zeros(m.row.shape, f32)
    m.row[0:1, 0:length] = m.tv[pl.ds(w.t, 1), :].astype(f32)
    ok = jnp.broadcast_to(m.row[0:1, :], (128, full)).T
    m.rm[...] = (ok * m.image[w.t].astype(f32)).astype(bf16)
    m.kb[...] = jnp.where((ok > 0) | (iota((full, 128), 0) == 0), 0.0, -1e9).astype(bf16)
    for i in range(dp - 1):
        vec_copy(i).wait()
    bias_copy.wait()
    m.vecs[...] = m.vbuf[0].astype(f32) + m.vbuf[1].astype(f32)
    m.qb[...] = jnp.zeros(m.qb.shape, f32)
    for side in (0, 1):
        b = m.bbuf[side].astype(f32)
        for r in range(4):
            at = (r // 2) * 4 + side * 2 + r % 2
            m.ub[at : at + 1, :] = b[r : r + 1]
        for i in (0, 1):
            at = 2 * i + side
            m.qb[at : at + 1, 0:blk] = b[4:5, i * blk : (i + 1) * blk]
            m.qb[at : at + 1, 2 * blk : 3 * blk] = b[5:6, i * blk : (i + 1) * blk]

    @pl.loop(0, full // ch)
    def _(r):
        rs = tile(r, ch)
        unit, _ = normalize(m.xs[rs, :].astype(f32))
        m.ln[rs, :] = (unit * m.vecs[0:1, :] + m.vecs[1:2, :]).astype(bf16)
        m.gr[rs, :] = (m.gr[rs, :].astype(f32) * m.rm[rs, 0:1].astype(f32)).astype(bf16)

    plan.after("pre1")

    def turn_copies(k):
        tt, lhs = m.turn, (m.lhs1, m.lhs3, m.lhs2, m.lhs3)[k]
        keep = pltpu.make_async_copy(tt.at[:, w.core], lhs.at[:, :, pl.ds(0, full)], m.t_sem.at[k])
        give = rcopy(
            tt.at[:, 1 - w.core], lhs.at[:, :, pl.ds(full, full)], m.t_s.at[k], m.t_r.at[k], w.sibling
        )
        return keep, give

    def turn(src, k):
        @pl.loop(0, width // 256)
        def _(j):
            m.turn[tile(j, 2)] = src[:, tile(j, 256)].T.reshape(2, 2, share, full)

        for cp in turn_copies(k):
            cp.start()

    def turned(k):
        for cp in turn_copies(k):
            cp.wait()

    turn(m.ln, 0)
    plan.after("pre2")
    turned(0)
    turn(m.gr, 1)
    plan.after("pre3")

    def at_cols(j, lo, size):
        return pl.ds(pl.multiple_of(j * n + lo, 128), size)

    def qkv_stream(i):
        def body(j, slot):
            p = mul(m.ln[0:rows, :], m.wt[slot], NN) + m.qb[pl.ds(2 * i + j, 1), :]
            p = p.astype(bf16).astype(f32)
            p = jnp.where(iota(p.shape, 1) < blk, p * HEAD_DIM**-0.5, p)
            m.qkvm[0:rows, at_cols(2 * i + j, 0, 3 * blk)] = p.astype(bf16)
            plan.tick(j, "qk", 2 * i, 2)

        src = lambda j: m.w1.at[i, :, tile(j, 3 * blk)]
        return stream(2, [(src, lambda slot: m.wt.at[slot])], m.s_sem, body)

    for i in (0, 1):
        begin, run = qkv_stream(i)
        begin()
        run()

        @pl.loop(0, 4)
        def _(j, i=i):
            attend_pair(m, 4 * i + j, rows, full, blk)
            plan.tick(j, "at", 4 * i, 4)

    def w_stream(ref, body):
        src = lambda j: ref.at[:, tile(j, 256), :]
        dst = lambda slot: m.wn.at[slot, :, :, pl.ds(0, ref.shape[2])]
        return stream(width // 256, [(src, dst)], m.s_sem, body)

    def out_cols(k):
        return (k % 2) * (2 * blk) + (k // 2) * blk

    def out_tile(j, slot):
        ds = tile(j, 256)
        total = m.xs[0:rows, ds].astype(f32) + m.vecs[2:3, ds]
        for k in range(4):
            own = m.qkvm[0:rows, k * n + 3 * blk : (k + 1) * n]
            total += mul(own, m.wn[slot, 0, :, out_cols(k) : out_cols(k) + blk], NT)
        m.mid[0:rows, ds] = total
        plan.tick(j, "out", 0, 4)

    out_src = lambda j: m.wo.at[tile(j, 256), :]
    out_dst = lambda slot: m.wn.at[slot, 0, :, pl.ds(0, 4 * blk)]
    begin, run = stream(width // 256, [(out_src, out_dst)], m.s_sem, out_tile)
    begin()
    m.lt[...] = m.logs[...].T[0 : m.lt.shape[0], :]
    run()
    mid_out = pltpu.make_async_copy(m.mid, m.mid_o, m.l_sem.at[0])
    mid_out.start()

    @pl.loop(0, full // ch)
    def _(r):
        rs = tile(r, ch)
        unit, _ = normalize(m.mid[rs, :])
        m.ln[rs, :] = (unit * m.vecs[3:4, :] + m.vecs[4:5, :]).astype(bf16)

    plan.after("ln2")
    turned(1)
    turn(m.ln, 2)
    plan.after("turn")

    def halves(ref, cs):
        return ref.at[pl.ds(0, full), cs], ref.at[pl.ds(full, full), cs]

    def act_copy(j):
        here, there = halves(m.big, tile(j, cols))
        return rcopy(here, there, m.a_s.at[j], m.a_r.at[j], w.sibling)

    def act_save(j):
        cs = tile(j, cols)
        return pltpu.make_async_copy(m.big.at[pl.ds(0, full), cs], m.act_o.at[:, cs], m.a_sem.at[0, j])

    def slope_save(j):
        return pltpu.make_async_copy(m.st.at[j % 2], m.slope_o.at[:, tile(j, cols)], m.a_sem.at[1, j])

    def up_stream(i):
        def body(j, slot):
            k = 4 * i + j
            cs = tile(k, cols)
            hidden = mul(m.ln[0:rows, :], m.wt[slot, :, 0:cols], NN) + m.ub[pl.ds(k, 1), :]
            phi = 0.5 * (1.0 + lax.erf(hidden * 0.7071067811865476))
            m.big[0:rows, cs] = (hidden * phi).astype(bf16)
            slope = phi + hidden * jnp.exp(-0.5 * hidden * hidden) * 0.3989422804014327

            @pl.when(k >= 2)
            def _():
                slope_save(k - 2).wait()

            m.st[k % 2, 0:rows, :] = slope.astype(bf16)
            for cp in (act_copy(k), act_save(k), slope_save(k)):
                cp.start()
            plan.tick(j, "up", 4 * i, 4)

        src = lambda j: m.w2.at[i, :, tile(j, cols)]
        return stream(4, [(src, lambda slot: m.wt.at[slot, :, pl.ds(0, cols)])], m.s_sem, body)

    def product(lhs, src):
        return mul(lhs[...].reshape(w.ring * share, 2 * full), m.big[:, src], NN).astype(bf16)

    m.st[:, zero_rows, :] = jnp.zeros((2, full - rows, cols), bf16)
    for i in (0, 1):
        begin, run = up_stream(i)
        begin()
        run()
        @pl.loop(0, 2)
        def _(j, i=i):
            for k in (0, 1):
                act_copy(4 * i + 2 * j + k).wait()
            m.part[i, :, :, tile(j, n)] = product(m.lhs3, tile(2 * i + j, n)).reshape(w.ring, share, n)
            plan.tick(j, "gw", 2 * i, 2)

    pl.semaphore_signal(m.clear, inc=1, device_id=w.sibling, device_id_type=MESH)

    def dh_copy(j):
        here, there = halves(m.big, tile(j, cols))
        return rcopy(here, there, m.h_s.at[j], m.h_r.at[j], w.sibling)

    def dh_stream(i):
        def body(j, slot):
            k = 4 * i + j
            d = mul(m.gr[0:rows, :], m.wt[slot, :, 0:cols], NN) * m.st[slot, 0:rows, :].astype(f32)
            d = d.astype(bf16)
            m.big[0:rows, tile(k, cols)] = d
            nat = (j // 2) * 4 + i * 2 + j % 2
            m.vsum[pl.ds(8 + nat // 2, 1), tile(nat % 2, cols)] = jnp.sum(d.astype(f32), axis=0, keepdims=True)
            dh_copy(k).start()
            plan.tick(j, "dh", 4 * i, 4)

        return stream(
            4,
            [
                (lambda j: m.w3.at[i, :, tile(j, cols)], lambda slot: m.wt.at[slot, :, pl.ds(0, cols)]),
                (lambda j: m.slope_o.at[:, tile(4 * i + j, cols)], lambda slot: m.st.at[slot]),
            ],
            m.s_sem,
            body,
        )

    for k in (6, 7):
        slope_save(jnp.int32(k)).wait()

    @pl.loop(0, 8)
    def _(j):
        act_save(j).wait()

    m.ln[zero_rows, :] = jnp.zeros((full - rows, width), bf16)
    pl.semaphore_wait(m.clear, 1)
    turned(2)

    def second_tile(j, slot):
        ds = tile(j, 256)
        m.acc[0:rows, ds] = mul(m.big[0:rows, 0 : 2 * n], m.wn[slot, 0], NT) + mul(
            m.big[0:rows, 2 * n :], m.wn[slot, 1], NT
        )
        plan.tick(j, "ds", 0, 4)

    for i in (0, 1):
        begin, run = dh_stream(i)
        begin()
        run()
        if i:
            begin, run = w_stream(m.w2, second_tile)
            begin()

        @pl.loop(0, 2)
        def _(j, i=i):
            for k in (0, 1):
                dh_copy(4 * i + 2 * j + k).wait()
            m.part[2 + i, :, :, tile(j, n)] = product(m.lhs2, tile(2 * i + j, n)).reshape(w.ring, share, n)
            plan.tick(j, "gu", 2 * i, 2)

    run()

    def mixed_tile(j, slot):
        m.ln[0:rows, tile(j, blk)] = mul(m.gr[0:rows, :], m.wt[slot, :, 0:blk], NN).astype(bf16)
        plan.tick(j, "mx", 0, 4)

    begin, run = stream(
        4,
        [(lambda j: m.wo.at[:, pl.ds(pl.multiple_of(out_cols(j), 128), blk)], lambda slot: m.wt.at[slot, :, pl.ds(0, blk)])],
        m.s_sem,
        mixed_tile,
    )
    begin()
    mid_out.wait()

    def fold(k, x):
        m.vacc[k] += jnp.sum(x.reshape(ch // 8, 8, width), axis=0)

    def norm_back(unit, scaled, gain, up):
        weighted = up * gain
        return scaled * (
            weighted
            - jnp.mean(weighted, axis=-1, keepdims=True)
            - unit * jnp.mean(weighted * unit, axis=-1, keepdims=True)
        )

    @pl.loop(0, full // ch)
    def _(r):
        rs = tile(r, ch)
        unit, scaled = normalize(m.mid[rs, :])
        up = m.acc[rs, :]
        grad = m.gr[rs, :].astype(f32)
        down = norm_back(unit, scaled, m.vecs[3:4, :], up) + grad
        m.mid[rs, :] = down
        m.gr[rs, :] = down.astype(bf16)
        fold(2, down)
        fold(3, up * unit)
        fold(4, up)
        fold(5, grad)

    plan.after("nb")
    turn(m.gr, 3)
    plan.after("tb")
    run()

    def lanes_mixed(k):
        return pl.ds(k * n + 3 * blk, blk)

    for k in range(4):
        m.big[0:full, lanes_mixed(k)] = m.qkvm[:, lanes_mixed(k)]
    turned(3)

    def mixed_copy(k):
        here, there = halves(m.big, lanes_mixed(k))
        return rcopy(here, there, m.x_s.at[k], m.x_r.at[k], w.sibling)

    for k in range(4):
        mixed_copy(k).start()

    def q_copy(k):
        here, there = halves(m.big, at_cols(k, 0, 3 * blk))
        return rcopy(here, there, m.q_s.at[k], m.q_r.at[k], w.sibling)

    def attention(first, count):
        @pl.loop(0, count)
        def _(j):
            attend_back(m, first + j, rows, full, blk)

            @pl.when((first + j) % 2 == 1)
            def _():
                q_copy((first + j) // 2).start()

            plan.tick(j, "ab", first, count)

    def weights(i, part):
        @pl.loop(0, 2)
        def _(j):
            k = 2 * i + j
            q_copy(k).wait()
            grad = product(m.lhs1, at_cols(k, 0, 3 * blk))
            part[:, :, tile(j, 3 * blk)] = grad.reshape(w.ring, share, 3 * blk)
            plan.tick(j, "ga", 2 * i, 2)

    attention(0, 2)
    sums7[0].drain()
    for k in range(4):
        mixed_copy(k).wait()
        grad = product(m.lhs3, lanes_mixed(k))
        m.part[0, :, :, out_cols(k) : out_cols(k) + blk] = grad.reshape(w.ring, share, blk)
    plan.after("og")
    attention(2, 3)
    sums7[1].drain()
    weights(0, m.part.at[1])
    attention(5, 3)

    def first_tile(j, slot):
        total = jnp.zeros((rows, 256), f32)
        for k in range(4):
            lo = (k % 2) * (3 * blk)
            total += mul(m.big[0:rows, k * n : k * n + 3 * blk], m.wn[slot, k // 2, :, lo : lo + 3 * blk], NT)
        m.acc[0:rows, tile(j, 256)] = total
        plan.tick(j, "df", 0, 4)

    begin, run = w_stream(m.w1, first_tile)
    begin()
    weights(1, m.part5)
    act_in = pltpu.make_async_copy(m.act_o, m.big.at[pl.ds(full, full)], m.l_sem.at[1])
    act_in.start()
    run()

    def block_tile(j, slot):
        ds = tile(j, 256)
        act = m.big.at[pl.ds(full, rows)]
        m.acc[0:rows, ds] = mul(act[:, 0 : 2 * n], m.wn[slot, 0], NT) + mul(act[:, 2 * n :], m.wn[slot, 1], NT)
        plan.tick(j, "bo", 0, 4)

    begin, run = w_stream(m.w3, block_tile)
    begin()

    @pl.loop(0, full // ch)
    def _(r):
        rs = tile(r, ch)
        unit, scaled = normalize(m.xs[rs, :].astype(f32))
        up = m.acc[rs, :]
        m.mid[rs, :] += norm_back(unit, scaled, m.vecs[0:1, :], up)
        fold(0, up * unit)
        fold(1, up)

    m.vsum[0:6, :] = jnp.sum(m.vacc[...], axis=1)
    gt_out = pltpu.make_async_copy(m.mid.at[pl.ds(0, length)], m.gt, m.l_sem.at[3])
    gt_out.start()

    def sum_copy(s):
        return rcopy(m.vsum, m.vswap.at[s], m.b_s.at[s], m.b_r.at[s], flips[s])

    def sum_step(s):
        if s:
            sum_copy(s - 1).wait()
            m.vsum[...] += m.vswap[s - 1]
        if s < len(flips):
            sum_copy(s).start()

    sum_step(0)
    plan.after("ln1")
    act_in.wait()
    run()
    sum_step(1)
    plan.after("v1")
    gt_out.wait()
    mid_in = pltpu.make_async_copy(m.mid_o, m.mid, m.l_sem.at[4])
    mid_in.start()
    sum_step(2)
    plan.after("v2")
    mid_in.wait()

    @pl.loop(0, full // ch)
    def _(r):
        rs = tile(r, ch)
        m.xs[rs, :] = (m.rm[rs, 0:1].astype(f32) * (m.mid[rs, :] + m.acc[rs, :] + m.vecs[5:6, :])).astype(bf16)

    bo_out = pltpu.make_async_copy(m.xs.at[pl.ds(0, length)], m.bo, m.l_sem.at[0])
    bo_out.start()
    sum_step(3)
    plan.after("v3")
    sum_step(4)
    plan.after("v4")
    sum_step(5)
    outs = [
        pltpu.make_async_copy(m.vsum, m.gv, m.l_sem.at[1]),
        pltpu.make_async_copy(m.og, m.go, m.l_sem.at[2]),
    ]
    outs[0].start()
    plan.after("fin")
    outs[1].start()
    for g in gathers + sums7[2:]:
        g.drain()
    bo_out.wait()
    for cp in outs:
        cp.wait()


LAYER_PLAN = {
    "go": (200, 0),
    "pre0": (100, 1, 201, 300, 2),
    "pre1": (101, 3),
    "pre2": (102, 5, 4, 202, 6, 103, 7, 301, 203),
    "pre3": (104, 400, 204, 8, 9, 105, 10, 106, 302, 206),
    "at0": (108, 401, 107, 205, 600),
    "at1": (109,),
    "at2": (303,),
    "at3": (402, 110),
    "qk2": (208, 207, 500),
    "qk3": (209, 305),
    "at5": (501, 403),
    "at6": (304, 307),
    "at7": (502, 404, 406, 601, 306, 308, 309, 405, 210),
    "out3": (310, 503),
    "turn": (602,),
    "up0": (407,),
    "up2": (505,),
    "gw0": (603, 504, 408, 409, 507),
    "gw1": (700, 410),
    "up5": (506, 508, 605),
    "up6": (509, 701),
    "gw3": (800, 702, 604, 606, 703, 607, 510),
    "dh1": (801,),
    "dh3": (704, 705),
    "gu0": (802, 803, 608, 609),
    "gu1": (610, 706, 707, 900, 804),
    "gu2": (901, 806),
    "gu3": (902,),
    "ds0": (1000, 708, 709, 903),
    "ds3": (1001, 805),
    "tb": (808, 1002, 1003, 904, 905, 906, 710),
    "ab1": (807, 1004),
    "og": (1100, 907),
    "ab2": (1006, 1101, 809),
    "ab3": (1005,),
    "ab4": (810,),
    "ga1": (1200, 1102, 1104, 1103, 1007),
    "ab6": (1201, 908),
    "ab7": (1008, 1202, 1203),
    "ga3": (1300, 1105),
    "df0": (1204, 1205),
    "df1": (909, 1301, 1009, 1106, 1206, 1107),
    "df3": (1302, 1303),
    "bo0": (1304, 1305, 1207),
    "bo1": (1108,),
    "bo3": (1306, 1307, 1308, 1109, 910),
    "v3": (1208, 1209),
    "v4": (1309, 1210, 1010, 1110, 1310),
}


def layer(args, dp, length, width, n, share):
    rows, full = -(-length // 16) * 16, -(-length // 128) * 128
    cols, blk = n // 2, n // 4
    ring = dp // 2
    far = ring // 2
    depth = share * dp
    heads = width // HEAD_DIM
    outers = [128 * o for o in OUTER[7:]]
    a, b = max(outers[:4]), min(outers[:4])
    a5, b5 = outers[6], 3 * blk - outers[6]
    steps = dp.bit_length()
    V, dma = pltpu.VMEM, pltpu.SemaphoreType.DMA
    S = jax.ShapeDtypeStruct
    out = dict(
        w1=S((2, depth, 6 * blk), bf16),
        wo=S((depth, 4 * blk), bf16),
        w2=S((2, depth, 2 * n), bf16),
        w3=S((2, depth, 2 * n), bf16),
        mid_o=S((full, width), f32),
        act_o=S((full, 4 * n), bf16),
        slope_o=S((full, 4 * n), bf16),
        bo=S((length, width), bf16),
        gt=S((length, width), f32),
        go=S((3, share, 2 * n), f32),
        gv=S((16, width), f32),
    )
    scratch = dict(
        sh1=V((2, share, 3 * blk), bf16),
        iwv=V((3, share, cols), bf16),
        sixv=V((6, 1, share), bf16),
        ubv=V((2 * n // 128, 128), bf16),
        biasf=V((8, cols), f32),
        ibv=V((2, cols), bf16),
        vecf=V((8, 128), f32),
        packv=V((8, cols), bf16),
        tv=V((2, length), jnp.int32),
        row=V((8, full), f32),
        vec=V((8, 128), bf16),
        kb=V((full, 128), bf16),
        rm=V((full, 128), bf16),
        vbuf=V((2, 8, width), bf16),
        bbuf=V((2, 8, cols), bf16),
        vecs=V((8, width), f32),
        ub=V((8, cols), f32),
        qb=V((8, 3 * blk), f32),
        xs=V((full, width), bf16),
        gr=V((full, width), bf16),
        ln=V((full, width), bf16),
        qkvm=V((full, 4 * n), bf16),
        lt=V((heads, full), f32),
        mid=V((full, width), f32),
        acc=V((full, width), f32),
        big=V((2 * full, 4 * n), bf16),
        st=V((2, full, cols), bf16),
        turn=V((ring, 2, share, full), bf16),
        lhs1=V((ring, share, 2 * full), bf16),
        lhs2=V((ring, share, 2 * full), bf16),
        lhs3=V((ring, share, 2 * full), bf16),
        wt=V((2, depth, 3 * blk), bf16),
        wn=V((2, 2, 256, 2 * n), bf16),
        part=V((4, ring, share, 2 * n), bf16),
        ry=V((4, ring, share, a), bf16),
        rr=V((4, far, share, 2 * n - b), bf16),
        rl=V((4, far, share, 2 * n - b), bf16),
        rb=V((4, share, n - b), bf16),
        part5=V((ring, share, 6 * blk), bf16),
        ry5=V((ring, share, a5), bf16),
        rr5=V((far, share, a5 + 2 * b5), bf16),
        rl5=V((far, share, a5 + 2 * b5), bf16),
        rb5=V((share, b5), bf16),
        og=V((3, share, 2 * n), f32),
        vsum=V((16, width), f32),
        vacc=V((6, 8, width), f32),
        vswap=V((steps, 16, width), f32),
        ring_s=dma((7, 2 * (far + 1))),
        ring_r=dma((7, 2 * (far + 1))),
        y_s=dma((7, 2 * far + 1)),
        y_r=dma((7, 2 * far + 1)),
        c_s=dma((7, 4 * far + 2)),
        c_r=dma((7, 4 * far + 2)),
        k_sem=dma((7,)),
        sy_s=dma((7, ring + 1)),
        sy_r=dma((7, ring + 1)),
        sr_s=dma((7, 2 * far)),
        sr_r=dma((7, 2 * far)),
        v_s=dma((dp,)),
        v_r=dma((dp,)),
        b_s=dma((steps,)),
        b_r=dma((steps,)),
        l_sem=dma((7,)),
        x_sem=dma((6,)),
        s_sem=dma((4, 2)),
        t_sem=dma((4,)),
        t_s=dma((4,)),
        t_r=dma((4,)),
        a_s=dma((8,)),
        a_r=dma((8,)),
        a_sem=dma((2, 8)),
        h_s=dma((8,)),
        h_r=dma((8,)),
        q_s=dma((4,)),
        q_r=dma((4,)),
        x_s=dma((4,)),
        x_r=dma((4,)),
        clear=pltpu.SemaphoreType.REGULAR,
    )
    names = LAYER_IN + tuple(out) + tuple(scratch)
    hbm = pl.BlockSpec(memory_space=pl.ANY)
    specs = [pl.BlockSpec(memory_space=pltpu.SMEM) if k == "image" else hbm for k in LAYER_IN]
    got = pl.pallas_call(
        functools.partial(layer_kernel, dp, rows, names, LAYER_PLAN),
        out_shape=list(out.values()),
        in_specs=specs,
        out_specs=[hbm] * len(out),
        scratch_shapes=list(scratch.values()),
        compiler_params=pltpu.CompilerParams(collective_id=1, has_side_effects=True, vmem_limit_bytes=VM_LIMIT),
        name="layer",
    )(*args)
    return types.SimpleNamespace(**dict(zip(out, got)))


def place_kernel(bo, gt, go, gv, *refs):
    bo_o, gt_o, iw_o, ow_o, uw_o, dw_o, ib_o, ub_o = refs[:8]
    vec_o, (bov, gtv, g, vs, iwv, ibv, ubv, vecv, sem) = refs[8:14], refs[14:]
    d, t = lax.axis_index("dp"), lax.axis_index("tensor")
    share, wide = g.shape[1:]
    n, blk = wide // 2, wide // 8
    cols = 2 * blk
    ins = [
        pltpu.make_async_copy(go, g, sem.at[0]),
        pltpu.make_async_copy(gt, gtv, sem.at[1]),
        pltpu.make_async_copy(bo, bov, sem.at[2]),
        pltpu.make_async_copy(gv, vs, sem.at[3]),
    ]
    for cp in ins:
        cp.start()
    outs = []

    def send(src, dst):
        cp = pltpu.make_async_copy(src, dst, sem.at[4 + len(outs)])
        cp.start()
        outs.append(cp)

    ins[0].wait()
    send(g.at[1], uw_o)
    send(g.at[0], dw_o)
    for i in (0, 1):
        part = slice(i * blk, (i + 1) * blk)
        for s in range(3):
            at = (3 * i + s) * blk
            iwv[s, :, part] = g[2, :, at : at + blk]
    send(iwv, iw_o)
    send(g.at[2, :, pl.ds(6 * blk, cols)], ow_o)
    ins[1].wait()
    send(gtv, gt_o)
    ins[2].wait()
    send(bov, bo_o)
    ins[3].wait()
    ibv[...] = vs[6:8, pl.ds(pl.multiple_of(t * cols, 128), cols)]
    send(ibv, ib_o)
    width = vs.shape[1]
    per = width // 128
    half = wide // width
    up = jnp.where(t == 0, vs[8 : 8 + half, :], vs[8 + half : 8 + 2 * half, :])
    for r in range(wide // 128):
        lo = (r % per) * 128
        ubv[r : r + 1, :] = up[r // per : r // per + 1, lo : lo + 128]
    send(ubv, ub_o)
    own = vs[0:8, pl.ds(pl.multiple_of((d // 2) * 128, 128), 128)]
    own = jnp.where(d % 2 == 0, own, pltpu.roll(own, share, 1))
    for i in range(6):
        vecv[i] = own[i : i + 1, 0:share]
        send(vecv.at[i], vec_o[i])
    for cp in outs:
        cp.wait()


def place(r, share, n):
    S = jax.ShapeDtypeStruct
    length, width = r.gt.shape
    cols = n // 2
    hbm = pl.BlockSpec(memory_space=pl.ANY)
    out = [
        S((length, width), bf16),
        S((length, width), f32),
        S((3, share, cols), f32),
        S((share, cols), f32),
        S((share, 2 * n), f32),
        S((share, 2 * n), f32),
        S((2, cols), f32),
        S((2 * n // 128, 128), f32),
    ] + [S((1, share), f32)] * 6
    V = pltpu.VMEM
    return pl.pallas_call(
        place_kernel,
        out_shape=out,
        in_specs=[hbm] * 4,
        out_specs=[hbm] * 14,
        scratch_shapes=[
            V((length, width), bf16),
            V((length, width), f32),
            V((3, share, 2 * n), f32),
            V((16, width), f32),
            V((3, share, cols), f32),
            V((2, cols), f32),
            V((2 * n // 128, 128), f32),
            V((6, 1, share), f32),
            pltpu.SemaphoreType.DMA((18,)),
        ],
        compiler_params=pltpu.CompilerParams(vmem_limit_bytes=VM_LIMIT),
        name="place",
    )(r.bo, r.gt, r.go, r.gv)


def paired_device(
    tokens, cotangent, token_valid, image_valid, first_gain, first_shift, input_weight, input_bias, output_weight,
    output_bias, second_gain, second_shift, up_weight, up_bias, down_weight, down_bias,
):
    dp = lax.axis_size("dp")
    length, width = tokens.shape
    share, wide = up_weight.shape
    n = wide // 2
    vectors = (first_gain, first_shift, output_bias, second_gain, second_shift, down_bias)
    args = tuple(v.reshape(1, share) for v in vectors) + (
        up_bias.reshape(-1, 128),
        input_bias,
        input_weight.transpose(1, 0, 2),
        output_weight.T,
        up_weight,
        down_weight.T,
        tokens,
        cotangent,
        token_valid,
        image_valid,
    )
    r = layer(args, dp, length, width, n, share)
    block_out, grad_tokens, g_in, g_out, g_up, g_down, g_in_bias, g_up_bias, *g_vec = place(r, share, n)
    g_vec = [v.reshape(share) for v in g_vec]
    return (
        block_out,
        grad_tokens,
        g_vec[0],
        g_vec[1],
        g_in.transpose(1, 0, 2),
        g_in_bias,
        g_out.T,
        g_vec[2],
        g_vec[3],
        g_vec[4],
        g_up,
        g_up_bias.reshape(wide),
        g_down.T,
        g_vec[5],
    )


def solution(mesh):
    in_specs = (
        P(("dp", "tensor"), None),
        P(("dp", "tensor"), None),
        P("dp", None),
        P("dp"),
        P("dp"),
        P("dp"),
        P("dp", None, "tensor"),
        P(None, "tensor"),
        P("tensor", "dp"),
        P("dp"),
        P("dp"),
        P("dp"),
        P("dp", "tensor"),
        P("tensor"),
        P("tensor", "dp"),
        P("dp"),
    )
    out_specs = (
        P(("dp", "tensor"), None),
        P(("dp", "tensor"), None),
        P("dp"),
        P("dp"),
        P("dp", None, "tensor"),
        P(None, "tensor"),
        P("tensor", "dp"),
        P("dp"),
        P("dp"),
        P("dp"),
        P("dp", "tensor"),
        P("tensor"),
        P("tensor", "dp"),
        P("dp"),
    )
    ready = mesh.shape["tensor"] == 2 and mesh.shape["dp"] == 16
    body = paired_device if ready else general_device
    return jax.shard_map(
        body, mesh=mesh, in_specs=in_specs, out_specs=out_specs, check_vma=False
    )
```

```python
import functools
import types

import jax
import jax.numpy as jnp
from jax import lax
from jax.experimental import pallas as pl
from jax.experimental.pallas import tpu as pltpu
from jax.sharding import PartitionSpec as P

HEAD_DIM = 64
MESH = pl.DeviceIdType.MESH
f32 = jnp.float32
bf16 = jnp.bfloat16
NN, NT, TN = ((1,), (0,)), ((1,), (1,)), ((0,), (0,))
VM_LIMIT = 127 << 19


def layer_norm(inputs, gain, shift):
    center = inputs - jnp.mean(inputs, axis=-1, keepdims=True)
    spread = jnp.mean(center * center, axis=-1, keepdims=True)
    return center * lax.rsqrt(spread + 1e-06) * gain + shift


def norm_backward(inputs, gain, upstream):
    center = inputs - jnp.mean(inputs, axis=-1, keepdims=True)
    spread = jnp.mean(center * center, axis=-1, keepdims=True)
    scaled = lax.rsqrt(spread + 1e-06)
    unit = center * scaled
    weighted = upstream * gain
    grad_inputs = scaled * (
        weighted
        - jnp.mean(weighted, axis=-1, keepdims=True)
        - unit * jnp.mean(weighted * unit, axis=-1, keepdims=True)
    )
    return (grad_inputs, jnp.sum(upstream * unit, axis=0), jnp.sum(upstream, axis=0))


def gelu_slope(hidden):
    return (
        0.5 * (1.0 + lax.erf(hidden * 0.7071067811865476))
        + hidden * jnp.exp(-0.5 * hidden * hidden) * 0.3989422804014327
    )


def general_device(
    tokens,
    cotangent,
    token_valid,
    image_valid,
    first_gain,
    first_shift,
    input_weight,
    input_bias,
    output_weight,
    output_bias,
    second_gain,
    second_shift,
    up_weight,
    up_bias,
    down_weight,
    down_bias,
):
    f32 = jnp.float32
    bf16 = jnp.bfloat16
    gathered = (
        lax.all_gather(first_gain, "dp", axis=0, tiled=True),
        lax.all_gather(first_shift, "dp", axis=0, tiled=True),
        lax.all_gather(input_weight, "dp", axis=0, tiled=True),
        lax.all_gather(output_weight, "dp", axis=1, tiled=True),
        lax.all_gather(output_bias, "dp", axis=0, tiled=True),
        lax.all_gather(second_gain, "dp", axis=0, tiled=True),
        lax.all_gather(second_shift, "dp", axis=0, tiled=True),
        lax.all_gather(up_weight, "dp", axis=0, tiled=True),
        lax.all_gather(down_weight, "dp", axis=1, tiled=True),
        lax.all_gather(down_bias, "dp", axis=0, tiled=True),
    )
    (
        gain_one,
        shift_one,
        in_full,
        out_full,
        out_shift,
        gain_two,
        shift_two,
        up_full,
        down_full,
        down_shift,
    ) = gathered
    gain_one = gain_one.astype(f32)
    shift_one = shift_one.astype(f32)
    out_shift = out_shift.astype(f32)
    gain_two = gain_two.astype(f32)
    shift_two = shift_two.astype(f32)
    down_shift = down_shift.astype(f32)
    tensor_at = lax.axis_index("tensor")
    groups = lax.axis_size("tensor")
    own_rows = tokens.shape[0]
    width = tokens.shape[1]
    length = token_valid.shape[1]
    positions = lax.broadcasted_iota(jnp.int32, token_valid.shape, 1)
    key_ok = (token_valid > 0) | (positions == 0)
    mask_all = (token_valid * image_valid[:, None]).astype(f32).reshape(-1)
    row_mask = lax.dynamic_slice_in_dim(mask_all, tensor_at * own_rows, own_rows)[:, None]
    images = token_valid.shape[0]
    local_width = in_full.shape[2]
    local_heads = local_width // HEAD_DIM
    hidden_width = up_full.shape[1]
    scale = HEAD_DIM ** (-0.5)
    head_shape = (images, length, local_heads, HEAD_DIM)
    inputs = tokens.astype(f32)
    first_own = layer_norm(inputs, gain_one, shift_one).astype(bf16)
    first_all = lax.all_gather(first_own, "tensor", axis=0, tiled=True)
    project = jnp.einsum("rd,dce->rce", first_all, in_full, preferred_element_type=f32)
    bias_in = input_bias.astype(f32)
    queries = (project[:, 0] + bias_in[0]).astype(bf16).reshape(head_shape)
    keyset = project[:, 1].astype(bf16).reshape(head_shape)
    values = (project[:, 2] + bias_in[1]).astype(bf16).reshape(head_shape)

    def scores_of(query_img, key_img, ok_img):
        scores = jnp.einsum("qhe,khe->hqk", query_img, key_img, preferred_element_type=f32) * scale
        return jnp.where(ok_img[None, None, :], scores, -1000000000.0)

    def attend(pieces):
        query_img, key_img, value_img, ok_img = pieces
        scores = scores_of(query_img, key_img, ok_img)
        highest = jnp.max(scores, axis=-1, keepdims=True)
        log_total = highest + jnp.log(jnp.sum(jnp.exp(scores - highest), axis=-1, keepdims=True))
        attn_probs = jnp.exp(scores - log_total).astype(bf16)
        mixed_img = jnp.einsum("hqk,khe->qhe", attn_probs, value_img, preferred_element_type=f32)
        return (mixed_img.astype(bf16), log_total)

    mixed, log_totals = lax.map(attend, (queries, keyset, values, key_ok))
    mixed_rows = mixed.reshape(images * length, local_width)
    attended = lax.psum_scatter(
        jnp.dot(mixed_rows, out_full, preferred_element_type=f32).astype(jnp.bfloat16),
        "tensor",
        scatter_dimension=0,
        tiled=True,
    ).astype(jnp.float32)
    middle = inputs + attended + out_shift
    second_own = layer_norm(middle, gain_two, shift_two).astype(bf16)
    second_all = lax.all_gather(second_own, "tensor", axis=0, tiled=True)
    hidden = jnp.dot(second_all, up_full, preferred_element_type=f32) + up_bias.astype(f32)
    active = jax.nn.gelu(hidden, approximate=False).astype(bf16)
    lifted = lax.psum_scatter(
        jnp.dot(active, down_full, preferred_element_type=f32).astype(jnp.bfloat16),
        "tensor",
        scatter_dimension=0,
        tiled=True,
    ).astype(jnp.float32)
    block_out = (row_mask * (middle + lifted + down_shift)).astype(bf16)
    grad_last = row_mask * cotangent.astype(f32)
    first_all, second_all = (
        lax.all_gather(first_own, "tensor", axis=0, tiled=True),
        lax.all_gather(second_own, "tensor", axis=0, tiled=True),
    )
    grad_lift = lax.all_gather(grad_last.astype(bf16), "tensor", axis=0, tiled=True)
    grad_active = jnp.einsum("rd,fd->rf", grad_lift, down_full, preferred_element_type=f32)
    grad_hidden = (grad_active * gelu_slope(hidden)).astype(bf16)
    grad_down = jnp.einsum("rf,rd->fd", active, grad_lift, preferred_element_type=f32)
    grad_up = jnp.einsum("rd,rf->df", second_all, grad_hidden, preferred_element_type=f32)
    grad_up_bias = jnp.sum(grad_hidden.astype(f32), axis=0)
    grad_second = lax.psum_scatter(
        jnp.einsum("rf,df->rd", grad_hidden, up_full, preferred_element_type=f32).astype(
            jnp.bfloat16
        ),
        "tensor",
        scatter_dimension=0,
        tiled=True,
    ).astype(jnp.float32)
    grad_middle, grad_gain_two, grad_shift_two = norm_backward(middle, gain_two, grad_second)
    grad_middle = grad_middle + grad_last
    grad_mid_all = lax.all_gather(grad_middle.astype(bf16), "tensor", axis=0, tiled=True)
    grad_mixed = jnp.einsum("rd,ed->re", grad_mid_all, out_full, preferred_element_type=f32).astype(
        bf16
    )
    grad_out_weight = jnp.einsum("re,rd->ed", mixed_rows, grad_mid_all, preferred_element_type=f32)

    def attend_back(pieces):
        query_img, key_img, value_img, ok_img, total_img, grad_img = pieces
        scores = scores_of(query_img, key_img, ok_img)
        attn_probs = jnp.exp(scores - total_img)
        grad_values = jnp.einsum(
            "hqk,qhe->khe", attn_probs.astype(bf16), grad_img, preferred_element_type=f32
        )
        grad_probs = jnp.einsum("qhe,khe->hqk", grad_img, value_img, preferred_element_type=f32)
        grad_scores = (
            attn_probs * (grad_probs - jnp.sum(attn_probs * grad_probs, axis=-1, keepdims=True))
        ).astype(bf16)
        grad_queries = (
            jnp.einsum("hqk,khe->qhe", grad_scores, key_img, preferred_element_type=f32) * scale
        )
        grad_keys = (
            jnp.einsum("hqk,qhe->khe", grad_scores, query_img, preferred_element_type=f32) * scale
        )
        return jnp.stack([grad_queries, grad_keys, grad_values], axis=1).astype(bf16)

    grad_project = lax.map(
        attend_back, (queries, keyset, values, key_ok, log_totals, grad_mixed.reshape(head_shape))
    )
    grad_project = grad_project.reshape(images * length, 3, local_width)
    grad_in_weight = jnp.einsum("rd,rce->dce", first_all, grad_project, preferred_element_type=f32)
    grad_in_bias = jnp.sum(grad_project[:, 0::2].astype(f32), axis=0)
    grad_first = lax.psum_scatter(
        jnp.einsum("rce,dce->rd", grad_project, in_full, preferred_element_type=f32).astype(
            jnp.bfloat16
        ),
        "tensor",
        scatter_dimension=0,
        tiled=True,
    ).astype(jnp.float32)
    grad_inputs, grad_gain_one, grad_shift_one = norm_backward(inputs, gain_one, grad_first)
    grad_inputs = grad_inputs + grad_middle
    grad_in_own, grad_out_own, grad_up_own, grad_down_own = (
        lax.psum_scatter(
            grad_in_weight.astype(jnp.bfloat16), "dp", scatter_dimension=0, tiled=True
        ).astype(jnp.float32),
        lax.psum_scatter(
            grad_out_weight.astype(jnp.bfloat16), "dp", scatter_dimension=1, tiled=True
        ).astype(jnp.float32),
        lax.psum_scatter(
            grad_up.astype(jnp.bfloat16), "dp", scatter_dimension=0, tiled=True
        ).astype(jnp.float32),
        lax.psum_scatter(
            grad_down.astype(jnp.bfloat16), "dp", scatter_dimension=1, tiled=True
        ).astype(jnp.float32),
    )
    vectors = jnp.stack(
        [
            grad_gain_one,
            grad_shift_one,
            jnp.sum(grad_middle, axis=0),
            grad_gain_two,
            grad_shift_two,
            jnp.sum(grad_last, axis=0),
        ]
    )
    bias_share = input_bias.shape[1]
    up_share = up_bias.shape[0]
    placed_bias = lax.dynamic_update_slice(
        jnp.zeros((2, width), f32), grad_in_bias, (0, tensor_at * local_width)
    )
    placed_up = lax.dynamic_update_slice(
        jnp.zeros((hidden_width * groups,), f32), grad_up_bias, (tensor_at * hidden_width,)
    )
    vectors, placed_bias, placed_up = lax.psum((vectors, placed_bias, placed_up), ("dp", "tensor"))
    share = first_gain.shape[0]
    dp_at = lax.axis_index("dp")
    vectors = lax.dynamic_slice_in_dim(vectors, dp_at * share, share, 1)
    bias_own = lax.dynamic_slice_in_dim(placed_bias, tensor_at * bias_share, bias_share, 1)
    up_bias_own = lax.dynamic_slice_in_dim(placed_up, tensor_at * up_share, up_share, 0)
    return (
        block_out,
        grad_inputs,
        vectors[0],
        vectors[1],
        grad_in_own,
        bias_own,
        grad_out_own,
        vectors[2],
        vectors[3],
        vectors[4],
        grad_up_own,
        up_bias_own,
        grad_down_own,
        vectors[5],
    )


def mul(a, b, dims):
    return lax.dot_general(a, b, (dims, ((), ())), preferred_element_type=f32)


def iota(shape, axis):
    return lax.broadcasted_iota(jnp.int32, shape, axis)


def tile(j, size):
    return pl.ds(pl.multiple_of(j * size, size), size)


class Place:
    def __init__(self, dp):
        d = lax.axis_index("dp")
        t = lax.axis_index("tensor")
        ring = dp // 2
        self.dp, self.d, self.t, self.ring, self.far = dp, d, t, ring, ring // 2
        self.chip, self.core = d // 2, d % 2
        self.pos = jnp.where(self.chip % 2 == 0, self.chip // 2, ring - 1 - self.chip // 2)
        self.right = (self.chip_at(1) * 2 + self.core, t)
        self.left = (self.chip_at(-1) * 2 + self.core, t)
        self.across = (d, 1 - t)
        self.sibling = (d + 1 - 2 * self.core, t)

    def chip_at(self, offset):
        ring = self.ring
        spot = (self.pos + offset + ring) % ring
        return jnp.where(spot < ring // 2, 2 * spot, 2 * (ring - 1 - spot) + 1)


class Columns:
    def __init__(self, w, n, a):
        t, b = w.t, n - a
        self.n, self.a, self.b = n, a, b
        self.own = (pl.multiple_of(t * n, 128), n)
        self.other = (pl.multiple_of((1 - t) * n, 128), n)
        self.ring = (pl.multiple_of(t * a, 128), 2 * n - a)
        self.mine_a = (pl.multiple_of(t * (2 * n - a), 128), a)
        self.their_a = (pl.multiple_of((1 - t) * (2 * n - a), 128), a)
        self.their_b = (pl.multiple_of(n - t * b, 128), b)
        self.mine_b = (pl.multiple_of(n - (1 - t) * b, 128), b)


OUTER = (4, 3, 2, 5, 4, 5, 4, 4, 4, 4, 5, 3, 4, 4)


def greet(targets):
    bar = pltpu.get_barrier_semaphore()
    for a in targets:
        pl.semaphore_signal(bar, inc=1, device_id=a, device_id_type=MESH)
    pl.semaphore_wait(bar, len(targets))


def rcopy(src, dst, send, recv, dev):
    return pltpu.make_async_remote_copy(
        src_ref=src, dst_ref=dst, send_sem=send, recv_sem=recv, device_id=dev, device_id_type=MESH
    )


class Gather:
    def __init__(self, w, g, shard, full, sems):
        self.w, self.g, self.shard, self.full, self.sems = w, g, shard, full, sems
        self.rows, n = shard.shape
        self.cols = Columns(w, n, 128 * OUTER[g])

    def block(self, offset, cols, span=None):
        w = self.w
        lo, size = span or (0, self.rows)
        base = w.chip_at(offset) * (2 * self.rows) + w.core * self.rows + lo
        return self.full.at[pl.ds(pl.multiple_of(base, 16), size), pl.ds(cols[0], cols[1])]

    def span(self, s, dirn):
        half = self.rows // 2
        return (0, self.rows) if s < self.w.far else (dirn * half, half)

    def off(self, s, dirn):
        return s if dirn else -s

    def make(self, kind, src, dst, k, dev):
        send, recv = self.sems[kind]
        return rcopy(src, dst, send.at[self.g, k], recv.at[self.g, k], dev)

    def y(self, s, dirn):
        if s == 0:
            return self.make("y", self.shard, self.block(0, self.cols.own), 0, self.w.across)
        ref = self.block(self.off(s, dirn), self.cols.mine_a, self.span(s, dirn))
        return self.make("y", ref, ref, 2 * s - 1 + dirn, self.w.across)

    def ring(self, s, dirn, part=0):
        dev = self.w.left if dirn else self.w.right
        k = dirn * (self.w.far + 1)
        if s == 1 and part == 0:
            return self.make("r", self.shard, self.block(0, self.cols.own), k, dev)
        if s == 1:
            ref = self.block(0, self.cols.their_b)
            return self.make("r", ref, ref, k + 1, dev)
        ref = self.block(self.off(s - 1, dirn), self.cols.ring, self.span(s, dirn))
        return self.make("r", ref, ref, k + s, dev)

    def sib(self, k):
        w = self.w
        if k == 0:
            src, dst = self.shard, self.block(0, self.cols.own)
        elif k == 1:
            src = dst = self.block(0, self.cols.other)
        else:
            which, rest = divmod(k - 2, 2 * w.far)
            s, dirn = rest // 2 + 1, rest % 2
            cols = self.cols.their_a if which else self.cols.ring
            src = dst = self.block(self.off(s, dirn), cols, self.span(s, dirn))
        return self.make("c", src, dst, k, w.sibling)

    def keep(self):
        return pltpu.make_async_copy(self.shard, self.block(0, self.cols.own), self.sems["k"].at[self.g])

    def S(self):
        self.y(0, 0).start()
        self.ring(1, 0).start()
        self.ring(1, 1).start()
        self.sib(0).start()
        self.keep().start()

    def Y(self):
        self.y(0, 0).wait_recv()
        self.ring(1, 0, 1).start()
        self.ring(1, 1, 1).start()
        self.sib(1).start()

    def h(self, s):
        for dirn in (0, 1):
            self.ring(s, dirn).wait_recv()
            if s == 1:
                self.ring(s, dirn, 1).wait_recv()
            if s < self.w.far:
                self.ring(s + 1, dirn).start()
            self.y(s, dirn).start()
            self.sib(2 * s + dirn).start()

    def c(self, s):
        for dirn in (0, 1):
            self.y(s, dirn).wait_recv()
            self.sib(2 + 2 * self.w.far + 2 * (s - 1) + dirn).start()

    def events(self):
        h, c = (lambda s: functools.partial(self.h, s)), (lambda s: functools.partial(self.c, s))
        return [self.S, self.Y, h(1), h(2), c(1), h(3), c(2), h(4), c(3), c(4), self.E]

    def E(self):
        for k in range(2 + 4 * self.w.far):
            self.sib(k).wait()
        self.keep().wait()

    def drain(self):
        far = self.w.far
        self.y(0, 0).wait_send()
        for dirn in (0, 1):
            self.ring(1, dirn).wait_send()
            self.ring(1, dirn, 1).wait_send()
            for s in range(1, far + 1):
                self.y(s, dirn).wait_send()
                if s > 1:
                    self.ring(s, dirn).wait_send()


class Scatter:
    def __init__(self, w, g, part, ry, rr, rl, rb, out, sems):
        self.w, self.g, self.part, self.sems, self.out = w, g, part, sems, out
        self.rows, n = part.shape[1], part.shape[2] // 2
        self.cols = c = Columns(w, n, 128 * OUTER[7 + g])
        self.ry = ry.at[:, :, pl.ds(0, c.a)]
        self.rr = rr.at[:, :, pl.ds(0, 2 * n - c.a)]
        self.rl = rl.at[:, :, pl.ds(0, 2 * n - c.a)]
        self.rb = rb.at[:, pl.ds(0, c.b)]
        far = w.far
        self.order = [far] + [k * sign for k in range(far - 1, 0, -1) for sign in (1, -1)] + [0]

    def make(self, kind, src, dst, k, dev):
        send, recv = self.sems[kind]
        return rcopy(src, dst, send.at[self.g, k], recv.at[self.g, k], dev)

    def cross(self, k):
        w = self.w
        chip = w.chip_at(k)
        src = self.part.at[chip, :, pl.ds(*self.cols.their_a)]
        return self.make("y", src, self.ry.at[chip], self.order.index(k), w.across)

    def ring(self, s, dirn):
        w = self.w
        chip = w.chip_at(s - w.far if dirn else w.far - s)
        half = self.rows // 2
        span = pl.ds(dirn * half, half) if s == 0 else pl.ds(0, self.rows)
        src = self.part.at[chip, span, pl.ds(*self.cols.ring)]
        dst = (self.rl if dirn else self.rr).at[s, span]
        return self.make("r", src, dst, dirn * w.far + s, w.left if dirn else w.right)

    def swap(self):
        w = self.w
        src = self.part.at[w.chip_at(0), :, pl.ds(*self.cols.their_b)]
        return self.make("y", src, self.rb, len(self.order), w.across)

    def add(self, k, lo, size, cols, other):
        chip = self.w.chip_at(k)
        part = self.part
        ch = 16

        @pl.loop(0, size // ch)
        def _(r):
            rs = pl.ds(pl.multiple_of(lo + r * ch, ch), ch)
            cs = pl.ds(cols[0], cols[1])
            part[chip, rs, cs] = (part[chip, rs, cs].astype(f32) + other[rs, :].astype(f32)).astype(bf16)

    def events(self):
        s, t = (lambda k: functools.partial(self.s, k)), (lambda k: functools.partial(self.t, k))
        return [self.A, self.L, t(3), s(1), t(2), s(2), t(1), s(3), t(0), self.F, self.Z]

    def both(self, k):
        return (k, -k) if k else (0,)

    def A(self):
        for k in (self.w.far, self.w.far - 1, 1 - self.w.far):
            self.cross(k).start()

    def take(self, k):
        self.cross(k).wait_recv()
        self.add(k, 0, self.rows, self.cols.mine_a, self.ry.at[self.w.chip_at(k)])

    def L(self):
        self.cross(self.w.far).wait_recv()
        for k in self.both(self.w.far - 2):
            self.cross(k).start()
        self.add(self.w.far, 0, self.rows, self.cols.mine_a, self.ry.at[self.w.chip_at(self.w.far)])
        self.ring(0, 0).start()
        self.ring(0, 1).start()

    def t(self, k):
        for i in self.both(k):
            self.take(i)
        if k > 1:
            for i in self.both(k - 2):
                self.cross(i).start()

    def s(self, s):
        far, half = self.w.far, self.rows // 2
        for dirn in (0, 1):
            self.ring(s - 1, dirn).wait_recv()
            k = s - far if dirn else far - s
            got = (self.rl if dirn else self.rr).at[s - 1]
            lo, size = (dirn * half, half) if s == 1 else (0, self.rows)
            self.add(k, lo, size, self.cols.ring, got)
            self.ring(s, dirn).start()

    def F(self):
        far = self.w.far
        for dirn in (0, 1):
            self.ring(far - 1, dirn).wait_recv()
            self.add(0, 0, self.rows, self.cols.ring, (self.rl if dirn else self.rr).at[far - 1])
        self.swap().start()

    def Z(self):
        self.swap().wait_recv()
        self.add(0, 0, self.rows, self.cols.mine_b, self.rb)
        chip = self.w.chip_at(0)
        self.out[...] = self.part[chip, :, pl.ds(*self.cols.own)].astype(f32)

    def drain(self):
        for k in self.order:
            self.cross(k).wait_send()
        for s in range(self.w.far):
            self.ring(s, 0).wait_send()
            self.ring(s, 1).wait_send()
        self.swap().wait_send()


class Plan:
    def __init__(self, groups, table):
        self.events, self.table = [g.events() for g in groups], table

    def after(self, name):
        for code in self.table.get(name, ()):
            self.events[code // 100][code % 100]()

    def tick(self, j, name, first, count):
        for k in range(count):
            at = name + str(first + k)
            if at in self.table:

                @pl.when(j == k)
                def _(at=at):
                    self.after(at)


def stream(count, parts, sem, body, begun=False):
    def copies(j):
        slot = lax.rem(j, 2)
        return [pltpu.make_async_copy(src(j), dst(slot), sem.at[i, slot]) for i, (src, dst) in enumerate(parts)]

    def begin():
        for cp in copies(jnp.int32(0)):
            cp.start()

    def run():
        @pl.loop(0, count)
        def _(j):
            @pl.when(j + 1 < count)
            def _():
                for cp in copies(j + 1):
                    cp.start()

            for cp in copies(j):
                cp.wait()
            body(j, lax.rem(j, 2))

    return begin, run


def normalize(x):
    center = x - jnp.mean(x, axis=-1, keepdims=True)
    scaled = lax.rsqrt(jnp.mean(center * center, axis=-1, keepdims=True) + 1e-06)
    return center * scaled, scaled


def lanes_of(pair, blk):
    base = (pair // 2) * (4 * blk) + (pair % 2) * 128
    return [pl.ds(pl.multiple_of(base + s * blk, 128), 128) for s in range(4)]


def attend_pair(m, i, rows, full, blk):
    qs, ks, vs, ms = lanes_of(i, blk)
    q2, k2, v2 = m.qkvm[0:rows, qs], m.qkvm[:, ks], m.qkvm[:, vs]
    lq, lk = iota((rows, 128), 1), iota((full, 128), 1)
    outs = []
    logs = m.logs[0:rows, :]
    for h in (0, 1):
        spare = 64 * (1 - h)
        own_q = (lq < 64) if h == 0 else (lq >= 64)
        own_k = (lk < 64) if h == 0 else (lk >= 64)
        qh = jnp.where(own_q, q2, jnp.where(lq == spare, 1.0, 0.0).astype(bf16))
        kh = jnp.where(lk == spare, m.kb[...], k2)
        scores = mul(qh, kh, NT)
        top = jnp.max(scores, axis=1, keepdims=True)
        probs = jnp.exp(scores - top).astype(bf16)
        out = mul(probs, jnp.where(own_k, v2, jnp.ones_like(v2)), NN)
        turned = pltpu.roll(out, 64, 1)
        outs.append(out / turned)
        total = jnp.where(own_q, turned, out)
        logs = jnp.where(lq == 2 * i + h, top + jnp.log(total), logs)
    m.logs[0:rows, :] = logs
    m.qkvm[0:rows, ms] = jnp.where(lq < 64, outs[0], outs[1]).astype(bf16)


def attend_back(m, i, rows, full, blk):
    qs, ks, vs, ms = lanes_of(i, blk)
    q2, do2 = m.qkvm[:, qs], m.ln[:, tile(i, 128)]
    k2, v2 = m.qkvm[0:rows, ks], m.qkvm[0:rows, vs]
    lq, lk = iota((full, 128), 1), iota((rows, 128), 1)
    both = (do2.astype(f32) * m.qkvm[:, ms].astype(f32)).T
    dqs, dks, dvs = [], [], []
    for h in (0, 1):
        spare = 64 * (1 - h)
        own_q = (lq < 64) if h == 0 else (lq >= 64)
        own_k = (lk < 64) if h == 0 else (lk >= 64)
        qh = jnp.where(own_q, q2, jnp.where(lq == spare, 1.0, 0.0).astype(bf16))
        kh = jnp.where(lk == spare, m.kb[0:rows, :], k2)
        probs = jnp.exp(mul(kh, qh, NT) - m.lt[pl.ds(2 * i + h, 1), :])
        dvs.append(mul(probs.astype(bf16), do2, NN))
        dprobs = mul(jnp.where(own_k, v2, jnp.zeros_like(v2)), do2, NT)
        inner = jnp.sum(both[64 * h : 64 * h + 64, :], axis=0, keepdims=True)
        ds = (probs * (dprobs - inner)).astype(bf16)
        dks.append(mul(ds, q2, NN))
        dqs.append(mul(ds, k2, TN))
    dv = jnp.where(lk < 64, dvs[0], dvs[1]).astype(bf16)
    dk = jnp.where(lk < 64, dks[0], dks[1]).astype(bf16)
    dq = (jnp.where(lq < 64, dqs[0], dqs[1]) * HEAD_DIM**-0.5).astype(bf16)
    m.big[0:full, qs] = dq
    m.big[0:rows, ks] = dk
    m.big[0:rows, vs] = dv
    at = ((i // 2) % 2) * (2 * blk) + (i // 4) * blk + (i % 2) * 128
    ns = pl.ds(pl.multiple_of(at, 128), 128)
    m.vsum[6:7, ns] = jnp.sum(dq.astype(f32), axis=0, keepdims=True)
    m.vsum[7:8, ns] = jnp.sum(dv.astype(f32), axis=0, keepdims=True)


LAYER_IN = ("v0", "v1", "v2", "v3", "v4", "v5", "ubias", "ibias", "iw", "ow", "uw", "dw", "tok", "cot", "valid", "image")


def layer_kernel(dp, rows, names, table, *refs):
    m = types.SimpleNamespace(**dict(zip(names, refs)))
    n = m.uw.shape[1] // 2
    w = Place(dp)
    length, width = m.tok.shape
    full = m.qkvm.shape[0]
    share = m.sh1.shape[1]
    cols, blk = n // 2, n // 4
    ch = 128
    sems = {"r": (m.ring_s, m.ring_r), "y": (m.y_s, m.y_r), "c": (m.c_s, m.c_r), "k": m.k_sem}
    groups = [Gather(w, i, m.sh1.at[i], m.w1.at[i], sems) for i in (0, 1)]
    groups.append(Gather(w, 2, m.ow, m.wo, sems))
    groups += [Gather(w, 3 + i, m.uw.at[:, pl.ds(i * n, n)], m.w2.at[i], sems) for i in (0, 1)]
    groups += [Gather(w, 5 + i, m.dw.at[:, pl.ds(i * n, n)], m.w3.at[i], sems) for i in (0, 1)]
    sums = {"y": (m.sy_s, m.sy_r), "r": (m.sr_s, m.sr_r)}
    slots = [tuple(ref.at[i] for ref in (m.part, m.ry, m.rr, m.rl, m.rb)) for i in range(4)]
    slots.append((m.part5, m.ry5, m.rr5, m.rl5, m.rb5))
    wide = (n, n, n, n, 2 * blk, 3 * blk, 3 * blk)
    lefts = (0, n, 0, n, 6 * blk, 0, 3 * blk)
    for g in range(7):
        part, *rest = slots[(0, 1, 2, 3, 0, 1, 4)[g]]
        part = part.at[:, :, pl.ds(0, 2 * wide[g])]
        where = m.og.at[(0, 0, 1, 1, 2, 2, 2)[g], :, pl.ds(lefts[g], wide[g])]
        groups.append(Scatter(w, g, part, *rest, where, sums))
    plan = Plan(groups, table)
    gathers, sums7 = groups[:7], groups[7:]

    def flip(k):
        return (w.d + k - 2 * k * ((w.d // k) % 2), w.t)

    flips = [w.across]
    k = 1
    while k < dp:
        flips.append(flip(k))
        k *= 2

    loads = [
        pltpu.make_async_copy(src, dst, m.l_sem.at[i])
        for i, (src, dst) in enumerate(
            (
                (m.iw, m.iwv),
                (m.ubias, m.ubv),
                (m.ibias, m.ibv),
                (m.tok, m.xs.at[pl.ds(0, length)]),
                (m.cot, m.gr.at[pl.ds(0, length)]),
                (m.valid, m.tv),
            )
        )
    ]
    loads += [
        pltpu.make_async_copy(src, m.sixv.at[i], m.x_sem.at[i])
        for i, src in enumerate((m.v0, m.v1, m.v2, m.v3, m.v4, m.v5))
    ]
    for cp in loads:
        cp.start()
    peers = [(lax.rem(w.d + i, dp), w.t) for i in range(1, dp)] + [w.across]
    bar = pltpu.get_barrier_semaphore()
    for a in peers:
        pl.semaphore_signal(bar, inc=1, device_id=a, device_id_type=MESH)
    loads[0].wait()
    for i in (0, 1):
        part = slice(i * blk, (i + 1) * blk)
        for s in range(3):
            m.sh1[i, :, s * blk : (s + 1) * blk] = m.iwv[s, :, part]
    pl.semaphore_wait(bar, len(peers))
    plan.after("go")
    for cp in loads[1:3] + loads[6:]:
        cp.wait()
    spot = pl.ds(pl.multiple_of(w.chip * 128, 128), 128)
    m.vecf[...] = jnp.zeros((8, 128), f32)
    for i in range(6):
        m.vecf[i : i + 1, 0:share] = m.sixv[i].astype(f32)
    vec = m.vecf[...]
    vec = jnp.where(w.core == 0, vec, pltpu.roll(vec, share, 1))
    m.biasf[...] = jnp.zeros(m.biasf.shape, f32)
    ub = m.ubv[...].astype(f32)
    for r in range(4 * cols // 128):
        q = r * 128 // cols
        lo = r * 128 - q * cols
        m.biasf[q : q + 1, lo : lo + 128] = ub[r : r + 1, :]
    m.biasf[4:6, :] = m.ibv[...].astype(f32)
    m.packv[...] = m.biasf[...].astype(bf16)
    m.vec[...] = vec.astype(bf16)

    def vec_copy(i):
        return rcopy(m.vec, m.vbuf.at[w.core, :, spot], m.v_s.at[i], m.v_r.at[i], peers[i])

    bias_copy = rcopy(m.packv, m.bbuf.at[w.t], m.v_s.at[dp - 1], m.v_r.at[dp - 1], w.across)
    for i in range(dp - 1):
        vec_copy(i).start()
    bias_copy.start()
    m.vbuf[w.core, :, spot] = m.vec[...]
    m.bbuf[w.t] = m.packv[...]
    plan.after("pre0")
    zero_rows = pl.ds(rows, full - rows)
    m.qkvm[zero_rows, :] = jnp.zeros((full - rows, 4 * n), bf16)
    m.big[zero_rows, :] = jnp.zeros((full - rows, 4 * n), bf16)
    m.acc[zero_rows, :] = jnp.zeros((full - rows, width), f32)
    m.mid[zero_rows, :] = jnp.zeros((full - rows, width), f32)
    m.logs = m.acc.at[:, pl.ds(0, 128)]
    m.logs[0:rows, :] = jnp.zeros((rows, 128), f32)
    m.vsum[...] = jnp.zeros(m.vsum.shape, f32)
    m.vacc[...] = jnp.zeros(m.vacc.shape, f32)
    for cp in loads[3:6]:
        cp.wait()
    tail = pl.ds(length, full - length)
    m.xs[tail, :] = jnp.zeros((full - length, width), bf16)
    m.gr[tail, :] = jnp.zeros((full - length, width), bf16)
    m.row[...] = jnp.zeros(m.row.shape, f32)
    m.row[0:1, 0:length] = m.tv[pl.ds(w.t, 1), :].astype(f32)
    ok = jnp.broadcast_to(m.row[0:1, :], (128, full)).T
    m.rm[...] = (ok * m.image[w.t].astype(f32)).astype(bf16)
    m.kb[...] = jnp.where((ok > 0) | (iota((full, 128), 0) == 0), 0.0, -1e9).astype(bf16)
    for i in range(dp - 1):
        vec_copy(i).wait()
    bias_copy.wait()
    m.vecs[...] = m.vbuf[0].astype(f32) + m.vbuf[1].astype(f32)
    m.qb[...] = jnp.zeros(m.qb.shape, f32)
    for side in (0, 1):
        b = m.bbuf[side].astype(f32)
        for r in range(4):
            at = (r // 2) * 4 + side * 2 + r % 2
            m.ub[at : at + 1, :] = b[r : r + 1]
        for i in (0, 1):
            at = 2 * i + side
            m.qb[at : at + 1, 0:blk] = b[4:5, i * blk : (i + 1) * blk]
            m.qb[at : at + 1, 2 * blk : 3 * blk] = b[5:6, i * blk : (i + 1) * blk]

    @pl.loop(0, full // ch)
    def _(r):
        rs = tile(r, ch)
        unit, _ = normalize(m.xs[rs, :].astype(f32))
        m.ln[rs, :] = (unit * m.vecs[0:1, :] + m.vecs[1:2, :]).astype(bf16)
        m.gr[rs, :] = (m.gr[rs, :].astype(f32) * m.rm[rs, 0:1].astype(f32)).astype(bf16)

    plan.after("pre1")

    def turn_copies(k):
        tt, lhs = m.turn, (m.lhs1, m.lhs3, m.lhs2, m.lhs3)[k]
        keep = pltpu.make_async_copy(tt.at[:, w.core], lhs.at[:, :, pl.ds(0, full)], m.t_sem.at[k])
        give = rcopy(
            tt.at[:, 1 - w.core], lhs.at[:, :, pl.ds(full, full)], m.t_s.at[k], m.t_r.at[k], w.sibling
        )
        return keep, give

    def turn(src, k):
        @pl.loop(0, width // 256)
        def _(j):
            m.turn[tile(j, 2)] = src[:, tile(j, 256)].T.reshape(2, 2, share, full)

        for cp in turn_copies(k):
            cp.start()

    def turned(k):
        for cp in turn_copies(k):
            cp.wait()

    turn(m.ln, 0)
    plan.after("pre2")
    turned(0)
    turn(m.gr, 1)
    plan.after("pre3")

    def at_cols(j, lo, size):
        return pl.ds(pl.multiple_of(j * n + lo, 128), size)

    def qkv_stream(i):
        def body(j, slot):
            p = mul(m.ln[0:rows, :], m.wt[slot], NN) + m.qb[pl.ds(2 * i + j, 1), :]
            p = p.astype(bf16).astype(f32)
            p = jnp.where(iota(p.shape, 1) < blk, p * HEAD_DIM**-0.5, p)
            m.qkvm[0:rows, at_cols(2 * i + j, 0, 3 * blk)] = p.astype(bf16)
            plan.tick(j, "qk", 2 * i, 2)

        src = lambda j: m.w1.at[i, :, tile(j, 3 * blk)]
        return stream(2, [(src, lambda slot: m.wt.at[slot])], m.s_sem, body)

    for i in (0, 1):
        begin, run = qkv_stream(i)
        begin()
        run()

        @pl.loop(0, 4)
        def _(j, i=i):
            attend_pair(m, 4 * i + j, rows, full, blk)
            plan.tick(j, "at", 4 * i, 4)

    def w_stream(ref, body):
        src = lambda j: ref.at[:, tile(j, 256), :]
        dst = lambda slot: m.wn.at[slot, :, :, pl.ds(0, ref.shape[2])]
        return stream(width // 256, [(src, dst)], m.s_sem, body)

    def out_cols(k):
        return (k % 2) * (2 * blk) + (k // 2) * blk

    def out_tile(j, slot):
        ds = tile(j, 256)
        total = m.xs[0:rows, ds].astype(f32) + m.vecs[2:3, ds]
        for k in range(4):
            own = m.qkvm[0:rows, k * n + 3 * blk : (k + 1) * n]
            total += mul(own, m.wn[slot, 0, :, out_cols(k) : out_cols(k) + blk], NT)
        m.mid[0:rows, ds] = total
        plan.tick(j, "out", 0, 4)

    out_src = lambda j: m.wo.at[tile(j, 256), :]
    out_dst = lambda slot: m.wn.at[slot, 0, :, pl.ds(0, 4 * blk)]
    begin, run = stream(width // 256, [(out_src, out_dst)], m.s_sem, out_tile)
    begin()
    m.lt[...] = m.logs[...].T[0 : m.lt.shape[0], :]
    run()
    mid_out = pltpu.make_async_copy(m.mid, m.mid_o, m.l_sem.at[0])
    mid_out.start()

    @pl.loop(0, full // ch)
    def _(r):
        rs = tile(r, ch)
        unit, _ = normalize(m.mid[rs, :])
        m.ln[rs, :] = (unit * m.vecs[3:4, :] + m.vecs[4:5, :]).astype(bf16)

    plan.after("ln2")
    turned(1)
    turn(m.ln, 2)
    plan.after("turn")

    def halves(ref, cs):
        return ref.at[pl.ds(0, full), cs], ref.at[pl.ds(full, full), cs]

    def act_copy(j):
        here, there = halves(m.big, tile(j, cols))
        return rcopy(here, there, m.a_s.at[j], m.a_r.at[j], w.sibling)

    def act_save(j):
        cs = tile(j, cols)
        return pltpu.make_async_copy(m.big.at[pl.ds(0, full), cs], m.act_o.at[:, cs], m.a_sem.at[0, j])

    def slope_save(j):
        return pltpu.make_async_copy(m.st.at[j % 2], m.slope_o.at[:, tile(j, cols)], m.a_sem.at[1, j])

    def up_stream(i):
        def body(j, slot):
            k = 4 * i + j
            cs = tile(k, cols)
            hidden = mul(m.ln[0:rows, :], m.wt[slot, :, 0:cols], NN) + m.ub[pl.ds(k, 1), :]
            phi = 0.5 * (1.0 + lax.erf(hidden * 0.7071067811865476))
            m.big[0:rows, cs] = (hidden * phi).astype(bf16)
            slope = phi + hidden * jnp.exp(-0.5 * hidden * hidden) * 0.3989422804014327

            @pl.when(k >= 2)
            def _():
                slope_save(k - 2).wait()

            m.st[k % 2, 0:rows, :] = slope.astype(bf16)
            for cp in (act_copy(k), act_save(k), slope_save(k)):
                cp.start()
            plan.tick(j, "up", 4 * i, 4)

        src = lambda j: m.w2.at[i, :, tile(j, cols)]
        return stream(4, [(src, lambda slot: m.wt.at[slot, :, pl.ds(0, cols)])], m.s_sem, body)

    def product(lhs, src):
        return mul(lhs[...].reshape(w.ring * share, 2 * full), m.big[:, src], NN).astype(bf16)

    m.st[:, zero_rows, :] = jnp.zeros((2, full - rows, cols), bf16)
    for i in (0, 1):
        begin, run = up_stream(i)
        begin()
        run()
        @pl.loop(0, 2)
        def _(j, i=i):
            for k in (0, 1):
                act_copy(4 * i + 2 * j + k).wait()
            m.part[i, :, :, tile(j, n)] = product(m.lhs3, tile(2 * i + j, n)).reshape(w.ring, share, n)
            plan.tick(j, "gw", 2 * i, 2)

    pl.semaphore_signal(m.clear, inc=1, device_id=w.sibling, device_id_type=MESH)

    def dh_copy(j):
        here, there = halves(m.big, tile(j, cols))
        return rcopy(here, there, m.h_s.at[j], m.h_r.at[j], w.sibling)

    def dh_stream(i):
        def body(j, slot):
            k = 4 * i + j
            d = mul(m.gr[0:rows, :], m.wt[slot, :, 0:cols], NN) * m.st[slot, 0:rows, :].astype(f32)
            d = d.astype(bf16)
            m.big[0:rows, tile(k, cols)] = d
            nat = (j // 2) * 4 + i * 2 + j % 2
            m.vsum[pl.ds(8 + nat // 2, 1), tile(nat % 2, cols)] = jnp.sum(d.astype(f32), axis=0, keepdims=True)
            dh_copy(k).start()
            plan.tick(j, "dh", 4 * i, 4)

        return stream(
            4,
            [
                (lambda j: m.w3.at[i, :, tile(j, cols)], lambda slot: m.wt.at[slot, :, pl.ds(0, cols)]),
                (lambda j: m.slope_o.at[:, tile(4 * i + j, cols)], lambda slot: m.st.at[slot]),
            ],
            m.s_sem,
            body,
        )

    for k in (6, 7):
        slope_save(jnp.int32(k)).wait()

    @pl.loop(0, 8)
    def _(j):
        act_save(j).wait()

    m.ln[zero_rows, :] = jnp.zeros((full - rows, width), bf16)
    pl.semaphore_wait(m.clear, 1)
    turned(2)

    def second_tile(j, slot):
        ds = tile(j, 256)
        m.acc[0:rows, ds] = mul(m.big[0:rows, 0 : 2 * n], m.wn[slot, 0], NT) + mul(
            m.big[0:rows, 2 * n :], m.wn[slot, 1], NT
        )
        plan.tick(j, "ds", 0, 4)

    for i in (0, 1):
        begin, run = dh_stream(i)
        begin()
        run()
        if i:
            begin, run = w_stream(m.w2, second_tile)
            begin()

        @pl.loop(0, 2)
        def _(j, i=i):
            for k in (0, 1):
                dh_copy(4 * i + 2 * j + k).wait()
            m.part[2 + i, :, :, tile(j, n)] = product(m.lhs2, tile(2 * i + j, n)).reshape(w.ring, share, n)
            plan.tick(j, "gu", 2 * i, 2)

    run()

    def mixed_tile(j, slot):
        m.ln[0:rows, tile(j, blk)] = mul(m.gr[0:rows, :], m.wt[slot, :, 0:blk], NN).astype(bf16)
        plan.tick(j, "mx", 0, 4)

    begin, run = stream(
        4,
        [(lambda j: m.wo.at[:, pl.ds(pl.multiple_of(out_cols(j), 128), blk)], lambda slot: m.wt.at[slot, :, pl.ds(0, blk)])],
        m.s_sem,
        mixed_tile,
    )
    begin()
    mid_out.wait()

    def fold(k, x):
        m.vacc[k] += jnp.sum(x.reshape(ch // 8, 8, width), axis=0)

    def norm_back(unit, scaled, gain, up):
        weighted = up * gain
        return scaled * (
            weighted
            - jnp.mean(weighted, axis=-1, keepdims=True)
            - unit * jnp.mean(weighted * unit, axis=-1, keepdims=True)
        )

    @pl.loop(0, full // ch)
    def _(r):
        rs = tile(r, ch)
        unit, scaled = normalize(m.mid[rs, :])
        up = m.acc[rs, :]
        grad = m.gr[rs, :].astype(f32)
        down = norm_back(unit, scaled, m.vecs[3:4, :], up) + grad
        m.mid[rs, :] = down
        m.gr[rs, :] = down.astype(bf16)
        fold(2, down)
        fold(3, up * unit)
        fold(4, up)
        fold(5, grad)

    plan.after("nb")
    turn(m.gr, 3)
    plan.after("tb")
    run()

    def lanes_mixed(k):
        return pl.ds(k * n + 3 * blk, blk)

    for k in range(4):
        m.big[0:full, lanes_mixed(k)] = m.qkvm[:, lanes_mixed(k)]
    turned(3)

    def mixed_copy(k):
        here, there = halves(m.big, lanes_mixed(k))
        return rcopy(here, there, m.x_s.at[k], m.x_r.at[k], w.sibling)

    for k in range(4):
        mixed_copy(k).start()

    def q_copy(k):
        here, there = halves(m.big, at_cols(k, 0, 3 * blk))
        return rcopy(here, there, m.q_s.at[k], m.q_r.at[k], w.sibling)

    def weights(i, part):
        @pl.loop(0, 2)
        def _(j):
            k = 2 * i + j
            q_copy(k).wait()
            grad = product(m.lhs1, at_cols(k, 0, 3 * blk))
            part[:, :, tile(j, 3 * blk)] = grad.reshape(w.ring, share, 3 * blk)
            plan.tick(j, "ga", 2 * i, 2)

    @pl.loop(0, width // 128)
    def _(j):
        attend_back(m, j, rows, full, blk)

        @pl.when(j % 2 == 1)
        def _():
            q_copy(j // 2).start()

        plan.tick(j, "ab", 0, 8)

        @pl.when(j == 1)
        def _():
            sums7[0].drain()
            for k in range(4):
                mixed_copy(k).wait()
                grad = product(m.lhs3, lanes_mixed(k))
                m.part[0, :, :, out_cols(k) : out_cols(k) + blk] = grad.reshape(w.ring, share, blk)
            plan.after("og")

        @pl.when(j == 4)
        def _():
            sums7[1].drain()
            weights(0, m.part.at[1])

    def first_tile(j, slot):
        total = jnp.zeros((rows, 256), f32)
        for k in range(4):
            lo = (k % 2) * (3 * blk)
            total += mul(m.big[0:rows, k * n : k * n + 3 * blk], m.wn[slot, k // 2, :, lo : lo + 3 * blk], NT)
        m.acc[0:rows, tile(j, 256)] = total
        plan.tick(j, "df", 0, 4)

    begin, run = w_stream(m.w1, first_tile)
    begin()
    weights(1, m.part5)
    act_in = pltpu.make_async_copy(m.act_o, m.big.at[pl.ds(full, full)], m.l_sem.at[1])
    act_in.start()
    run()

    def block_tile(j, slot):
        ds = tile(j, 256)
        act = m.big.at[pl.ds(full, rows)]
        m.acc[0:rows, ds] = mul(act[:, 0 : 2 * n], m.wn[slot, 0], NT) + mul(act[:, 2 * n :], m.wn[slot, 1], NT)
        plan.tick(j, "bo", 0, 4)

    begin, run = w_stream(m.w3, block_tile)
    begin()

    @pl.loop(0, full // ch)
    def _(r):
        rs = tile(r, ch)
        unit, scaled = normalize(m.xs[rs, :].astype(f32))
        up = m.acc[rs, :]
        m.mid[rs, :] += norm_back(unit, scaled, m.vecs[0:1, :], up)
        fold(0, up * unit)
        fold(1, up)

    m.vsum[0:6, :] = jnp.sum(m.vacc[...], axis=1)
    gt_out = pltpu.make_async_copy(m.mid.at[pl.ds(0, length)], m.gt, m.l_sem.at[3])
    gt_out.start()

    def sum_copy(s):
        return rcopy(m.vsum, m.vswap.at[s], m.b_s.at[s], m.b_r.at[s], flips[s])

    def sum_step(s):
        if s:
            sum_copy(s - 1).wait()
            m.vsum[...] += m.vswap[s - 1]
        if s < len(flips):
            sum_copy(s).start()

    sum_step(0)
    plan.after("ln1")
    act_in.wait()
    run()
    sum_step(1)
    plan.after("v1")
    gt_out.wait()
    mid_in = pltpu.make_async_copy(m.mid_o, m.mid, m.l_sem.at[4])
    mid_in.start()
    sum_step(2)
    plan.after("v2")
    mid_in.wait()

    @pl.loop(0, full // ch)
    def _(r):
        rs = tile(r, ch)
        m.xs[rs, :] = (m.rm[rs, 0:1].astype(f32) * (m.mid[rs, :] + m.acc[rs, :] + m.vecs[5:6, :])).astype(bf16)

    bo_out = pltpu.make_async_copy(m.xs.at[pl.ds(0, length)], m.bo, m.l_sem.at[0])
    bo_out.start()
    sum_step(3)
    plan.after("v3")
    sum_step(4)
    plan.after("v4")
    sum_step(5)
    outs = [
        pltpu.make_async_copy(m.vsum, m.gv, m.l_sem.at[1]),
        pltpu.make_async_copy(m.og, m.go, m.l_sem.at[2]),
    ]
    outs[0].start()
    plan.after("fin")
    outs[1].start()
    for g in gathers + sums7[2:]:
        g.drain()
    bo_out.wait()
    for cp in outs:
        cp.wait()


LAYER_PLAN = {
    "go": (200, 0),
    "pre0": (100, 1, 201, 300, 2),
    "pre1": (101, 3),
    "pre2": (102, 5, 4, 202, 6, 103, 7, 301, 203),
    "pre3": (104, 400, 204, 8, 9, 105, 10, 106, 302, 206),
    "at0": (108, 401, 107, 205, 600),
    "at1": (109,),
    "at2": (303,),
    "at3": (402, 110),
    "qk2": (208, 207, 500),
    "qk3": (209, 305),
    "at5": (501, 403),
    "at6": (304, 307),
    "at7": (502, 404, 406, 601, 306, 308, 309, 405, 210),
    "out3": (310, 503),
    "turn": (602,),
    "up0": (407,),
    "up2": (505,),
    "gw0": (603, 504, 408, 409, 507),
    "gw1": (700, 410),
    "up5": (506, 508, 605),
    "up6": (509, 701),
    "gw3": (800, 702, 604, 606, 703, 607, 510),
    "dh1": (801,),
    "dh3": (704, 705),
    "gu0": (802, 803, 608, 609),
    "gu1": (610, 706, 707, 900, 804),
    "gu2": (901, 806),
    "gu3": (902,),
    "ds0": (1000, 708, 709, 903),
    "ds3": (1001, 805),
    "tb": (808, 1002, 1003, 904, 905, 906, 710),
    "ab1": (807, 1004),
    "og": (1100, 907),
    "ab2": (1006, 1101, 809),
    "ab3": (1005,),
    "ab4": (810,),
    "ga1": (1200, 1102, 1104, 1103, 1007),
    "ab6": (1201, 908),
    "ab7": (1008, 1202, 1203),
    "ga3": (1300, 1105),
    "df0": (1204, 1205),
    "df1": (909, 1301, 1009, 1106, 1206, 1107),
    "df3": (1302, 1303),
    "bo0": (1304, 1305, 1207),
    "bo1": (1108,),
    "bo3": (1306, 1307, 1308, 1109, 910),
    "v3": (1208, 1209),
    "v4": (1309, 1210, 1010, 1110, 1310),
}


def layer(args, dp, length, width, n, share):
    rows, full = -(-length // 16) * 16, -(-length // 128) * 128
    cols, blk = n // 2, n // 4
    ring = dp // 2
    far = ring // 2
    depth = share * dp
    heads = width // HEAD_DIM
    outers = [128 * o for o in OUTER[7:]]
    a, b = max(outers[:4]), min(outers[:4])
    a5, b5 = outers[6], 3 * blk - outers[6]
    steps = dp.bit_length()
    V, dma = pltpu.VMEM, pltpu.SemaphoreType.DMA
    S = jax.ShapeDtypeStruct
    out = dict(
        w1=S((2, depth, 6 * blk), bf16),
        wo=S((depth, 4 * blk), bf16),
        w2=S((2, depth, 2 * n), bf16),
        w3=S((2, depth, 2 * n), bf16),
        mid_o=S((full, width), f32),
        act_o=S((full, 4 * n), bf16),
        slope_o=S((full, 4 * n), bf16),
        bo=S((length, width), bf16),
        gt=S((length, width), f32),
        go=S((3, share, 2 * n), f32),
        gv=S((16, width), f32),
    )
    scratch = dict(
        sh1=V((2, share, 3 * blk), bf16),
        iwv=V((3, share, cols), bf16),
        sixv=V((6, 1, share), bf16),
        ubv=V((2 * n // 128, 128), bf16),
        biasf=V((8, cols), f32),
        ibv=V((2, cols), bf16),
        vecf=V((8, 128), f32),
        packv=V((8, cols), bf16),
        tv=V((2, length), jnp.int32),
        row=V((8, full), f32),
        vec=V((8, 128), bf16),
        kb=V((full, 128), bf16),
        rm=V((full, 128), bf16),
        vbuf=V((2, 8, width), bf16),
        bbuf=V((2, 8, cols), bf16),
        vecs=V((8, width), f32),
        ub=V((8, cols), f32),
        qb=V((8, 3 * blk), f32),
        xs=V((full, width), bf16),
        gr=V((full, width), bf16),
        ln=V((full, width), bf16),
        qkvm=V((full, 4 * n), bf16),
        lt=V((heads, full), f32),
        mid=V((full, width), f32),
        acc=V((full, width), f32),
        big=V((2 * full, 4 * n), bf16),
        st=V((2, full, cols), bf16),
        turn=V((ring, 2, share, full), bf16),
        lhs1=V((ring, share, 2 * full), bf16),
        lhs2=V((ring, share, 2 * full), bf16),
        lhs3=V((ring, share, 2 * full), bf16),
        wt=V((2, depth, 3 * blk), bf16),
        wn=V((2, 2, 256, 2 * n), bf16),
        part=V((4, ring, share, 2 * n), bf16),
        ry=V((4, ring, share, a), bf16),
        rr=V((4, far, share, 2 * n - b), bf16),
        rl=V((4, far, share, 2 * n - b), bf16),
        rb=V((4, share, n - b), bf16),
        part5=V((ring, share, 6 * blk), bf16),
        ry5=V((ring, share, a5), bf16),
        rr5=V((far, share, a5 + 2 * b5), bf16),
        rl5=V((far, share, a5 + 2 * b5), bf16),
        rb5=V((share, b5), bf16),
        og=V((3, share, 2 * n), f32),
        vsum=V((16, width), f32),
        vacc=V((6, 8, width), f32),
        vswap=V((steps, 16, width), f32),
        ring_s=dma((7, 2 * (far + 1))),
        ring_r=dma((7, 2 * (far + 1))),
        y_s=dma((7, 2 * far + 1)),
        y_r=dma((7, 2 * far + 1)),
        c_s=dma((7, 4 * far + 2)),
        c_r=dma((7, 4 * far + 2)),
        k_sem=dma((7,)),
        sy_s=dma((7, ring + 1)),
        sy_r=dma((7, ring + 1)),
        sr_s=dma((7, 2 * far)),
        sr_r=dma((7, 2 * far)),
        v_s=dma((dp,)),
        v_r=dma((dp,)),
        b_s=dma((steps,)),
        b_r=dma((steps,)),
        l_sem=dma((7,)),
        x_sem=dma((6,)),
        s_sem=dma((4, 2)),
        t_sem=dma((4,)),
        t_s=dma((4,)),
        t_r=dma((4,)),
        a_s=dma((8,)),
        a_r=dma((8,)),
        a_sem=dma((2, 8)),
        h_s=dma((8,)),
        h_r=dma((8,)),
        q_s=dma((4,)),
        q_r=dma((4,)),
        x_s=dma((4,)),
        x_r=dma((4,)),
        clear=pltpu.SemaphoreType.REGULAR,
    )
    names = LAYER_IN + tuple(out) + tuple(scratch)
    hbm = pl.BlockSpec(memory_space=pl.ANY)
    specs = [pl.BlockSpec(memory_space=pltpu.SMEM) if k == "image" else hbm for k in LAYER_IN]
    got = pl.pallas_call(
        functools.partial(layer_kernel, dp, rows, names, LAYER_PLAN),
        out_shape=list(out.values()),
        in_specs=specs,
        out_specs=[hbm] * len(out),
        scratch_shapes=list(scratch.values()),
        compiler_params=pltpu.CompilerParams(collective_id=1, has_side_effects=True, vmem_limit_bytes=VM_LIMIT),
        name="layer",
    )(*args)
    return types.SimpleNamespace(**dict(zip(out, got)))


def place_kernel(bo, gt, go, gv, *refs):
    bo_o, gt_o, iw_o, ow_o, uw_o, dw_o, ib_o, ub_o = refs[:8]
    vec_o, (bov, gtv, g, vs, iwv, ibv, ubv, vecv, sem) = refs[8:14], refs[14:]
    d, t = lax.axis_index("dp"), lax.axis_index("tensor")
    share, wide = g.shape[1:]
    n, blk = wide // 2, wide // 8
    cols = 2 * blk
    ins = [
        pltpu.make_async_copy(go, g, sem.at[0]),
        pltpu.make_async_copy(gt, gtv, sem.at[1]),
        pltpu.make_async_copy(bo, bov, sem.at[2]),
        pltpu.make_async_copy(gv, vs, sem.at[3]),
    ]
    for cp in ins:
        cp.start()
    outs = []

    def send(src, dst):
        cp = pltpu.make_async_copy(src, dst, sem.at[4 + len(outs)])
        cp.start()
        outs.append(cp)

    ins[0].wait()
    send(g.at[1], uw_o)
    send(g.at[0], dw_o)
    for i in (0, 1):
        part = slice(i * blk, (i + 1) * blk)
        for s in range(3):
            at = (3 * i + s) * blk
            iwv[s, :, part] = g[2, :, at : at + blk]
    send(iwv, iw_o)
    send(g.at[2, :, pl.ds(6 * blk, cols)], ow_o)
    ins[1].wait()
    send(gtv, gt_o)
    ins[2].wait()
    send(bov, bo_o)
    ins[3].wait()
    ibv[...] = vs[6:8, pl.ds(pl.multiple_of(t * cols, 128), cols)]
    send(ibv, ib_o)
    width = vs.shape[1]
    per = width // 128
    half = wide // width
    up = jnp.where(t == 0, vs[8 : 8 + half, :], vs[8 + half : 8 + 2 * half, :])
    for r in range(wide // 128):
        lo = (r % per) * 128
        ubv[r : r + 1, :] = up[r // per : r // per + 1, lo : lo + 128]
    send(ubv, ub_o)
    own = vs[0:8, pl.ds(pl.multiple_of((d // 2) * 128, 128), 128)]
    own = jnp.where(d % 2 == 0, own, pltpu.roll(own, share, 1))
    for i in range(6):
        vecv[i] = own[i : i + 1, 0:share]
        send(vecv.at[i], vec_o[i])
    for cp in outs:
        cp.wait()


def place(r, share, n):
    S = jax.ShapeDtypeStruct
    length, width = r.gt.shape
    cols = n // 2
    hbm = pl.BlockSpec(memory_space=pl.ANY)
    out = [
        S((length, width), bf16),
        S((length, width), f32),
        S((3, share, cols), f32),
        S((share, cols), f32),
        S((share, 2 * n), f32),
        S((share, 2 * n), f32),
        S((2, cols), f32),
        S((2 * n // 128, 128), f32),
    ] + [S((1, share), f32)] * 6
    V = pltpu.VMEM
    return pl.pallas_call(
        place_kernel,
        out_shape=out,
        in_specs=[hbm] * 4,
        out_specs=[hbm] * 14,
        scratch_shapes=[
            V((length, width), bf16),
            V((length, width), f32),
            V((3, share, 2 * n), f32),
            V((16, width), f32),
            V((3, share, cols), f32),
            V((2, cols), f32),
            V((2 * n // 128, 128), f32),
            V((6, 1, share), f32),
            pltpu.SemaphoreType.DMA((18,)),
        ],
        compiler_params=pltpu.CompilerParams(vmem_limit_bytes=VM_LIMIT),
        name="place",
    )(r.bo, r.gt, r.go, r.gv)


def paired_device(
    tokens, cotangent, token_valid, image_valid, first_gain, first_shift, input_weight, input_bias, output_weight,
    output_bias, second_gain, second_shift, up_weight, up_bias, down_weight, down_bias,
):
    dp = lax.axis_size("dp")
    length, width = tokens.shape
    share, wide = up_weight.shape
    n = wide // 2
    vectors = (first_gain, first_shift, output_bias, second_gain, second_shift, down_bias)
    args = tuple(v.reshape(1, share) for v in vectors) + (
        up_bias.reshape(-1, 128),
        input_bias,
        input_weight.transpose(1, 0, 2),
        output_weight.T,
        up_weight,
        down_weight.T,
        tokens,
        cotangent,
        token_valid,
        image_valid,
    )
    r = layer(args, dp, length, width, n, share)
    block_out, grad_tokens, g_in, g_out, g_up, g_down, g_in_bias, g_up_bias, *g_vec = place(r, share, n)
    g_vec = [v.reshape(share) for v in g_vec]
    return (
        block_out,
        grad_tokens,
        g_vec[0],
        g_vec[1],
        g_in.transpose(1, 0, 2),
        g_in_bias,
        g_out.T,
        g_vec[2],
        g_vec[3],
        g_vec[4],
        g_up,
        g_up_bias.reshape(wide),
        g_down.T,
        g_vec[5],
    )


def solution(mesh):
    in_specs = (
        P(("dp", "tensor"), None),
        P(("dp", "tensor"), None),
        P("dp", None),
        P("dp"),
        P("dp"),
        P("dp"),
        P("dp", None, "tensor"),
        P(None, "tensor"),
        P("tensor", "dp"),
        P("dp"),
        P("dp"),
        P("dp"),
        P("dp", "tensor"),
        P("tensor"),
        P("tensor", "dp"),
        P("dp"),
    )
    out_specs = (
        P(("dp", "tensor"), None),
        P(("dp", "tensor"), None),
        P("dp"),
        P("dp"),
        P("dp", None, "tensor"),
        P(None, "tensor"),
        P("tensor", "dp"),
        P("dp"),
        P("dp"),
        P("dp"),
        P("dp", "tensor"),
        P("tensor"),
        P("tensor", "dp"),
        P("dp"),
    )
    ready = mesh.shape["tensor"] == 2 and mesh.shape["dp"] == 16
    body = paired_device if ready else general_device
    return jax.shard_map(
        body, mesh=mesh, in_specs=in_specs, out_specs=out_specs, check_vma=False
    )
```

```python
import functools
import types

import jax
import jax.numpy as jnp
from jax import lax
from jax.experimental import pallas as pl
from jax.experimental.pallas import tpu as pltpu
from jax.sharding import PartitionSpec as P

HEAD_DIM = 64
MESH = pl.DeviceIdType.MESH
f32 = jnp.float32
bf16 = jnp.bfloat16
NN, NT, TN = ((1,), (0,)), ((1,), (1,)), ((0,), (0,))
VM_LIMIT = 127 << 19


def layer_norm(inputs, gain, shift):
    center = inputs - jnp.mean(inputs, axis=-1, keepdims=True)
    spread = jnp.mean(center * center, axis=-1, keepdims=True)
    return center * lax.rsqrt(spread + 1e-06) * gain + shift


def norm_backward(inputs, gain, upstream):
    center = inputs - jnp.mean(inputs, axis=-1, keepdims=True)
    spread = jnp.mean(center * center, axis=-1, keepdims=True)
    scaled = lax.rsqrt(spread + 1e-06)
    unit = center * scaled
    weighted = upstream * gain
    grad_inputs = scaled * (
        weighted
        - jnp.mean(weighted, axis=-1, keepdims=True)
        - unit * jnp.mean(weighted * unit, axis=-1, keepdims=True)
    )
    return (grad_inputs, jnp.sum(upstream * unit, axis=0), jnp.sum(upstream, axis=0))


def gelu_slope(hidden):
    return (
        0.5 * (1.0 + lax.erf(hidden * 0.7071067811865476))
        + hidden * jnp.exp(-0.5 * hidden * hidden) * 0.3989422804014327
    )


def general_device(
    tokens,
    cotangent,
    token_valid,
    image_valid,
    first_gain,
    first_shift,
    input_weight,
    input_bias,
    output_weight,
    output_bias,
    second_gain,
    second_shift,
    up_weight,
    up_bias,
    down_weight,
    down_bias,
):
    f32 = jnp.float32
    bf16 = jnp.bfloat16
    gathered = (
        lax.all_gather(first_gain, "dp", axis=0, tiled=True),
        lax.all_gather(first_shift, "dp", axis=0, tiled=True),
        lax.all_gather(input_weight, "dp", axis=0, tiled=True),
        lax.all_gather(output_weight, "dp", axis=1, tiled=True),
        lax.all_gather(output_bias, "dp", axis=0, tiled=True),
        lax.all_gather(second_gain, "dp", axis=0, tiled=True),
        lax.all_gather(second_shift, "dp", axis=0, tiled=True),
        lax.all_gather(up_weight, "dp", axis=0, tiled=True),
        lax.all_gather(down_weight, "dp", axis=1, tiled=True),
        lax.all_gather(down_bias, "dp", axis=0, tiled=True),
    )
    (
        gain_one,
        shift_one,
        in_full,
        out_full,
        out_shift,
        gain_two,
        shift_two,
        up_full,
        down_full,
        down_shift,
    ) = gathered
    gain_one = gain_one.astype(f32)
    shift_one = shift_one.astype(f32)
    out_shift = out_shift.astype(f32)
    gain_two = gain_two.astype(f32)
    shift_two = shift_two.astype(f32)
    down_shift = down_shift.astype(f32)
    tensor_at = lax.axis_index("tensor")
    groups = lax.axis_size("tensor")
    own_rows = tokens.shape[0]
    width = tokens.shape[1]
    length = token_valid.shape[1]
    positions = lax.broadcasted_iota(jnp.int32, token_valid.shape, 1)
    key_ok = (token_valid > 0) | (positions == 0)
    mask_all = (token_valid * image_valid[:, None]).astype(f32).reshape(-1)
    row_mask = lax.dynamic_slice_in_dim(mask_all, tensor_at * own_rows, own_rows)[:, None]
    images = token_valid.shape[0]
    local_width = in_full.shape[2]
    local_heads = local_width // HEAD_DIM
    hidden_width = up_full.shape[1]
    scale = HEAD_DIM ** (-0.5)
    head_shape = (images, length, local_heads, HEAD_DIM)
    inputs = tokens.astype(f32)
    first_own = layer_norm(inputs, gain_one, shift_one).astype(bf16)
    first_all = lax.all_gather(first_own, "tensor", axis=0, tiled=True)
    project = jnp.einsum("rd,dce->rce", first_all, in_full, preferred_element_type=f32)
    bias_in = input_bias.astype(f32)
    queries = (project[:, 0] + bias_in[0]).astype(bf16).reshape(head_shape)
    keyset = project[:, 1].astype(bf16).reshape(head_shape)
    values = (project[:, 2] + bias_in[1]).astype(bf16).reshape(head_shape)

    def scores_of(query_img, key_img, ok_img):
        scores = jnp.einsum("qhe,khe->hqk", query_img, key_img, preferred_element_type=f32) * scale
        return jnp.where(ok_img[None, None, :], scores, -1000000000.0)

    def attend(pieces):
        query_img, key_img, value_img, ok_img = pieces
        scores = scores_of(query_img, key_img, ok_img)
        highest = jnp.max(scores, axis=-1, keepdims=True)
        log_total = highest + jnp.log(jnp.sum(jnp.exp(scores - highest), axis=-1, keepdims=True))
        attn_probs = jnp.exp(scores - log_total).astype(bf16)
        mixed_img = jnp.einsum("hqk,khe->qhe", attn_probs, value_img, preferred_element_type=f32)
        return (mixed_img.astype(bf16), log_total)

    mixed, log_totals = lax.map(attend, (queries, keyset, values, key_ok))
    mixed_rows = mixed.reshape(images * length, local_width)
    attended = lax.psum_scatter(
        jnp.dot(mixed_rows, out_full, preferred_element_type=f32).astype(jnp.bfloat16),
        "tensor",
        scatter_dimension=0,
        tiled=True,
    ).astype(jnp.float32)
    middle = inputs + attended + out_shift
    second_own = layer_norm(middle, gain_two, shift_two).astype(bf16)
    second_all = lax.all_gather(second_own, "tensor", axis=0, tiled=True)
    hidden = jnp.dot(second_all, up_full, preferred_element_type=f32) + up_bias.astype(f32)
    active = jax.nn.gelu(hidden, approximate=False).astype(bf16)
    lifted = lax.psum_scatter(
        jnp.dot(active, down_full, preferred_element_type=f32).astype(jnp.bfloat16),
        "tensor",
        scatter_dimension=0,
        tiled=True,
    ).astype(jnp.float32)
    block_out = (row_mask * (middle + lifted + down_shift)).astype(bf16)
    grad_last = row_mask * cotangent.astype(f32)
    first_all, second_all = (
        lax.all_gather(first_own, "tensor", axis=0, tiled=True),
        lax.all_gather(second_own, "tensor", axis=0, tiled=True),
    )
    grad_lift = lax.all_gather(grad_last.astype(bf16), "tensor", axis=0, tiled=True)
    grad_active = jnp.einsum("rd,fd->rf", grad_lift, down_full, preferred_element_type=f32)
    grad_hidden = (grad_active * gelu_slope(hidden)).astype(bf16)
    grad_down = jnp.einsum("rf,rd->fd", active, grad_lift, preferred_element_type=f32)
    grad_up = jnp.einsum("rd,rf->df", second_all, grad_hidden, preferred_element_type=f32)
    grad_up_bias = jnp.sum(grad_hidden.astype(f32), axis=0)
    grad_second = lax.psum_scatter(
        jnp.einsum("rf,df->rd", grad_hidden, up_full, preferred_element_type=f32).astype(
            jnp.bfloat16
        ),
        "tensor",
        scatter_dimension=0,
        tiled=True,
    ).astype(jnp.float32)
    grad_middle, grad_gain_two, grad_shift_two = norm_backward(middle, gain_two, grad_second)
    grad_middle = grad_middle + grad_last
    grad_mid_all = lax.all_gather(grad_middle.astype(bf16), "tensor", axis=0, tiled=True)
    grad_mixed = jnp.einsum("rd,ed->re", grad_mid_all, out_full, preferred_element_type=f32).astype(
        bf16
    )
    grad_out_weight = jnp.einsum("re,rd->ed", mixed_rows, grad_mid_all, preferred_element_type=f32)

    def attend_back(pieces):
        query_img, key_img, value_img, ok_img, total_img, grad_img = pieces
        scores = scores_of(query_img, key_img, ok_img)
        attn_probs = jnp.exp(scores - total_img)
        grad_values = jnp.einsum(
            "hqk,qhe->khe", attn_probs.astype(bf16), grad_img, preferred_element_type=f32
        )
        grad_probs = jnp.einsum("qhe,khe->hqk", grad_img, value_img, preferred_element_type=f32)
        grad_scores = (
            attn_probs * (grad_probs - jnp.sum(attn_probs * grad_probs, axis=-1, keepdims=True))
        ).astype(bf16)
        grad_queries = (
            jnp.einsum("hqk,khe->qhe", grad_scores, key_img, preferred_element_type=f32) * scale
        )
        grad_keys = (
            jnp.einsum("hqk,qhe->khe", grad_scores, query_img, preferred_element_type=f32) * scale
        )
        return jnp.stack([grad_queries, grad_keys, grad_values], axis=1).astype(bf16)

    grad_project = lax.map(
        attend_back, (queries, keyset, values, key_ok, log_totals, grad_mixed.reshape(head_shape))
    )
    grad_project = grad_project.reshape(images * length, 3, local_width)
    grad_in_weight = jnp.einsum("rd,rce->dce", first_all, grad_project, preferred_element_type=f32)
    grad_in_bias = jnp.sum(grad_project[:, 0::2].astype(f32), axis=0)
    grad_first = lax.psum_scatter(
        jnp.einsum("rce,dce->rd", grad_project, in_full, preferred_element_type=f32).astype(
            jnp.bfloat16
        ),
        "tensor",
        scatter_dimension=0,
        tiled=True,
    ).astype(jnp.float32)
    grad_inputs, grad_gain_one, grad_shift_one = norm_backward(inputs, gain_one, grad_first)
    grad_inputs = grad_inputs + grad_middle
    grad_in_own, grad_out_own, grad_up_own, grad_down_own = (
        lax.psum_scatter(
            grad_in_weight.astype(jnp.bfloat16), "dp", scatter_dimension=0, tiled=True
        ).astype(jnp.float32),
        lax.psum_scatter(
            grad_out_weight.astype(jnp.bfloat16), "dp", scatter_dimension=1, tiled=True
        ).astype(jnp.float32),
        lax.psum_scatter(
            grad_up.astype(jnp.bfloat16), "dp", scatter_dimension=0, tiled=True
        ).astype(jnp.float32),
        lax.psum_scatter(
            grad_down.astype(jnp.bfloat16), "dp", scatter_dimension=1, tiled=True
        ).astype(jnp.float32),
    )
    vectors = jnp.stack(
        [
            grad_gain_one,
            grad_shift_one,
            jnp.sum(grad_middle, axis=0),
            grad_gain_two,
            grad_shift_two,
            jnp.sum(grad_last, axis=0),
        ]
    )
    bias_share = input_bias.shape[1]
    up_share = up_bias.shape[0]
    placed_bias = lax.dynamic_update_slice(
        jnp.zeros((2, width), f32), grad_in_bias, (0, tensor_at * local_width)
    )
    placed_up = lax.dynamic_update_slice(
        jnp.zeros((hidden_width * groups,), f32), grad_up_bias, (tensor_at * hidden_width,)
    )
    vectors, placed_bias, placed_up = lax.psum((vectors, placed_bias, placed_up), ("dp", "tensor"))
    share = first_gain.shape[0]
    dp_at = lax.axis_index("dp")
    vectors = lax.dynamic_slice_in_dim(vectors, dp_at * share, share, 1)
    bias_own = lax.dynamic_slice_in_dim(placed_bias, tensor_at * bias_share, bias_share, 1)
    up_bias_own = lax.dynamic_slice_in_dim(placed_up, tensor_at * up_share, up_share, 0)
    return (
        block_out,
        grad_inputs,
        vectors[0],
        vectors[1],
        grad_in_own,
        bias_own,
        grad_out_own,
        vectors[2],
        vectors[3],
        vectors[4],
        grad_up_own,
        up_bias_own,
        grad_down_own,
        vectors[5],
    )


def mul(a, b, dims):
    return lax.dot_general(a, b, (dims, ((), ())), preferred_element_type=f32)


def iota(shape, axis):
    return lax.broadcasted_iota(jnp.int32, shape, axis)


def tile(j, size):
    return pl.ds(pl.multiple_of(j * size, size), size)


class Place:
    def __init__(self, dp):
        d = lax.axis_index("dp")
        t = lax.axis_index("tensor")
        ring = dp // 2
        self.dp, self.d, self.t, self.ring, self.far = dp, d, t, ring, ring // 2
        self.chip, self.core = d // 2, d % 2
        self.pos = jnp.where(self.chip % 2 == 0, self.chip // 2, ring - 1 - self.chip // 2)
        self.right = (self.chip_at(1) * 2 + self.core, t)
        self.left = (self.chip_at(-1) * 2 + self.core, t)
        self.across = (d, 1 - t)
        self.sibling = (d + 1 - 2 * self.core, t)

    def chip_at(self, offset):
        ring = self.ring
        spot = (self.pos + offset + ring) % ring
        return jnp.where(spot < ring // 2, 2 * spot, 2 * (ring - 1 - spot) + 1)


class Columns:
    def __init__(self, w, n, a):
        t, b = w.t, n - a
        self.n, self.a, self.b = n, a, b
        self.own = (pl.multiple_of(t * n, 128), n)
        self.other = (pl.multiple_of((1 - t) * n, 128), n)
        self.ring = (pl.multiple_of(t * a, 128), 2 * n - a)
        self.mine_a = (pl.multiple_of(t * (2 * n - a), 128), a)
        self.their_a = (pl.multiple_of((1 - t) * (2 * n - a), 128), a)
        self.their_b = (pl.multiple_of(n - t * b, 128), b)
        self.mine_b = (pl.multiple_of(n - (1 - t) * b, 128), b)


OUTER = (4, 3, 2, 5, 4, 5, 4, 4, 4, 4, 5, 3, 4, 4)


def greet(targets):
    bar = pltpu.get_barrier_semaphore()
    for a in targets:
        pl.semaphore_signal(bar, inc=1, device_id=a, device_id_type=MESH)
    pl.semaphore_wait(bar, len(targets))


def rcopy(src, dst, send, recv, dev):
    return pltpu.make_async_remote_copy(
        src_ref=src, dst_ref=dst, send_sem=send, recv_sem=recv, device_id=dev, device_id_type=MESH
    )


class Gather:
    def __init__(self, w, g, shard, full, sems):
        self.w, self.g, self.shard, self.full, self.sems = w, g, shard, full, sems
        self.rows, n = shard.shape
        self.cols = Columns(w, n, 128 * OUTER[g])

    def block(self, offset, cols, span=None):
        w = self.w
        lo, size = span or (0, self.rows)
        base = w.chip_at(offset) * (2 * self.rows) + w.core * self.rows + lo
        return self.full.at[pl.ds(pl.multiple_of(base, 16), size), pl.ds(cols[0], cols[1])]

    def span(self, s, dirn):
        half = self.rows // 2
        return (0, self.rows) if s < self.w.far else (dirn * half, half)

    def off(self, s, dirn):
        return s if dirn else -s

    def make(self, kind, src, dst, k, dev):
        send, recv = self.sems[kind]
        return rcopy(src, dst, send.at[self.g, k], recv.at[self.g, k], dev)

    def y(self, s, dirn):
        if s == 0:
            return self.make("y", self.shard, self.block(0, self.cols.own), 0, self.w.across)
        ref = self.block(self.off(s, dirn), self.cols.mine_a, self.span(s, dirn))
        return self.make("y", ref, ref, 2 * s - 1 + dirn, self.w.across)

    def ring(self, s, dirn, part=0):
        dev = self.w.left if dirn else self.w.right
        k = dirn * (self.w.far + 1)
        if s == 1 and part == 0:
            return self.make("r", self.shard, self.block(0, self.cols.own), k, dev)
        if s == 1:
            ref = self.block(0, self.cols.their_b)
            return self.make("r", ref, ref, k + 1, dev)
        ref = self.block(self.off(s - 1, dirn), self.cols.ring, self.span(s, dirn))
        return self.make("r", ref, ref, k + s, dev)

    def sib(self, k):
        w = self.w
        if k == 0:
            src, dst = self.shard, self.block(0, self.cols.own)
        elif k == 1:
            src = dst = self.block(0, self.cols.other)
        else:
            which, rest = divmod(k - 2, 2 * w.far)
            s, dirn = rest // 2 + 1, rest % 2
            cols = self.cols.their_a if which else self.cols.ring
            src = dst = self.block(self.off(s, dirn), cols, self.span(s, dirn))
        return self.make("c", src, dst, k, w.sibling)

    def keep(self):
        return pltpu.make_async_copy(self.shard, self.block(0, self.cols.own), self.sems["k"].at[self.g])

    def S(self):
        self.y(0, 0).start()
        self.ring(1, 0).start()
        self.ring(1, 1).start()
        self.sib(0).start()
        self.keep().start()

    def Y(self):
        self.y(0, 0).wait_recv()
        self.ring(1, 0, 1).start()
        self.ring(1, 1, 1).start()
        self.sib(1).start()

    def h(self, s):
        for dirn in (0, 1):
            self.ring(s, dirn).wait_recv()
            if s == 1:
                self.ring(s, dirn, 1).wait_recv()
            if s < self.w.far:
                self.ring(s + 1, dirn).start()
            self.y(s, dirn).start()
            self.sib(2 * s + dirn).start()

    def c(self, s):
        for dirn in (0, 1):
            self.y(s, dirn).wait_recv()
            self.sib(2 + 2 * self.w.far + 2 * (s - 1) + dirn).start()

    def events(self):
        h, c = (lambda s: functools.partial(self.h, s)), (lambda s: functools.partial(self.c, s))
        return [self.S, self.Y, h(1), h(2), c(1), h(3), c(2), h(4), c(3), c(4), self.E]

    def E(self):
        for k in range(2 + 4 * self.w.far):
            self.sib(k).wait()
        self.keep().wait()

    def drain(self):
        far = self.w.far
        self.y(0, 0).wait_send()
        for dirn in (0, 1):
            self.ring(1, dirn).wait_send()
            self.ring(1, dirn, 1).wait_send()
            for s in range(1, far + 1):
                self.y(s, dirn).wait_send()
                if s > 1:
                    self.ring(s, dirn).wait_send()


class Scatter:
    def __init__(self, w, g, part, ry, rr, rl, rb, out, sems):
        self.w, self.g, self.part, self.sems, self.out = w, g, part, sems, out
        self.rows, n = part.shape[1], part.shape[2] // 2
        self.cols = c = Columns(w, n, 128 * OUTER[7 + g])
        self.ry = ry.at[:, :, pl.ds(0, c.a)]
        self.rr = rr.at[:, :, pl.ds(0, 2 * n - c.a)]
        self.rl = rl.at[:, :, pl.ds(0, 2 * n - c.a)]
        self.rb = rb.at[:, pl.ds(0, c.b)]
        far = w.far
        self.order = [far] + [k * sign for k in range(far - 1, 0, -1) for sign in (1, -1)] + [0]

    def make(self, kind, src, dst, k, dev):
        send, recv = self.sems[kind]
        return rcopy(src, dst, send.at[self.g, k], recv.at[self.g, k], dev)

    def cross(self, k):
        w = self.w
        chip = w.chip_at(k)
        src = self.part.at[chip, :, pl.ds(*self.cols.their_a)]
        return self.make("y", src, self.ry.at[chip], self.order.index(k), w.across)

    def ring(self, s, dirn):
        w = self.w
        chip = w.chip_at(s - w.far if dirn else w.far - s)
        half = self.rows // 2
        span = pl.ds(dirn * half, half) if s == 0 else pl.ds(0, self.rows)
        src = self.part.at[chip, span, pl.ds(*self.cols.ring)]
        dst = (self.rl if dirn else self.rr).at[s, span]
        return self.make("r", src, dst, dirn * w.far + s, w.left if dirn else w.right)

    def swap(self):
        w = self.w
        src = self.part.at[w.chip_at(0), :, pl.ds(*self.cols.their_b)]
        return self.make("y", src, self.rb, len(self.order), w.across)

    def add(self, k, lo, size, cols, other):
        chip = self.w.chip_at(k)
        part = self.part
        ch = 16

        @pl.loop(0, size // ch)
        def _(r):
            rs = pl.ds(pl.multiple_of(lo + r * ch, ch), ch)
            cs = pl.ds(cols[0], cols[1])
            part[chip, rs, cs] = (part[chip, rs, cs].astype(f32) + other[rs, :].astype(f32)).astype(bf16)

    def events(self):
        s, t = (lambda k: functools.partial(self.s, k)), (lambda k: functools.partial(self.t, k))
        return [self.A, self.L, t(3), s(1), t(2), s(2), t(1), s(3), t(0), self.F, self.Z]

    def both(self, k):
        return (k, -k) if k else (0,)

    def A(self):
        for k in (self.w.far, self.w.far - 1, 1 - self.w.far):
            self.cross(k).start()

    def take(self, k):
        self.cross(k).wait_recv()
        self.add(k, 0, self.rows, self.cols.mine_a, self.ry.at[self.w.chip_at(k)])

    def L(self):
        self.cross(self.w.far).wait_recv()
        for k in self.both(self.w.far - 2):
            self.cross(k).start()
        self.add(self.w.far, 0, self.rows, self.cols.mine_a, self.ry.at[self.w.chip_at(self.w.far)])
        self.ring(0, 0).start()
        self.ring(0, 1).start()

    def t(self, k):
        for i in self.both(k):
            self.take(i)
        if k > 1:
            for i in self.both(k - 2):
                self.cross(i).start()

    def s(self, s):
        far, half = self.w.far, self.rows // 2
        for dirn in (0, 1):
            self.ring(s - 1, dirn).wait_recv()
            k = s - far if dirn else far - s
            got = (self.rl if dirn else self.rr).at[s - 1]
            lo, size = (dirn * half, half) if s == 1 else (0, self.rows)
            self.add(k, lo, size, self.cols.ring, got)
            self.ring(s, dirn).start()

    def F(self):
        far = self.w.far
        for dirn in (0, 1):
            self.ring(far - 1, dirn).wait_recv()
            self.add(0, 0, self.rows, self.cols.ring, (self.rl if dirn else self.rr).at[far - 1])
        self.swap().start()

    def Z(self):
        self.swap().wait_recv()
        self.add(0, 0, self.rows, self.cols.mine_b, self.rb)
        chip = self.w.chip_at(0)
        self.out[...] = self.part[chip, :, pl.ds(*self.cols.own)].astype(f32)

    def drain(self):
        for k in self.order:
            self.cross(k).wait_send()
        for s in range(self.w.far):
            self.ring(s, 0).wait_send()
            self.ring(s, 1).wait_send()
        self.swap().wait_send()


class Plan:
    def __init__(self, groups, table):
        self.events, self.table = [g.events() for g in groups], table

    def after(self, name):
        for code in self.table.get(name, ()):
            self.events[code // 100][code % 100]()

    def tick(self, j, name, first, count):
        for k in range(count):
            at = name + str(first + k)
            if at in self.table:

                @pl.when(j == k)
                def _(at=at):
                    self.after(at)


def stream(count, parts, sem, body, begun=False):
    def copies(j):
        slot = lax.rem(j, 2)
        return [pltpu.make_async_copy(src(j), dst(slot), sem.at[i, slot]) for i, (src, dst) in enumerate(parts)]

    def begin():
        for cp in copies(jnp.int32(0)):
            cp.start()

    def run():
        @pl.loop(0, count)
        def _(j):
            @pl.when(j + 1 < count)
            def _():
                for cp in copies(j + 1):
                    cp.start()

            for cp in copies(j):
                cp.wait()
            body(j, lax.rem(j, 2))

    return begin, run


def normalize(x):
    center = x - jnp.mean(x, axis=-1, keepdims=True)
    scaled = lax.rsqrt(jnp.mean(center * center, axis=-1, keepdims=True) + 1e-06)
    return center * scaled, scaled


def lanes_of(pair, blk):
    base = (pair // 2) * (4 * blk) + (pair % 2) * 128
    return [pl.ds(pl.multiple_of(base + s * blk, 128), 128) for s in range(4)]


def attend_pair(m, i, rows, full, blk):
    qs, ks, vs, ms = lanes_of(i, blk)
    q2, k2, v2 = m.qkvm[0:rows, qs], m.qkvm[:, ks], m.qkvm[:, vs]
    lq, lk = iota((rows, 128), 1), iota((full, 128), 1)
    outs = []
    logs = m.logs[0:rows, :]
    for h in (0, 1):
        spare = 64 * (1 - h)
        own_q = (lq < 64) if h == 0 else (lq >= 64)
        own_k = (lk < 64) if h == 0 else (lk >= 64)
        qh = jnp.where(own_q, q2, jnp.where(lq == spare, 1.0, 0.0).astype(bf16))
        kh = jnp.where(lk == spare, m.kb[...], k2)
        scores = mul(qh, kh, NT)
        top = jnp.max(scores, axis=1, keepdims=True)
        probs = jnp.exp(scores - top).astype(bf16)
        out = mul(probs, jnp.where(own_k, v2, jnp.ones_like(v2)), NN)
        turned = pltpu.roll(out, 64, 1)
        outs.append(out / turned)
        total = jnp.where(own_q, turned, out)
        logs = jnp.where(lq == 2 * i + h, top + jnp.log(total), logs)
    m.logs[0:rows, :] = logs
    m.qkvm[0:rows, ms] = jnp.where(lq < 64, outs[0], outs[1]).astype(bf16)


def attend_back(m, i, rows, full, blk):
    qs, ks, vs, ms = lanes_of(i, blk)
    q2, do2 = m.qkvm[:, qs], m.ln[:, tile(i, 128)]
    k2, v2 = m.qkvm[0:rows, ks], m.qkvm[0:rows, vs]
    lq, lk = iota((full, 128), 1), iota((rows, 128), 1)
    both = (do2.astype(f32) * m.qkvm[:, ms].astype(f32)).T
    dqs, dks, dvs = [], [], []
    for h in (0, 1):
        spare = 64 * (1 - h)
        own_q = (lq < 64) if h == 0 else (lq >= 64)
        own_k = (lk < 64) if h == 0 else (lk >= 64)
        qh = jnp.where(own_q, q2, jnp.where(lq == spare, 1.0, 0.0).astype(bf16))
        kh = jnp.where(lk == spare, m.kb[0:rows, :], k2)
        probs = jnp.exp(mul(kh, qh, NT) - m.lt[pl.ds(2 * i + h, 1), :])
        dvs.append(mul(probs.astype(bf16), do2, NN))
        dprobs = mul(jnp.where(own_k, v2, jnp.zeros_like(v2)), do2, NT)
        inner = jnp.sum(both[64 * h : 64 * h + 64, :], axis=0, keepdims=True)
        ds = (probs * (dprobs - inner)).astype(bf16)
        dks.append(mul(ds, q2, NN))
        dqs.append(mul(ds, k2, TN))
    dv = jnp.where(lk < 64, dvs[0], dvs[1]).astype(bf16)
    dk = jnp.where(lk < 64, dks[0], dks[1]).astype(bf16)
    dq = (jnp.where(lq < 64, dqs[0], dqs[1]) * HEAD_DIM**-0.5).astype(bf16)
    m.big[0:full, qs] = dq
    m.big[0:rows, ks] = dk
    m.big[0:rows, vs] = dv
    at = ((i // 2) % 2) * (2 * blk) + (i // 4) * blk + (i % 2) * 128
    ns = pl.ds(pl.multiple_of(at, 128), 128)
    m.vsum[6:7, ns] = jnp.sum(dq.astype(f32), axis=0, keepdims=True)
    m.vsum[7:8, ns] = jnp.sum(dv.astype(f32), axis=0, keepdims=True)


LAYER_IN = ("v0", "v1", "v2", "v3", "v4", "v5", "ubias", "ibias", "iw", "ow", "uw", "dw", "tok", "cot", "valid", "image")


def layer_kernel(dp, rows, names, table, *refs):
    m = types.SimpleNamespace(**dict(zip(names, refs)))
    n = m.uw.shape[1] // 2
    w = Place(dp)
    length, width = m.tok.shape
    full = m.qkvm.shape[0]
    share = m.sh1.shape[1]
    cols, blk = n // 2, n // 4
    ch = 128
    sems = {"r": (m.ring_s, m.ring_r), "y": (m.y_s, m.y_r), "c": (m.c_s, m.c_r), "k": m.k_sem}
    groups = [Gather(w, i, m.sh1.at[i], m.w1.at[i], sems) for i in (0, 1)]
    groups.append(Gather(w, 2, m.ow, m.wo, sems))
    groups += [Gather(w, 3 + i, m.uw.at[:, pl.ds(i * n, n)], m.w2.at[i], sems) for i in (0, 1)]
    groups += [Gather(w, 5 + i, m.dw.at[:, pl.ds(i * n, n)], m.w3.at[i], sems) for i in (0, 1)]
    sums = {"y": (m.sy_s, m.sy_r), "r": (m.sr_s, m.sr_r)}
    slots = [tuple(ref.at[i] for ref in (m.part, m.ry, m.rr, m.rl, m.rb)) for i in range(4)]
    slots.append((m.part5, m.ry5, m.rr5, m.rl5, m.rb5))
    wide = (n, n, n, n, 2 * blk, 3 * blk, 3 * blk)
    lefts = (0, n, 0, n, 6 * blk, 0, 3 * blk)
    for g in range(7):
        part, *rest = slots[(0, 1, 2, 3, 0, 1, 4)[g]]
        part = part.at[:, :, pl.ds(0, 2 * wide[g])]
        where = m.og.at[(0, 0, 1, 1, 2, 2, 2)[g], :, pl.ds(lefts[g], wide[g])]
        groups.append(Scatter(w, g, part, *rest, where, sums))
    plan = Plan(groups, table)
    gathers, sums7 = groups[:7], groups[7:]

    def flip(k):
        return (w.d + k - 2 * k * ((w.d // k) % 2), w.t)

    flips = [w.across]
    k = 1
    while k < dp:
        flips.append(flip(k))
        k *= 2

    loads = [
        pltpu.make_async_copy(src, dst, m.l_sem.at[i])
        for i, (src, dst) in enumerate(
            (
                (m.iw, m.iwv),
                (m.ubias, m.ubv),
                (m.ibias, m.ibv),
                (m.tok, m.xs.at[pl.ds(0, length)]),
                (m.cot, m.gr.at[pl.ds(0, length)]),
                (m.valid, m.tv),
            )
        )
    ]
    loads += [
        pltpu.make_async_copy(src, m.sixv.at[i], m.x_sem.at[i])
        for i, src in enumerate((m.v0, m.v1, m.v2, m.v3, m.v4, m.v5))
    ]
    for cp in loads:
        cp.start()
    peers = [(lax.rem(w.d + i, dp), w.t) for i in range(1, dp)] + [w.across]
    bar = pltpu.get_barrier_semaphore()
    for a in peers:
        pl.semaphore_signal(bar, inc=1, device_id=a, device_id_type=MESH)
    loads[0].wait()
    for i in (0, 1):
        part = slice(i * blk, (i + 1) * blk)
        for s in range(3):
            m.sh1[i, :, s * blk : (s + 1) * blk] = m.iwv[s, :, part]
    pl.semaphore_wait(bar, len(peers))
    plan.after("go")
    for cp in loads[1:3] + loads[6:]:
        cp.wait()
    spot = pl.ds(pl.multiple_of(w.chip * 128, 128), 128)
    m.vecf[...] = jnp.zeros((8, 128), f32)
    for i in range(6):
        m.vecf[i : i + 1, 0:share] = m.sixv[i].astype(f32)
    vec = m.vecf[...]
    vec = jnp.where(w.core == 0, vec, pltpu.roll(vec, share, 1))
    m.biasf[...] = jnp.zeros(m.biasf.shape, f32)
    ub = m.ubv[...].astype(f32)
    for r in range(4 * cols // 128):
        q = r * 128 // cols
        lo = r * 128 - q * cols
        m.biasf[q : q + 1, lo : lo + 128] = ub[r : r + 1, :]
    m.biasf[4:6, :] = m.ibv[...].astype(f32)
    m.packv[...] = m.biasf[...].astype(bf16)
    m.vec[...] = vec.astype(bf16)

    def vec_copy(i):
        return rcopy(m.vec, m.vbuf.at[w.core, :, spot], m.v_s.at[i], m.v_r.at[i], peers[i])

    bias_copy = rcopy(m.packv, m.bbuf.at[w.t], m.v_s.at[dp - 1], m.v_r.at[dp - 1], w.across)
    for i in range(dp - 1):
        vec_copy(i).start()
    bias_copy.start()
    m.vbuf[w.core, :, spot] = m.vec[...]
    m.bbuf[w.t] = m.packv[...]
    plan.after("pre0")
    zero_rows = pl.ds(rows, full - rows)
    m.qkvm[zero_rows, :] = jnp.zeros((full - rows, 4 * n), bf16)
    m.big[zero_rows, :] = jnp.zeros((full - rows, 4 * n), bf16)
    m.acc[zero_rows, :] = jnp.zeros((full - rows, width), f32)
    m.mid[zero_rows, :] = jnp.zeros((full - rows, width), f32)
    m.logs = m.acc.at[:, pl.ds(0, 128)]
    m.logs[0:rows, :] = jnp.zeros((rows, 128), f32)
    m.vsum[...] = jnp.zeros(m.vsum.shape, f32)
    m.vacc[...] = jnp.zeros(m.vacc.shape, f32)
    for cp in loads[3:6]:
        cp.wait()
    tail = pl.ds(length, full - length)
    m.xs[tail, :] = jnp.zeros((full - length, width), bf16)
    m.gr[tail, :] = jnp.zeros((full - length, width), bf16)
    m.row[...] = jnp.zeros(m.row.shape, f32)
    m.row[0:1, 0:length] = m.tv[pl.ds(w.t, 1), :].astype(f32)
    ok = jnp.broadcast_to(m.row[0:1, :], (128, full)).T
    m.rm[...] = (ok * m.image[w.t].astype(f32)).astype(bf16)
    m.kb[...] = jnp.where((ok > 0) | (iota((full, 128), 0) == 0), 0.0, -1e9).astype(bf16)
    for i in range(dp - 1):
        vec_copy(i).wait()
    bias_copy.wait()
    m.vecs[...] = m.vbuf[0].astype(f32) + m.vbuf[1].astype(f32)
    m.qb[...] = jnp.zeros(m.qb.shape, f32)
    for side in (0, 1):
        b = m.bbuf[side].astype(f32)
        for r in range(4):
            at = (r // 2) * 4 + side * 2 + r % 2
            m.ub[at : at + 1, :] = b[r : r + 1]
        for i in (0, 1):
            at = 2 * i + side
            m.qb[at : at + 1, 0:blk] = b[4:5, i * blk : (i + 1) * blk]
            m.qb[at : at + 1, 2 * blk : 3 * blk] = b[5:6, i * blk : (i + 1) * blk]

    @pl.loop(0, full // ch)
    def _(r):
        rs = tile(r, ch)
        unit, _ = normalize(m.xs[rs, :].astype(f32))
        m.ln[rs, :] = (unit * m.vecs[0:1, :] + m.vecs[1:2, :]).astype(bf16)
        m.gr[rs, :] = (m.gr[rs, :].astype(f32) * m.rm[rs, 0:1].astype(f32)).astype(bf16)

    plan.after("pre1")

    def turn_copies(k):
        tt, lhs = m.turn, (m.lhs1, m.lhs3, m.lhs2, m.lhs3)[k]
        keep = pltpu.make_async_copy(tt.at[:, w.core], lhs.at[:, :, pl.ds(0, full)], m.t_sem.at[k])
        give = rcopy(
            tt.at[:, 1 - w.core], lhs.at[:, :, pl.ds(full, full)], m.t_s.at[k], m.t_r.at[k], w.sibling
        )
        return keep, give

    def turn(src, k):
        @pl.loop(0, width // 256)
        def _(j):
            m.turn[tile(j, 2)] = src[:, tile(j, 256)].T.reshape(2, 2, share, full)

        for cp in turn_copies(k):
            cp.start()

    def turned(k):
        for cp in turn_copies(k):
            cp.wait()

    turn(m.ln, 0)
    plan.after("pre2")
    turned(0)
    turn(m.gr, 1)
    plan.after("pre3")

    def at_cols(j, lo, size):
        return pl.ds(pl.multiple_of(j * n + lo, 128), size)

    def qkv_stream(i):
        def body(j, slot):
            p = mul(m.ln[0:rows, :], m.wt[slot], NN) + m.qb[pl.ds(2 * i + j, 1), :]
            p = p.astype(bf16).astype(f32)
            p = jnp.where(iota(p.shape, 1) < blk, p * HEAD_DIM**-0.5, p)
            m.qkvm[0:rows, at_cols(2 * i + j, 0, 3 * blk)] = p.astype(bf16)
            plan.tick(j, "qk", 2 * i, 2)

        src = lambda j: m.w1.at[i, :, tile(j, 3 * blk)]
        return stream(2, [(src, lambda slot: m.wt.at[slot])], m.s_sem, body)

    for i in (0, 1):
        begin, run = qkv_stream(i)
        begin()
        run()

        @pl.loop(0, 4)
        def _(j, i=i):
            attend_pair(m, 4 * i + j, rows, full, blk)
            plan.tick(j, "at", 4 * i, 4)

    def w_stream(ref, body):
        src = lambda j: ref.at[:, tile(j, 256), :]
        dst = lambda slot: m.wn.at[slot, :, :, pl.ds(0, ref.shape[2])]
        return stream(width // 256, [(src, dst)], m.s_sem, body)

    def out_cols(k):
        return (k % 2) * (2 * blk) + (k // 2) * blk

    def out_tile(j, slot):
        ds = tile(j, 256)
        total = m.xs[0:rows, ds].astype(f32) + m.vecs[2:3, ds]
        for k in range(4):
            own = m.qkvm[0:rows, k * n + 3 * blk : (k + 1) * n]
            total += mul(own, m.wn[slot, 0, :, out_cols(k) : out_cols(k) + blk], NT)
        m.mid[0:rows, ds] = total
        plan.tick(j, "out", 0, 4)

    out_src = lambda j: m.wo.at[tile(j, 256), :]
    out_dst = lambda slot: m.wn.at[slot, 0, :, pl.ds(0, 4 * blk)]
    begin, run = stream(width // 256, [(out_src, out_dst)], m.s_sem, out_tile)
    begin()
    m.lt[...] = m.logs[...].T[0 : m.lt.shape[0], :]
    run()
    mid_out = pltpu.make_async_copy(m.mid, m.mid_o, m.l_sem.at[0])
    mid_out.start()

    @pl.loop(0, full // ch)
    def _(r):
        rs = tile(r, ch)
        unit, _ = normalize(m.mid[rs, :])
        m.ln[rs, :] = (unit * m.vecs[3:4, :] + m.vecs[4:5, :]).astype(bf16)

    plan.after("ln2")
    turned(1)
    turn(m.ln, 2)
    plan.after("turn")

    def halves(ref, cs):
        return ref.at[pl.ds(0, full), cs], ref.at[pl.ds(full, full), cs]

    def act_copy(j):
        here, there = halves(m.big, tile(j, cols))
        return rcopy(here, there, m.a_s.at[j], m.a_r.at[j], w.sibling)

    def act_save(j):
        cs = tile(j, cols)
        return pltpu.make_async_copy(m.big.at[pl.ds(0, full), cs], m.act_o.at[:, cs], m.a_sem.at[0, j])

    def slope_save(j):
        return pltpu.make_async_copy(m.st.at[j % 2], m.slope_o.at[:, tile(j, cols)], m.a_sem.at[1, j])

    def up_stream(i):
        def body(j, slot):
            k = 4 * i + j
            cs = tile(k, cols)
            hidden = mul(m.ln[0:rows, :], m.wt[slot, :, 0:cols], NN) + m.ub[pl.ds(k, 1), :]
            phi = 0.5 * (1.0 + lax.erf(hidden * 0.7071067811865476))
            m.big[0:rows, cs] = (hidden * phi).astype(bf16)
            slope = phi + hidden * jnp.exp(-0.5 * hidden * hidden) * 0.3989422804014327

            @pl.when(k >= 2)
            def _():
                slope_save(k - 2).wait()

            m.st[k % 2, 0:rows, :] = slope.astype(bf16)
            for cp in (act_copy(k), act_save(k), slope_save(k)):
                cp.start()
            plan.tick(j, "up", 4 * i, 4)

        src = lambda j: m.w2.at[i, :, tile(j, cols)]
        return stream(4, [(src, lambda slot: m.wt.at[slot, :, pl.ds(0, cols)])], m.s_sem, body)

    def product(lhs, src):
        return mul(lhs[...].reshape(w.ring * share, 2 * full), m.big[:, src], NN).astype(bf16)

    m.st[:, zero_rows, :] = jnp.zeros((2, full - rows, cols), bf16)
    for i in (0, 1):
        begin, run = up_stream(i)
        begin()
        run()
        @pl.loop(0, 2)
        def _(j, i=i):
            for k in (0, 1):
                act_copy(4 * i + 2 * j + k).wait()
            m.part[i, :, :, tile(j, n)] = product(m.lhs3, tile(2 * i + j, n)).reshape(w.ring, share, n)
            plan.tick(j, "gw", 2 * i, 2)

    pl.semaphore_signal(m.clear, inc=1, device_id=w.sibling, device_id_type=MESH)

    def dh_copy(j):
        here, there = halves(m.big, tile(j, cols))
        return rcopy(here, there, m.h_s.at[j], m.h_r.at[j], w.sibling)

    def dh_stream(i):
        def body(j, slot):
            k = 4 * i + j
            d = mul(m.gr[0:rows, :], m.wt[slot, :, 0:cols], NN) * m.st[slot, 0:rows, :].astype(f32)
            d = d.astype(bf16)
            m.big[0:rows, tile(k, cols)] = d
            nat = (j // 2) * 4 + i * 2 + j % 2
            m.vsum[pl.ds(8 + nat // 2, 1), tile(nat % 2, cols)] = jnp.sum(d.astype(f32), axis=0, keepdims=True)
            dh_copy(k).start()
            plan.tick(j, "dh", 4 * i, 4)

        return stream(
            4,
            [
                (lambda j: m.w3.at[i, :, tile(j, cols)], lambda slot: m.wt.at[slot, :, pl.ds(0, cols)]),
                (lambda j: m.slope_o.at[:, tile(4 * i + j, cols)], lambda slot: m.st.at[slot]),
            ],
            m.s_sem,
            body,
        )

    for k in (6, 7):
        slope_save(jnp.int32(k)).wait()

    @pl.loop(0, 8)
    def _(j):
        act_save(j).wait()

    m.ln[zero_rows, :] = jnp.zeros((full - rows, width), bf16)
    pl.semaphore_wait(m.clear, 1)
    turned(2)

    def second_tile(j, slot):
        ds = tile(j, 256)
        m.acc[0:rows, ds] = mul(m.big[0:rows, 0 : 2 * n], m.wn[slot, 0], NT) + mul(
            m.big[0:rows, 2 * n :], m.wn[slot, 1], NT
        )
        plan.tick(j, "ds", 0, 4)

    for i in (0, 1):
        begin, run = dh_stream(i)
        begin()
        run()
        if i:
            begin, run = w_stream(m.w2, second_tile)
            begin()

        @pl.loop(0, 2)
        def _(j, i=i):
            for k in (0, 1):
                dh_copy(4 * i + 2 * j + k).wait()
            m.part[2 + i, :, :, tile(j, n)] = product(m.lhs2, tile(2 * i + j, n)).reshape(w.ring, share, n)
            plan.tick(j, "gu", 2 * i, 2)

    run()

    def mixed_tile(j, slot):
        m.ln[0:rows, tile(j, blk)] = mul(m.gr[0:rows, :], m.wt[slot, :, 0:blk], NN).astype(bf16)
        plan.tick(j, "mx", 0, 4)

    begin, run = stream(
        4,
        [(lambda j: m.wo.at[:, pl.ds(pl.multiple_of(out_cols(j), 128), blk)], lambda slot: m.wt.at[slot, :, pl.ds(0, blk)])],
        m.s_sem,
        mixed_tile,
    )
    begin()
    mid_out.wait()

    def fold(k, x):
        m.vacc[k] += jnp.sum(x.reshape(ch // 8, 8, width), axis=0)

    def norm_back(unit, scaled, gain, up):
        weighted = up * gain
        return scaled * (
            weighted
            - jnp.mean(weighted, axis=-1, keepdims=True)
            - unit * jnp.mean(weighted * unit, axis=-1, keepdims=True)
        )

    @pl.loop(0, full // ch)
    def _(r):
        rs = tile(r, ch)
        unit, scaled = normalize(m.mid[rs, :])
        up = m.acc[rs, :]
        grad = m.gr[rs, :].astype(f32)
        down = norm_back(unit, scaled, m.vecs[3:4, :], up) + grad
        m.mid[rs, :] = down
        m.gr[rs, :] = down.astype(bf16)
        fold(2, down)
        fold(3, up * unit)
        fold(4, up)
        fold(5, grad)

    plan.after("nb")
    turn(m.gr, 3)
    plan.after("tb")
    run()

    def lanes_mixed(k):
        return pl.ds(k * n + 3 * blk, blk)

    for k in range(4):
        m.big[0:full, lanes_mixed(k)] = m.qkvm[:, lanes_mixed(k)]
    turned(3)

    def mixed_copy(k):
        here, there = halves(m.big, lanes_mixed(k))
        return rcopy(here, there, m.x_s.at[k], m.x_r.at[k], w.sibling)

    for k in range(4):
        mixed_copy(k).start()

    def q_copy(k):
        here, there = halves(m.big, at_cols(k, 0, 3 * blk))
        return rcopy(here, there, m.q_s.at[k], m.q_r.at[k], w.sibling)

    def weights(i, part):
        @pl.loop(0, 2)
        def _(j):
            k = 2 * i + j
            q_copy(k).wait()
            grad = product(m.lhs1, at_cols(k, 0, 3 * blk))
            part[:, :, tile(j, 3 * blk)] = grad.reshape(w.ring, share, 3 * blk)
            plan.tick(j, "ga", 2 * i, 2)

    @pl.loop(0, width // 128)
    def _(j):
        attend_back(m, j, rows, full, blk)

        @pl.when(j % 2 == 1)
        def _():
            q_copy(j // 2).start()

        plan.tick(j, "ab", 0, 8)

        @pl.when(j == 1)
        def _():
            sums7[0].drain()
            for k in range(4):
                mixed_copy(k).wait()
                grad = product(m.lhs3, lanes_mixed(k))
                m.part[0, :, :, out_cols(k) : out_cols(k) + blk] = grad.reshape(w.ring, share, blk)
            plan.after("og")

        @pl.when(j == 4)
        def _():
            sums7[1].drain()
            weights(0, m.part.at[1])

    def first_tile(j, slot):
        total = jnp.zeros((rows, 256), f32)
        for k in range(4):
            lo = (k % 2) * (3 * blk)
            total += mul(m.big[0:rows, k * n : k * n + 3 * blk], m.wn[slot, k // 2, :, lo : lo + 3 * blk], NT)
        m.acc[0:rows, tile(j, 256)] = total
        plan.tick(j, "df", 0, 4)

    begin, run = w_stream(m.w1, first_tile)
    begin()
    weights(1, m.part5)
    act_in = pltpu.make_async_copy(m.act_o, m.big.at[pl.ds(full, full)], m.l_sem.at[1])
    act_in.start()
    run()

    def block_tile(j, slot):
        ds = tile(j, 256)
        act = m.big.at[pl.ds(full, rows)]
        m.acc[0:rows, ds] = mul(act[:, 0 : 2 * n], m.wn[slot, 0], NT) + mul(act[:, 2 * n :], m.wn[slot, 1], NT)
        plan.tick(j, "bo", 0, 4)

    begin, run = w_stream(m.w3, block_tile)
    begin()

    @pl.loop(0, full // ch)
    def _(r):
        rs = tile(r, ch)
        unit, scaled = normalize(m.xs[rs, :].astype(f32))
        up = m.acc[rs, :]
        m.mid[rs, :] += norm_back(unit, scaled, m.vecs[0:1, :], up)
        fold(0, up * unit)
        fold(1, up)

    m.vsum[0:6, :] = jnp.sum(m.vacc[...], axis=1)
    gt_out = pltpu.make_async_copy(m.mid.at[pl.ds(0, length)], m.gt, m.l_sem.at[3])
    gt_out.start()

    def sum_copy(s):
        return rcopy(m.vsum, m.vswap.at[s], m.b_s.at[s], m.b_r.at[s], flips[s])

    def sum_step(s):
        if s:
            sum_copy(s - 1).wait()
            m.vsum[...] += m.vswap[s - 1]
        if s < len(flips):
            sum_copy(s).start()

    sum_step(0)
    plan.after("ln1")
    act_in.wait()
    run()
    sum_step(1)
    plan.after("v1")
    gt_out.wait()
    mid_in = pltpu.make_async_copy(m.mid_o, m.mid, m.l_sem.at[4])
    mid_in.start()
    sum_step(2)
    plan.after("v2")
    mid_in.wait()

    @pl.loop(0, full // ch)
    def _(r):
        rs = tile(r, ch)
        m.xs[rs, :] = (m.rm[rs, 0:1].astype(f32) * (m.mid[rs, :] + m.acc[rs, :] + m.vecs[5:6, :])).astype(bf16)

    bo_out = pltpu.make_async_copy(m.xs.at[pl.ds(0, length)], m.bo, m.l_sem.at[0])
    bo_out.start()
    sum_step(3)
    plan.after("v3")
    sum_step(4)
    plan.after("v4")
    sum_step(5)
    outs = [
        pltpu.make_async_copy(m.vsum, m.gv, m.l_sem.at[1]),
        pltpu.make_async_copy(m.og, m.go, m.l_sem.at[2]),
    ]
    outs[0].start()
    plan.after("fin")
    outs[1].start()
    for g in gathers + sums7[2:]:
        g.drain()
    bo_out.wait()
    for cp in outs:
        cp.wait()


LAYER_PLAN = {
    "go": (0, 200, 300),
    "pre1": (1, 100, 2),
    "pre3": (301, 101, 3, 102, 5, 302, 4, 6, 7, 201, 103, 202, 400, 8, 9, 10),
    "qk0": (105, 204, 303),
    "at0": (500, 203, 104),
    "at1": (401, 107),
    "at2": (304, 106),
    "at3": (108, 109, 305, 205, 501, 402, 110),
    "qk3": (306, 207, 600),
    "at5": (307, 404, 403),
    "at6": (206, 208, 209, 308, 502),
    "at7": (210, 309, 601),
    "out2": (405,),
    "ln2": (503,),
    "turn": (310,),
    "up1": (407, 406, 602),
    "up3": (505, 408, 409),
    "gw1": (700, 603, 410),
    "up7": (507, 604, 605, 504, 506, 701),
    "gw3": (508, 509, 800, 606, 607, 702, 703, 608, 510),
    "dh3": (801,),
    "gu0": (704, 705, 609),
    "gu1": (900, 802, 803, 610),
    "dh7": (804, 706, 707, 901),
    "ds0": (708, 1000, 805),
    "ds2": (902, 903, 806, 808),
    "ds3": (904,),
    "nb": (807, 1001, 709),
    "ab0": (905, 906, 809),
    "ab1": (1002, 1003, 710),
    "og": (1100,),
    "ab3": (907, 1101, 810),
    "ab4": (1004, 1006, 1005, 1102),
    "ga1": (1200, 1104, 1103),
    "ab5": (1008,),
    "ab6": (1106, 1007, 1201, 1105),
    "ga3": (1300, 908, 909, 1202, 1203),
    "df1": (1301, 1107),
    "df3": (1302, 1303, 1204, 1009, 1205),
    "ln1": (1206, 1304, 1305, 1108, 1109),
    "bo0": (910, 1207),
    "bo1": (1306, 1307),
    "bo3": (1010, 1308, 1208, 1209),
    "v2": (1110, 1309),
    "v4": (1210, 1310),
}


def layer(args, dp, length, width, n, share):
    rows, full = -(-length // 16) * 16, -(-length // 128) * 128
    cols, blk = n // 2, n // 4
    ring = dp // 2
    far = ring // 2
    depth = share * dp
    heads = width // HEAD_DIM
    outers = [128 * o for o in OUTER[7:]]
    a, b = max(outers[:4]), min(outers[:4])
    a5, b5 = outers[6], 3 * blk - outers[6]
    steps = dp.bit_length()
    V, dma = pltpu.VMEM, pltpu.SemaphoreType.DMA
    S = jax.ShapeDtypeStruct
    out = dict(
        w1=S((2, depth, 6 * blk), bf16),
        wo=S((depth, 4 * blk), bf16),
        w2=S((2, depth, 2 * n), bf16),
        w3=S((2, depth, 2 * n), bf16),
        mid_o=S((full, width), f32),
        act_o=S((full, 4 * n), bf16),
        slope_o=S((full, 4 * n), bf16),
        bo=S((length, width), bf16),
        gt=S((length, width), f32),
        go=S((3, share, 2 * n), f32),
        gv=S((16, width), f32),
    )
    scratch = dict(
        sh1=V((2, share, 3 * blk), bf16),
        iwv=V((3, share, cols), bf16),
        sixv=V((6, 1, share), bf16),
        ubv=V((2 * n // 128, 128), bf16),
        biasf=V((8, cols), f32),
        ibv=V((2, cols), bf16),
        vecf=V((8, 128), f32),
        packv=V((8, cols), bf16),
        tv=V((2, length), jnp.int32),
        row=V((8, full), f32),
        vec=V((8, 128), bf16),
        kb=V((full, 128), bf16),
        rm=V((full, 128), bf16),
        vbuf=V((2, 8, width), bf16),
        bbuf=V((2, 8, cols), bf16),
        vecs=V((8, width), f32),
        ub=V((8, cols), f32),
        qb=V((8, 3 * blk), f32),
        xs=V((full, width), bf16),
        gr=V((full, width), bf16),
        ln=V((full, width), bf16),
        qkvm=V((full, 4 * n), bf16),
        lt=V((heads, full), f32),
        mid=V((full, width), f32),
        acc=V((full, width), f32),
        big=V((2 * full, 4 * n), bf16),
        st=V((2, full, cols), bf16),
        turn=V((ring, 2, share, full), bf16),
        lhs1=V((ring, share, 2 * full), bf16),
        lhs2=V((ring, share, 2 * full), bf16),
        lhs3=V((ring, share, 2 * full), bf16),
        wt=V((2, depth, 3 * blk), bf16),
        wn=V((2, 2, 256, 2 * n), bf16),
        part=V((4, ring, share, 2 * n), bf16),
        ry=V((4, ring, share, a), bf16),
        rr=V((4, far, share, 2 * n - b), bf16),
        rl=V((4, far, share, 2 * n - b), bf16),
        rb=V((4, share, n - b), bf16),
        part5=V((ring, share, 6 * blk), bf16),
        ry5=V((ring, share, a5), bf16),
        rr5=V((far, share, a5 + 2 * b5), bf16),
        rl5=V((far, share, a5 + 2 * b5), bf16),
        rb5=V((share, b5), bf16),
        og=V((3, share, 2 * n), f32),
        vsum=V((16, width), f32),
        vacc=V((6, 8, width), f32),
        vswap=V((steps, 16, width), f32),
        ring_s=dma((7, 2 * (far + 1))),
        ring_r=dma((7, 2 * (far + 1))),
        y_s=dma((7, 2 * far + 1)),
        y_r=dma((7, 2 * far + 1)),
        c_s=dma((7, 4 * far + 2)),
        c_r=dma((7, 4 * far + 2)),
        k_sem=dma((7,)),
        sy_s=dma((7, ring + 1)),
        sy_r=dma((7, ring + 1)),
        sr_s=dma((7, 2 * far)),
        sr_r=dma((7, 2 * far)),
        v_s=dma((dp,)),
        v_r=dma((dp,)),
        b_s=dma((steps,)),
        b_r=dma((steps,)),
        l_sem=dma((7,)),
        x_sem=dma((6,)),
        s_sem=dma((4, 2)),
        t_sem=dma((4,)),
        t_s=dma((4,)),
        t_r=dma((4,)),
        a_s=dma((8,)),
        a_r=dma((8,)),
        a_sem=dma((2, 8)),
        h_s=dma((8,)),
        h_r=dma((8,)),
        q_s=dma((4,)),
        q_r=dma((4,)),
        x_s=dma((4,)),
        x_r=dma((4,)),
        clear=pltpu.SemaphoreType.REGULAR,
    )
    names = LAYER_IN + tuple(out) + tuple(scratch)
    hbm = pl.BlockSpec(memory_space=pl.ANY)
    specs = [pl.BlockSpec(memory_space=pltpu.SMEM) if k == "image" else hbm for k in LAYER_IN]
    got = pl.pallas_call(
        functools.partial(layer_kernel, dp, rows, names, LAYER_PLAN),
        out_shape=list(out.values()),
        in_specs=specs,
        out_specs=[hbm] * len(out),
        scratch_shapes=list(scratch.values()),
        compiler_params=pltpu.CompilerParams(collective_id=1, has_side_effects=True, vmem_limit_bytes=VM_LIMIT),
        name="layer",
    )(*args)
    return types.SimpleNamespace(**dict(zip(out, got)))


def place_kernel(bo, gt, go, gv, *refs):
    bo_o, gt_o, iw_o, ow_o, uw_o, dw_o, ib_o, ub_o = refs[:8]
    vec_o, (bov, gtv, g, vs, iwv, ibv, ubv, vecv, sem) = refs[8:14], refs[14:]
    d, t = lax.axis_index("dp"), lax.axis_index("tensor")
    share, wide = g.shape[1:]
    n, blk = wide // 2, wide // 8
    cols = 2 * blk
    ins = [
        pltpu.make_async_copy(go, g, sem.at[0]),
        pltpu.make_async_copy(gt, gtv, sem.at[1]),
        pltpu.make_async_copy(bo, bov, sem.at[2]),
        pltpu.make_async_copy(gv, vs, sem.at[3]),
    ]
    for cp in ins:
        cp.start()
    outs = []

    def send(src, dst):
        cp = pltpu.make_async_copy(src, dst, sem.at[4 + len(outs)])
        cp.start()
        outs.append(cp)

    ins[0].wait()
    send(g.at[1], uw_o)
    send(g.at[0], dw_o)
    for i in (0, 1):
        part = slice(i * blk, (i + 1) * blk)
        for s in range(3):
            at = (3 * i + s) * blk
            iwv[s, :, part] = g[2, :, at : at + blk]
    send(iwv, iw_o)
    send(g.at[2, :, pl.ds(6 * blk, cols)], ow_o)
    ins[1].wait()
    send(gtv, gt_o)
    ins[2].wait()
    send(bov, bo_o)
    ins[3].wait()
    ibv[...] = vs[6:8, pl.ds(pl.multiple_of(t * cols, 128), cols)]
    send(ibv, ib_o)
    width = vs.shape[1]
    per = width // 128
    half = wide // width
    up = jnp.where(t == 0, vs[8 : 8 + half, :], vs[8 + half : 8 + 2 * half, :])
    for r in range(wide // 128):
        lo = (r % per) * 128
        ubv[r : r + 1, :] = up[r // per : r // per + 1, lo : lo + 128]
    send(ubv, ub_o)
    own = vs[0:8, pl.ds(pl.multiple_of((d // 2) * 128, 128), 128)]
    own = jnp.where(d % 2 == 0, own, pltpu.roll(own, share, 1))
    for i in range(6):
        vecv[i] = own[i : i + 1, 0:share]
        send(vecv.at[i], vec_o[i])
    for cp in outs:
        cp.wait()


def place(r, share, n):
    S = jax.ShapeDtypeStruct
    length, width = r.gt.shape
    cols = n // 2
    hbm = pl.BlockSpec(memory_space=pl.ANY)
    out = [
        S((length, width), bf16),
        S((length, width), f32),
        S((3, share, cols), f32),
        S((share, cols), f32),
        S((share, 2 * n), f32),
        S((share, 2 * n), f32),
        S((2, cols), f32),
        S((2 * n // 128, 128), f32),
    ] + [S((1, share), f32)] * 6
    V = pltpu.VMEM
    return pl.pallas_call(
        place_kernel,
        out_shape=out,
        in_specs=[hbm] * 4,
        out_specs=[hbm] * 14,
        scratch_shapes=[
            V((length, width), bf16),
            V((length, width), f32),
            V((3, share, 2 * n), f32),
            V((16, width), f32),
            V((3, share, cols), f32),
            V((2, cols), f32),
            V((2 * n // 128, 128), f32),
            V((6, 1, share), f32),
            pltpu.SemaphoreType.DMA((18,)),
        ],
        compiler_params=pltpu.CompilerParams(vmem_limit_bytes=VM_LIMIT),
        name="place",
    )(r.bo, r.gt, r.go, r.gv)


def paired_device(
    tokens, cotangent, token_valid, image_valid, first_gain, first_shift, input_weight, input_bias, output_weight,
    output_bias, second_gain, second_shift, up_weight, up_bias, down_weight, down_bias,
):
    dp = lax.axis_size("dp")
    length, width = tokens.shape
    share, wide = up_weight.shape
    n = wide // 2
    vectors = (first_gain, first_shift, output_bias, second_gain, second_shift, down_bias)
    args = tuple(v.reshape(1, share) for v in vectors) + (
        up_bias.reshape(-1, 128),
        input_bias,
        input_weight.transpose(1, 0, 2),
        output_weight.T,
        up_weight,
        down_weight.T,
        tokens,
        cotangent,
        token_valid,
        image_valid,
    )
    r = layer(args, dp, length, width, n, share)
    block_out, grad_tokens, g_in, g_out, g_up, g_down, g_in_bias, g_up_bias, *g_vec = place(r, share, n)
    g_vec = [v.reshape(share) for v in g_vec]
    return (
        block_out,
        grad_tokens,
        g_vec[0],
        g_vec[1],
        g_in.transpose(1, 0, 2),
        g_in_bias,
        g_out.T,
        g_vec[2],
        g_vec[3],
        g_vec[4],
        g_up,
        g_up_bias.reshape(wide),
        g_down.T,
        g_vec[5],
    )


def solution(mesh):
    in_specs = (
        P(("dp", "tensor"), None),
        P(("dp", "tensor"), None),
        P("dp", None),
        P("dp"),
        P("dp"),
        P("dp"),
        P("dp", None, "tensor"),
        P(None, "tensor"),
        P("tensor", "dp"),
        P("dp"),
        P("dp"),
        P("dp"),
        P("dp", "tensor"),
        P("tensor"),
        P("tensor", "dp"),
        P("dp"),
    )
    out_specs = (
        P(("dp", "tensor"), None),
        P(("dp", "tensor"), None),
        P("dp"),
        P("dp"),
        P("dp", None, "tensor"),
        P(None, "tensor"),
        P("tensor", "dp"),
        P("dp"),
        P("dp"),
        P("dp"),
        P("dp", "tensor"),
        P("tensor"),
        P("tensor", "dp"),
        P("dp"),
    )
    ready = mesh.shape["tensor"] == 2 and mesh.shape["dp"] == 16
    body = paired_device if ready else general_device
    return jax.shard_map(
        body, mesh=mesh, in_specs=in_specs, out_specs=out_specs, check_vma=False
    )
```
